32 devices in a mesh: wt: 4 (over y, x), ctx: 8 (over z, core).
Axes of the slice: x: 2, y: 2, z: 4, core: 2. Of those that a mesh axis runs over, the one named last changes fastest.
Arguments:
- tokens: bfloat16 [4, 2048, 768], P('wt', 'ctx'), may hold values from -6 to 6
- pairing: int32 [12], replicated, may hold values from 0 to 1, as said below
- w_qkv: bfloat16 [768, 2304], P('wt'), may hold values from -0.21875 to 0.21875
- bias_q: bfloat16 [768], P('wt'), may hold values from -1.75 to 1.75
- bias_v: bfloat16 [768], P('wt'), may hold values from -1.75 to 1.75
- w_out: bfloat16 [768, 768], P('wt'), may hold values from -4 to 4
- bias_out: bfloat16 [768], P('wt'), may hold values from -1.75 to 1.75
- gain_one: bfloat16 [768], P('wt'), may hold values from 0.5 to 1.5
- shift_one: bfloat16 [768], P('wt'), may hold values from -1.75 to 1.75
- w_up: bfloat16 [768, 3072], P('wt'), may hold values from -0.21875 to 0.21875
- bias_up: bfloat16 [3072], P('wt'), may hold values from -1.75 to 1.75
- w_down: bfloat16 [3072, 768], P('wt'), may hold values from -0.109375 to 0.109375
- bias_down: bfloat16 [768], P('wt'), may hold values from -1.75 to 1.75
- gain_two: bfloat16 [768], P('wt'), may hold values from 0.5 to 1.5
- shift_two: bfloat16 [768], P('wt'), may hold values from -1.75 to 1.75
- cotangent: bfloat16 [4, 2048, 768], P('wt', 'ctx'), may hold values from -6 to 6
Outputs:
- output: float32 [4, 2048, 768], P('wt', 'ctx')
- grad_tokens: float32 [4, 2048, 768], P('wt', 'ctx')
- grad_w_qkv: float32 [768, 2304], P('wt')
- grad_bias_q: float32 [768], P('wt')
- grad_bias_v: float32 [768], P('wt')
- grad_w_out: float32 [768, 768], P('wt')
- grad_bias_out: float32 [768], P('wt')
- grad_gain_one: float32 [768], P('wt')
- grad_shift_one: float32 [768], P('wt')
- grad_w_up: float32 [768, 3072], P('wt')
- grad_bias_up: float32 [3072], P('wt')
- grad_w_down: float32 [3072, 768], P('wt')
- grad_bias_down: float32 [768], P('wt')
- grad_gain_two: float32 [768], P('wt')
- grad_shift_two: float32 [768], P('wt')
The draws below stay inside these ranges and needn't reach their ends.
Inputs may be any that keep to these rules, and one draw needn't show every extreme that they name: pairing[h] is 1 where head h pairs each block of 1024 queries with the other block of its sequence, 0 where with its own; exactly half of the 12 heads have 1.
All inputs are finite; a program needn't handle non-finite values.
Results may differ from the reference program's by a relative error of at most 0.023.
Values may be sent and summed in bfloat16 or wider, within the bound.
A program may use at most 256 MiB of HBM per device.

```python
import jax
import jax.numpy as jnp
from jax import lax

D = 768
HEADS = 12
HEAD = 64
FF = 3072
SEQ_LEN = 2048
SEQS = 4


def draw_pairing(key, part):
    order = jax.random.permutation(key, HEADS)
    return (order % 2).astype(jnp.int32)


def block_scale(stream_key, dims, pieces, least, largest):
    gain, own = 1.0, jax.random.fold_in(stream_key, 6)
    for dim, blocks in pieces:
        steps = jnp.exp(jax.random.uniform(jax.random.fold_in(own, dim), (blocks,), jnp.float32, least / len(pieces), largest / len(pieces)))
        gain = gain * jnp.repeat(steps, dims[dim] // blocks).reshape([-1 if axis == dim else 1 for axis in range(len(dims))])
    return gain


def scatter_about(rng, shape, scale, bound, shards=(), dtype=jnp.bfloat16):
    array = scale * jax.random.normal(rng, shape, jnp.float32)
    if shards:
        array = array * block_scale(rng, shape, shards, -0.22, 0.18)
    return jnp.clip(array, -bound, bound).astype(dtype)


def setup_inputs(seed: int = 0) -> dict:
    splits = jax.random.split(jax.random.key(seed), 17)
    tokens = scatter_about(splits[0], (SEQS, SEQ_LEN, D), 1.0, 6.0, ((0, 4), (1, 8)))
    pairing = draw_pairing(jax.random.fold_in(splits[16], 71), 0)
    w_qkv = scatter_about(splits[2], (D, 3 * D), D ** -0.5, 0.21875, ((0, 4),))
    bias_q = scatter_about(splits[3], (D,), 0.3, 1.75, ((0, 4),))
    bias_v = scatter_about(splits[4], (D,), 0.3, 1.75, ((0, 4),))
    w_out = scatter_about(splits[5], (D, D), ((SEQ_LEN // 6) ** 0.5 * D ** -0.5), 4.0, ((0, 4),))
    bias_out = scatter_about(splits[6], (D,), 0.3, 1.75, ((0, 4),))
    gain_one = jnp.clip(1.0 + 0.1 * jax.random.normal(splits[7], (D,), jnp.float32), 0.5, 1.5).astype(jnp.bfloat16)
    shift_one = scatter_about(splits[8], (D,), 0.3, 1.75, ((0, 4),))
    w_up = scatter_about(splits[9], (D, FF), D ** -0.5, 0.21875, ((0, 4),))
    bias_up = scatter_about(splits[10], (FF,), 0.3, 1.75, ((0, 4),))
    w_down = scatter_about(splits[11], (FF, D), FF ** -0.5, 0.109375, ((0, 4),))
    bias_down = scatter_about(splits[12], (D,), 0.3, 1.75, ((0, 4),))
    gain_two = jnp.clip(1.0 + 0.1 * jax.random.normal(splits[13], (D,), jnp.float32), 0.5, 1.5).astype(jnp.bfloat16)
    shift_two = scatter_about(splits[14], (D,), 0.3, 1.75, ((0, 4),))
    cotangent = scatter_about(splits[15], (SEQS, SEQ_LEN, D), 1.0, 6.0, ((0, 4), (1, 8)))
    return dict(tokens=tokens, pairing=pairing, w_qkv=w_qkv, bias_q=bias_q, bias_v=bias_v, w_out=w_out, bias_out=bias_out, gain_one=gain_one, shift_one=shift_one, w_up=w_up, bias_up=bias_up, w_down=w_down, bias_down=bias_down, gain_two=gain_two, shift_two=shift_two, cotangent=cotangent)


@jax.custom_vjp
def low(v):
    return lax.optimization_barrier(v.astype(jnp.bfloat16)).astype(jnp.float32)

@jax.custom_vjp
def low_back(v):
    return v

def low_keep(v):
    return (low(v), None)

def low_pass(kept, grad):
    return (grad,)

def back_keep(v):
    return (v, None)

def back_low(kept, grad):
    return (low(grad),)
low.defvjp(low_keep, low_pass)
low_back.defvjp(back_keep, back_low)
highest = lax.Precision.HIGHEST

def norm_rows(values, gains, shifts):
    average = lax.optimization_barrier(jnp.mean(values, axis=-1, keepdims=True))
    centred = values - average
    spread = lax.optimization_barrier(jnp.mean(centred * centred, axis=-1, keepdims=True))
    return centred * lax.rsqrt(spread + 1e-12) * gains + shifts

def attend_block(queries, keys_pair, values_pair):
    scores = jnp.einsum('thd,khd->htk', queries, keys_pair, precision=highest) * 0.125
    scores = low_back(scores)
    weights = low(jax.nn.softmax(scores, axis=-1))
    return jnp.einsum('htk,khd->thd', weights, values_pair, precision=highest)

def sequence_layer(tokens_seq, swapped, params):
    w_qkv, bias_q, bias_v, w_out, bias_out, gain_one, shift_one, w_up, bias_up, w_down, bias_down, gain_two, shift_two = params
    length = tokens_seq.shape[0]
    model_width = w_out.shape[0]
    half_len = length // 2
    projected = jnp.dot(tokens_seq, w_qkv, precision=highest)
    projected = projected + jnp.concatenate([bias_q, jnp.zeros_like(bias_q), bias_v])
    projected = low_back(low(projected))
    queries = projected[:, :model_width].reshape(length, HEADS, HEAD)
    key_rows = projected[:, model_width:2 * model_width].reshape(2, half_len, HEADS, HEAD)
    value_rows = projected[:, 2 * model_width:].reshape(2, half_len, HEADS, HEAD)
    flip = (swapped == 1)[None, :, None]
    keys_pair = jnp.stack([jnp.where(flip, key_rows[1], key_rows[0]), jnp.where(flip, key_rows[0], key_rows[1])])
    values_pair = jnp.stack([jnp.where(flip, value_rows[1], value_rows[0]), jnp.where(flip, value_rows[0], value_rows[1])])
    block_rows = min(512, half_len)
    block_count = length // block_rows
    query_blocks = queries.reshape(block_count, block_rows, HEADS, HEAD)
    halves = jnp.arange(block_count) * block_rows // half_len

    def one_block(item):
        block_queries, which_half = item
        return attend_block(block_queries, keys_pair[which_half], values_pair[which_half])
    context = lax.map(jax.checkpoint(one_block), (query_blocks, halves))
    context = low_back(low(context.reshape(length, model_width)))
    branch = low_back(jnp.dot(context, w_out, precision=highest) + bias_out)
    hidden = norm_rows(tokens_seq + branch, gain_one, shift_one)
    pre_active = low_back(jnp.dot(low(hidden), w_up, precision=highest) + bias_up)
    active = low(jax.nn.gelu(pre_active, approximate=False))
    ffn_out = low_back(jnp.dot(active, w_down, precision=highest) + bias_down)
    return norm_rows(hidden + ffn_out, gain_two, shift_two)

def reference(tokens, pairing, w_qkv, bias_q, bias_v, w_out, bias_out, gain_one, shift_one, w_up, bias_up, w_down, bias_down, gain_two, shift_two, cotangent):
    params = tuple((item.astype(jnp.float32) for item in (w_qkv, bias_q, bias_v, w_out, bias_out, gain_one, shift_one, w_up, bias_up, w_down, bias_down, gain_two, shift_two)))
    tokens_f = tokens.astype(jnp.float32)

    def forward(tokens_all, params_all):

        def scan_step(running, tokens_seq):
            return (running, sequence_layer(tokens_seq, pairing, params_all))
        unused, outputs = lax.scan(scan_step, jnp.zeros((), jnp.float32), tokens_all)
        return outputs
    output, pullback = jax.vjp(forward, tokens_f, params)
    grad_tokens, grads = pullback(cotangent.astype(jnp.float32))
    return (output, grad_tokens, grads[0], grads[1], grads[2], grads[3], grads[4], grads[5], grads[6], grads[7], grads[8], grads[9], grads[10], grads[11], grads[12])
```

```python
import jax
import jax.numpy as jnp
from jax import lax
from jax.experimental import pallas as pl
from jax.experimental.pallas import tpu as pltpu
from jax.sharding import PartitionSpec as P

MESH = pl.DeviceIdType.MESH
far_below = -1e30


class Wire:
    def __init__(self, sends, receives, anyone):
        self.sends, self.receives, self.anyone = sends, receives, anyone
        self.numbers, self.started = {}, []

    def number(self, name):
        return self.numbers.setdefault(name, len(self.numbers))

    def send(self, name, source, target, where):
        slot = self.number(name)
        copy = pltpu.make_async_remote_copy(
            src_ref=source,
            dst_ref=target,
            send_sem=self.sends.at[slot],
            recv_sem=self.receives.at[slot],
            device_id=where,
            device_id_type=MESH,
        )
        copy.start()
        self.started.append(copy)

    def arrived(self, name, target):
        slot = self.number(name)
        pltpu.make_async_remote_copy(
            src_ref=target,
            dst_ref=target,
            send_sem=self.sends.at[slot],
            recv_sem=self.receives.at[slot],
            device_id=self.anyone,
            device_id_type=MESH,
        ).wait_recv()

    def close(self):
        for copy in self.started:
            copy.wait_send()
        self.started = []


class Place:
    def __init__(self):
        self.w = w = lax.axis_index("wt")
        self.c = c = lax.axis_index("ctx")
        self.core = core = c % 2
        self.other = 1 - core
        self.nx = w + 1 - 2 * (w % 2)
        self.ny = (w + 2) % 4
        self.nd = 3 - w
        self.sib = (w, c + 1 - 2 * core)
        self.to_x, self.to_y, self.to_d = (self.nx, c), (self.ny, c), (self.nd, c)


def greet(peers):
    barrier = pltpu.get_barrier_semaphore()
    for peer in peers:
        pl.semaphore_signal(barrier, inc=1, device_id=peer, device_id_type=MESH)
    pl.semaphore_wait(barrier, len(peers))


class Part:
    def __init__(self, name, local, full, first, columns, place):
        self.name, self.local, self.full, self.place = name, local, full, place
        self.rows = local.shape[0]
        self.first, self.columns = first, columns // 2

    def piece(self, owner, core, half=None):
        rows, start = self.rows, owner * self.rows
        if half is not None:
            rows = self.rows // 2
            start = start + half * rows
        return self.full.at[
            pl.ds(pl.multiple_of(start, 16), rows),
            pl.ds(pl.multiple_of(self.first + core * self.columns, 128), self.columns),
        ]

    def begin(self, wire):
        pls = self.place
        mine = self.local.at[
            :, pl.ds(pl.multiple_of(self.first + pls.core * self.columns, 128), self.columns)
        ]
        target = self.piece(pls.w, pls.core)
        wire.send(self.name + "a", mine, target, pls.to_x)
        wire.send(self.name + "b", mine, target, pls.to_y)

    def relay(self, wire):
        pls = self.place
        block = self.piece(pls.nx, pls.core)
        wire.arrived(self.name + "a", block)
        half = self.piece(pls.nx, pls.core, 0)
        wire.send(self.name + "c", half, half, pls.to_y)
        wire.send(self.name + "d", block, block, pls.sib)
        block = self.piece(pls.ny, pls.core)
        wire.arrived(self.name + "b", block)
        half = self.piece(pls.ny, pls.core, 1)
        wire.send(self.name + "e", half, half, pls.to_x)
        wire.send(self.name + "f", block, block, pls.sib)

    def share(self, wire):
        pls = self.place
        wire.arrived(self.name + "c", self.piece(pls.nd, pls.core, 0))
        wire.arrived(self.name + "e", self.piece(pls.nd, pls.core, 1))
        block = self.piece(pls.nd, pls.core)
        wire.send(self.name + "g", block, block, pls.sib)

    def finish(self, wire):
        pls = self.place
        wire.arrived(self.name + "d", self.piece(pls.nx, pls.other))
        wire.arrived(self.name + "f", self.piece(pls.ny, pls.other))
        wire.arrived(self.name + "g", self.piece(pls.nd, pls.other))


def gather_kernel(qkv_l, out_l, up_l, down_l, qkv, out, up, down, sends, receives, locals_sem):
    pls = Place()
    wire = Wire(sends, receives, pls.sib)
    width = out.shape[1]
    greet([pls.sib, pls.to_x, pls.to_y])
    parts = [
        Part("kv", qkv_l, qkv, width, 2 * width, pls),
        Part("q", qkv_l, qkv, 0, width, pls),
        Part("o", out_l, out, 0, width, pls),
        Part("u", up_l, up, 0, up.shape[1], pls),
        Part("d", down_l, down, 0, width, pls),
    ]
    parts[0].begin(wire)
    copies = []
    for slot, (local, full) in enumerate(((qkv_l, qkv), (out_l, out), (up_l, up), (down_l, down))):
        rows = local.shape[0]
        copies.append(
            pltpu.make_async_copy(
                local, full.at[pl.ds(pl.multiple_of(pls.w * rows, 16), rows)], locals_sem.at[slot]
            )
        )
        copies[-1].start()
    for index, part in enumerate(parts):
        if index + 1 < len(parts):
            parts[index + 1].begin(wire)
        part.relay(wire)
        if index:
            parts[index - 1].share(wire)
    parts[-1].share(wire)
    for part in parts:
        part.finish(wire)
    for copy in copies:
        copy.wait()
    wire.close()


def gather_weights(w_qkv, w_out, w_up, w_down):
    n = lax.axis_size("wt")
    shapes = [(n * v.shape[0], v.shape[1]) for v in (w_qkv, w_out, w_up, w_down)]
    return pl.pallas_call(
        gather_kernel,
        out_shape=[jax.ShapeDtypeStruct(s, jnp.bfloat16) for s in shapes],
        in_specs=[pl.BlockSpec(memory_space=pl.ANY)] * 4,
        out_specs=[pl.BlockSpec(memory_space=pltpu.VMEM)] * 4,
        scratch_shapes=[
            pltpu.SemaphoreType.DMA((35,)),
            pltpu.SemaphoreType.DMA((35,)),
            pltpu.SemaphoreType.DMA((4,)),
        ],
        compiler_params=pltpu.CompilerParams(
            collective_id=0, has_side_effects=True, vmem_limit_bytes=40 << 20
        ),
        name="gather_weights",
    )(w_qkv, w_out, w_up, w_down)


def passed_along(value, axis, steps):
    count = lax.axis_size(axis)
    pairs = [(source, (source + steps) % count) for source in range(count)]
    return lax.ppermute(value, axis, pairs)


def norm_rows(values, gains, shifts):
    average = jnp.mean(values, axis=-1, keepdims=True)
    centred = values - average
    spread = jnp.mean(centred * centred, axis=-1, keepdims=True)
    return centred * lax.rsqrt(spread + 1e-12) * gains + shifts


def gelu_exact(pre_active):
    return jax.nn.gelu(pre_active, approximate=False)


def scores_of(queries, key_heads):
    return (
        jnp.einsum("thd,khd->htk", queries, key_heads, preferred_element_type=jnp.float32) * 0.125
    )


def unchanged(running):
    return running


def local(
    tokens,
    pairing,
    w_qkv,
    bias_q,
    bias_v,
    w_out,
    bias_out,
    gain_one,
    shift_one,
    w_up,
    bias_up,
    w_down,
    bias_down,
    gain_two,
    shift_two,
    cotangent,
):
    local_params = (
        w_qkv,
        bias_q,
        bias_v,
        w_out,
        bias_out,
        gain_one,
        shift_one,
        w_up,
        bias_up,
        w_down,
        bias_down,
        gain_two,
        shift_two,
    )
    fast = lax.axis_size("wt") == 4 and lax.axis_size("ctx") == 8
    if fast:
        wqkv_g, wout_g, wup_g, wdown_g = gather_weights(w_qkv, w_out, w_up, w_down)
        gathered = tuple(
            {0: wqkv_g, 3: wout_g, 7: wup_g, 9: wdown_g}.get(place)
            if place in (0, 3, 7, 9)
            else lax.all_gather(local_params[place], "wt", axis=0, tiled=True)
            for place in range(13)
        )
    else:
        gathered = tuple(lax.all_gather(v, "wt", axis=0, tiled=True) for v in local_params)
    (
        wqkv_full,
        biasq_full,
        biasv_full,
        wout_full,
        biasout_full,
        gainone_full,
        shiftone_full,
        wup_full,
        biasup_full,
        wdown_full,
        biasdown_full,
        gaintwo_full,
        shifttwo_full,
    ) = gathered
    tok_rows = tokens.shape[1]
    model_width = tokens.shape[2]
    head_count = pairing.shape[0]
    head_size = model_width // head_count
    group_size = lax.axis_size("ctx")
    position_ctx = lax.axis_index("ctx")
    half_len = tok_rows * group_size // 2
    own_half = position_ctx * tok_rows // half_len
    flipped = pairing == 1
    inputs = tokens[0]
    bias_cat = jnp.concatenate(
        [
            biasq_full.astype(jnp.float32),
            jnp.zeros((model_width,), jnp.float32),
            biasv_full.astype(jnp.float32),
        ]
    )
    projected = jnp.dot(inputs, wqkv_full, preferred_element_type=jnp.float32) + bias_cat
    projected_low = projected.astype(jnp.bfloat16)
    queries = projected_low[:, :model_width].reshape(tok_rows, head_count, head_size)
    key_rows = projected_low[:, model_width : 2 * model_width]
    value_rows = projected_low[:, 2 * model_width :]

    def online_update(state, portion_keys, portion_values, needed):
        row_top, row_total, accumulated = state
        key_count = portion_keys.shape[0]
        key_heads = portion_keys.reshape(key_count, head_count, head_size)
        value_heads = portion_values.reshape(key_count, head_count, head_size)
        scores = scores_of(queries, key_heads)
        scores = jnp.where(needed[:, None, :], scores, far_below)
        new_top = jnp.maximum(row_top, jnp.max(scores, axis=-1))
        factor = jnp.exp(row_top - new_top)
        weights = jnp.exp(scores - new_top[..., None])
        row_total = jnp.sum(weights, axis=-1)
        added = jnp.einsum(
            "htk,khd->thd",
            weights.astype(jnp.bfloat16),
            value_heads,
            preferred_element_type=jnp.float32,
        )
        accumulated = accumulated * factor.T[..., None] + added
        return (new_top, row_total, accumulated)

    start_state = (
        jnp.full((head_count, tok_rows), far_below, jnp.float32),
        jnp.zeros((head_count, tok_rows), jnp.float32),
        jnp.zeros((tok_rows, head_count, head_size), jnp.float32),
    )

    def wanted(offset, key_count):
        key_half = (offset + jnp.arange(key_count)) // half_len
        target = jnp.where(flipped, 1 - own_half, own_half)
        return key_half[None, :] == target[:, None]

    portion_keys = lax.all_gather(key_rows, "ctx", axis=0, tiled=True)
    portion_values = lax.all_gather(value_rows, "ctx", axis=0, tiled=True)
    needed = wanted(jnp.int32(0), portion_keys.shape[0])

    def update(state):
        return online_update(state, portion_keys, portion_values, needed)

    row_top, row_total, accumulated = lax.cond(jnp.any(needed), update, unchanged, start_state)
    context = accumulated / row_total.T[..., None]
    log_sum = row_top + jnp.log(row_total)
    context_low = context.reshape(tok_rows, model_width).astype(jnp.bfloat16)
    branch = jnp.dot(
        context_low, wout_full, preferred_element_type=jnp.float32
    ) + biasout_full.astype(jnp.float32)
    summed_one = inputs.astype(jnp.float32) + branch
    hidden, norm_one_back = jax.vjp(
        norm_rows, summed_one, gainone_full.astype(jnp.float32), shiftone_full.astype(jnp.float32)
    )
    hidden_low = hidden.astype(jnp.bfloat16)
    pre_active = jnp.dot(
        hidden_low, wup_full, preferred_element_type=jnp.float32
    ) + biasup_full.astype(jnp.float32)
    active, gelu_back = jax.vjp(gelu_exact, pre_active)
    active_low = active.astype(jnp.bfloat16)
    ffn_out = jnp.dot(
        active_low, wdown_full, preferred_element_type=jnp.float32
    ) + biasdown_full.astype(jnp.float32)
    output, norm_two_back = jax.vjp(
        norm_rows,
        hidden + ffn_out,
        gaintwo_full.astype(jnp.float32),
        shifttwo_full.astype(jnp.float32),
    )
    again = gathered
    wqkv_back = again[0]
    wout_back = again[3]
    wup_back = again[7]
    wdown_back = again[9]
    grad_two, grad_gain_two, grad_shift_two = norm_two_back(cotangent[0].astype(jnp.float32))
    grad_ffn = grad_two.astype(jnp.bfloat16)
    grad_bias_down = jnp.sum(grad_ffn.astype(jnp.float32), axis=0)
    grad_w_down = jnp.einsum("tf,td->fd", active_low, grad_ffn, preferred_element_type=jnp.float32)
    grad_active = jnp.einsum("td,fd->tf", grad_ffn, wdown_back, preferred_element_type=jnp.float32)
    (grad_pre_f,) = gelu_back(grad_active)
    grad_pre = grad_pre_f.astype(jnp.bfloat16)
    grad_bias_up = jnp.sum(grad_pre.astype(jnp.float32), axis=0)
    grad_w_up = jnp.einsum("tc,tf->cf", hidden_low, grad_pre, preferred_element_type=jnp.float32)
    grad_hidden = grad_two + jnp.einsum(
        "tf,cf->tc", grad_pre, wup_back, preferred_element_type=jnp.float32
    )
    grad_one, grad_gain_one, grad_shift_one = norm_one_back(grad_hidden)
    grad_branch = grad_one.astype(jnp.bfloat16)
    grad_bias_out = jnp.sum(grad_branch.astype(jnp.float32), axis=0)
    grad_w_out = jnp.einsum(
        "tc,td->cd", context_low, grad_branch, preferred_element_type=jnp.float32
    )
    grad_context = jnp.einsum(
        "td,cd->tc", grad_branch, wout_back, preferred_element_type=jnp.float32
    )
    grad_context = grad_context.astype(jnp.bfloat16).reshape(tok_rows, head_count, head_size)
    row_delta = jnp.sum(grad_context.astype(jnp.float32) * context, axis=-1).T

    def piece_grads(portion_keys, portion_values, needed):
        key_count = portion_keys.shape[0]
        key_heads = portion_keys.reshape(key_count, head_count, head_size)
        value_heads = portion_values.reshape(key_count, head_count, head_size)
        scores = scores_of(queries, key_heads)
        scores = jnp.where(needed[:, None, :], scores, far_below)
        probs = jnp.exp(scores - log_sum[..., None])
        probs_low = probs.astype(jnp.bfloat16)
        piece_v = jnp.einsum(
            "htk,thd->khd", probs_low, grad_context, preferred_element_type=jnp.float32
        ).reshape(key_count, model_width)
        grad_weights = jnp.einsum(
            "thd,khd->htk", grad_context, value_heads, preferred_element_type=jnp.float32
        )
        grad_scores = (probs * (grad_weights - row_delta[..., None])).astype(jnp.bfloat16)
        piece_q = 0.125 * jnp.einsum(
            "htk,khd->thd", grad_scores, key_heads, preferred_element_type=jnp.float32
        )
        piece_k = 0.125 * jnp.einsum(
            "htk,thd->khd", grad_scores, queries, preferred_element_type=jnp.float32
        ).reshape(key_count, model_width)
        return (piece_k, piece_v, piece_q)

    zero_queries = jnp.zeros((tok_rows, head_count, head_size), jnp.float32)

    def circle_step(step_index, running):
        turn_keys, turn_values, grad_keys, grad_values, grad_queries = running
        owner = (position_ctx - step_index) % group_size
        needed = wanted(owner * tok_rows, tok_rows)

        def update_grads(state):
            grad_k, grad_v, grad_q = state
            piece_k, piece_v, piece_q = piece_grads(turn_keys, turn_values, needed)
            return (grad_k + piece_k, grad_v + piece_v, grad_q + piece_q)

        grad_keys, grad_values, grad_queries = lax.cond(
            jnp.any(needed), update_grads, unchanged, (grad_keys, grad_values, grad_queries)
        )
        turn_keys, turn_values = passed_along((turn_keys, turn_values), "ctx", 1)
        grad_keys, grad_values = (
            passed_along(grad_keys.astype(jnp.bfloat16), "ctx", 1).astype(grad_keys.dtype),
            passed_along(grad_values.astype(jnp.bfloat16), "ctx", 1).astype(grad_values.dtype),
        )
        return (turn_keys, turn_values, grad_keys, grad_values, grad_queries)

    zero_rows = jnp.zeros((tok_rows, model_width), jnp.float32)
    circle_start = (key_rows, value_rows, zero_rows, zero_rows, zero_queries)
    circle_end = lax.fori_loop(0, group_size, circle_step, circle_start)
    grad_keys = circle_end[2]
    grad_values = circle_end[3]
    grad_queries = circle_end[4]
    grad_projected = jnp.concatenate(
        [grad_queries.reshape(tok_rows, model_width), grad_keys, grad_values], axis=1
    ).astype(jnp.bfloat16)
    grad_bias_q = jnp.sum(grad_projected[:, :model_width].astype(jnp.float32), axis=0)
    grad_bias_v = jnp.sum(grad_projected[:, 2 * model_width :].astype(jnp.float32), axis=0)
    grad_w_qkv = jnp.einsum("tc,tj->cj", inputs, grad_projected, preferred_element_type=jnp.float32)
    grad_inputs = grad_one + jnp.einsum(
        "tj,cj->tc", grad_projected, wqkv_back, preferred_element_type=jnp.float32
    )
    terms = (
        grad_w_qkv,
        grad_bias_q,
        grad_bias_v,
        grad_w_out,
        grad_bias_out,
        grad_gain_one,
        grad_shift_one,
        grad_w_up,
        grad_bias_up,
        grad_w_down,
        grad_bias_down,
        grad_gain_two,
        grad_shift_two,
    )
    owned = (
        lax.psum_scatter(
            terms[0].astype(jnp.bfloat16), "wt", scatter_dimension=0, tiled=True
        ).astype(jnp.float32),
        lax.psum_scatter(
            terms[1].astype(jnp.bfloat16), "wt", scatter_dimension=0, tiled=True
        ).astype(jnp.float32),
        lax.psum_scatter(
            terms[2].astype(jnp.bfloat16), "wt", scatter_dimension=0, tiled=True
        ).astype(jnp.float32),
        lax.psum_scatter(
            terms[3].astype(jnp.bfloat16), "wt", scatter_dimension=0, tiled=True
        ).astype(jnp.float32),
        lax.psum_scatter(
            terms[4].astype(jnp.bfloat16), "wt", scatter_dimension=0, tiled=True
        ).astype(jnp.float32),
        lax.psum_scatter(
            terms[5].astype(jnp.bfloat16), "wt", scatter_dimension=0, tiled=True
        ).astype(jnp.float32),
        lax.psum_scatter(
            terms[6].astype(jnp.bfloat16), "wt", scatter_dimension=0, tiled=True
        ).astype(jnp.float32),
        lax.psum_scatter(
            terms[7].astype(jnp.bfloat16), "wt", scatter_dimension=0, tiled=True
        ).astype(jnp.float32),
        lax.psum_scatter(
            terms[8].astype(jnp.bfloat16), "wt", scatter_dimension=0, tiled=True
        ).astype(jnp.float32),
        lax.psum_scatter(
            terms[9].astype(jnp.bfloat16), "wt", scatter_dimension=0, tiled=True
        ).astype(jnp.float32),
        lax.psum_scatter(
            terms[10].astype(jnp.bfloat16), "wt", scatter_dimension=0, tiled=True
        ).astype(jnp.float32),
        lax.psum_scatter(
            terms[11].astype(jnp.bfloat16), "wt", scatter_dimension=0, tiled=True
        ).astype(jnp.float32),
        lax.psum_scatter(
            terms[12].astype(jnp.bfloat16), "wt", scatter_dimension=0, tiled=True
        ).astype(jnp.float32),
    )
    totals = (
        lax.psum(owned[0].astype(jnp.bfloat16), "ctx").astype(jnp.float32),
        lax.psum(owned[1].astype(jnp.bfloat16), "ctx").astype(jnp.float32),
        lax.psum(owned[2].astype(jnp.bfloat16), "ctx").astype(jnp.float32),
        lax.psum(owned[3].astype(jnp.bfloat16), "ctx").astype(jnp.float32),
        lax.psum(owned[4].astype(jnp.bfloat16), "ctx").astype(jnp.float32),
        lax.psum(owned[5].astype(jnp.bfloat16), "ctx").astype(jnp.float32),
        lax.psum(owned[6].astype(jnp.bfloat16), "ctx").astype(jnp.float32),
        lax.psum(owned[7].astype(jnp.bfloat16), "ctx").astype(jnp.float32),
        lax.psum(owned[8].astype(jnp.bfloat16), "ctx").astype(jnp.float32),
        lax.psum(owned[9].astype(jnp.bfloat16), "ctx").astype(jnp.float32),
        lax.psum(owned[10].astype(jnp.bfloat16), "ctx").astype(jnp.float32),
        lax.psum(owned[11].astype(jnp.bfloat16), "ctx").astype(jnp.float32),
        lax.psum(owned[12].astype(jnp.bfloat16), "ctx").astype(jnp.float32),
    )
    return (
        output[None],
        grad_inputs[None],
        totals[0],
        totals[1],
        totals[2],
        totals[3],
        totals[4],
        totals[5],
        totals[6],
        totals[7],
        totals[8],
        totals[9],
        totals[10],
        totals[11],
        totals[12],
    )


def solution(mesh):
    in_specs = (
        P("wt", "ctx", None),
        P(),
        P("wt", None),
        P("wt"),
        P("wt"),
        P("wt", None),
        P("wt"),
        P("wt"),
        P("wt"),
        P("wt", None),
        P("wt"),
        P("wt", None),
        P("wt"),
        P("wt"),
        P("wt"),
        P("wt", "ctx", None),
    )
    out_specs = (
        P("wt", "ctx", None),
        P("wt", "ctx", None),
        P("wt", None),
        P("wt"),
        P("wt"),
        P("wt", None),
        P("wt"),
        P("wt"),
        P("wt"),
        P("wt", None),
        P("wt"),
        P("wt", None),
        P("wt"),
        P("wt"),
        P("wt"),
    )
    return jax.shard_map(local, mesh=mesh, in_specs=in_specs, out_specs=out_specs, check_vma=False)
```

```python
import functools

import jax
import jax.numpy as jnp
from jax import lax
from jax.experimental import pallas as pl
from jax.experimental.pallas import tpu as pltpu
from jax.sharding import PartitionSpec as P

F32, BF16 = jnp.float32, jnp.bfloat16
MESH = pl.DeviceIdType.MESH
BAND = 32


def nn(a, b):
    return jnp.dot(a, b, preferred_element_type=F32)


def nt(a, b):
    return lax.dot_general(a, b, (((1,), (1,)), ((), ())), preferred_element_type=F32)


def aligned(start, multiple):
    return start if isinstance(start, int) else pl.multiple_of(start, multiple)


def chunk_of(index, size):
    return pl.ds(aligned(index * size, size), size)


class Wire:
    def __init__(self, sends, receives, anyone):
        self.sends, self.receives, self.anyone = sends, receives, anyone
        self.firsts, self.used, self.started = {}, 0, {}

    def slot(self, name, count=1):
        if name not in self.firsts:
            self.firsts[name] = self.used, count
            self.used += count
        first, had = self.firsts[name]
        assert had == count
        return first

    def copy(self, slot, source, target, where):
        return pltpu.make_async_remote_copy(
            src_ref=source,
            dst_ref=target,
            send_sem=self.sends.at[slot],
            recv_sem=self.receives.at[slot],
            device_id=where,
            device_id_type=MESH,
        )

    def send(self, name, source, target, where):
        copy = self.copy(self.slot(name), source, target, where)
        copy.start()
        self.started[name] = copy

    def arrived(self, name, target):
        self.copy(self.slot(name), target, target, self.anyone).wait_recv()

    def left(self, *names):
        for name in names:
            self.started.pop(name).wait_send()

    def close(self):
        self.left(*tuple(self.started))


class Place:
    def __init__(self):
        self.w = w = lax.axis_index("wt")
        self.c = c = lax.axis_index("ctx")
        self.core = core = c % 2
        self.other = 1 - core
        self.z = z = c // 2
        self.near = z % 2
        self.far = 1 - self.near
        self.nx = w + 1 - 2 * (w % 2)
        self.ny = (w + 2) % 4
        self.nd = 3 - w
        self.sib = (w, c + 1 - 2 * core)
        self.to_x, self.to_y, self.to_d = (self.nx, c), (self.ny, c), (self.nd, c)
        self.cross = (w, c + 2 - 4 * self.near)
        self.partner = (w, (c + 4) % 8)
        self.lines = [(w, spot * 2 + core) for spot in (z + 1 - 2 * (z % 2), (z + 2) % 4, 3 - z)]
        self.others = [(w, (c + step) % 8) for step in range(1, 8)]
        self.mate, self.middle = self.lines[0], self.lines[2]
        self.outer, self.inner = (z == 0) | (z == 3), (z == 1) | (z == 2)


def greet(peers):
    barrier = pltpu.get_barrier_semaphore()
    for peer in peers:
        pl.semaphore_signal(barrier, inc=1, device_id=peer, device_id_type=MESH)
    pl.semaphore_wait(barrier, len(peers))


class Part:
    def __init__(self, name, local, full, first, columns, place, wire):
        self.name, self.local, self.full, self.place, self.wire = name, local, full, place, wire
        self.rows = local.shape[0]
        self.first, self.columns = first, columns // 2

    def piece(self, owner, core, half=None):
        rows, start = self.rows, owner * self.rows
        if half is not None:
            rows = self.rows // 2
            start = start + half * rows
        return self.full.at[
            pl.ds(aligned(start, 16), rows),
            pl.ds(aligned(self.first + core * self.columns, 128), self.columns),
        ]

    def begin(self):
        at, wire = self.place, self.wire
        mine = self.local.at[
            :, pl.ds(aligned(self.first + at.core * self.columns, 128), self.columns)
        ]
        target = self.piece(at.w, at.core)
        wire.send(self.name + "a", mine, target, at.to_x)
        wire.send(self.name + "b", mine, target, at.to_y)

    def relay(self):
        at, wire = self.place, self.wire
        block = self.piece(at.nx, at.core)
        wire.arrived(self.name + "a", block)
        half = self.piece(at.nx, at.core, 0)
        wire.send(self.name + "c", half, half, at.to_y)
        wire.send(self.name + "d", block, block, at.sib)
        block = self.piece(at.ny, at.core)
        wire.arrived(self.name + "b", block)
        half = self.piece(at.ny, at.core, 1)
        wire.send(self.name + "e", half, half, at.to_x)
        wire.send(self.name + "f", block, block, at.sib)

    def share(self):
        at, wire = self.place, self.wire
        wire.arrived(self.name + "c", self.piece(at.nd, at.core, 0))
        wire.arrived(self.name + "e", self.piece(at.nd, at.core, 1))
        block = self.piece(at.nd, at.core)
        wire.send(self.name + "g", block, block, at.sib)

    def finish(self):
        at, wire = self.place, self.wire
        wire.arrived(self.name + "d", self.piece(at.nx, at.other))
        wire.arrived(self.name + "f", self.piece(at.ny, at.other))
        wire.arrived(self.name + "g", self.piece(at.nd, at.other))


def add_into(target, *sources):
    rows, columns = sources[0].shape
    band = 16
    while columns * band * 2 <= 1 << 15 and rows % (band * 2) == 0:
        band *= 2

    @pl.loop(0, rows // band)
    def _(index):
        where = chunk_of(index, band)
        total = sources[0][where, :].astype(F32)
        for source in sources[1:]:
            total = total + source[where, :].astype(F32)
        target[where, :] = total.astype(target.dtype)


class Grad:
    def __init__(self, name, blocks, buffers, finals, place, wire, local_sems):
        self.name, self.blocks, self.finals = name, blocks, finals
        self.place, self.wire, self.local_sems = place, wire, local_sems
        self.from_x, self.from_y, self.diag_x, self.diag_y, self.low, self.high = buffers
        self.rows, self.columns = self.from_x.shape

    def half(self, ref, index):
        return ref.at[pl.ds(index * (self.rows // 2), self.rows // 2), :]

    def begin(self):
        at, wire = self.place, self.wire
        block = self.blocks(at.nd)
        wire.send(self.name + "a", self.half(block, 0), self.diag_x, at.to_x)
        wire.send(self.name + "b", self.half(block, 1), self.diag_y, at.to_y)

    def mid(self):
        at, wire = self.place, self.wire
        wire.arrived(self.name + "a", self.diag_x)
        block = self.blocks(at.ny)
        part = self.half(block, 0)
        add_into(part, part, self.diag_x)
        wire.send(self.name + "d", block, self.from_y, at.to_y)
        wire.arrived(self.name + "b", self.diag_y)
        block = self.blocks(at.nx)
        part = self.half(block, 1)
        add_into(part, part, self.diag_y)
        wire.send(self.name + "c", block, self.from_x, at.to_x)

    def outward(self):
        return self.wire.copy(
            self.wire.slot(self.name + "u"), self.blocks(self.place.w), self.low, self.place.mate
        )

    def across(self):
        return self.wire.copy(
            self.wire.slot(self.name + "v"), self.from_x, self.high, self.place.middle
        )

    def back(self):
        return self.wire.copy(
            self.wire.slot(self.name + "t"), self.from_y, self.high, self.place.mate
        )

    def own(self):
        at, wire = self.place, self.wire
        wire.arrived(self.name + "c", self.from_x)
        wire.arrived(self.name + "d", self.from_y)
        block = self.blocks(at.w)
        add_into(block, block, self.from_x, self.from_y)

        @pl.when(at.outer)
        def _():
            self.outward().start()

    def chain(self):
        at = self.place

        @pl.when(at.inner)
        def _():
            self.outward().wait_recv()
            add_into(self.from_x, self.blocks(at.w), self.low)
            self.across().start()

    def copies(self, source):
        at, wire = self.place, self.wire
        found = []
        for index, (piece, target) in enumerate(self.finals(source)):
            keep = pltpu.make_async_copy(piece, target(at.core), self.local_sems.at[index])
            slot = wire.slot(self.name + "s" + str(index))
            found.append((keep, wire.copy(slot, piece, target(at.core), at.sib)))
        return found

    def total(self):
        at = self.place

        @pl.when(at.inner)
        def _():
            self.across().wait_recv()
            add_into(self.from_y, self.from_x, self.high)
            self.back().start()
            for keep, share in self.copies(self.from_y):
                keep.start()
                share.start()

        @pl.when(at.outer)
        def _():
            self.back().wait_recv()
            for keep, share in self.copies(self.high):
                keep.start()
                share.start()

    def close(self):
        at = self.place
        for keep, share in self.copies(self.from_y):
            keep.wait()
            share.wait()

        @pl.when(at.outer)
        def _():
            self.outward().wait_send()

        @pl.when(at.inner)
        def _():
            self.across().wait_send()
            self.back().wait_send()


def layer_scratch(rows, width, inner, heads):
    pairs = heads // 2
    some = pairs // 2
    share = width // 4
    half = width // 2
    groups = 8

    def low(*shape):
        return pltpu.VMEM(shape, BF16)

    def wide(*shape):
        return pltpu.VMEM(shape, F32)

    scratch = dict(
        wqkv=low(width, 3 * width),
        wo=low(width, width),
        wu=low(width, inner),
        wd=low(inner, width),
        order=low(width, width),
        tok=low(2, rows, width),
        small_in=low(3, 16, width),
        small=wide(16, width),
        bias_qkv=wide(8, 3 * width),
        bias_up=wide(8, inner),
        kv=low(pairs, 4, rows, 256),
        proj=low(rows, 3 * width),
        q=low(pairs, rows, 128),
        q_out=low(some, rows, 128),
        exps=low(heads, 4 * rows, rows),
        inverse=wide(heads, 1, rows),
        out_t=wide(pairs, 128, rows),
        ctx=low(pairs, rows, 128),
        ctx_out=low(some, rows, 128),
        ctx_nat=low(2, rows, width),
        hat_one=wide(rows, width),
        r_one=wide(rows, 1),
        flow=wide(rows, width),
        stage=wide(rows, width),
        result=wide(rows, width),
        hid=low(2, rows, width),
        act=low(2, rows, inner),
        slope=low(rows, inner),
        slope_in=low(rows, inner // 2),
        gf=low(rows, width),
        gf_in=low(rows, half),
        gb=low(rows, width),
        gb_in=low(rows, half),
        do=low(pairs, rows, 128),
        do_out=low(some, rows, 128),
        dq=low(pairs, rows, 128),
        dq_out=low(some, rows, 128),
        dkv_in=low(pairs, rows, 512),
        dkv_far=low(pairs, rows, 256),
        gkv=low(2, rows, width),
        gj_in=low(rows, 3 * half),
        sums=wide(16, groups, width),
        sums_up=wide(groups, inner),
        vec=wide(16, width),
        vec_in=wide(7, 16, width),
        dwd=low(4, inner // 4, half),
    )
    shapes = dict(
        d=(inner // 4, half), u=(2 * share, width), o=(share, half), q=(3 * share, half)
    )
    for name, (r, c) in shapes.items():
        for kind in ("fx", "fy", "lo", "hi"):
            scratch["g" + name + kind] = low(r, c)
        for kind in ("dx", "dy"):
            scratch["g" + name + kind] = low(r // 2, c)
    scratch["sends"] = pltpu.SemaphoreType.DMA((160,))
    scratch["receives"] = pltpu.SemaphoreType.DMA((160,))
    scratch["own_sems"] = pltpu.SemaphoreType.DMA((20,))
    return scratch


def layer_kernel(names, *refs):
    (
        tokens,
        cot,
        pairing,
        small_own,
        qkv_l,
        out_l,
        up_l,
        down_l,
        output,
        grad_tokens,
        g_qkv,
        g_out,
        g_up,
        g_down,
        g_small,
    ) = refs[:15]
    s = dict(zip(names, refs[15:]))
    at = Place()
    wire = Wire(s["sends"], s["receives"], at.sib)
    rows, width = tokens.shape
    inner = up_l.shape[1]
    heads = pairing.shape[0]
    pairs, some = heads // 2, heads // 4
    size = width // heads
    half = width // 2
    keys = 4 * rows
    chunks = width // 256
    share = width // 4
    core, other = at.core, at.other

    greet([at.to_x, at.to_y, at.to_d] + at.others)

    part_kv = Part("kv", qkv_l, s["wqkv"], width, 2 * width, at, wire)
    part_q = Part("q", qkv_l, s["wqkv"], 0, width, at, wire)
    part_o = Part("o", out_l, s["wo"], 0, width, at, wire)
    part_u = Part("u", up_l, s["wu"], 0, inner, at, wire)
    part_d = Part("d", down_l, s["wd"], 0, width, at, wire)
    part_kv.begin()
    for index, where in enumerate((at.to_x, at.to_y, at.to_d)):
        wire.send("sm" + str(index), small_own, s["small_in"].at[index], where)
    keeps = []
    for slot, (local, full) in enumerate(
        (
            (qkv_l, s["wqkv"].at[pl.ds(aligned(at.w * share, 16), share)]),
            (tokens, s["tok"].at[core]),
            (out_l, s["wo"].at[pl.ds(aligned(at.w * share, 16), share)]),
            (up_l, s["wu"].at[pl.ds(aligned(at.w * share, 16), share)]),
            (down_l, s["wd"].at[pl.ds(aligned(at.w * (inner // 4), 16), inner // 4)]),
        )
    ):
        keeps.append(pltpu.make_async_copy(local, full, s["own_sems"].at[slot]))
        keeps[-1].start()
    part_q.begin()
    wire.send("tok", tokens, s["tok"].at[core], at.sib)

    before = 0
    for head in range(heads):
        flag = pairing[head]
        spot = flag * (heads // 2 + before) + (1 - flag) * (head - before)
        before = before + flag
        row = lax.broadcasted_iota(jnp.int32, (size, width), 0)
        column = lax.broadcasted_iota(jnp.int32, (size, width), 1)
        s["order"][head * size : (head + 1) * size, :] = jnp.where(
            column - row == spot * size, 1.0, 0.0
        ).astype(BF16)

    part_kv.relay()
    part_o.begin()
    part_q.relay()
    part_u.begin()
    part_kv.share()
    part_q.share()
    for index in range(3):
        wire.arrived("sm" + str(index), s["small_in"].at[index])
    small = s["small"]
    small[...] = (
        small_own[...].astype(F32)
        + s["small_in"][0].astype(F32)
        + s["small_in"][1].astype(F32)
        + s["small_in"][2].astype(F32)
    )
    s["bias_qkv"][0:1, 0:width] = small[0:1, :]
    s["bias_qkv"][0:1, width : 2 * width] = jnp.zeros((1, width), F32)
    s["bias_qkv"][0:1, 2 * width :] = small[1:2, :]
    for index in range(inner // width):
        s["bias_up"][0:1, index * width : (index + 1) * width] = small[8 + index : 9 + index, :]
    keeps[0].wait()
    keeps[1].wait()
    part_kv.finish()

    tok, proj, order, kv = s["tok"], s["proj"], s["order"], s["kv"]
    own_slot = core * 2 + at.near

    def project(first, count):
        @pl.loop(first, first + count)
        def _(index):
            where = chunk_of(index, 256)
            made = nn(tok[core], s["wqkv"][:, where]) + s["bias_qkv"][0:1, where]
            proj[:, where] = made.astype(BF16)

    project(chunks, 2 * chunks)
    for index in range(chunks):
        columns = order[:, index * 256 : (index + 1) * 256]
        for kind in range(2):
            moved = nn(proj[:, (1 + kind) * width : (2 + kind) * width], columns).astype(BF16)
            for e in range(2):
                kv[2 * index + e, own_slot, :, kind * 128 : (kind + 1) * 128] = moved[
                    :, e * 128 : (e + 1) * 128
                ]
    sequence = [(index + some) % pairs for index in range(pairs)]
    near_base = wire.slot("near kv", pairs)
    far_base = wire.slot("far kv", pairs)
    pass_base = wire.slot("passed kv", pairs)

    def kv_copy(base, pair, slot, where):
        block = kv.at[pair, slot]
        return wire.copy(base + pair, block, block, where)

    for pair in sequence:
        kv_copy(far_base, pair, own_slot, at.cross).start()
        kv_copy(near_base, pair, own_slot, at.sib).start()
    part_q.finish()
    project(0, chunks)
    q, q_out = s["q"], s["q_out"]
    for index in range(chunks):
        moved = nn(proj[:, 0:width], order[:, index * 256 : (index + 1) * 256]).astype(BF16)
        for e in range(2):
            pair = 2 * index + e
            block = moved[:, e * 128 : (e + 1) * 128]
            if pair < some:
                q[pair] = block
            else:
                q_out[pair - some] = block
    wire.send("q", q_out, q.at[pl.ds(some, some)], at.partner)
    part_o.relay()
    part_d.begin()
    part_o.share()

    exps, inverse, out_t = s["exps"], s["inverse"], s["out_t"]

    def both(pair, first):
        return kv[pair, :, :, first : first + 128].reshape(keys, 128)

    def masked(block, e, axis=1):
        spot = lax.broadcasted_iota(jnp.int32, block.shape, axis)
        mine = spot < size if e == 0 else spot >= size
        return jnp.where(mine, block, jnp.zeros_like(block))

    def attend(pair):
        key_rows, value_rows = both(pair, 0), both(pair, 128)
        values_t = value_rows.T
        queries = q[pair] * jnp.asarray(size**-0.5, BF16)
        parts = []
        for e in range(2):
            scores = nt(key_rows, masked(queries, e))
            top = jnp.max(scores, axis=0, keepdims=True)
            raised = jnp.exp(scores - top)
            total = jnp.sum(raised, axis=0, keepdims=True)
            low = raised.astype(BF16)
            exps[2 * pair + e] = low
            one_over = 1.0 / total
            inverse[2 * pair + e] = one_over
            parts.append(nn(values_t[e * size : (e + 1) * size], low) * one_over)
        merged = jnp.concatenate(parts, axis=0)
        out_t[pair] = merged
        return merged.T.astype(BF16)

    def receive_kv(pair):
        kv_copy(far_base, pair, core * 2 + at.far, at.cross).wait_recv()
        kv_copy(pass_base, pair, core * 2 + at.far, at.sib).start()
        kv_copy(near_base, pair, other * 2 + at.near, at.sib).wait_recv()
        kv_copy(pass_base, pair, other * 2 + at.far, at.sib).wait_recv()

    ctx, ctx_out = s["ctx"], s["ctx_out"]
    back_base = wire.slot("ctx", some)

    def ctx_copy(index):
        return wire.copy(back_base + index, ctx_out.at[index], ctx.at[some + index], at.partner)

    wire.arrived("q", q.at[pl.ds(some, some)])

    @pl.loop(0, some)
    def _(index):
        receive_kv(index + some)
        ctx_out[index] = attend(index + some)
        ctx_copy(index).start()

    @pl.loop(0, some)
    def _(index):
        receive_kv(index)
        ctx[index] = attend(index)

    part_u.relay()
    part_o.finish()
    keeps[2].wait()
    part_u.share()
    for index in range(some):
        ctx_copy(index).wait_recv()
    permuted = jnp.concatenate([ctx[pair] for pair in range(pairs)], axis=1)
    ctx_nat, stage = s["ctx_nat"], s["stage"]
    for index in range(chunks):
        where = slice(index * 256, (index + 1) * 256)
        ctx_nat[core, :, where] = nt(permuted, order[where, :]).astype(BF16)
    wire.send("ctxn", ctx_nat.at[core], ctx_nat.at[core], at.sib)

    @pl.loop(0, chunks)
    def _(index):
        where = chunk_of(index, 256)
        stage[:, where] = nn(ctx_nat[core], s["wo"][:, where])

    hat_one, r_one, flow, hid = s["hat_one"], s["r_one"], s["flow"], s["hid"]
    inv_width = 1.0 / width

    def mean(values):
        return jnp.sum(values, axis=-1, keepdims=True) * inv_width

    @pl.loop(0, rows // BAND)
    def _(index):
        where = chunk_of(index, BAND)
        total = tok[core, where, :].astype(F32) + stage[where, :] + small[2:3, :]
        centred = total - mean(total)
        scale = lax.rsqrt(mean(centred * centred) + 1e-12)
        hat = centred * scale
        hat_one[where, :] = hat
        r_one[where, :] = scale
        hidden = hat * small[3:4, :] + small[4:5, :]
        flow[where, :] = hidden
        hid[core, where, :] = hidden.astype(BF16)

    wire.send("hid", hid.at[core], hid.at[core], at.sib)
    part_u.finish()
    keeps[3].wait()
    act, slope = s["act"], s["slope"]

    @pl.loop(0, inner // 256)
    def _(index):
        where = chunk_of(index, 256)
        pre = nn(hid[core], s["wu"][:, where]) + s["bias_up"][0:1, where]
        below = 0.5 * (1.0 + lax.erf(pre * (0.5**0.5)))
        act[core, :, where] = (pre * below).astype(BF16)
        density = jnp.exp(pre * pre * -0.5) * 0.3989422804014327
        slope[:, where] = (below + pre * density).astype(BF16)

    wire.send("act", act.at[core], act.at[core], at.sib)
    part_d.relay()
    part_d.share()
    part_d.finish()
    keeps[4].wait()

    @pl.loop(0, chunks)
    def _(index):
        where = chunk_of(index, 256)
        stage[:, where] = nn(act[core], s["wd"][:, where])

    result, gf = s["result"], s["gf"]
    sums, sums_up = s["sums"], s["sums_up"]
    sums[...] = jnp.zeros_like(sums)

    def gather_rows(values):
        return jnp.sum(values.reshape(BAND // 8, 8, values.shape[-1]), axis=0)

    @pl.loop(0, rows // BAND)
    def _(index):
        where = chunk_of(index, BAND)
        total = flow[where, :] + stage[where, :] + small[5:6, :]
        centred = total - mean(total)
        scale = lax.rsqrt(mean(centred * centred) + 1e-12)
        hat = centred * scale
        result[where, :] = hat * small[6:7, :] + small[7:8, :]
        back = cot[where, :].astype(F32)
        g = back * small[6:7, :]
        grad = scale * (g - mean(g) - hat * mean(g * hat))
        flow[where, :] = grad
        low = grad.astype(BF16)
        gf[where, :] = low
        sums[6] += gather_rows(back * hat)
        sums[7] += gather_rows(back)
        sums[5] += gather_rows(low.astype(F32))

    keep_out = pltpu.make_async_copy(result, output, s["own_sems"].at[5])
    keep_out.start()

    def columns_of(which, count):
        return pl.ds(aligned(which * count, 128), count)

    wire.send("gf", gf.at[:, columns_of(other, half)], s["gf_in"], at.sib)

    def buffers(name):
        return [s["g" + name + kind] for kind in ("fx", "fy", "dx", "dy", "lo", "hi")]

    dwd, wd, wu = s["dwd"], s["wd"], s["wu"]

    def side_by_side(first, count, owner):
        return wd.at[
            pl.ds(aligned(first + (owner // 2) * count, 16), count),
            pl.ds(aligned((owner % 2) * half, 128), half),
        ]

    def dwo(owner):
        return side_by_side(2 * width + 6 * share, share, owner)

    def dwq(owner):
        return side_by_side(2 * width, 3 * share, owner)

    grad_d = Grad(
        "gd",
        lambda r: dwd.at[r],
        buffers("d"),
        lambda final: [(final, lambda k: g_down.at[:, columns_of(k, half)])],
        at,
        wire,
        s["own_sems"].at[pl.ds(6, 1)],
    )
    grad_u = Grad(
        "gu",
        lambda r: wd.at[pl.ds(aligned(r * (2 * share), 16), 2 * share), :],
        buffers("u"),
        lambda final: [
            (
                final.at[pl.ds(i * share, share), :],
                lambda k, i=i: g_up.at[:, columns_of(2 * k + i, width)],
            )
            for i in range(2)
        ],
        at,
        wire,
        s["own_sems"].at[pl.ds(7, 2)],
    )
    grad_o = Grad(
        "go",
        dwo,
        buffers("o"),
        lambda final: [(final, lambda k: g_out.at[:, columns_of(k, half)])],
        at,
        wire,
        s["own_sems"].at[pl.ds(9, 1)],
    )
    grad_q = Grad(
        "gq",
        dwq,
        buffers("q"),
        lambda final: [
            (
                final.at[pl.ds(i * share, share), :],
                lambda k, i=i: g_qkv.at[:, columns_of(3 * k + i, half)],
            )
            for i in range(3)
        ],
        at,
        wire,
        s["own_sems"].at[pl.ds(10, 3)],
    )

    wire.arrived("act", act.at[other])
    wire.arrived("gf", s["gf_in"])
    gf_mine = gf[:, columns_of(core, half)]
    gf_theirs = s["gf_in"][...]
    quarter = inner // 4
    for owner in (at.nd, at.nx, at.ny, at.w):
        where = pl.ds(aligned(owner * quarter, 128), quarter)
        made = nn(act[core, :, where].T, gf_mine) + nn(act[other, :, where].T, gf_theirs)
        dwd[owner] = made.astype(BF16)
        if owner is at.nd:
            grad_d.begin()

    @pl.loop(0, inner // 256)
    def _(index):
        where = chunk_of(index, 256)
        grad = nt(gf[...], wd[where, :]) * slope[:, where].astype(F32)
        low = grad.astype(BF16)
        slope[:, where] = low
        sums_up[:, where] = jnp.sum(low.astype(F32).reshape(rows // 8, 8, 256), axis=0)

    wire.send("slope", slope.at[:, columns_of(other, inner // 2)], s["slope_in"], at.sib)

    @pl.loop(0, chunks)
    def _(index):
        where = chunk_of(index, 256)
        stage[:, where] = nt(slope[...], wu[where, :])

    gb = s["gb"]

    @pl.loop(0, rows // BAND)
    def _(index):
        where = chunk_of(index, BAND)
        grad_hidden = flow[where, :] + stage[where, :]
        hat = hat_one[where, :]
        g = grad_hidden * small[3:4, :]
        grad = r_one[where, :] * (g - mean(g) - hat * mean(g * hat))
        flow[where, :] = grad
        low = grad.astype(BF16)
        gb[where, :] = low
        sums[3] += gather_rows(grad_hidden * hat)
        sums[4] += gather_rows(grad_hidden)
        sums[2] += gather_rows(low.astype(F32))

    wire.send("gb", gb.at[:, columns_of(other, half)], s["gb_in"], at.sib)

    @pl.loop(0, chunks)
    def _(index):
        where = chunk_of(index, 256)
        proj[:, where] = nt(gb[...], s["wo"][where, :]).astype(BF16)

    do, do_out = s["do"], s["do_out"]
    for index in range(chunks):
        moved = nn(proj[:, 0:width], order[:, index * 256 : (index + 1) * 256]).astype(BF16)
        for e in range(2):
            pair = 2 * index + e
            block = moved[:, e * 128 : (e + 1) * 128]
            if pair < some:
                do[pair] = block
            else:
                do_out[pair - some] = block
    wire.send("do", do_out, do.at[pl.ds(some, some)], at.partner)
    grad_d.mid()

    wire.left("dc", "dd", "de", "df", "dg")
    wire.arrived("hid", hid.at[other])
    wire.arrived("slope", s["slope_in"])
    mine_t, theirs_t = hid[core].T, hid[other].T
    for index in range(inner // 2 // half):
        where = pl.ds(aligned(core * (inner // 2) + index * half, 128), half)
        made = nn(mine_t, slope[:, where]) + nn(
            theirs_t, s["slope_in"][:, index * half : (index + 1) * half]
        )
        made = made.astype(BF16)
        for owner in range(4):
            first = owner * 2 * share + (index // 2) * share
            wd[first : first + share, (index % 2) * half : (index % 2 + 1) * half] = made[
                owner * share : (owner + 1) * share
            ]
    grad_u.begin()
    wire.arrived("ctxn", ctx_nat.at[other])
    wire.arrived("gb", s["gb_in"])
    made = nn(ctx_nat[core].T, gb[:, columns_of(core, half)]) + nn(
        ctx_nat[other].T, s["gb_in"][...]
    )
    made = made.astype(BF16)
    for owner in range(4):
        dwo(owner)[...] = made[owner * share : (owner + 1) * share]
    grad_o.begin()

    wire.left("uc", "ud", "ue", "uf", "ug")
    dq, dq_out, dkv_in, dkv_far = s["dq"], s["dq_out"], s["dkv_in"], s["dkv_far"]
    near_d = wire.slot("near dkv", pairs)
    far_d = wire.slot("far dkv", pairs)
    dq_base = wire.slot("dq", some)
    lots = inner // 1024

    def tile(pair, slot, count=1):
        band = pair // lots
        column = (pair % lots) * 1024 + slot * 256
        return wu.at[
            pl.ds(aligned(band * rows, 16), rows),
            pl.ds(aligned(column, 256), 256 * count),
        ]

    def spare(pair):
        bands = -(-pairs // lots)
        band = bands + pair // (4 * lots)
        return wu.at[
            pl.ds(aligned(band * rows, 16), rows),
            pl.ds(aligned((pair % (4 * lots)) * 256, 256), 256),
        ]

    def dkv_near(pair):
        return wire.copy(near_d + pair, tile(pair, other * 2, 2), dkv_in.at[pair], at.sib)

    def dkv_cross(pair):
        return wire.copy(far_d + pair, spare(pair), dkv_far.at[pair], at.cross)

    def attend_back(pair):
        key_rows, value_rows = both(pair, 0), both(pair, 128)
        keys_t = key_rows.T
        queries = q[pair] * jnp.asarray(size**-0.5, BF16)
        do_t = do[pair].astype(F32).T
        scaled = jnp.concatenate(
            [do_t[e * size : (e + 1) * size] * inverse[2 * pair + e] for e in range(2)], axis=0
        )
        product = scaled * out_t[pair]
        scaled_low = scaled.astype(BF16)
        scaled_rows = scaled.T.astype(BF16)
        dv = dk = None
        dq_parts = []
        for e in range(2):
            delta = jnp.sum(product[e * size : (e + 1) * size], axis=0, keepdims=True)
            grad_w = nn(value_rows, masked(scaled_low, e, 0))
            low = exps[2 * pair + e]
            grad_s = (low.astype(F32) * (grad_w - delta)).astype(BF16)
            more_v = nn(low, masked(scaled_rows, e))
            more_k = nn(grad_s, masked(queries, e))
            dv = more_v if dv is None else dv + more_v
            dk = more_k if dk is None else dk + more_k
            dq_parts.append(nn(keys_t[e * size : (e + 1) * size], grad_s))
        made = jnp.concatenate([dk, dv], axis=1).astype(BF16)
        for slot in range(4):
            tile(pair, slot)[...] = made[slot * rows : (slot + 1) * rows]
        dkv_near(pair).start()
        return (jnp.concatenate(dq_parts, axis=0).T * size**-0.5).astype(BF16)

    def pass_on(pair):
        dkv_near(pair).wait_recv()
        add_into(
            spare(pair), tile(pair, core * 2 + at.far), dkv_in.at[pair, :, columns_of(at.far, 256)]
        )
        dkv_cross(pair).start()

    def dq_copy(index):
        return wire.copy(dq_base + index, dq_out.at[index], dq.at[some + index], at.partner)

    wire.arrived("do", do.at[pl.ds(some, some)])

    @pl.loop(0, some)
    def _(index):
        dq_out[index] = attend_back(index + some)
        dq_copy(index).start()

        @pl.when(index > 0)
        def _():
            pass_on(index + some - 1)

    grad_u.mid()
    grad_o.mid()
    grad_d.own()

    @pl.loop(0, some)
    def _(index):
        dq[index] = attend_back(index)

        @pl.when(index > 0)
        def _():
            pass_on(index - 1)

        @pl.when(index == 0)
        def _():
            pass_on(pairs - 1)

    pass_on(some - 1)
    grad_d.chain()
    grad_u.own()
    grad_o.own()

    gkv = s["gkv"]
    for pair in sequence:
        dkv_cross(pair).wait_recv()
        own = tile(pair, own_slot)
        near = dkv_in.at[pair, :, columns_of(at.near, 256)]
        for kind in range(2):
            cut = slice(kind * 128, (kind + 1) * 128)
            gkv[kind, :, pair * 128 : (pair + 1) * 128] = (
                own[:, cut].astype(F32)
                + near[:, cut].astype(F32)
                + dkv_far[pair, :, cut].astype(F32)
            ).astype(BF16)
    for index in range(some):
        dq_copy(index).wait_recv()
    merged = jnp.concatenate([dq[pair] for pair in range(pairs)], axis=1)
    for index in range(chunks):
        where = slice(index * 256, (index + 1) * 256)
        rows_of = order[where, :]
        for kind in range(3):
            source = merged if kind == 0 else gkv[kind - 1]
            low = nt(source, rows_of).astype(BF16)
            proj[:, kind * width + index * 256 : kind * width + (index + 1) * 256] = low
            if kind != 1:
                sums[kind // 2, :, where] = jnp.sum(
                    low.astype(F32).reshape(rows // 8, 8, 256), axis=0
                )
    wire.send("gj", proj.at[:, columns_of(other, 3 * half)], s["gj_in"], at.sib)

    vec, vec_in = s["vec"], s["vec_in"]
    for row in range(8):
        vec[row : row + 1, :] = jnp.sum(sums[row], axis=0, keepdims=True)
    for index in range(inner // width):
        vec[8 + index : 9 + index, :] = jnp.sum(
            sums_up[:, index * width : (index + 1) * width], axis=0, keepdims=True
        )
    for row in range(8 + inner // width, 16):
        vec[row : row + 1, :] = jnp.zeros((1, width), F32)
    wire.send("va", vec, vec_in.at[0], at.sib)

    wire.arrived("tok", tok.at[other])
    wire.arrived("gj", s["gj_in"])
    mine_t, theirs_t = tok[core].T, tok[other].T
    for index in range(3):
        where = pl.ds(aligned(core * (3 * half) + index * half, 128), half)
        made = nn(mine_t, proj[:, where]) + nn(
            theirs_t, s["gj_in"][:, index * half : (index + 1) * half]
        )
        made = made.astype(BF16)
        for owner in range(4):
            dwq(owner)[index * share : (index + 1) * share, :] = made[
                owner * share : (owner + 1) * share
            ]
    grad_q.begin()

    wire.arrived("va", vec_in.at[0])
    vec_in[0] = vec_in[0] + vec[...]
    for index, where in enumerate((at.to_x, at.to_y, at.to_d)):
        wire.send("vb" + str(index), vec_in.at[0], vec_in.at[1 + index], where)

    grad_u.chain()
    grad_o.chain()
    keep_out.wait()

    @pl.loop(0, chunks)
    def _(index):
        where = chunk_of(index, 256)
        result[:, where] = nt(proj[...], s["wqkv"][where, :]) + flow[:, where]

    keep_grad = pltpu.make_async_copy(result, grad_tokens, s["own_sems"].at[5])
    keep_grad.start()
    grad_q.mid()
    for index in range(3):
        wire.arrived("vb" + str(index), vec_in.at[1 + index])
    wire.left("va")
    vec[...] = (vec_in[0] + vec_in[1]) + (vec_in[2] + vec_in[3])
    for index, where in enumerate(at.lines):
        wire.send("vc" + str(index), vec, vec_in.at[4 + index], where)
    grad_d.total()
    grad_u.total()
    grad_o.total()
    grad_q.own()
    grad_q.chain()
    for index in range(3):
        wire.arrived("vc" + str(index), vec_in.at[4 + index])
    g_small[...] = (vec[...] + vec_in[4]) + (vec_in[5] + vec_in[6])
    grad_q.total()
    for grad in (grad_d, grad_u, grad_o, grad_q):
        grad.close()
    keep_grad.wait()
    for pair in range(pairs):
        kv_copy(far_base, pair, own_slot, at.cross).wait_send()
        kv_copy(near_base, pair, own_slot, at.sib).wait_send()
        kv_copy(pass_base, pair, core * 2 + at.far, at.sib).wait_send()
        dkv_near(pair).wait_send()
        dkv_cross(pair).wait_send()
    for index in range(some):
        ctx_copy(index).wait_send()
        dq_copy(index).wait_send()
    wire.close()


def whole_layer(tokens, cotangent, pairing, small_own, w_qkv, w_out, w_up, w_down):
    rows, width = tokens.shape
    inner = w_up.shape[1]
    scratch = layer_scratch(rows, width, inner, pairing.shape[0])
    hbm = pl.BlockSpec(memory_space=pl.ANY)
    vmem = pl.BlockSpec(memory_space=pltpu.VMEM)
    smem = pl.BlockSpec(memory_space=pltpu.SMEM)
    return pl.pallas_call(
        functools.partial(layer_kernel, tuple(scratch)),
        out_shape=[
            jax.ShapeDtypeStruct((rows, width), F32),
            jax.ShapeDtypeStruct((rows, width), F32),
            jax.ShapeDtypeStruct(w_qkv.shape, BF16),
            jax.ShapeDtypeStruct(w_out.shape, BF16),
            jax.ShapeDtypeStruct(w_up.shape, BF16),
            jax.ShapeDtypeStruct(w_down.shape, BF16),
            jax.ShapeDtypeStruct((16, width), F32),
        ],
        in_specs=[hbm, vmem, smem, vmem, hbm, hbm, hbm, hbm],
        out_specs=[hbm] * 6 + [vmem],
        scratch_shapes=list(scratch.values()),
        compiler_params=pltpu.CompilerParams(
            collective_id=0, has_side_effects=True, vmem_limit_bytes=60 << 20
        ),
        name="whole_layer",
    )(tokens, cotangent, pairing, small_own, w_qkv, w_out, w_up, w_down)


far_below = -1e30


def passed_along(value, axis, steps):
    count = lax.axis_size(axis)
    pairs = [(source, (source + steps) % count) for source in range(count)]
    return lax.ppermute(value, axis, pairs)


def norm_rows(values, gains, shifts):
    average = jnp.mean(values, axis=-1, keepdims=True)
    centred = values - average
    spread = jnp.mean(centred * centred, axis=-1, keepdims=True)
    return centred * lax.rsqrt(spread + 1e-12) * gains + shifts


def gelu_exact(pre_active):
    return jax.nn.gelu(pre_active, approximate=False)


def scores_of(queries, key_heads):
    return (
        jnp.einsum("thd,khd->htk", queries, key_heads, preferred_element_type=jnp.float32) * 0.125
    )


def unchanged(running):
    return running


def general_layer(
    tokens,
    pairing,
    w_qkv,
    bias_q,
    bias_v,
    w_out,
    bias_out,
    gain_one,
    shift_one,
    w_up,
    bias_up,
    w_down,
    bias_down,
    gain_two,
    shift_two,
    cotangent,
):
    local_params = (
        w_qkv,
        bias_q,
        bias_v,
        w_out,
        bias_out,
        gain_one,
        shift_one,
        w_up,
        bias_up,
        w_down,
        bias_down,
        gain_two,
        shift_two,
    )
    gathered = tuple(lax.all_gather(v, "wt", axis=0, tiled=True) for v in local_params)
    (
        wqkv_full,
        biasq_full,
        biasv_full,
        wout_full,
        biasout_full,
        gainone_full,
        shiftone_full,
        wup_full,
        biasup_full,
        wdown_full,
        biasdown_full,
        gaintwo_full,
        shifttwo_full,
    ) = gathered
    tok_rows = tokens.shape[1]
    model_width = tokens.shape[2]
    head_count = pairing.shape[0]
    head_size = model_width // head_count
    group_size = lax.axis_size("ctx")
    position_ctx = lax.axis_index("ctx")
    half_len = tok_rows * group_size // 2
    own_half = position_ctx * tok_rows // half_len
    flipped = pairing == 1
    inputs = tokens[0]
    bias_cat = jnp.concatenate(
        [
            biasq_full.astype(jnp.float32),
            jnp.zeros((model_width,), jnp.float32),
            biasv_full.astype(jnp.float32),
        ]
    )
    projected = jnp.dot(inputs, wqkv_full, preferred_element_type=jnp.float32) + bias_cat
    projected_low = projected.astype(jnp.bfloat16)
    queries = projected_low[:, :model_width].reshape(tok_rows, head_count, head_size)
    key_rows = projected_low[:, model_width : 2 * model_width]
    value_rows = projected_low[:, 2 * model_width :]

    def online_update(state, portion_keys, portion_values, needed):
        row_top, row_total, accumulated = state
        key_count = portion_keys.shape[0]
        key_heads = portion_keys.reshape(key_count, head_count, head_size)
        value_heads = portion_values.reshape(key_count, head_count, head_size)
        scores = scores_of(queries, key_heads)
        scores = jnp.where(needed[:, None, :], scores, far_below)
        new_top = jnp.maximum(row_top, jnp.max(scores, axis=-1))
        factor = jnp.exp(row_top - new_top)
        weights = jnp.exp(scores - new_top[..., None])
        row_total = jnp.sum(weights, axis=-1)
        added = jnp.einsum(
            "htk,khd->thd",
            weights.astype(jnp.bfloat16),
            value_heads,
            preferred_element_type=jnp.float32,
        )
        accumulated = accumulated * factor.T[..., None] + added
        return (new_top, row_total, accumulated)

    start_state = (
        jnp.full((head_count, tok_rows), far_below, jnp.float32),
        jnp.zeros((head_count, tok_rows), jnp.float32),
        jnp.zeros((tok_rows, head_count, head_size), jnp.float32),
    )

    def wanted(offset, key_count):
        key_half = (offset + jnp.arange(key_count)) // half_len
        target = jnp.where(flipped, 1 - own_half, own_half)
        return key_half[None, :] == target[:, None]

    portion_keys = lax.all_gather(key_rows, "ctx", axis=0, tiled=True)
    portion_values = lax.all_gather(value_rows, "ctx", axis=0, tiled=True)
    needed = wanted(jnp.int32(0), portion_keys.shape[0])

    def update(state):
        return online_update(state, portion_keys, portion_values, needed)

    row_top, row_total, accumulated = lax.cond(jnp.any(needed), update, unchanged, start_state)
    context = accumulated / row_total.T[..., None]
    log_sum = row_top + jnp.log(row_total)
    context_low = context.reshape(tok_rows, model_width).astype(jnp.bfloat16)
    branch = jnp.dot(
        context_low, wout_full, preferred_element_type=jnp.float32
    ) + biasout_full.astype(jnp.float32)
    summed_one = inputs.astype(jnp.float32) + branch
    hidden, norm_one_back = jax.vjp(
        norm_rows, summed_one, gainone_full.astype(jnp.float32), shiftone_full.astype(jnp.float32)
    )
    hidden_low = hidden.astype(jnp.bfloat16)
    pre_active = jnp.dot(
        hidden_low, wup_full, preferred_element_type=jnp.float32
    ) + biasup_full.astype(jnp.float32)
    active, gelu_back = jax.vjp(gelu_exact, pre_active)
    active_low = active.astype(jnp.bfloat16)
    ffn_out = jnp.dot(
        active_low, wdown_full, preferred_element_type=jnp.float32
    ) + biasdown_full.astype(jnp.float32)
    output, norm_two_back = jax.vjp(
        norm_rows,
        hidden + ffn_out,
        gaintwo_full.astype(jnp.float32),
        shifttwo_full.astype(jnp.float32),
    )
    again = gathered
    wqkv_back = again[0]
    wout_back = again[3]
    wup_back = again[7]
    wdown_back = again[9]
    grad_two, grad_gain_two, grad_shift_two = norm_two_back(cotangent[0].astype(jnp.float32))
    grad_ffn = grad_two.astype(jnp.bfloat16)
    grad_bias_down = jnp.sum(grad_ffn.astype(jnp.float32), axis=0)
    grad_w_down = jnp.einsum("tf,td->fd", active_low, grad_ffn, preferred_element_type=jnp.float32)
    grad_active = jnp.einsum("td,fd->tf", grad_ffn, wdown_back, preferred_element_type=jnp.float32)
    (grad_pre_f,) = gelu_back(grad_active)
    grad_pre = grad_pre_f.astype(jnp.bfloat16)
    grad_bias_up = jnp.sum(grad_pre.astype(jnp.float32), axis=0)
    grad_w_up = jnp.einsum("tc,tf->cf", hidden_low, grad_pre, preferred_element_type=jnp.float32)
    grad_hidden = grad_two + jnp.einsum(
        "tf,cf->tc", grad_pre, wup_back, preferred_element_type=jnp.float32
    )
    grad_one, grad_gain_one, grad_shift_one = norm_one_back(grad_hidden)
    grad_branch = grad_one.astype(jnp.bfloat16)
    grad_bias_out = jnp.sum(grad_branch.astype(jnp.float32), axis=0)
    grad_w_out = jnp.einsum(
        "tc,td->cd", context_low, grad_branch, preferred_element_type=jnp.float32
    )
    grad_context = jnp.einsum(
        "td,cd->tc", grad_branch, wout_back, preferred_element_type=jnp.float32
    )
    grad_context = grad_context.astype(jnp.bfloat16).reshape(tok_rows, head_count, head_size)
    row_delta = jnp.sum(grad_context.astype(jnp.float32) * context, axis=-1).T

    def piece_grads(portion_keys, portion_values, needed):
        key_count = portion_keys.shape[0]
        key_heads = portion_keys.reshape(key_count, head_count, head_size)
        value_heads = portion_values.reshape(key_count, head_count, head_size)
        scores = scores_of(queries, key_heads)
        scores = jnp.where(needed[:, None, :], scores, far_below)
        probs = jnp.exp(scores - log_sum[..., None])
        probs_low = probs.astype(jnp.bfloat16)
        piece_v = jnp.einsum(
            "htk,thd->khd", probs_low, grad_context, preferred_element_type=jnp.float32
        ).reshape(key_count, model_width)
        grad_weights = jnp.einsum(
            "thd,khd->htk", grad_context, value_heads, preferred_element_type=jnp.float32
        )
        grad_scores = (probs * (grad_weights - row_delta[..., None])).astype(jnp.bfloat16)
        piece_q = 0.125 * jnp.einsum(
            "htk,khd->thd", grad_scores, key_heads, preferred_element_type=jnp.float32
        )
        piece_k = 0.125 * jnp.einsum(
            "htk,thd->khd", grad_scores, queries, preferred_element_type=jnp.float32
        ).reshape(key_count, model_width)
        return (piece_k, piece_v, piece_q)

    zero_queries = jnp.zeros((tok_rows, head_count, head_size), jnp.float32)

    def circle_step(step_index, running):
        turn_keys, turn_values, grad_keys, grad_values, grad_queries = running
        owner = (position_ctx - step_index) % group_size
        needed = wanted(owner * tok_rows, tok_rows)

        def update_grads(state):
            grad_k, grad_v, grad_q = state
            piece_k, piece_v, piece_q = piece_grads(turn_keys, turn_values, needed)
            return (grad_k + piece_k, grad_v + piece_v, grad_q + piece_q)

        grad_keys, grad_values, grad_queries = lax.cond(
            jnp.any(needed), update_grads, unchanged, (grad_keys, grad_values, grad_queries)
        )
        turn_keys, turn_values = passed_along((turn_keys, turn_values), "ctx", 1)
        grad_keys, grad_values = (
            passed_along(grad_keys.astype(jnp.bfloat16), "ctx", 1).astype(grad_keys.dtype),
            passed_along(grad_values.astype(jnp.bfloat16), "ctx", 1).astype(grad_values.dtype),
        )
        return (turn_keys, turn_values, grad_keys, grad_values, grad_queries)

    zero_rows = jnp.zeros((tok_rows, model_width), jnp.float32)
    circle_start = (key_rows, value_rows, zero_rows, zero_rows, zero_queries)
    circle_end = lax.fori_loop(0, group_size, circle_step, circle_start)
    grad_keys = circle_end[2]
    grad_values = circle_end[3]
    grad_queries = circle_end[4]
    grad_projected = jnp.concatenate(
        [grad_queries.reshape(tok_rows, model_width), grad_keys, grad_values], axis=1
    ).astype(jnp.bfloat16)
    grad_bias_q = jnp.sum(grad_projected[:, :model_width].astype(jnp.float32), axis=0)
    grad_bias_v = jnp.sum(grad_projected[:, 2 * model_width :].astype(jnp.float32), axis=0)
    grad_w_qkv = jnp.einsum("tc,tj->cj", inputs, grad_projected, preferred_element_type=jnp.float32)
    grad_inputs = grad_one + jnp.einsum(
        "tj,cj->tc", grad_projected, wqkv_back, preferred_element_type=jnp.float32
    )
    terms = (
        grad_w_qkv,
        grad_bias_q,
        grad_bias_v,
        grad_w_out,
        grad_bias_out,
        grad_gain_one,
        grad_shift_one,
        grad_w_up,
        grad_bias_up,
        grad_w_down,
        grad_bias_down,
        grad_gain_two,
        grad_shift_two,
    )
    owned = tuple(
        lax.psum_scatter(term.astype(jnp.bfloat16), "wt", scatter_dimension=0, tiled=True)
        for term in terms
    )
    totals = tuple(lax.psum(term, "ctx").astype(jnp.float32) for term in owned)
    return (
        output[None],
        grad_inputs[None],
        totals[0],
        totals[1],
        totals[2],
        totals[3],
        totals[4],
        totals[5],
        totals[6],
        totals[7],
        totals[8],
        totals[9],
        totals[10],
        totals[11],
        totals[12],
    )


def fast_layer(
    tokens,
    pairing,
    w_qkv,
    bias_q,
    bias_v,
    w_out,
    bias_out,
    gain_one,
    shift_one,
    w_up,
    bias_up,
    w_down,
    bias_down,
    gain_two,
    shift_two,
    cotangent,
):
    width = tokens.shape[2]
    share = width // 4
    position = lax.axis_index("wt")
    vectors = (bias_q, bias_v, bias_out, gain_one, shift_one, bias_down, gain_two, shift_two)
    spread = jnp.tile(jnp.stack(vectors), (1, 4))
    owner = lax.broadcasted_iota(jnp.int32, spread.shape, 1) // share
    spread = jnp.where(owner == position, spread, jnp.zeros_like(spread))
    row = lax.broadcasted_iota(jnp.int32, (8, width), 0)
    lower = jnp.where(row == position, bias_up[None, :], jnp.zeros((8, width), bias_up.dtype))
    small_own = jnp.concatenate([spread, lower])
    output, grad_tokens, g_qkv, g_out, g_up, g_down, g_small = whole_layer(
        tokens[0], cotangent[0], pairing, small_own, w_qkv, w_out, w_up, w_down
    )
    mine = lax.dynamic_slice(g_small, (0, position * share), (8, share))
    grad_bias_up = lax.dynamic_slice(g_small, (8 + position, 0), (1, width))[0]
    wide = tuple(v.astype(jnp.float32) for v in (g_qkv, g_out, g_up, g_down))
    return (
        output[None],
        grad_tokens[None],
        wide[0],
        mine[0],
        mine[1],
        wide[1],
        mine[2],
        mine[3],
        mine[4],
        wide[2],
        grad_bias_up,
        wide[3],
        mine[5],
        mine[6],
        mine[7],
    )


def local(tokens, pairing, *rest):
    rows, width = tokens.shape[1:]
    heads = pairing.shape[0]
    inner = rest[7].shape[1]
    fits = (
        lax.axis_size("wt") == 4
        and lax.axis_size("ctx") == 8
        and tokens.shape[0] == 1
        and rows % BAND == 0
        and 3 * rows <= width
        and width % 256 == 0
        and heads % 4 == 0
        and width == 64 * heads
        and inner == 4 * width
    )
    layer = fast_layer if fits else general_layer
    return layer(tokens, pairing, *rest)


def solution(mesh):
    in_specs = (
        P("wt", "ctx", None),
        P(),
        P("wt", None),
        P("wt"),
        P("wt"),
        P("wt", None),
        P("wt"),
        P("wt"),
        P("wt"),
        P("wt", None),
        P("wt"),
        P("wt", None),
        P("wt"),
        P("wt"),
        P("wt"),
        P("wt", "ctx", None),
    )
    out_specs = (
        P("wt", "ctx", None),
        P("wt", "ctx", None),
        P("wt", None),
        P("wt"),
        P("wt"),
        P("wt", None),
        P("wt"),
        P("wt"),
        P("wt"),
        P("wt", None),
        P("wt"),
        P("wt", None),
        P("wt"),
        P("wt"),
        P("wt"),
    )
    return jax.shard_map(local, mesh=mesh, in_specs=in_specs, out_specs=out_specs, check_vma=False)
```

```python
import functools

import jax
import jax.numpy as jnp
from jax import lax
from jax.experimental import pallas as pl
from jax.experimental.pallas import tpu as pltpu
from jax.sharding import PartitionSpec as P

F32, BF16 = jnp.float32, jnp.bfloat16
MESH = pl.DeviceIdType.MESH
BAND = 32


def nn(a, b):
    return jnp.dot(a, b, preferred_element_type=F32)


def nt(a, b):
    return lax.dot_general(a, b, (((1,), (1,)), ((), ())), preferred_element_type=F32)


def aligned(start, multiple):
    return start if isinstance(start, int) else pl.multiple_of(start, multiple)


def chunk_of(index, size):
    return pl.ds(aligned(index * size, size), size)


class Wire:
    def __init__(self, sends, receives, anyone):
        self.sends, self.receives, self.anyone = sends, receives, anyone
        self.firsts, self.used, self.started = {}, 0, {}

    def slot(self, name, count=1):
        if name not in self.firsts:
            self.firsts[name] = self.used, count
            self.used += count
        first, had = self.firsts[name]
        assert had == count
        return first

    def copy(self, slot, source, target, where):
        return pltpu.make_async_remote_copy(
            src_ref=source,
            dst_ref=target,
            send_sem=self.sends.at[slot],
            recv_sem=self.receives.at[slot],
            device_id=where,
            device_id_type=MESH,
        )

    def send(self, name, source, target, where):
        copy = self.copy(self.slot(name), source, target, where)
        copy.start()
        self.started[name] = copy

    def arrived(self, name, target):
        self.copy(self.slot(name), target, target, self.anyone).wait_recv()

    def left(self, *names):
        for name in names:
            self.started.pop(name).wait_send()

    def close(self):
        self.left(*tuple(self.started))


class Place:
    def __init__(self):
        self.w = w = lax.axis_index("wt")
        self.c = c = lax.axis_index("ctx")
        self.core = core = c % 2
        self.other = 1 - core
        self.z = z = c // 2
        self.near = z % 2
        self.far = 1 - self.near
        self.nx = w + 1 - 2 * (w % 2)
        self.ny = (w + 2) % 4
        self.nd = 3 - w
        self.sib = (w, c + 1 - 2 * core)
        self.to_x, self.to_y, self.to_d = (self.nx, c), (self.ny, c), (self.nd, c)
        self.cross = (w, c + 2 - 4 * self.near)
        self.partner = (w, (c + 4) % 8)
        self.lines = [(w, spot * 2 + core) for spot in (z + 1 - 2 * (z % 2), (z + 2) % 4, 3 - z)]
        self.others = [(w, (c + step) % 8) for step in range(1, 8)]
        self.mate, self.middle = self.lines[0], self.lines[2]
        self.outer, self.inner = (z == 0) | (z == 3), (z == 1) | (z == 2)


def greet(peers):
    barrier = pltpu.get_barrier_semaphore()
    for peer in peers:
        pl.semaphore_signal(barrier, inc=1, device_id=peer, device_id_type=MESH)
    pl.semaphore_wait(barrier, len(peers))


class Part:
    def __init__(self, name, local, full, first, columns, place, wire):
        self.name, self.local, self.full, self.place, self.wire = name, local, full, place, wire
        self.rows = local.shape[0]
        self.first, self.columns = first, columns // 2

    def piece(self, owner, core, half=None):
        rows, start = self.rows, owner * self.rows
        if half is not None:
            rows = self.rows // 2
            start = start + half * rows
        return self.full.at[
            pl.ds(aligned(start, 16), rows),
            pl.ds(aligned(self.first + core * self.columns, 128), self.columns),
        ]

    def begin(self):
        at, wire = self.place, self.wire
        mine = self.local.at[
            :, pl.ds(aligned(self.first + at.core * self.columns, 128), self.columns)
        ]
        target = self.piece(at.w, at.core)
        wire.send(self.name + "a", mine, target, at.to_x)
        wire.send(self.name + "b", mine, target, at.to_y)

    def relay(self):
        at, wire = self.place, self.wire
        block = self.piece(at.nx, at.core)
        wire.arrived(self.name + "a", block)
        half = self.piece(at.nx, at.core, 0)
        wire.send(self.name + "c", half, half, at.to_y)
        wire.send(self.name + "d", block, block, at.sib)
        block = self.piece(at.ny, at.core)
        wire.arrived(self.name + "b", block)
        half = self.piece(at.ny, at.core, 1)
        wire.send(self.name + "e", half, half, at.to_x)
        wire.send(self.name + "f", block, block, at.sib)

    def share(self):
        at, wire = self.place, self.wire
        wire.arrived(self.name + "c", self.piece(at.nd, at.core, 0))
        wire.arrived(self.name + "e", self.piece(at.nd, at.core, 1))
        block = self.piece(at.nd, at.core)
        wire.send(self.name + "g", block, block, at.sib)

    def finish(self):
        at, wire = self.place, self.wire
        wire.arrived(self.name + "d", self.piece(at.nx, at.other))
        wire.arrived(self.name + "f", self.piece(at.ny, at.other))
        wire.arrived(self.name + "g", self.piece(at.nd, at.other))


def add_into(target, *sources):
    rows, columns = sources[0].shape
    band = 16
    while columns * band * 2 <= 1 << 15 and rows % (band * 2) == 0:
        band *= 2

    @pl.loop(0, rows // band)
    def _(index):
        where = chunk_of(index, band)
        total = sources[0][where, :].astype(F32)
        for source in sources[1:]:
            total = total + source[where, :].astype(F32)
        target[where, :] = total.astype(target.dtype)


class Grad:
    def __init__(self, name, chunks, blocks, buffers, finals, place, wire, local_sems):
        self.name, self.chunks, self.blocks, self.finals = name, chunks, blocks, finals
        self.place, self.wire, self.local_sems = place, wire, local_sems
        self.from_x, self.from_y, self.diag_x, self.diag_y, self.low, self.high = buffers
        self.rows, self.columns = self.from_x.shape

    def half(self, ref, index):
        return ref.at[pl.ds(index * (self.rows // 2), self.rows // 2), :]

    def begin(self):
        at, wire = self.place, self.wire
        block = self.blocks(at.nd)
        wire.send(self.name + "a", self.half(block, 0), self.diag_x, at.to_x)
        wire.send(self.name + "b", self.half(block, 1), self.diag_y, at.to_y)

    def mid(self):
        at, wire = self.place, self.wire
        wire.arrived(self.name + "a", self.diag_x)
        block = self.blocks(at.ny)
        part = self.half(block, 0)
        add_into(part, part, self.diag_x)
        wire.send(self.name + "d", block, self.from_y, at.to_y)
        wire.arrived(self.name + "b", self.diag_y)
        block = self.blocks(at.nx)
        part = self.half(block, 1)
        add_into(part, part, self.diag_y)
        wire.send(self.name + "c", block, self.from_x, at.to_x)

    def cut(self, ref, chunk):
        count = self.rows // self.chunks
        return ref.at[pl.ds(chunk * count, count), :]

    def hop(self, kind, chunk, source, target, where):
        slot = self.wire.slot(self.name + kind, self.chunks) + chunk
        return self.wire.copy(slot, self.cut(source, chunk), self.cut(target, chunk), where)

    def outward(self, chunk):
        return self.hop("u", chunk, self.blocks(self.place.w), self.low, self.place.mate)

    def across(self, chunk):
        return self.hop("v", chunk, self.from_x, self.high, self.place.middle)

    def back(self, chunk):
        return self.hop("t", chunk, self.from_y, self.high, self.place.mate)

    def own(self):
        at, wire = self.place, self.wire
        wire.arrived(self.name + "c", self.from_x)
        wire.arrived(self.name + "d", self.from_y)
        block = self.blocks(at.w)
        for chunk in range(self.chunks):
            part = self.cut(block, chunk)
            add_into(part, part, self.cut(self.from_x, chunk), self.cut(self.from_y, chunk))

            @pl.when(at.outer)
            def _(chunk=chunk):
                self.outward(chunk).start()

    def chain(self, chunk):
        at = self.place

        @pl.when(at.inner)
        def _():
            self.outward(chunk).wait_recv()
            block = self.blocks(at.w)
            add_into(
                self.cut(self.from_x, chunk), self.cut(block, chunk), self.cut(self.low, chunk)
            )
            self.across(chunk).start()

    def total(self, chunk):
        at = self.place

        @pl.when(at.inner)
        def _():
            self.across(chunk).wait_recv()
            add_into(
                self.cut(self.from_y, chunk),
                self.cut(self.from_x, chunk),
                self.cut(self.high, chunk),
            )
            self.back(chunk).start()
            for copy in self.copies(chunk, self.from_y):
                copy.start()

    def copies(self, chunk, source):
        at, wire = self.place, self.wire
        piece, target = self.cut(source, chunk), self.finals(chunk, at.core)
        keep = pltpu.make_async_copy(piece, target, self.local_sems.at[chunk])
        slot = wire.slot(self.name + "s", self.chunks) + chunk
        return keep, wire.copy(slot, piece, target, at.sib)

    def give(self, chunk):
        at = self.place

        @pl.when(at.outer)
        def _():
            self.back(chunk).wait_recv()
            for copy in self.copies(chunk, self.high):
                copy.start()

    def close(self):
        at = self.place
        for chunk in range(self.chunks):
            for copy in self.copies(chunk, self.from_y):
                copy.wait()

            @pl.when(at.outer)
            def _(chunk=chunk):
                self.outward(chunk).wait_send()

            @pl.when(at.inner)
            def _(chunk=chunk):
                self.across(chunk).wait_send()
                self.back(chunk).wait_send()


def layer_scratch(rows, width, inner, heads):
    pairs = heads // 2
    some = pairs // 2
    share = width // 4
    half = width // 2
    groups = 8

    def low(*shape):
        return pltpu.VMEM(shape, BF16)

    def wide(*shape):
        return pltpu.VMEM(shape, F32)

    scratch = dict(
        wqkv=low(width, 3 * width),
        wo=low(width, width),
        wu=low(width, inner),
        wd=low(inner, width),
        order=low(width, width),
        tok=low(2, rows, width),
        small_own=low(16, width),
        small_in=low(3, 16, width),
        small=wide(16, width),
        bias_qkv=wide(8, 3 * width),
        bias_up=wide(8, inner),
        kv=low(pairs, 4, rows, 256),
        proj=low(rows, 3 * width),
        q=low(pairs, rows, 128),
        q_out=low(some, rows, 128),
        exps=low(heads, 4 * rows, rows),
        inverse=wide(heads, 1, rows),
        out_t=wide(pairs, 128, rows),
        ctx=low(pairs, rows, 128),
        ctx_out=low(some, rows, 128),
        ctx_nat=low(2, rows, width),
        hat_one=wide(rows, width),
        r_one=wide(rows, 1),
        flow=wide(rows, width),
        stage=wide(rows, width),
        result=wide(rows, width),
        hid=low(2, rows, width),
        act=low(2, rows, inner),
        slope=low(rows, inner),
        slope_in=low(rows, inner // 2),
        gf=low(rows, width),
        gf_in=low(rows, half),
        gb=low(rows, width),
        gb_in=low(rows, half),
        do=low(pairs, rows, 128),
        do_out=low(some, rows, 128),
        dq=low(pairs, rows, 128),
        dq_out=low(some, rows, 128),
        dkv_in=low(pairs, rows, 512),
        dkv_far=low(pairs, rows, 256),
        gkv=low(2, rows, width),
        gj_in=low(rows, 3 * half),
        sums=wide(16, groups, width),
        sums_up=wide(groups, inner),
        vec=wide(16, width),
        vec_in=wide(7, 16, width),
        dwd=low(4, inner // 4, half),
    )
    shapes = dict(
        d=(inner // 4, half), u=(2 * share, width), o=(share, half), q=(3 * share, half)
    )
    for name, (r, c) in shapes.items():
        for kind in ("fx", "fy", "lo", "hi"):
            scratch["g" + name + kind] = low(r, c)
        for kind in ("dx", "dy"):
            scratch["g" + name + kind] = low(r // 2, c)
    scratch["sends"] = pltpu.SemaphoreType.DMA((160,))
    scratch["receives"] = pltpu.SemaphoreType.DMA((160,))
    scratch["own_sems"] = pltpu.SemaphoreType.DMA((20,))
    return scratch


def layer_kernel(names, *refs):
    (
        tokens,
        cot,
        pairing,
        small_raw,
        qkv_l,
        out_l,
        up_l,
        down_l,
        output,
        grad_tokens,
        g_qkv,
        g_out,
        g_up,
        g_down,
        g_small,
    ) = refs[:15]
    s = dict(zip(names, refs[15:]))
    at = Place()
    wire = Wire(s["sends"], s["receives"], at.sib)
    rows, width = tokens.shape
    inner = up_l.shape[1]
    heads = pairing.shape[0]
    pairs, some = heads // 2, heads // 4
    size = width // heads
    half = width // 2
    keys = 4 * rows
    chunks = width // 256
    share = width // 4
    core, other = at.core, at.other

    greet([at.to_x, at.to_y, at.to_d] + at.others)

    part_kv = Part("kv", qkv_l, s["wqkv"], width, 2 * width, at, wire)
    part_q = Part("q", qkv_l, s["wqkv"], 0, width, at, wire)
    part_o = Part("o", out_l, s["wo"], 0, width, at, wire)
    part_u = Part("u", up_l, s["wu"], 0, inner, at, wire)
    part_d = Part("d", down_l, s["wd"], 0, width, at, wire)
    part_kv.begin()
    raw = small_raw[...]
    row = lax.broadcasted_iota(jnp.int32, (share, width), 0)
    column = lax.broadcasted_iota(jnp.int32, (share, width), 1)

    def spread(values, spot):
        place = jnp.where(column - row == spot * share, 1.0, 0.0).astype(BF16)
        return nn(values, place)

    own_row = lax.broadcasted_iota(jnp.int32, (8, width), 0) == at.w
    line = spread(raw[8:16], 0)[0:1]
    for index in range(1, 4):
        line = line + spread(raw[8:16], index)[index : index + 1]
    small_own = s["small_own"]
    small_own[...] = jnp.concatenate(
        [spread(raw[:8], at.w), jnp.where(own_row, line, 0.0)], axis=0
    ).astype(BF16)
    for index, where in enumerate((at.to_x, at.to_y, at.to_d)):
        wire.send("sm" + str(index), small_own, s["small_in"].at[index], where)
    keeps = []
    for slot, (local, full) in enumerate(
        (
            (qkv_l, s["wqkv"].at[pl.ds(aligned(at.w * share, 16), share)]),
            (tokens, s["tok"].at[core]),
            (out_l, s["wo"].at[pl.ds(aligned(at.w * share, 16), share)]),
            (up_l, s["wu"].at[pl.ds(aligned(at.w * share, 16), share)]),
            (down_l, s["wd"].at[pl.ds(aligned(at.w * (inner // 4), 16), inner // 4)]),
        )
    ):
        keeps.append(pltpu.make_async_copy(local, full, s["own_sems"].at[slot]))
        keeps[-1].start()
    wire.send("tok", tokens, s["tok"].at[core], at.sib)

    before = 0
    for head in range(heads):
        flag = pairing[head]
        spot = flag * (heads // 2 + before) + (1 - flag) * (head - before)
        before = before + flag
        row = lax.broadcasted_iota(jnp.int32, (size, width), 0)
        column = lax.broadcasted_iota(jnp.int32, (size, width), 1)
        s["order"][head * size : (head + 1) * size, :] = jnp.where(
            column - row == spot * size, 1.0, 0.0
        ).astype(BF16)

    part_kv.relay()
    part_kv.share()
    part_q.begin()
    for index in range(3):
        wire.arrived("sm" + str(index), s["small_in"].at[index])
    small = s["small"]
    small[...] = (
        small_own[...].astype(F32)
        + s["small_in"][0].astype(F32)
        + s["small_in"][1].astype(F32)
        + s["small_in"][2].astype(F32)
    )
    s["bias_qkv"][0:1, 0:width] = small[0:1, :]
    s["bias_qkv"][0:1, width : 2 * width] = jnp.zeros((1, width), F32)
    s["bias_qkv"][0:1, 2 * width :] = small[1:2, :]
    for index in range(inner // width):
        s["bias_up"][0:1, index * width : (index + 1) * width] = small[8 + index : 9 + index, :]
    keeps[0].wait()
    keeps[1].wait()
    part_kv.finish()

    tok, proj, order, kv = s["tok"], s["proj"], s["order"], s["kv"]
    own_slot = core * 2 + at.near

    def project(first, count):
        @pl.loop(first, first + count)
        def _(index):
            where = chunk_of(index, 256)
            made = nn(tok[core], s["wqkv"][:, where]) + s["bias_qkv"][0:1, where]
            proj[:, where] = made.astype(BF16)

    project(chunks, 2 * chunks)
    for index in range(chunks):
        columns = order[:, index * 256 : (index + 1) * 256]
        for kind in range(2):
            moved = nn(proj[:, (1 + kind) * width : (2 + kind) * width], columns).astype(BF16)
            for e in range(2):
                kv[2 * index + e, own_slot, :, kind * 128 : (kind + 1) * 128] = moved[
                    :, e * 128 : (e + 1) * 128
                ]
    sequence = [(index + some) % pairs for index in range(pairs)]
    near_base = wire.slot("near kv", pairs)
    far_base = wire.slot("far kv", pairs)
    pass_base = wire.slot("passed kv", pairs)

    def kv_copy(base, pair, slot, where):
        block = kv.at[pair, slot]
        return wire.copy(base + pair, block, block, where)

    for pair in sequence:
        if pair >= some:
            kv_copy(far_base, pair, own_slot, at.cross).start()
        kv_copy(near_base, pair, own_slot, at.sib).start()
    part_q.relay()
    part_o.begin()
    part_q.share()
    part_q.finish()
    project(0, chunks)
    q, q_out = s["q"], s["q_out"]
    for index in range(chunks):
        moved = nn(proj[:, 0:width], order[:, index * 256 : (index + 1) * 256]).astype(BF16)
        for e in range(2):
            pair = 2 * index + e
            block = moved[:, e * 128 : (e + 1) * 128]
            if pair < some:
                q[pair] = block
            else:
                q_out[pair - some] = block
    wire.send("q", q_out, q.at[pl.ds(some, some)], at.partner)
    kv_copy(far_base, 0, own_slot, at.cross).start()
    part_o.relay()
    part_u.begin()
    part_o.share()

    exps, inverse, out_t = s["exps"], s["inverse"], s["out_t"]

    def both(pair, first):
        return kv[pair, :, :, first : first + 128].reshape(keys, 128)

    def masked(block, e, axis=1):
        spot = lax.broadcasted_iota(jnp.int32, block.shape, axis)
        mine = spot < size if e == 0 else spot >= size
        return jnp.where(mine, block, jnp.zeros_like(block))

    def attend(pair):
        key_rows, value_rows = both(pair, 0), both(pair, 128)
        values_t = value_rows.T
        queries = q[pair] * jnp.asarray(size**-0.5, BF16)
        parts = []
        for e in range(2):
            scores = nt(key_rows, masked(queries, e))
            top = jnp.max(scores, axis=0, keepdims=True)
            raised = jnp.exp(scores - top)
            total = jnp.sum(raised, axis=0, keepdims=True)
            low = raised.astype(BF16)
            exps[2 * pair + e] = low
            one_over = 1.0 / total
            inverse[2 * pair + e] = one_over
            parts.append(nn(values_t[e * size : (e + 1) * size], low) * one_over)
        merged = jnp.concatenate(parts, axis=0)
        out_t[pair] = merged
        return merged.T.astype(BF16)

    def receive_kv(pair):
        kv_copy(far_base, pair, core * 2 + at.far, at.cross).wait_recv()
        kv_copy(pass_base, pair, core * 2 + at.far, at.sib).start()
        kv_copy(near_base, pair, other * 2 + at.near, at.sib).wait_recv()
        kv_copy(pass_base, pair, other * 2 + at.far, at.sib).wait_recv()

    ctx, ctx_out = s["ctx"], s["ctx_out"]
    back_base = wire.slot("ctx", some)

    def ctx_copy(index):
        return wire.copy(back_base + index, ctx_out.at[index], ctx.at[some + index], at.partner)

    wire.arrived("q", q.at[pl.ds(some, some)])
    part_d.begin()

    @pl.loop(0, some)
    def _(index):
        receive_kv(index + some)

        @pl.when(index + 1 < some)
        def _():
            kv_copy(far_base, index + 1, own_slot, at.cross).start()

        ctx_out[index] = attend(index + some)
        ctx_copy(index).start()

    part_u.relay()
    part_o.finish()

    @pl.loop(0, some)
    def _(index):
        receive_kv(index)
        ctx[index] = attend(index)

    part_d.relay()
    part_u.share()
    keeps[2].wait()
    for index in range(some):
        ctx_copy(index).wait_recv()
    permuted = jnp.concatenate([ctx[pair] for pair in range(pairs)], axis=1)
    ctx_nat, stage = s["ctx_nat"], s["stage"]
    for index in range(chunks):
        where = slice(index * 256, (index + 1) * 256)
        ctx_nat[core, :, where] = nt(permuted, order[where, :]).astype(BF16)
    wire.send("ctxn", ctx_nat.at[core], ctx_nat.at[core], at.sib)

    @pl.loop(0, chunks)
    def _(index):
        where = chunk_of(index, 256)
        stage[:, where] = nn(ctx_nat[core], s["wo"][:, where])

    hat_one, r_one, flow, hid = s["hat_one"], s["r_one"], s["flow"], s["hid"]
    inv_width = 1.0 / width

    def mean(values):
        return jnp.sum(values, axis=-1, keepdims=True) * inv_width

    @pl.loop(0, rows // BAND)
    def _(index):
        where = chunk_of(index, BAND)
        total = tok[core, where, :].astype(F32) + stage[where, :] + small[2:3, :]
        centred = total - mean(total)
        scale = lax.rsqrt(mean(centred * centred) + 1e-12)
        hat = centred * scale
        hat_one[where, :] = hat
        r_one[where, :] = scale
        hidden = hat * small[3:4, :] + small[4:5, :]
        flow[where, :] = hidden
        hid[core, where, :] = hidden.astype(BF16)

    wire.send("hid", hid.at[core], hid.at[core], at.sib)
    part_u.finish()
    keeps[3].wait()
    act, slope = s["act"], s["slope"]

    @pl.loop(0, inner // 256)
    def _(index):
        where = chunk_of(index, 256)
        pre = nn(hid[core], s["wu"][:, where]) + s["bias_up"][0:1, where]
        below = 0.5 * (1.0 + lax.erf(pre * (0.5**0.5)))
        act[core, :, where] = (pre * below).astype(BF16)
        density = jnp.exp(pre * pre * -0.5) * 0.3989422804014327
        slope[:, where] = (below + pre * density).astype(BF16)

    wire.send("act", act.at[core], act.at[core], at.sib)
    part_d.share()
    part_d.finish()
    keeps[4].wait()

    @pl.loop(0, chunks)
    def _(index):
        where = chunk_of(index, 256)
        stage[:, where] = nn(act[core], s["wd"][:, where])

    result, gf = s["result"], s["gf"]
    sums, sums_up = s["sums"], s["sums_up"]
    sums[...] = jnp.zeros_like(sums)

    def gather_rows(values):
        return jnp.sum(values.reshape(BAND // 8, 8, values.shape[-1]), axis=0)

    @pl.loop(0, rows // BAND)
    def _(index):
        where = chunk_of(index, BAND)
        total = flow[where, :] + stage[where, :] + small[5:6, :]
        centred = total - mean(total)
        scale = lax.rsqrt(mean(centred * centred) + 1e-12)
        hat = centred * scale
        result[where, :] = hat * small[6:7, :] + small[7:8, :]
        back = cot[where, :].astype(F32)
        g = back * small[6:7, :]
        grad = scale * (g - mean(g) - hat * mean(g * hat))
        flow[where, :] = grad
        low = grad.astype(BF16)
        gf[where, :] = low
        sums[6] += gather_rows(back * hat)
        sums[7] += gather_rows(back)
        sums[5] += gather_rows(low.astype(F32))

    keep_out = pltpu.make_async_copy(result, output, s["own_sems"].at[5])
    keep_out.start()

    def columns_of(which, count):
        return pl.ds(aligned(which * count, 128), count)

    wire.send("gf", gf.at[:, columns_of(other, half)], s["gf_in"], at.sib)

    def buffers(name):
        return [s["g" + name + kind] for kind in ("fx", "fy", "dx", "dy", "lo", "hi")]

    dwd, wd, wu = s["dwd"], s["wd"], s["wu"]

    def side_by_side(first, count, owner):
        return wd.at[
            pl.ds(aligned(first + (owner // 2) * count, 16), count),
            pl.ds(aligned((owner % 2) * half, 128), half),
        ]

    def dwo(owner):
        return side_by_side(2 * width + 6 * share, share, owner)

    def dwq(owner):
        return side_by_side(2 * width, 3 * share, owner)

    grad_d = Grad(
        "gd",
        2,
        lambda r: dwd.at[r],
        buffers("d"),
        lambda i, k: g_down.at[pl.ds(i * (inner // 8), inner // 8), columns_of(k, half)],
        at,
        wire,
        s["own_sems"].at[pl.ds(6, 2)],
    )
    grad_u = Grad(
        "gu",
        2,
        lambda r: wd.at[pl.ds(aligned(r * (2 * share), 16), 2 * share), :],
        buffers("u"),
        lambda i, k: g_up.at[:, columns_of(2 * k + i, width)],
        at,
        wire,
        s["own_sems"].at[pl.ds(8, 2)],
    )
    grad_o = Grad(
        "go",
        1,
        dwo,
        buffers("o"),
        lambda i, k: g_out.at[:, columns_of(k, half)],
        at,
        wire,
        s["own_sems"].at[pl.ds(10, 1)],
    )
    grad_q = Grad(
        "gq",
        3,
        dwq,
        buffers("q"),
        lambda i, k: g_qkv.at[:, columns_of(3 * k + i, half)],
        at,
        wire,
        s["own_sems"].at[pl.ds(11, 3)],
    )

    wire.arrived("act", act.at[other])
    wire.arrived("gf", s["gf_in"])
    gf_mine = gf[:, columns_of(core, half)]
    gf_theirs = s["gf_in"][...]
    quarter = inner // 4
    for owner in (at.nd, at.nx, at.ny, at.w):
        where = pl.ds(aligned(owner * quarter, 128), quarter)
        made = nn(act[core, :, where].T, gf_mine) + nn(act[other, :, where].T, gf_theirs)
        dwd[owner] = made.astype(BF16)
        if owner is at.nd:
            grad_d.begin()

    @pl.loop(0, inner // 256)
    def _(index):
        where = chunk_of(index, 256)
        grad = nt(gf[...], wd[where, :]) * slope[:, where].astype(F32)
        low = grad.astype(BF16)
        slope[:, where] = low
        sums_up[:, where] = jnp.sum(low.astype(F32).reshape(rows // 8, 8, 256), axis=0)

    wire.send("slope", slope.at[:, columns_of(other, inner // 2)], s["slope_in"], at.sib)
    grad_d.mid()

    @pl.loop(0, chunks)
    def _(index):
        where = chunk_of(index, 256)
        stage[:, where] = nt(slope[...], wu[where, :])

    gb = s["gb"]

    @pl.loop(0, rows // BAND)
    def _(index):
        where = chunk_of(index, BAND)
        grad_hidden = flow[where, :] + stage[where, :]
        hat = hat_one[where, :]
        g = grad_hidden * small[3:4, :]
        grad = r_one[where, :] * (g - mean(g) - hat * mean(g * hat))
        flow[where, :] = grad
        low = grad.astype(BF16)
        gb[where, :] = low
        sums[3] += gather_rows(grad_hidden * hat)
        sums[4] += gather_rows(grad_hidden)
        sums[2] += gather_rows(low.astype(F32))

    wire.send("gb", gb.at[:, columns_of(other, half)], s["gb_in"], at.sib)

    @pl.loop(0, chunks)
    def _(index):
        where = chunk_of(index, 256)
        proj[:, where] = nt(gb[...], s["wo"][where, :]).astype(BF16)

    do, do_out = s["do"], s["do_out"]
    for index in range(chunks):
        moved = nn(proj[:, 0:width], order[:, index * 256 : (index + 1) * 256]).astype(BF16)
        for e in range(2):
            pair = 2 * index + e
            block = moved[:, e * 128 : (e + 1) * 128]
            if pair < some:
                do[pair] = block
            else:
                do_out[pair - some] = block
    wire.send("do", do_out, do.at[pl.ds(some, some)], at.partner)

    wire.left("dc", "dd", "de", "df", "dg")
    wire.arrived("hid", hid.at[other])
    wire.arrived("slope", s["slope_in"])
    mine_t, theirs_t = hid[core].T, hid[other].T
    for index in range(inner // 2 // half):
        where = pl.ds(aligned(core * (inner // 2) + index * half, 128), half)
        made = nn(mine_t, slope[:, where]) + nn(
            theirs_t, s["slope_in"][:, index * half : (index + 1) * half]
        )
        made = made.astype(BF16)
        for owner in range(4):
            first = owner * 2 * share + (index // 2) * share
            wd[first : first + share, (index % 2) * half : (index % 2 + 1) * half] = made[
                owner * share : (owner + 1) * share
            ]
    grad_u.begin()
    wire.arrived("ctxn", ctx_nat.at[other])
    wire.arrived("gb", s["gb_in"])
    made = nn(ctx_nat[core].T, gb[:, columns_of(core, half)]) + nn(
        ctx_nat[other].T, s["gb_in"][...]
    )
    made = made.astype(BF16)
    for owner in range(4):
        dwo(owner)[...] = made[owner * share : (owner + 1) * share]
    grad_o.begin()

    wire.left("uc", "ud", "ue", "uf", "ug")
    dq, dq_out, dkv_in, dkv_far = s["dq"], s["dq_out"], s["dkv_in"], s["dkv_far"]
    near_d = wire.slot("near dkv", pairs)
    far_d = wire.slot("far dkv", pairs)
    dq_base = wire.slot("dq", some)
    lots = inner // 1024

    def tile(pair, slot, count=1):
        band = pair // lots
        column = (pair % lots) * 1024 + slot * 256
        return wu.at[
            pl.ds(aligned(band * rows, 16), rows),
            pl.ds(aligned(column, 256), 256 * count),
        ]

    def spare(pair):
        bands = -(-pairs // lots)
        band = bands + pair // (4 * lots)
        return wu.at[
            pl.ds(aligned(band * rows, 16), rows),
            pl.ds(aligned((pair % (4 * lots)) * 256, 256), 256),
        ]

    def dkv_near(pair):
        return wire.copy(near_d + pair, tile(pair, other * 2, 2), dkv_in.at[pair], at.sib)

    def dkv_cross(pair):
        return wire.copy(far_d + pair, spare(pair), dkv_far.at[pair], at.cross)

    def attend_back(pair):
        key_rows, value_rows = both(pair, 0), both(pair, 128)
        keys_t = key_rows.T
        queries = q[pair] * jnp.asarray(size**-0.5, BF16)
        do_t = do[pair].astype(F32).T
        scaled = jnp.concatenate(
            [do_t[e * size : (e + 1) * size] * inverse[2 * pair + e] for e in range(2)], axis=0
        )
        product = scaled * out_t[pair]
        scaled_low = scaled.astype(BF16)
        scaled_rows = scaled.T.astype(BF16)
        dv = dk = None
        dq_parts = []
        for e in range(2):
            delta = jnp.sum(product[e * size : (e + 1) * size], axis=0, keepdims=True)
            grad_w = nn(value_rows, masked(scaled_low, e, 0))
            low = exps[2 * pair + e]
            grad_s = (low.astype(F32) * (grad_w - delta)).astype(BF16)
            more_v = nn(low, masked(scaled_rows, e))
            more_k = nn(grad_s, masked(queries, e))
            dv = more_v if dv is None else dv + more_v
            dk = more_k if dk is None else dk + more_k
            dq_parts.append(nn(keys_t[e * size : (e + 1) * size], grad_s))
        made = jnp.concatenate([dk, dv], axis=1).astype(BF16)
        for slot in range(4):
            tile(pair, slot)[...] = made[slot * rows : (slot + 1) * rows]
        dkv_near(pair).start()
        return (jnp.concatenate(dq_parts, axis=0).T * size**-0.5).astype(BF16)

    def pass_on(pair):
        dkv_near(pair).wait_recv()
        add_into(
            spare(pair), tile(pair, core * 2 + at.far), dkv_in.at[pair, :, columns_of(at.far, 256)]
        )
        dkv_cross(pair).start()

    def dq_copy(index):
        return wire.copy(dq_base + index, dq_out.at[index], dq.at[some + index], at.partner)

    @pl.loop(0, some)
    def _(index):
        dq[index] = attend_back(index)

        @pl.when(index > 0)
        def _():
            pass_on(index - 1)

    wire.arrived("do", do.at[pl.ds(some, some)])

    @pl.loop(0, some)
    def _(index):
        dq_out[index] = attend_back(index + some)
        dq_copy(index).start()
        pass_on(index + some - 1)

    pass_on(pairs - 1)
    grad_u.mid()
    grad_o.mid()

    gkv = s["gkv"]
    for pair in range(pairs):
        dkv_cross(pair).wait_recv()
    grad_d.own()
    for pair in range(pairs):
        own = tile(pair, own_slot)
        near = dkv_in.at[pair, :, columns_of(at.near, 256)]
        for kind in range(2):
            cut = slice(kind * 128, (kind + 1) * 128)
            gkv[kind, :, pair * 128 : (pair + 1) * 128] = (
                own[:, cut].astype(F32)
                + near[:, cut].astype(F32)
                + dkv_far[pair, :, cut].astype(F32)
            ).astype(BF16)
    for index in range(some):
        dq_copy(index).wait_recv()
    merged = jnp.concatenate([dq[pair] for pair in range(pairs)], axis=1)
    for index in range(chunks):
        where = slice(index * 256, (index + 1) * 256)
        rows_of = order[where, :]
        for kind in range(3):
            source = merged if kind == 0 else gkv[kind - 1]
            low = nt(source, rows_of).astype(BF16)
            proj[:, kind * width + index * 256 : kind * width + (index + 1) * 256] = low
            if kind != 1:
                sums[kind // 2, :, where] = jnp.sum(
                    low.astype(F32).reshape(rows // 8, 8, 256), axis=0
                )
    wire.send("gj", proj.at[:, columns_of(other, 3 * half)], s["gj_in"], at.sib)

    vec, vec_in = s["vec"], s["vec_in"]
    for row in range(8):
        vec[row : row + 1, :] = jnp.sum(sums[row], axis=0, keepdims=True)
    for index in range(inner // width):
        vec[8 + index : 9 + index, :] = jnp.sum(
            sums_up[:, index * width : (index + 1) * width], axis=0, keepdims=True
        )
    for row in range(8 + inner // width, 16):
        vec[row : row + 1, :] = jnp.zeros((1, width), F32)
    wire.send("va", vec, vec_in.at[0], at.sib)

    wire.arrived("tok", tok.at[other])
    wire.arrived("gj", s["gj_in"])
    mine_t, theirs_t = tok[core].T, tok[other].T
    for index in range(3):
        where = pl.ds(aligned(core * (3 * half) + index * half, 128), half)
        made = nn(mine_t, proj[:, where]) + nn(
            theirs_t, s["gj_in"][:, index * half : (index + 1) * half]
        )
        made = made.astype(BF16)
        for owner in range(4):
            dwq(owner)[index * share : (index + 1) * share, :] = made[
                owner * share : (owner + 1) * share
            ]
    grad_q.begin()

    wire.arrived("va", vec_in.at[0])
    vec_in[0] = vec_in[0] + vec[...]
    for index, where in enumerate((at.to_x, at.to_y, at.to_d)):
        wire.send("vb" + str(index), vec_in.at[0], vec_in.at[1 + index], where)
    grad_u.own()
    grad_d.chain(0)
    keep_out.wait()

    @pl.loop(0, chunks)
    def _(index):
        where = chunk_of(index, 256)
        result[:, where] = nt(proj[...], s["wqkv"][where, :]) + flow[:, where]

    keep_grad = pltpu.make_async_copy(result, grad_tokens, s["own_sems"].at[5])
    keep_grad.start()
    grad_q.mid()
    grad_o.own()
    grad_d.chain(1)
    for index in range(3):
        wire.arrived("vb" + str(index), vec_in.at[1 + index])
    wire.left("va")
    vec[...] = (vec_in[0] + vec_in[1]) + (vec_in[2] + vec_in[3])
    for index, where in enumerate(at.lines):
        wire.send("vc" + str(index), vec, vec_in.at[4 + index], where)
    grad_d.total(0)
    grad_u.chain(0)
    grad_d.total(1)
    grad_q.own()
    grad_u.chain(1)
    grad_u.total(0)
    grad_o.chain(0)
    grad_q.chain(0)
    grad_u.total(1)
    grad_o.total(0)
    grad_q.chain(1)
    grad_q.total(0)
    grad_q.chain(2)
    grad_q.total(1)
    for index in range(3):
        wire.arrived("vc" + str(index), vec_in.at[4 + index])
    g_small[...] = (vec[...] + vec_in[4]) + (vec_in[5] + vec_in[6])
    grad_q.total(2)
    for grad in (grad_d, grad_u, grad_o, grad_q):
        for chunk in range(grad.chunks):
            grad.give(chunk)
    for grad in (grad_d, grad_u, grad_o, grad_q):
        grad.close()
    keep_grad.wait()
    for pair in range(pairs):
        kv_copy(far_base, pair, own_slot, at.cross).wait_send()
        kv_copy(near_base, pair, own_slot, at.sib).wait_send()
        kv_copy(pass_base, pair, core * 2 + at.far, at.sib).wait_send()
        dkv_near(pair).wait_send()
        dkv_cross(pair).wait_send()
    for index in range(some):
        ctx_copy(index).wait_send()
        dq_copy(index).wait_send()
    wire.close()


def whole_layer(tokens, cotangent, pairing, small_raw, w_qkv, w_out, w_up, w_down):
    rows, width = tokens.shape
    inner = w_up.shape[1]
    scratch = layer_scratch(rows, width, inner, pairing.shape[0])
    hbm = pl.BlockSpec(memory_space=pl.ANY)
    vmem = pl.BlockSpec(memory_space=pltpu.VMEM)
    smem = pl.BlockSpec(memory_space=pltpu.SMEM)
    return pl.pallas_call(
        functools.partial(layer_kernel, tuple(scratch)),
        out_shape=[
            jax.ShapeDtypeStruct((rows, width), F32),
            jax.ShapeDtypeStruct((rows, width), F32),
            jax.ShapeDtypeStruct(w_qkv.shape, BF16),
            jax.ShapeDtypeStruct(w_out.shape, BF16),
            jax.ShapeDtypeStruct(w_up.shape, BF16),
            jax.ShapeDtypeStruct(w_down.shape, BF16),
            jax.ShapeDtypeStruct((16, width), F32),
        ],
        in_specs=[hbm, vmem, smem, vmem, hbm, hbm, hbm, hbm],
        out_specs=[hbm] * 6 + [vmem],
        scratch_shapes=list(scratch.values()),
        compiler_params=pltpu.CompilerParams(
            collective_id=0, has_side_effects=True, vmem_limit_bytes=60 << 20
        ),
        name="whole_layer",
    )(tokens, cotangent, pairing, small_raw, w_qkv, w_out, w_up, w_down)


def finish_kernel(share, *refs):
    wide, small, outs = refs[:6], refs[6], refs[7:]
    for source, target in zip(wide, outs[:6]):
        target[...] = source[...].astype(F32)

    @pl.when(pl.program_id(0) == 0)
    def _():
        w = lax.axis_index("wt")
        values = small[...]
        mine = jnp.zeros((8, share), F32)
        line = jnp.zeros((1, 4 * share), F32)
        for owner in range(4):
            mine = mine + jnp.where(
                w == owner, values[:8, owner * share : (owner + 1) * share], 0.0
            )
            line = line + jnp.where(w == owner, values[8 + owner : 9 + owner], 0.0)
        for row in range(8):
            outs[6 + row][...] = mine[row : row + 1]
        outs[14][...] = line


def finish(*arrays):
    steps = 4
    wide, small = arrays[:6], arrays[6]
    share = small.shape[1] // 4

    def blocks(array):
        return pl.BlockSpec((array.shape[0] // steps, array.shape[1]), lambda i: (i, 0))

    def fixed(shape):
        return pl.BlockSpec(shape, lambda i: (0, 0))

    shapes = [(1, share)] * 8 + [(1, 4 * share)]
    return pl.pallas_call(
        functools.partial(finish_kernel, share),
        grid=(steps,),
        out_shape=[jax.ShapeDtypeStruct(v.shape, F32) for v in wide]
        + [jax.ShapeDtypeStruct(v, F32) for v in shapes],
        in_specs=[blocks(v) for v in wide] + [fixed(small.shape)],
        out_specs=[blocks(v) for v in wide] + [fixed(v) for v in shapes],
        compiler_params=pltpu.CompilerParams(vmem_limit_bytes=40 << 20),
        name="finish",
    )(*arrays)


far_below = -1e30


def passed_along(value, axis, steps):
    count = lax.axis_size(axis)
    pairs = [(source, (source + steps) % count) for source in range(count)]
    return lax.ppermute(value, axis, pairs)


def norm_rows(values, gains, shifts):
    average = jnp.mean(values, axis=-1, keepdims=True)
    centred = values - average
    spread = jnp.mean(centred * centred, axis=-1, keepdims=True)
    return centred * lax.rsqrt(spread + 1e-12) * gains + shifts


def gelu_exact(pre_active):
    return jax.nn.gelu(pre_active, approximate=False)


def scores_of(queries, key_heads):
    return (
        jnp.einsum("thd,khd->htk", queries, key_heads, preferred_element_type=jnp.float32) * 0.125
    )


def unchanged(running):
    return running


def general_layer(
    tokens,
    pairing,
    w_qkv,
    bias_q,
    bias_v,
    w_out,
    bias_out,
    gain_one,
    shift_one,
    w_up,
    bias_up,
    w_down,
    bias_down,
    gain_two,
    shift_two,
    cotangent,
):
    local_params = (
        w_qkv,
        bias_q,
        bias_v,
        w_out,
        bias_out,
        gain_one,
        shift_one,
        w_up,
        bias_up,
        w_down,
        bias_down,
        gain_two,
        shift_two,
    )
    gathered = tuple(lax.all_gather(v, "wt", axis=0, tiled=True) for v in local_params)
    (
        wqkv_full,
        biasq_full,
        biasv_full,
        wout_full,
        biasout_full,
        gainone_full,
        shiftone_full,
        wup_full,
        biasup_full,
        wdown_full,
        biasdown_full,
        gaintwo_full,
        shifttwo_full,
    ) = gathered
    tok_rows = tokens.shape[1]
    model_width = tokens.shape[2]
    head_count = pairing.shape[0]
    head_size = model_width // head_count
    group_size = lax.axis_size("ctx")
    position_ctx = lax.axis_index("ctx")
    half_len = tok_rows * group_size // 2
    own_half = position_ctx * tok_rows // half_len
    flipped = pairing == 1
    inputs = tokens[0]
    bias_cat = jnp.concatenate(
        [
            biasq_full.astype(jnp.float32),
            jnp.zeros((model_width,), jnp.float32),
            biasv_full.astype(jnp.float32),
        ]
    )
    projected = jnp.dot(inputs, wqkv_full, preferred_element_type=jnp.float32) + bias_cat
    projected_low = projected.astype(jnp.bfloat16)
    queries = projected_low[:, :model_width].reshape(tok_rows, head_count, head_size)
    key_rows = projected_low[:, model_width : 2 * model_width]
    value_rows = projected_low[:, 2 * model_width :]

    def online_update(state, portion_keys, portion_values, needed):
        row_top, row_total, accumulated = state
        key_count = portion_keys.shape[0]
        key_heads = portion_keys.reshape(key_count, head_count, head_size)
        value_heads = portion_values.reshape(key_count, head_count, head_size)
        scores = scores_of(queries, key_heads)
        scores = jnp.where(needed[:, None, :], scores, far_below)
        new_top = jnp.maximum(row_top, jnp.max(scores, axis=-1))
        factor = jnp.exp(row_top - new_top)
        weights = jnp.exp(scores - new_top[..., None])
        row_total = jnp.sum(weights, axis=-1)
        added = jnp.einsum(
            "htk,khd->thd",
            weights.astype(jnp.bfloat16),
            value_heads,
            preferred_element_type=jnp.float32,
        )
        accumulated = accumulated * factor.T[..., None] + added
        return (new_top, row_total, accumulated)

    start_state = (
        jnp.full((head_count, tok_rows), far_below, jnp.float32),
        jnp.zeros((head_count, tok_rows), jnp.float32),
        jnp.zeros((tok_rows, head_count, head_size), jnp.float32),
    )

    def wanted(offset, key_count):
        key_half = (offset + jnp.arange(key_count)) // half_len
        target = jnp.where(flipped, 1 - own_half, own_half)
        return key_half[None, :] == target[:, None]

    portion_keys = lax.all_gather(key_rows, "ctx", axis=0, tiled=True)
    portion_values = lax.all_gather(value_rows, "ctx", axis=0, tiled=True)
    needed = wanted(jnp.int32(0), portion_keys.shape[0])

    def update(state):
        return online_update(state, portion_keys, portion_values, needed)

    row_top, row_total, accumulated = lax.cond(jnp.any(needed), update, unchanged, start_state)
    context = accumulated / row_total.T[..., None]
    log_sum = row_top + jnp.log(row_total)
    context_low = context.reshape(tok_rows, model_width).astype(jnp.bfloat16)
    branch = jnp.dot(
        context_low, wout_full, preferred_element_type=jnp.float32
    ) + biasout_full.astype(jnp.float32)
    summed_one = inputs.astype(jnp.float32) + branch
    hidden, norm_one_back = jax.vjp(
        norm_rows, summed_one, gainone_full.astype(jnp.float32), shiftone_full.astype(jnp.float32)
    )
    hidden_low = hidden.astype(jnp.bfloat16)
    pre_active = jnp.dot(
        hidden_low, wup_full, preferred_element_type=jnp.float32
    ) + biasup_full.astype(jnp.float32)
    active, gelu_back = jax.vjp(gelu_exact, pre_active)
    active_low = active.astype(jnp.bfloat16)
    ffn_out = jnp.dot(
        active_low, wdown_full, preferred_element_type=jnp.float32
    ) + biasdown_full.astype(jnp.float32)
    output, norm_two_back = jax.vjp(
        norm_rows,
        hidden + ffn_out,
        gaintwo_full.astype(jnp.float32),
        shifttwo_full.astype(jnp.float32),
    )
    again = gathered
    wqkv_back = again[0]
    wout_back = again[3]
    wup_back = again[7]
    wdown_back = again[9]
    grad_two, grad_gain_two, grad_shift_two = norm_two_back(cotangent[0].astype(jnp.float32))
    grad_ffn = grad_two.astype(jnp.bfloat16)
    grad_bias_down = jnp.sum(grad_ffn.astype(jnp.float32), axis=0)
    grad_w_down = jnp.einsum("tf,td->fd", active_low, grad_ffn, preferred_element_type=jnp.float32)
    grad_active = jnp.einsum("td,fd->tf", grad_ffn, wdown_back, preferred_element_type=jnp.float32)
    (grad_pre_f,) = gelu_back(grad_active)
    grad_pre = grad_pre_f.astype(jnp.bfloat16)
    grad_bias_up = jnp.sum(grad_pre.astype(jnp.float32), axis=0)
    grad_w_up = jnp.einsum("tc,tf->cf", hidden_low, grad_pre, preferred_element_type=jnp.float32)
    grad_hidden = grad_two + jnp.einsum(
        "tf,cf->tc", grad_pre, wup_back, preferred_element_type=jnp.float32
    )
    grad_one, grad_gain_one, grad_shift_one = norm_one_back(grad_hidden)
    grad_branch = grad_one.astype(jnp.bfloat16)
    grad_bias_out = jnp.sum(grad_branch.astype(jnp.float32), axis=0)
    grad_w_out = jnp.einsum(
        "tc,td->cd", context_low, grad_branch, preferred_element_type=jnp.float32
    )
    grad_context = jnp.einsum(
        "td,cd->tc", grad_branch, wout_back, preferred_element_type=jnp.float32
    )
    grad_context = grad_context.astype(jnp.bfloat16).reshape(tok_rows, head_count, head_size)
    row_delta = jnp.sum(grad_context.astype(jnp.float32) * context, axis=-1).T

    def piece_grads(portion_keys, portion_values, needed):
        key_count = portion_keys.shape[0]
        key_heads = portion_keys.reshape(key_count, head_count, head_size)
        value_heads = portion_values.reshape(key_count, head_count, head_size)
        scores = scores_of(queries, key_heads)
        scores = jnp.where(needed[:, None, :], scores, far_below)
        probs = jnp.exp(scores - log_sum[..., None])
        probs_low = probs.astype(jnp.bfloat16)
        piece_v = jnp.einsum(
            "htk,thd->khd", probs_low, grad_context, preferred_element_type=jnp.float32
        ).reshape(key_count, model_width)
        grad_weights = jnp.einsum(
            "thd,khd->htk", grad_context, value_heads, preferred_element_type=jnp.float32
        )
        grad_scores = (probs * (grad_weights - row_delta[..., None])).astype(jnp.bfloat16)
        piece_q = 0.125 * jnp.einsum(
            "htk,khd->thd", grad_scores, key_heads, preferred_element_type=jnp.float32
        )
        piece_k = 0.125 * jnp.einsum(
            "htk,thd->khd", grad_scores, queries, preferred_element_type=jnp.float32
        ).reshape(key_count, model_width)
        return (piece_k, piece_v, piece_q)

    zero_queries = jnp.zeros((tok_rows, head_count, head_size), jnp.float32)

    def circle_step(step_index, running):
        turn_keys, turn_values, grad_keys, grad_values, grad_queries = running
        owner = (position_ctx - step_index) % group_size
        needed = wanted(owner * tok_rows, tok_rows)

        def update_grads(state):
            grad_k, grad_v, grad_q = state
            piece_k, piece_v, piece_q = piece_grads(turn_keys, turn_values, needed)
            return (grad_k + piece_k, grad_v + piece_v, grad_q + piece_q)

        grad_keys, grad_values, grad_queries = lax.cond(
            jnp.any(needed), update_grads, unchanged, (grad_keys, grad_values, grad_queries)
        )
        turn_keys, turn_values = passed_along((turn_keys, turn_values), "ctx", 1)
        grad_keys, grad_values = (
            passed_along(grad_keys.astype(jnp.bfloat16), "ctx", 1).astype(grad_keys.dtype),
            passed_along(grad_values.astype(jnp.bfloat16), "ctx", 1).astype(grad_values.dtype),
        )
        return (turn_keys, turn_values, grad_keys, grad_values, grad_queries)

    zero_rows = jnp.zeros((tok_rows, model_width), jnp.float32)
    circle_start = (key_rows, value_rows, zero_rows, zero_rows, zero_queries)
    circle_end = lax.fori_loop(0, group_size, circle_step, circle_start)
    grad_keys = circle_end[2]
    grad_values = circle_end[3]
    grad_queries = circle_end[4]
    grad_projected = jnp.concatenate(
        [grad_queries.reshape(tok_rows, model_width), grad_keys, grad_values], axis=1
    ).astype(jnp.bfloat16)
    grad_bias_q = jnp.sum(grad_projected[:, :model_width].astype(jnp.float32), axis=0)
    grad_bias_v = jnp.sum(grad_projected[:, 2 * model_width :].astype(jnp.float32), axis=0)
    grad_w_qkv = jnp.einsum("tc,tj->cj", inputs, grad_projected, preferred_element_type=jnp.float32)
    grad_inputs = grad_one + jnp.einsum(
        "tj,cj->tc", grad_projected, wqkv_back, preferred_element_type=jnp.float32
    )
    terms = (
        grad_w_qkv,
        grad_bias_q,
        grad_bias_v,
        grad_w_out,
        grad_bias_out,
        grad_gain_one,
        grad_shift_one,
        grad_w_up,
        grad_bias_up,
        grad_w_down,
        grad_bias_down,
        grad_gain_two,
        grad_shift_two,
    )
    owned = tuple(
        lax.psum_scatter(term.astype(jnp.bfloat16), "wt", scatter_dimension=0, tiled=True)
        for term in terms
    )
    totals = tuple(lax.psum(term, "ctx").astype(jnp.float32) for term in owned)
    return (
        output[None],
        grad_inputs[None],
        totals[0],
        totals[1],
        totals[2],
        totals[3],
        totals[4],
        totals[5],
        totals[6],
        totals[7],
        totals[8],
        totals[9],
        totals[10],
        totals[11],
        totals[12],
    )


def fast_layer(
    tokens,
    pairing,
    w_qkv,
    bias_q,
    bias_v,
    w_out,
    bias_out,
    gain_one,
    shift_one,
    w_up,
    bias_up,
    w_down,
    bias_down,
    gain_two,
    shift_two,
    cotangent,
):
    share = tokens.shape[2] // 4
    vectors = (bias_q, bias_v, bias_out, gain_one, shift_one, bias_down, gain_two, shift_two)
    vectors = vectors + tuple(bias_up[k * share : (k + 1) * share] for k in range(4))
    row = lax.broadcasted_iota(jnp.int32, (16, share), 0)
    small_raw = jnp.zeros((16, share), jnp.bfloat16)
    for index, vector in enumerate(vectors):
        small_raw = jnp.where(row == index, vector[None, :], small_raw)
    made = whole_layer(
        tokens[0], cotangent[0], pairing, small_raw, w_qkv, w_out, w_up, w_down
    )
    output, grad_tokens, g_qkv, g_out, g_up, g_down, *small = finish(*made)
    small = [v[0] for v in small]
    return (
        output[None],
        grad_tokens[None],
        g_qkv,
        small[0],
        small[1],
        g_out,
        small[2],
        small[3],
        small[4],
        g_up,
        small[8],
        g_down,
        small[5],
        small[6],
        small[7],
    )


def local(tokens, pairing, *rest):
    rows, width = tokens.shape[1:]
    heads = pairing.shape[0]
    inner = rest[7].shape[1]
    fits = (
        lax.axis_size("wt") == 4
        and lax.axis_size("ctx") == 8
        and tokens.shape[0] == 1
        and rows % BAND == 0
        and 3 * rows <= width
        and width % 256 == 0
        and heads % 4 == 0
        and width == 64 * heads
        and inner == 4 * width
    )
    layer = fast_layer if fits else general_layer
    return layer(tokens, pairing, *rest)


def solution(mesh):
    in_specs = (
        P("wt", "ctx", None),
        P(),
        P("wt", None),
        P("wt"),
        P("wt"),
        P("wt", None),
        P("wt"),
        P("wt"),
        P("wt"),
        P("wt", None),
        P("wt"),
        P("wt", None),
        P("wt"),
        P("wt"),
        P("wt"),
        P("wt", "ctx", None),
    )
    out_specs = (
        P("wt", "ctx", None),
        P("wt", "ctx", None),
        P("wt", None),
        P("wt"),
        P("wt"),
        P("wt", None),
        P("wt"),
        P("wt"),
        P("wt"),
        P("wt", None),
        P("wt"),
        P("wt", None),
        P("wt"),
        P("wt"),
        P("wt"),
    )
    return jax.shard_map(local, mesh=mesh, in_specs=in_specs, out_specs=out_specs, check_vma=False)
```

```python
import functools

import jax
import jax.numpy as jnp
from jax import lax
from jax.experimental import pallas as pl
from jax.experimental.pallas import tpu as pltpu
from jax.sharding import PartitionSpec as P

F32, BF16 = jnp.float32, jnp.bfloat16
MESH = pl.DeviceIdType.MESH
BAND = 32


def nn(a, b):
    return jnp.dot(a, b, preferred_element_type=F32)


def nt(a, b):
    return lax.dot_general(a, b, (((1,), (1,)), ((), ())), preferred_element_type=F32)


def aligned(start, multiple):
    return start if isinstance(start, int) else pl.multiple_of(start, multiple)


def chunk_of(index, size):
    return pl.ds(aligned(index * size, size), size)


class Wire:
    def __init__(self, sends, receives, anyone):
        self.sends, self.receives, self.anyone = sends, receives, anyone
        self.firsts, self.used, self.started = {}, 0, {}

    def slot(self, name, count=1):
        if name not in self.firsts:
            self.firsts[name] = self.used, count
            self.used += count
            assert self.used <= self.sends.shape[0]
        first, had = self.firsts[name]
        assert had == count
        return first

    def copy(self, slot, source, target, where):
        return pltpu.make_async_remote_copy(
            src_ref=source,
            dst_ref=target,
            send_sem=self.sends.at[slot],
            recv_sem=self.receives.at[slot],
            device_id=where,
            device_id_type=MESH,
        )

    def send(self, name, source, target, where):
        copy = self.copy(self.slot(name), source, target, where)
        copy.start()
        self.started[name] = copy

    def arrived(self, name, target):
        self.copy(self.slot(name), target, target, self.anyone).wait_recv()

    def left(self, *names):
        for name in names:
            self.started.pop(name).wait_send()

    def close(self):
        self.left(*tuple(self.started))


class Place:
    def __init__(self):
        self.w = w = lax.axis_index("wt")
        self.c = c = lax.axis_index("ctx")
        self.core = core = c % 2
        self.other = 1 - core
        self.z = z = c // 2
        self.near = z % 2
        self.far = 1 - self.near
        self.nx = w + 1 - 2 * (w % 2)
        self.ny = (w + 2) % 4
        self.nd = 3 - w
        self.sib = (w, c + 1 - 2 * core)
        self.to_x, self.to_y, self.to_d = (self.nx, c), (self.ny, c), (self.nd, c)
        self.cross = (w, c + 2 - 4 * self.near)
        self.partner = (w, (c + 4) % 8)
        self.lines = [(w, spot * 2 + core) for spot in (z + 1 - 2 * (z % 2), (z + 2) % 4, 3 - z)]
        self.others = [(w, (c + step) % 8) for step in range(1, 8)]
        self.mate, self.middle = self.lines[0], self.lines[2]
        self.outer, self.inner = (z == 0) | (z == 3), (z == 1) | (z == 2)


def greet(peers):
    barrier = pltpu.get_barrier_semaphore()
    for peer in peers:
        pl.semaphore_signal(barrier, inc=1, device_id=peer, device_id_type=MESH)
    pl.semaphore_wait(barrier, len(peers))


class Part:
    def __init__(self, name, local, full, first, columns, place, wire):
        self.name, self.local, self.full, self.place, self.wire = name, local, full, place, wire
        self.rows = local.shape[0]
        self.first, self.columns = first, columns // 2

    def piece(self, owner, core, half=None):
        rows, start = self.rows, owner * self.rows
        if half is not None:
            rows = self.rows // 2
            start = start + half * rows
        return self.full.at[
            pl.ds(aligned(start, 16), rows),
            pl.ds(aligned(self.first + core * self.columns, 128), self.columns),
        ]

    def begin(self):
        at, wire = self.place, self.wire
        mine = self.local.at[
            :, pl.ds(aligned(self.first + at.core * self.columns, 128), self.columns)
        ]
        target = self.piece(at.w, at.core)
        wire.send(self.name + "a", mine, target, at.to_x)
        wire.send(self.name + "b", mine, target, at.to_y)

    def relay(self):
        at, wire = self.place, self.wire
        block = self.piece(at.nx, at.core)
        wire.arrived(self.name + "a", block)
        half = self.piece(at.nx, at.core, 0)
        wire.send(self.name + "c", half, half, at.to_y)
        wire.send(self.name + "d", block, block, at.sib)
        block = self.piece(at.ny, at.core)
        wire.arrived(self.name + "b", block)
        half = self.piece(at.ny, at.core, 1)
        wire.send(self.name + "e", half, half, at.to_x)
        wire.send(self.name + "f", block, block, at.sib)

    def share(self):
        at, wire = self.place, self.wire
        wire.arrived(self.name + "c", self.piece(at.nd, at.core, 0))
        wire.arrived(self.name + "e", self.piece(at.nd, at.core, 1))
        block = self.piece(at.nd, at.core)
        wire.send(self.name + "g", block, block, at.sib)

    def finish(self):
        at, wire = self.place, self.wire
        wire.arrived(self.name + "d", self.piece(at.nx, at.other))
        wire.arrived(self.name + "f", self.piece(at.ny, at.other))
        wire.arrived(self.name + "g", self.piece(at.nd, at.other))


def add_into(target, *sources):
    rows, columns = sources[0].shape
    band = 16
    while columns * band * 2 <= 1 << 15 and rows % (band * 2) == 0:
        band *= 2

    @pl.loop(0, rows // band)
    def _(index):
        where = chunk_of(index, band)
        total = sources[0][where, :].astype(F32)
        for source in sources[1:]:
            total = total + source[where, :].astype(F32)
        target[where, :] = total.astype(target.dtype)


class Grad:
    def __init__(self, name, chunks, blocks, buffers, finals, place, wire, local_sems):
        self.name, self.chunks, self.blocks, self.finals = name, chunks, blocks, finals
        self.place, self.wire, self.local_sems = place, wire, local_sems
        self.from_x, self.from_y, self.diag_x, self.diag_y, self.low, self.high = buffers
        self.rows, self.columns = self.from_x.shape

    def half(self, ref, index):
        return ref.at[pl.ds(index * (self.rows // 2), self.rows // 2), :]

    def begin(self):
        at, wire = self.place, self.wire
        block = self.blocks(at.nd)
        wire.send(self.name + "a", self.half(block, 0), self.diag_x, at.to_x)
        wire.send(self.name + "b", self.half(block, 1), self.diag_y, at.to_y)

    def mid(self):
        at, wire = self.place, self.wire
        wire.arrived(self.name + "a", self.diag_x)
        block = self.blocks(at.ny)
        part = self.half(block, 0)
        add_into(part, part, self.diag_x)
        wire.send(self.name + "d", block, self.from_y, at.to_y)
        wire.arrived(self.name + "b", self.diag_y)
        block = self.blocks(at.nx)
        part = self.half(block, 1)
        add_into(part, part, self.diag_y)
        wire.send(self.name + "c", block, self.from_x, at.to_x)

    def cut(self, ref, chunk):
        count = self.rows // self.chunks
        return ref.at[pl.ds(chunk * count, count), :]

    def hop(self, kind, chunk, source, target, where):
        slot = self.wire.slot(self.name + kind, self.chunks) + chunk
        return self.wire.copy(slot, self.cut(source, chunk), self.cut(target, chunk), where)

    def outward(self, chunk):
        return self.hop("u", chunk, self.blocks(self.place.w), self.low, self.place.mate)

    def across(self, chunk):
        return self.hop("v", chunk, self.from_x, self.high, self.place.middle)

    def back(self, chunk):
        return self.hop("t", chunk, self.from_y, self.high, self.place.mate)

    def own(self):
        at, wire = self.place, self.wire
        wire.arrived(self.name + "c", self.from_x)
        wire.arrived(self.name + "d", self.from_y)
        block = self.blocks(at.w)
        for chunk in range(self.chunks):
            part = self.cut(block, chunk)
            add_into(part, part, self.cut(self.from_x, chunk), self.cut(self.from_y, chunk))

    def out(self, chunk):
        @pl.when(self.place.outer)
        def _():
            self.outward(chunk).start()

    def chain(self, chunk):
        at = self.place

        @pl.when(at.inner)
        def _():
            self.outward(chunk).wait_recv()
            block = self.blocks(at.w)
            add_into(
                self.cut(self.from_x, chunk), self.cut(block, chunk), self.cut(self.low, chunk)
            )
            self.across(chunk).start()

    def total(self, chunk):
        at = self.place

        @pl.when(at.inner)
        def _():
            self.across(chunk).wait_recv()
            add_into(
                self.cut(self.from_y, chunk),
                self.cut(self.from_x, chunk),
                self.cut(self.high, chunk),
            )
            self.back(chunk).start()
            for copy in self.copies(chunk, self.from_y):
                copy.start()

    def copies(self, chunk, source):
        at, wire = self.place, self.wire
        piece, target = self.cut(source, chunk), self.finals(chunk, at.core)
        keep = pltpu.make_async_copy(piece, target, self.local_sems.at[chunk])
        slot = wire.slot(self.name + "s", self.chunks) + chunk
        return keep, wire.copy(slot, piece, target, at.sib)

    def give(self, chunk):
        at = self.place

        @pl.when(at.outer)
        def _():
            self.back(chunk).wait_recv()
            for copy in self.copies(chunk, self.high):
                copy.start()

    def close(self):
        at = self.place
        for chunk in range(self.chunks):
            for copy in self.copies(chunk, self.from_y):
                copy.wait()

            @pl.when(at.outer)
            def _(chunk=chunk):
                self.outward(chunk).wait_send()

            @pl.when(at.inner)
            def _(chunk=chunk):
                self.across(chunk).wait_send()
                self.back(chunk).wait_send()


def layer_scratch(rows, width, inner, heads):
    pairs = heads // 2
    some = pairs // 2
    share = width // 4
    half = width // 2
    groups = 8

    def low(*shape):
        return pltpu.VMEM(shape, BF16)

    def wide(*shape):
        return pltpu.VMEM(shape, F32)

    scratch = dict(
        wqkv=low(width, 3 * width),
        wo=low(width, width),
        wu=low(width, inner),
        wd=low(inner, width),
        order=low(width, width),
        tok=low(2, rows, width),
        cot=low(rows, width),
        small_own=low(16, width),
        small_in=low(3, 16, width),
        small=wide(16, width),
        bias_qkv=wide(8, 3 * width),
        bias_up=wide(8, inner),
        kv=low(pairs, 4, rows, 256),
        proj=low(rows, 3 * width),
        q=low(pairs, rows, 128),
        q_out=low(some, rows, 128),
        exps=low(heads, 4 * rows, rows),
        inverse=wide(heads, 1, rows),
        out_t=wide(pairs, 128, rows),
        ctx=low(pairs, rows, 128),
        ctx_out=low(some, rows, 128),
        ctx_nat=low(2, rows, width),
        hat_one=wide(rows, width),
        r_one=wide(rows, 1),
        flow=wide(rows, width),
        stage=wide(rows, width),
        result=wide(rows, width),
        hid=low(2, rows, width),
        act=low(2, rows, inner),
        slope=low(rows, inner),
        slope_in=low(rows, inner // 2),
        gf=low(rows, width),
        gf_in=low(rows, half),
        gb=low(rows, width),
        gb_in=low(rows, half),
        do=low(pairs, rows, 128),
        do_out=low(some, rows, 128),
        dq=low(pairs, rows, 128),
        dq_out=low(some, rows, 128),
        dkv_in=low(pairs, rows, 512),
        dkv_far=low(pairs, rows, 256),
        gkv=low(2, rows, width),
        gj_in=low(rows, 3 * half),
        sums=wide(16, groups, width),
        sums_up=wide(groups, inner),
        vec=wide(16, width),
        vec_in=wide(7, 16, width),
        dwd=low(4, inner // 4, half),
    )
    shapes = dict(
        d=(inner // 4, half), u=(2 * share, width), o=(share, half), q=(3 * share, half)
    )
    for name, (r, c) in shapes.items():
        for kind in ("fx", "fy", "lo", "hi"):
            scratch["g" + name + kind] = low(r, c)
        for kind in ("dx", "dy"):
            scratch["g" + name + kind] = low(r // 2, c)
    scratch["sends"] = pltpu.SemaphoreType.DMA((168,))
    scratch["receives"] = pltpu.SemaphoreType.DMA((168,))
    scratch["own_sems"] = pltpu.SemaphoreType.DMA((24,))
    return scratch


def layer_kernel(names, *refs):
    (
        tokens,
        cot_l,
        pairing,
        small_raw,
        qkv_l,
        out_l,
        up_l,
        down_l,
        output,
        grad_tokens,
        g_qkv,
        g_out,
        g_up,
        g_down,
        g_small,
    ) = refs[:15]
    s = dict(zip(names, refs[15:]))
    at = Place()
    wire = Wire(s["sends"], s["receives"], at.sib)
    rows, width = tokens.shape
    inner = up_l.shape[1]
    heads = pairing.shape[0]
    pairs, some = heads // 2, heads // 4
    size = width // heads
    half = width // 2
    keys = 4 * rows
    chunks = width // 256
    share = width // 4
    core, other = at.core, at.other

    greet([at.to_x, at.to_y, at.to_d] + at.others)

    part_kv = Part("kv", qkv_l, s["wqkv"], width, 2 * width, at, wire)
    part_q = Part("q", qkv_l, s["wqkv"], 0, width, at, wire)
    part_o = Part("o", out_l, s["wo"], 0, width, at, wire)
    part_u = Part("u", up_l, s["wu"], 0, inner, at, wire)
    part_d = Part("d", down_l, s["wd"], 0, width, at, wire)
    part_kv.begin()
    part_q.begin()
    raw = small_raw[...]
    row = lax.broadcasted_iota(jnp.int32, (share, width), 0)
    column = lax.broadcasted_iota(jnp.int32, (share, width), 1)

    def spread(values, spot):
        place = jnp.where(column - row == spot * share, 1.0, 0.0).astype(BF16)
        return nn(values, place)

    own_row = lax.broadcasted_iota(jnp.int32, (8, width), 0) == at.w
    line = spread(raw[8:16], 0)[0:1]
    for index in range(1, 4):
        line = line + spread(raw[8:16], index)[index : index + 1]
    small_own = s["small_own"]
    small_own[...] = jnp.concatenate(
        [spread(raw[:8], at.w), jnp.where(own_row, line, 0.0)], axis=0
    ).astype(BF16)
    for index, where in enumerate((at.to_x, at.to_y, at.to_d)):
        wire.send("sm" + str(index), small_own, s["small_in"].at[index], where)
    keeps = []
    for slot, (local, full) in enumerate(
        (
            (qkv_l, s["wqkv"].at[pl.ds(aligned(at.w * share, 16), share)]),
            (tokens, s["tok"].at[core]),
            (cot_l, s["cot"]),
            (out_l, s["wo"].at[pl.ds(aligned(at.w * share, 16), share)]),
            (up_l, s["wu"].at[pl.ds(aligned(at.w * share, 16), share)]),
            (down_l, s["wd"].at[pl.ds(aligned(at.w * (inner // 4), 16), inner // 4)]),
        )
    ):
        keeps.append(pltpu.make_async_copy(local, full, s["own_sems"].at[slot]))
        keeps[-1].start()
    wire.send("tok", tokens, s["tok"].at[core], at.sib)

    before = 0
    for head in range(heads):
        flag = pairing[head]
        spot = flag * (heads // 2 + before) + (1 - flag) * (head - before)
        before = before + flag
        row = lax.broadcasted_iota(jnp.int32, (size, width), 0)
        column = lax.broadcasted_iota(jnp.int32, (size, width), 1)
        s["order"][head * size : (head + 1) * size, :] = jnp.where(
            column - row == spot * size, 1.0, 0.0
        ).astype(BF16)

    part_kv.relay()
    part_q.relay()
    part_o.begin()
    part_kv.share()
    for index in range(3):
        wire.arrived("sm" + str(index), s["small_in"].at[index])
    small = s["small"]
    small[...] = (
        small_own[...].astype(F32)
        + s["small_in"][0].astype(F32)
        + s["small_in"][1].astype(F32)
        + s["small_in"][2].astype(F32)
    )
    s["bias_qkv"][0:1, 0:width] = small[0:1, :]
    s["bias_qkv"][0:1, width : 2 * width] = jnp.zeros((1, width), F32)
    s["bias_qkv"][0:1, 2 * width :] = small[1:2, :]
    for index in range(inner // width):
        s["bias_up"][0:1, index * width : (index + 1) * width] = small[8 + index : 9 + index, :]
    keeps[0].wait()
    keeps[1].wait()
    part_kv.finish()

    tok, proj, order, kv = s["tok"], s["proj"], s["order"], s["kv"]
    own_slot = core * 2 + at.near

    def project(first, count):
        @pl.loop(first, first + count)
        def _(index):
            where = chunk_of(index, 256)
            made = nn(tok[core], s["wqkv"][:, where]) + s["bias_qkv"][0:1, where]
            proj[:, where] = made.astype(BF16)

    project(chunks, 2 * chunks)
    for index in range(chunks):
        columns = order[:, index * 256 : (index + 1) * 256]
        for kind in range(2):
            moved = nn(proj[:, (1 + kind) * width : (2 + kind) * width], columns).astype(BF16)
            for e in range(2):
                kv[2 * index + e, own_slot, :, kind * 128 : (kind + 1) * 128] = moved[
                    :, e * 128 : (e + 1) * 128
                ]
    near_base = wire.slot("near kv", pairs)
    far_base = wire.slot("far kv", pairs)
    pass_base = wire.slot("passed kv", pairs)

    def kv_copy(base, pair, slot, where):
        block = kv.at[pair, slot]
        return wire.copy(base + pair, block, block, where)

    for pair in range(pairs):
        if pair < some:
            kv_copy(far_base, pair, own_slot, at.cross).start()
        kv_copy(near_base, pair, own_slot, at.sib).start()
    part_q.share()
    part_u.begin()
    part_q.finish()
    project(0, chunks)
    q, q_out = s["q"], s["q_out"]
    for index in range(chunks):
        moved = nn(proj[:, 0:width], order[:, index * 256 : (index + 1) * 256]).astype(BF16)
        for e in range(2):
            pair = 2 * index + e
            block = moved[:, e * 128 : (e + 1) * 128]
            if pair < some:
                q[pair] = block
            else:
                q_out[pair - some] = block
    wire.send("q", q_out, q.at[pl.ds(some, some)], at.partner)
    part_o.relay()

    exps, inverse, out_t = s["exps"], s["inverse"], s["out_t"]

    def both(pair, first):
        return kv[pair, :, :, first : first + 128].reshape(keys, 128)

    def masked(block, e, axis=1):
        spot = lax.broadcasted_iota(jnp.int32, block.shape, axis)
        mine = spot < size if e == 0 else spot >= size
        return jnp.where(mine, block, jnp.zeros_like(block))

    def attend(pair):
        key_rows, value_rows = both(pair, 0), both(pair, 128)
        values_t = value_rows.T
        queries = q[pair] * jnp.asarray(size**-0.5, BF16)
        parts = []
        for e in range(2):
            scores = nt(key_rows, masked(queries, e))
            top = jnp.max(scores, axis=0, keepdims=True)
            raised = jnp.exp(scores - top)
            total = jnp.sum(raised, axis=0, keepdims=True)
            low = raised.astype(BF16)
            exps[2 * pair + e] = low
            one_over = 1.0 / total
            inverse[2 * pair + e] = one_over
            parts.append(nn(values_t[e * size : (e + 1) * size], low) * one_over)
        merged = jnp.concatenate(parts, axis=0)
        out_t[pair] = merged
        return merged.T.astype(BF16)

    def receive_kv(pair):
        kv_copy(far_base, pair, core * 2 + at.far, at.cross).wait_recv()
        kv_copy(pass_base, pair, core * 2 + at.far, at.sib).start()
        kv_copy(near_base, pair, other * 2 + at.near, at.sib).wait_recv()
        kv_copy(pass_base, pair, other * 2 + at.far, at.sib).wait_recv()

    ctx, ctx_out = s["ctx"], s["ctx_out"]
    back_base = wire.slot("ctx", some)

    def ctx_copy(index):
        return wire.copy(back_base + index, ctx_out.at[index], ctx.at[some + index], at.partner)

    def attend_far(index):
        receive_kv(index + some)
        ctx_out[index] = attend(index + some)
        ctx_copy(index).start()

    @pl.loop(0, some)
    def _(index):
        receive_kv(index)
        kv_copy(far_base, index + some, own_slot, at.cross).start()
        ctx[index] = attend(index)

    part_o.share()
    part_d.begin()
    wire.arrived("q", q.at[pl.ds(some, some)])
    attend_far(0)
    part_u.relay()

    @pl.loop(1, some)
    def _(index):
        attend_far(index)

    part_o.finish()
    keeps[2].wait()
    keeps[3].wait()
    for index in range(some):
        ctx_copy(index).wait_recv()
    permuted = jnp.concatenate([ctx[pair] for pair in range(pairs)], axis=1)
    ctx_nat, stage = s["ctx_nat"], s["stage"]
    for index in range(chunks):
        where = slice(index * 256, (index + 1) * 256)
        ctx_nat[core, :, where] = nt(permuted, order[where, :]).astype(BF16)
    wire.send("ctxn", ctx_nat.at[core], ctx_nat.at[core], at.sib)

    @pl.loop(0, chunks)
    def _(index):
        where = chunk_of(index, 256)
        stage[:, where] = nn(ctx_nat[core], s["wo"][:, where])

    hat_one, r_one, flow, hid = s["hat_one"], s["r_one"], s["flow"], s["hid"]
    inv_width = 1.0 / width

    def mean(values):
        return jnp.sum(values, axis=-1, keepdims=True) * inv_width

    @pl.loop(0, rows // BAND)
    def _(index):
        where = chunk_of(index, BAND)
        total = tok[core, where, :].astype(F32) + stage[where, :] + small[2:3, :]
        centred = total - mean(total)
        scale = lax.rsqrt(mean(centred * centred) + 1e-12)
        hat = centred * scale
        hat_one[where, :] = hat
        r_one[where, :] = scale
        hidden = hat * small[3:4, :] + small[4:5, :]
        flow[where, :] = hidden
        hid[core, where, :] = hidden.astype(BF16)

    wire.send("hid", hid.at[core], hid.at[core], at.sib)
    part_d.relay()
    part_u.share()
    part_u.finish()
    keeps[4].wait()
    act, slope = s["act"], s["slope"]

    @pl.loop(0, inner // 256, unroll=2)
    def _(index):
        where = chunk_of(index, 256)
        pre = nn(hid[core], s["wu"][:, where]) + s["bias_up"][0:1, where]
        below = 0.5 * (1.0 + lax.erf(pre * (0.5**0.5)))
        act[core, :, where] = (pre * below).astype(BF16)
        density = jnp.exp(pre * pre * -0.5) * 0.3989422804014327
        slope[:, where] = (below + pre * density).astype(BF16)

    wire.send("act", act.at[core], act.at[core], at.sib)
    part_d.share()
    part_d.finish()
    keeps[5].wait()

    @pl.loop(0, chunks)
    def _(index):
        where = chunk_of(index, 256)
        stage[:, where] = nn(act[core], s["wd"][:, where])

    result, gf, cot = s["result"], s["gf"], s["cot"]
    sums, sums_up = s["sums"], s["sums_up"]
    sums[...] = jnp.zeros_like(sums)

    def gather_rows(values):
        return jnp.sum(values.reshape(BAND // 8, 8, values.shape[-1]), axis=0)

    @pl.loop(0, rows // BAND)
    def _(index):
        where = chunk_of(index, BAND)
        total = flow[where, :] + stage[where, :] + small[5:6, :]
        centred = total - mean(total)
        scale = lax.rsqrt(mean(centred * centred) + 1e-12)
        hat = centred * scale
        result[where, :] = hat * small[6:7, :] + small[7:8, :]
        back = cot[where, :].astype(F32)
        g = back * small[6:7, :]
        grad = scale * (g - mean(g) - hat * mean(g * hat))
        flow[where, :] = grad
        low = grad.astype(BF16)
        gf[where, :] = low
        sums[6] += gather_rows(back * hat)
        sums[7] += gather_rows(back)
        sums[5] += gather_rows(low.astype(F32))

    keep_out = pltpu.make_async_copy(result, output, s["own_sems"].at[7])
    keep_out.start()

    def columns_of(which, count):
        return pl.ds(aligned(which * count, 128), count)

    wire.send("gf", gf.at[:, columns_of(other, half)], s["gf_in"], at.sib)

    def buffers(name):
        return [s["g" + name + kind] for kind in ("fx", "fy", "dx", "dy", "lo", "hi")]

    dwd, wd, wu = s["dwd"], s["wd"], s["wu"]

    def side_by_side(first, count, owner):
        return wd.at[
            pl.ds(aligned(first + (owner // 2) * count, 16), count),
            pl.ds(aligned((owner % 2) * half, 128), half),
        ]

    def dwo(owner):
        return side_by_side(2 * width + 6 * share, share, owner)

    def dwq(owner):
        return side_by_side(2 * width, 3 * share, owner)

    grad_d = Grad(
        "gd",
        4,
        lambda r: dwd.at[r],
        buffers("d"),
        lambda i, k: g_down.at[pl.ds(i * (inner // 16), inner // 16), columns_of(k, half)],
        at,
        wire,
        s["own_sems"].at[pl.ds(8, 4)],
    )
    grad_u = Grad(
        "gu",
        4,
        lambda r: wd.at[pl.ds(aligned(r * (2 * share), 16), 2 * share), :],
        buffers("u"),
        lambda i, k: g_up.at[
            pl.ds((i % 2) * (share // 2), share // 2), columns_of(2 * k + i // 2, width)
        ],
        at,
        wire,
        s["own_sems"].at[pl.ds(12, 4)],
    )
    grad_o = Grad(
        "go",
        1,
        dwo,
        buffers("o"),
        lambda i, k: g_out.at[:, columns_of(k, half)],
        at,
        wire,
        s["own_sems"].at[pl.ds(16, 1)],
    )
    grad_q = Grad(
        "gq",
        6,
        dwq,
        buffers("q"),
        lambda i, k: g_qkv.at[
            pl.ds((i % 2) * (share // 2), share // 2), columns_of(3 * k + i // 2, half)
        ],
        at,
        wire,
        s["own_sems"].at[pl.ds(17, 6)],
    )

    wire.arrived("act", act.at[other])
    wire.arrived("gf", s["gf_in"])
    gf_mine = gf[:, columns_of(core, half)]
    gf_theirs = s["gf_in"][...]
    quarter = inner // 4
    for owner in (at.nd, at.nx, at.ny, at.w):
        where = pl.ds(aligned(owner * quarter, 128), quarter)
        made = nn(act[core, :, where].T, gf_mine) + nn(act[other, :, where].T, gf_theirs)
        dwd[owner] = made.astype(BF16)
        if owner is at.nd:
            grad_d.begin()

    @pl.loop(0, inner // 256, unroll=2)
    def _(index):
        where = chunk_of(index, 256)
        grad = nt(gf[...], wd[where, :]) * slope[:, where].astype(F32)
        low = grad.astype(BF16)
        slope[:, where] = low
        sums_up[:, where] = jnp.sum(low.astype(F32).reshape(rows // 8, 8, 256), axis=0)

    wire.send("slope", slope.at[:, columns_of(other, inner // 2)], s["slope_in"], at.sib)

    @pl.loop(0, chunks)
    def _(index):
        where = chunk_of(index, 256)
        stage[:, where] = nt(slope[...], wu[where, :])

    grad_d.mid()

    gb = s["gb"]

    @pl.loop(0, rows // BAND)
    def _(index):
        where = chunk_of(index, BAND)
        grad_hidden = flow[where, :] + stage[where, :]
        hat = hat_one[where, :]
        g = grad_hidden * small[3:4, :]
        grad = r_one[where, :] * (g - mean(g) - hat * mean(g * hat))
        flow[where, :] = grad
        low = grad.astype(BF16)
        gb[where, :] = low
        sums[3] += gather_rows(grad_hidden * hat)
        sums[4] += gather_rows(grad_hidden)
        sums[2] += gather_rows(low.astype(F32))

    wire.send("gb", gb.at[:, columns_of(other, half)], s["gb_in"], at.sib)

    @pl.loop(0, chunks)
    def _(index):
        where = chunk_of(index, 256)
        proj[:, where] = nt(gb[...], s["wo"][where, :]).astype(BF16)

    do, do_out = s["do"], s["do_out"]
    for index in range(chunks):
        moved = nn(proj[:, 0:width], order[:, index * 256 : (index + 1) * 256]).astype(BF16)
        for e in range(2):
            pair = 2 * index + e
            block = moved[:, e * 128 : (e + 1) * 128]
            if pair < some:
                do[pair] = block
            else:
                do_out[pair - some] = block
    wire.send("do", do_out, do.at[pl.ds(some, some)], at.partner)

    wire.left("dc", "dd", "de", "df", "dg")
    wire.arrived("hid", hid.at[other])
    wire.arrived("slope", s["slope_in"])
    mine_t, theirs_t = hid[core].T, hid[other].T
    for index in range(inner // 2 // half):
        where = pl.ds(aligned(core * (inner // 2) + index * half, 128), half)
        made = nn(mine_t, slope[:, where]) + nn(
            theirs_t, s["slope_in"][:, index * half : (index + 1) * half]
        )
        made = made.astype(BF16)
        for owner in range(4):
            first = owner * 2 * share + (index // 2) * share
            wd[first : first + share, (index % 2) * half : (index % 2 + 1) * half] = made[
                owner * share : (owner + 1) * share
            ]
    grad_u.begin()
    wire.arrived("ctxn", ctx_nat.at[other])
    wire.arrived("gb", s["gb_in"])
    made = nn(ctx_nat[core].T, gb[:, columns_of(core, half)]) + nn(
        ctx_nat[other].T, s["gb_in"][...]
    )
    made = made.astype(BF16)
    for owner in range(4):
        dwo(owner)[...] = made[owner * share : (owner + 1) * share]
    grad_o.begin()

    wire.left("uc", "ud", "ue", "uf", "ug")
    dq, dq_out, dkv_in, dkv_far = s["dq"], s["dq_out"], s["dkv_in"], s["dkv_far"]
    near_d = wire.slot("near dkv", pairs)
    far_d = wire.slot("far dkv", pairs)
    dq_base = wire.slot("dq", some)
    lots = inner // 1024

    def tile(pair, slot, count=1):
        band = pair // lots
        column = (pair % lots) * 1024 + slot * 256
        return wu.at[
            pl.ds(aligned(band * rows, 16), rows),
            pl.ds(aligned(column, 256), 256 * count),
        ]

    def spare(pair):
        bands = -(-pairs // lots)
        band = bands + pair // (4 * lots)
        return wu.at[
            pl.ds(aligned(band * rows, 16), rows),
            pl.ds(aligned((pair % (4 * lots)) * 256, 256), 256),
        ]

    def dkv_near(pair):
        return wire.copy(near_d + pair, tile(pair, other * 2, 2), dkv_in.at[pair], at.sib)

    def dkv_cross(pair):
        return wire.copy(far_d + pair, spare(pair), dkv_far.at[pair], at.cross)

    def attend_back(pair):
        key_rows, value_rows = both(pair, 0), both(pair, 128)
        keys_t = key_rows.T
        queries = q[pair] * jnp.asarray(size**-0.5, BF16)
        do_t = do[pair].astype(F32).T
        scaled = jnp.concatenate(
            [do_t[e * size : (e + 1) * size] * inverse[2 * pair + e] for e in range(2)], axis=0
        )
        product = scaled * out_t[pair]
        scaled_low = scaled.astype(BF16)
        scaled_rows = scaled.T.astype(BF16)
        dv = dk = None
        dq_parts = []
        for e in range(2):
            delta = jnp.sum(product[e * size : (e + 1) * size], axis=0, keepdims=True)
            grad_w = nn(value_rows, masked(scaled_low, e, 0))
            low = exps[2 * pair + e]
            grad_s = (low.astype(F32) * (grad_w - delta)).astype(BF16)
            more_v = nn(low, masked(scaled_rows, e))
            more_k = nn(grad_s, masked(queries, e))
            dv = more_v if dv is None else dv + more_v
            dk = more_k if dk is None else dk + more_k
            dq_parts.append(nn(keys_t[e * size : (e + 1) * size], grad_s))
        made = jnp.concatenate([dk, dv], axis=1).astype(BF16)
        for slot in range(4):
            tile(pair, slot)[...] = made[slot * rows : (slot + 1) * rows]
        dkv_near(pair).start()
        return (jnp.concatenate(dq_parts, axis=0).T * size**-0.5).astype(BF16)

    def pass_on(pair):
        dkv_near(pair).wait_recv()
        add_into(
            spare(pair), tile(pair, core * 2 + at.far), dkv_in.at[pair, :, columns_of(at.far, 256)]
        )
        dkv_cross(pair).start()

    def dq_copy(index):
        return wire.copy(dq_base + index, dq_out.at[index], dq.at[some + index], at.partner)

    @pl.loop(0, some)
    def _(index):
        dq[index] = attend_back(index)

        @pl.when(index > 0)
        def _():
            pass_on(index - 1)

    wire.arrived("do", do.at[pl.ds(some, some)])

    def attend_back_far(index):
        dq_out[index] = attend_back(index + some)
        dq_copy(index).start()
        pass_on(index + some - 1)

    @pl.loop(0, some)
    def _(index):
        attend_back_far(index)

    pass_on(pairs - 1)
    grad_d.own()
    grad_d.out(0)
    grad_u.mid()
    grad_o.mid()
    wire.left(*[name for name in wire.started if name[:2] not in ("gd", "gu", "go")])
    for pair in range(pairs):
        kv_copy(far_base, pair, own_slot, at.cross).wait_send()
        kv_copy(near_base, pair, own_slot, at.sib).wait_send()
        kv_copy(pass_base, pair, core * 2 + at.far, at.sib).wait_send()
    for index in range(some):
        ctx_copy(index).wait_send()

    gkv = s["gkv"]
    for pair in range(pairs):
        dkv_cross(pair).wait_recv()
    for chunk in range(1, 4):
        grad_d.out(chunk)
    for pair in range(pairs):
        own = tile(pair, own_slot)
        near = dkv_in.at[pair, :, columns_of(at.near, 256)]
        for kind in range(2):
            cut = slice(kind * 128, (kind + 1) * 128)
            gkv[kind, :, pair * 128 : (pair + 1) * 128] = (
                own[:, cut].astype(F32)
                + near[:, cut].astype(F32)
                + dkv_far[pair, :, cut].astype(F32)
            ).astype(BF16)
    for index in range(some):
        dq_copy(index).wait_recv()
    merged = jnp.concatenate([dq[pair] for pair in range(pairs)], axis=1)
    for index in range(chunks):
        where = slice(index * 256, (index + 1) * 256)
        rows_of = order[where, :]
        for kind in range(3):
            source = merged if kind == 0 else gkv[kind - 1]
            low = nt(source, rows_of).astype(BF16)
            proj[:, kind * width + index * 256 : kind * width + (index + 1) * 256] = low
            if kind != 1:
                sums[kind // 2, :, where] = jnp.sum(
                    low.astype(F32).reshape(rows // 8, 8, 256), axis=0
                )
    wire.send("gj", proj.at[:, columns_of(other, 3 * half)], s["gj_in"], at.sib)
    grad_d.chain(0)
    grad_u.own()
    for chunk in range(4):
        grad_u.out(chunk)

    vec, vec_in = s["vec"], s["vec_in"]
    for row in range(8):
        vec[row : row + 1, :] = jnp.sum(sums[row], axis=0, keepdims=True)
    for index in range(inner // width):
        vec[8 + index : 9 + index, :] = jnp.sum(
            sums_up[:, index * width : (index + 1) * width], axis=0, keepdims=True
        )
    for row in range(8 + inner // width, 16):
        vec[row : row + 1, :] = jnp.zeros((1, width), F32)
    wire.send("va", vec, vec_in.at[0], at.sib)

    wire.arrived("tok", tok.at[other])
    wire.arrived("gj", s["gj_in"])
    mine_t, theirs_t = tok[core].T, tok[other].T
    for index in range(3):
        where = pl.ds(aligned(core * (3 * half) + index * half, 128), half)
        made = nn(mine_t, proj[:, where]) + nn(
            theirs_t, s["gj_in"][:, index * half : (index + 1) * half]
        )
        made = made.astype(BF16)
        for owner in range(4):
            dwq(owner)[index * share : (index + 1) * share, :] = made[
                owner * share : (owner + 1) * share
            ]
    grad_q.begin()

    wire.arrived("va", vec_in.at[0])
    vec_in[0] = vec_in[0] + vec[...]
    for index, where in enumerate((at.to_x, at.to_y, at.to_d)):
        wire.send("vb" + str(index), vec_in.at[0], vec_in.at[1 + index], where)
    keep_out.wait()

    @pl.loop(0, chunks)
    def _(index):
        where = chunk_of(index, 256)
        result[:, where] = nt(proj[...], s["wqkv"][where, :]) + flow[:, where]

    keep_grad = pltpu.make_async_copy(result, grad_tokens, s["own_sems"].at[7])
    keep_grad.start()
    grad_d.chain(1)
    grad_d.total(0)
    grad_d.chain(2)
    grad_q.mid()
    grad_o.own()
    grad_o.out(0)
    grad_d.total(1)
    grad_d.chain(3)
    for index in range(3):
        wire.arrived("vb" + str(index), vec_in.at[1 + index])
    wire.left("va")
    vec[...] = (vec_in[0] + vec_in[1]) + (vec_in[2] + vec_in[3])
    wire.left("vb0", "vb1", "vb2")
    for index, where in enumerate(at.lines):
        wire.send("vc" + str(index), vec, vec_in.at[4 + index], where)
    grad_d.total(2)
    grad_u.chain(0)
    grad_d.total(3)
    grad_u.chain(1)
    grad_u.total(0)
    grad_u.chain(2)
    grad_q.own()
    for chunk in range(6):
        grad_q.out(chunk)
    grad_u.total(1)
    grad_u.chain(3)
    grad_u.total(2)
    grad_o.chain(0)
    grad_q.chain(0)
    grad_u.total(3)
    grad_q.chain(1)
    grad_o.total(0)
    grad_q.chain(2)
    grad_q.total(0)
    grad_q.chain(3)
    grad_q.total(1)
    grad_q.chain(4)
    grad_q.total(2)
    grad_q.chain(5)
    grad_q.total(3)
    for index in range(3):
        wire.arrived("vc" + str(index), vec_in.at[4 + index])
    vec_in[0] = (vec[...] + vec_in[4]) + (vec_in[5] + vec_in[6])
    keep_small = pltpu.make_async_copy(vec_in.at[0], g_small, s["own_sems"].at[6])
    keep_small.start()
    grad_q.total(4)
    grad_q.total(5)
    for chunk in range(4):
        grad_d.give(chunk)
    for chunk in range(4):
        grad_u.give(chunk)
    grad_o.give(0)
    for chunk in range(6):
        grad_q.give(chunk)
    grad_d.close()
    grad_u.close()
    grad_o.close()
    grad_q.close()
    keep_grad.wait()
    keep_small.wait()
    for pair in range(pairs):
        dkv_near(pair).wait_send()
        dkv_cross(pair).wait_send()
    for index in range(some):
        dq_copy(index).wait_send()
    wire.close()


def whole_layer(tokens, cotangent, pairing, small_raw, w_qkv, w_out, w_up, w_down):
    rows, width = tokens.shape
    inner = w_up.shape[1]
    scratch = layer_scratch(rows, width, inner, pairing.shape[0])
    hbm = pl.BlockSpec(memory_space=pl.ANY)
    vmem = pl.BlockSpec(memory_space=pltpu.VMEM)
    smem = pl.BlockSpec(memory_space=pltpu.SMEM)
    return pl.pallas_call(
        functools.partial(layer_kernel, tuple(scratch)),
        out_shape=[
            jax.ShapeDtypeStruct((rows, width), F32),
            jax.ShapeDtypeStruct((rows, width), F32),
            jax.ShapeDtypeStruct(w_qkv.shape, BF16),
            jax.ShapeDtypeStruct(w_out.shape, BF16),
            jax.ShapeDtypeStruct(w_up.shape, BF16),
            jax.ShapeDtypeStruct(w_down.shape, BF16),
            jax.ShapeDtypeStruct((16, width), F32),
        ],
        in_specs=[hbm, hbm, smem, vmem, hbm, hbm, hbm, hbm],
        out_specs=[hbm] * 7,
        scratch_shapes=list(scratch.values()),
        compiler_params=pltpu.CompilerParams(
            collective_id=0, has_side_effects=True, vmem_limit_bytes=60 << 20
        ),
        name="whole_layer",
    )(tokens, cotangent, pairing, small_raw, w_qkv, w_out, w_up, w_down)


def finish_kernel(share, *refs):
    wide, small, outs = refs[:6], refs[6], refs[7:]
    for source, target in zip(wide, outs[:6]):
        target[...] = source[...].astype(F32)

    @pl.when(pl.program_id(0) == 0)
    def _():
        w = lax.axis_index("wt")
        values = small[...]
        mine = jnp.zeros((8, share), F32)
        line = jnp.zeros((1, 4 * share), F32)
        for owner in range(4):
            mine = mine + jnp.where(
                w == owner, values[:8, owner * share : (owner + 1) * share], 0.0
            )
            line = line + jnp.where(w == owner, values[8 + owner : 9 + owner], 0.0)
        for row in range(8):
            outs[6 + row][...] = mine[row : row + 1]
        outs[14][...] = line.reshape(4 * share)


def finish(*arrays):
    steps = 2
    wide, small = arrays[:6], arrays[6]
    share = small.shape[1] // 4

    def blocks(array):
        return pl.BlockSpec((array.shape[0] // steps, array.shape[1]), lambda i: (i, 0))

    def fixed(shape):
        return pl.BlockSpec(shape, lambda i: (0,) * len(shape))

    shapes = [(1, share)] * 8 + [(4 * share,)]
    return pl.pallas_call(
        functools.partial(finish_kernel, share),
        grid=(steps,),
        out_shape=[jax.ShapeDtypeStruct(v.shape, F32) for v in wide]
        + [jax.ShapeDtypeStruct(v, F32) for v in shapes],
        in_specs=[blocks(v) for v in wide] + [fixed(small.shape)],
        out_specs=[blocks(v) for v in wide] + [fixed(v) for v in shapes],
        compiler_params=pltpu.CompilerParams(vmem_limit_bytes=60 << 20),
        name="finish",
    )(*arrays)


far_below = -1e30


def passed_along(value, axis, steps):
    count = lax.axis_size(axis)
    pairs = [(source, (source + steps) % count) for source in range(count)]
    return lax.ppermute(value, axis, pairs)


def norm_rows(values, gains, shifts):
    average = jnp.mean(values, axis=-1, keepdims=True)
    centred = values - average
    spread = jnp.mean(centred * centred, axis=-1, keepdims=True)
    return centred * lax.rsqrt(spread + 1e-12) * gains + shifts


def gelu_exact(pre_active):
    return jax.nn.gelu(pre_active, approximate=False)


def scores_of(queries, key_heads):
    return (
        jnp.einsum("thd,khd->htk", queries, key_heads, preferred_element_type=jnp.float32) * 0.125
    )


def unchanged(running):
    return running


def general_layer(
    tokens,
    pairing,
    w_qkv,
    bias_q,
    bias_v,
    w_out,
    bias_out,
    gain_one,
    shift_one,
    w_up,
    bias_up,
    w_down,
    bias_down,
    gain_two,
    shift_two,
    cotangent,
):
    local_params = (
        w_qkv,
        bias_q,
        bias_v,
        w_out,
        bias_out,
        gain_one,
        shift_one,
        w_up,
        bias_up,
        w_down,
        bias_down,
        gain_two,
        shift_two,
    )
    gathered = tuple(lax.all_gather(v, "wt", axis=0, tiled=True) for v in local_params)
    (
        wqkv_full,
        biasq_full,
        biasv_full,
        wout_full,
        biasout_full,
        gainone_full,
        shiftone_full,
        wup_full,
        biasup_full,
        wdown_full,
        biasdown_full,
        gaintwo_full,
        shifttwo_full,
    ) = gathered
    tok_rows = tokens.shape[1]
    model_width = tokens.shape[2]
    head_count = pairing.shape[0]
    head_size = model_width // head_count
    group_size = lax.axis_size("ctx")
    position_ctx = lax.axis_index("ctx")
    half_len = tok_rows * group_size // 2
    own_half = position_ctx * tok_rows // half_len
    flipped = pairing == 1
    inputs = tokens[0]
    bias_cat = jnp.concatenate(
        [
            biasq_full.astype(jnp.float32),
            jnp.zeros((model_width,), jnp.float32),
            biasv_full.astype(jnp.float32),
        ]
    )
    projected = jnp.dot(inputs, wqkv_full, preferred_element_type=jnp.float32) + bias_cat
    projected_low = projected.astype(jnp.bfloat16)
    queries = projected_low[:, :model_width].reshape(tok_rows, head_count, head_size)
    key_rows = projected_low[:, model_width : 2 * model_width]
    value_rows = projected_low[:, 2 * model_width :]

    def online_update(state, portion_keys, portion_values, needed):
        row_top, row_total, accumulated = state
        key_count = portion_keys.shape[0]
        key_heads = portion_keys.reshape(key_count, head_count, head_size)
        value_heads = portion_values.reshape(key_count, head_count, head_size)
        scores = scores_of(queries, key_heads)
        scores = jnp.where(needed[:, None, :], scores, far_below)
        new_top = jnp.maximum(row_top, jnp.max(scores, axis=-1))
        factor = jnp.exp(row_top - new_top)
        weights = jnp.exp(scores - new_top[..., None])
        row_total = jnp.sum(weights, axis=-1)
        added = jnp.einsum(
            "htk,khd->thd",
            weights.astype(jnp.bfloat16),
            value_heads,
            preferred_element_type=jnp.float32,
        )
        accumulated = accumulated * factor.T[..., None] + added
        return (new_top, row_total, accumulated)

    start_state = (
        jnp.full((head_count, tok_rows), far_below, jnp.float32),
        jnp.zeros((head_count, tok_rows), jnp.float32),
        jnp.zeros((tok_rows, head_count, head_size), jnp.float32),
    )

    def wanted(offset, key_count):
        key_half = (offset + jnp.arange(key_count)) // half_len
        target = jnp.where(flipped, 1 - own_half, own_half)
        return key_half[None, :] == target[:, None]

    portion_keys = lax.all_gather(key_rows, "ctx", axis=0, tiled=True)
    portion_values = lax.all_gather(value_rows, "ctx", axis=0, tiled=True)
    needed = wanted(jnp.int32(0), portion_keys.shape[0])

    def update(state):
        return online_update(state, portion_keys, portion_values, needed)

    row_top, row_total, accumulated = lax.cond(jnp.any(needed), update, unchanged, start_state)
    context = accumulated / row_total.T[..., None]
    log_sum = row_top + jnp.log(row_total)
    context_low = context.reshape(tok_rows, model_width).astype(jnp.bfloat16)
    branch = jnp.dot(
        context_low, wout_full, preferred_element_type=jnp.float32
    ) + biasout_full.astype(jnp.float32)
    summed_one = inputs.astype(jnp.float32) + branch
    hidden, norm_one_back = jax.vjp(
        norm_rows, summed_one, gainone_full.astype(jnp.float32), shiftone_full.astype(jnp.float32)
    )
    hidden_low = hidden.astype(jnp.bfloat16)
    pre_active = jnp.dot(
        hidden_low, wup_full, preferred_element_type=jnp.float32
    ) + biasup_full.astype(jnp.float32)
    active, gelu_back = jax.vjp(gelu_exact, pre_active)
    active_low = active.astype(jnp.bfloat16)
    ffn_out = jnp.dot(
        active_low, wdown_full, preferred_element_type=jnp.float32
    ) + biasdown_full.astype(jnp.float32)
    output, norm_two_back = jax.vjp(
        norm_rows,
        hidden + ffn_out,
        gaintwo_full.astype(jnp.float32),
        shifttwo_full.astype(jnp.float32),
    )
    again = gathered
    wqkv_back = again[0]
    wout_back = again[3]
    wup_back = again[7]
    wdown_back = again[9]
    grad_two, grad_gain_two, grad_shift_two = norm_two_back(cotangent[0].astype(jnp.float32))
    grad_ffn = grad_two.astype(jnp.bfloat16)
    grad_bias_down = jnp.sum(grad_ffn.astype(jnp.float32), axis=0)
    grad_w_down = jnp.einsum("tf,td->fd", active_low, grad_ffn, preferred_element_type=jnp.float32)
    grad_active = jnp.einsum("td,fd->tf", grad_ffn, wdown_back, preferred_element_type=jnp.float32)
    (grad_pre_f,) = gelu_back(grad_active)
    grad_pre = grad_pre_f.astype(jnp.bfloat16)
    grad_bias_up = jnp.sum(grad_pre.astype(jnp.float32), axis=0)
    grad_w_up = jnp.einsum("tc,tf->cf", hidden_low, grad_pre, preferred_element_type=jnp.float32)
    grad_hidden = grad_two + jnp.einsum(
        "tf,cf->tc", grad_pre, wup_back, preferred_element_type=jnp.float32
    )
    grad_one, grad_gain_one, grad_shift_one = norm_one_back(grad_hidden)
    grad_branch = grad_one.astype(jnp.bfloat16)
    grad_bias_out = jnp.sum(grad_branch.astype(jnp.float32), axis=0)
    grad_w_out = jnp.einsum(
        "tc,td->cd", context_low, grad_branch, preferred_element_type=jnp.float32
    )
    grad_context = jnp.einsum(
        "td,cd->tc", grad_branch, wout_back, preferred_element_type=jnp.float32
    )
    grad_context = grad_context.astype(jnp.bfloat16).reshape(tok_rows, head_count, head_size)
    row_delta = jnp.sum(grad_context.astype(jnp.float32) * context, axis=-1).T

    def piece_grads(portion_keys, portion_values, needed):
        key_count = portion_keys.shape[0]
        key_heads = portion_keys.reshape(key_count, head_count, head_size)
        value_heads = portion_values.reshape(key_count, head_count, head_size)
        scores = scores_of(queries, key_heads)
        scores = jnp.where(needed[:, None, :], scores, far_below)
        probs = jnp.exp(scores - log_sum[..., None])
        probs_low = probs.astype(jnp.bfloat16)
        piece_v = jnp.einsum(
            "htk,thd->khd", probs_low, grad_context, preferred_element_type=jnp.float32
        ).reshape(key_count, model_width)
        grad_weights = jnp.einsum(
            "thd,khd->htk", grad_context, value_heads, preferred_element_type=jnp.float32
        )
        grad_scores = (probs * (grad_weights - row_delta[..., None])).astype(jnp.bfloat16)
        piece_q = 0.125 * jnp.einsum(
            "htk,khd->thd", grad_scores, key_heads, preferred_element_type=jnp.float32
        )
        piece_k = 0.125 * jnp.einsum(
            "htk,thd->khd", grad_scores, queries, preferred_element_type=jnp.float32
        ).reshape(key_count, model_width)
        return (piece_k, piece_v, piece_q)

    zero_queries = jnp.zeros((tok_rows, head_count, head_size), jnp.float32)

    def circle_step(step_index, running):
        turn_keys, turn_values, grad_keys, grad_values, grad_queries = running
        owner = (position_ctx - step_index) % group_size
        needed = wanted(owner * tok_rows, tok_rows)

        def update_grads(state):
            grad_k, grad_v, grad_q = state
            piece_k, piece_v, piece_q = piece_grads(turn_keys, turn_values, needed)
            return (grad_k + piece_k, grad_v + piece_v, grad_q + piece_q)

        grad_keys, grad_values, grad_queries = lax.cond(
            jnp.any(needed), update_grads, unchanged, (grad_keys, grad_values, grad_queries)
        )
        turn_keys, turn_values = passed_along((turn_keys, turn_values), "ctx", 1)
        grad_keys, grad_values = (
            passed_along(grad_keys.astype(jnp.bfloat16), "ctx", 1).astype(grad_keys.dtype),
            passed_along(grad_values.astype(jnp.bfloat16), "ctx", 1).astype(grad_values.dtype),
        )
        return (turn_keys, turn_values, grad_keys, grad_values, grad_queries)

    zero_rows = jnp.zeros((tok_rows, model_width), jnp.float32)
    circle_start = (key_rows, value_rows, zero_rows, zero_rows, zero_queries)
    circle_end = lax.fori_loop(0, group_size, circle_step, circle_start)
    grad_keys = circle_end[2]
    grad_values = circle_end[3]
    grad_queries = circle_end[4]
    grad_projected = jnp.concatenate(
        [grad_queries.reshape(tok_rows, model_width), grad_keys, grad_values], axis=1
    ).astype(jnp.bfloat16)
    grad_bias_q = jnp.sum(grad_projected[:, :model_width].astype(jnp.float32), axis=0)
    grad_bias_v = jnp.sum(grad_projected[:, 2 * model_width :].astype(jnp.float32), axis=0)
    grad_w_qkv = jnp.einsum("tc,tj->cj", inputs, grad_projected, preferred_element_type=jnp.float32)
    grad_inputs = grad_one + jnp.einsum(
        "tj,cj->tc", grad_projected, wqkv_back, preferred_element_type=jnp.float32
    )
    terms = (
        grad_w_qkv,
        grad_bias_q,
        grad_bias_v,
        grad_w_out,
        grad_bias_out,
        grad_gain_one,
        grad_shift_one,
        grad_w_up,
        grad_bias_up,
        grad_w_down,
        grad_bias_down,
        grad_gain_two,
        grad_shift_two,
    )
    owned = tuple(
        lax.psum_scatter(term.astype(jnp.bfloat16), "wt", scatter_dimension=0, tiled=True)
        for term in terms
    )
    totals = tuple(lax.psum(term, "ctx").astype(jnp.float32) for term in owned)
    return (
        output[None],
        grad_inputs[None],
        totals[0],
        totals[1],
        totals[2],
        totals[3],
        totals[4],
        totals[5],
        totals[6],
        totals[7],
        totals[8],
        totals[9],
        totals[10],
        totals[11],
        totals[12],
    )


def fast_layer(
    tokens,
    pairing,
    w_qkv,
    bias_q,
    bias_v,
    w_out,
    bias_out,
    gain_one,
    shift_one,
    w_up,
    bias_up,
    w_down,
    bias_down,
    gain_two,
    shift_two,
    cotangent,
):
    share = tokens.shape[2] // 4
    vectors = (bias_q, bias_v, bias_out, gain_one, shift_one, bias_down, gain_two, shift_two)
    vectors = vectors + tuple(bias_up[k * share : (k + 1) * share] for k in range(4))
    row = lax.broadcasted_iota(jnp.int32, (16, share), 0)
    small_raw = jnp.zeros((16, share), jnp.bfloat16)
    for index, vector in enumerate(vectors):
        small_raw = jnp.where(row == index, vector[None, :], small_raw)
    made = whole_layer(
        tokens[0], cotangent[0], pairing, small_raw, w_qkv, w_out, w_up, w_down
    )
    output, grad_tokens, g_qkv, g_out, g_up, g_down, *small = finish(*made)
    small = [v.reshape(-1) for v in small]
    return (
        output[None],
        grad_tokens[None],
        g_qkv,
        small[0],
        small[1],
        g_out,
        small[2],
        small[3],
        small[4],
        g_up,
        small[8],
        g_down,
        small[5],
        small[6],
        small[7],
    )


def local(tokens, pairing, *rest):
    rows, width = tokens.shape[1:]
    heads = pairing.shape[0]
    inner = rest[7].shape[1]
    fits = (
        lax.axis_size("wt") == 4
        and lax.axis_size("ctx") == 8
        and tokens.shape[0] == 1
        and rows % BAND == 0
        and 3 * rows <= width
        and width % 256 == 0
        and heads % 4 == 0
        and width == 64 * heads
        and inner == 4 * width
    )
    layer = fast_layer if fits else general_layer
    return layer(tokens, pairing, *rest)


def solution(mesh):
    in_specs = (
        P("wt", "ctx", None),
        P(),
        P("wt", None),
        P("wt"),
        P("wt"),
        P("wt", None),
        P("wt"),
        P("wt"),
        P("wt"),
        P("wt", None),
        P("wt"),
        P("wt", None),
        P("wt"),
        P("wt"),
        P("wt"),
        P("wt", "ctx", None),
    )
    out_specs = (
        P("wt", "ctx", None),
        P("wt", "ctx", None),
        P("wt", None),
        P("wt"),
        P("wt"),
        P("wt", None),
        P("wt"),
        P("wt"),
        P("wt"),
        P("wt", None),
        P("wt"),
        P("wt", None),
        P("wt"),
        P("wt"),
        P("wt"),
    )
    return jax.shard_map(local, mesh=mesh, in_specs=in_specs, out_specs=out_specs, check_vma=False)
```

```python
import functools

import jax
import jax.numpy as jnp
from jax import lax
from jax.experimental import pallas as pl
from jax.experimental.pallas import tpu as pltpu
from jax.sharding import PartitionSpec as P

F32, BF16 = jnp.float32, jnp.bfloat16
MESH = pl.DeviceIdType.MESH
BAND = 32


def nn(a, b):
    return jnp.dot(a, b, preferred_element_type=F32)


def nt(a, b):
    return lax.dot_general(a, b, (((1,), (1,)), ((), ())), preferred_element_type=F32)


def aligned(start, multiple):
    return start if isinstance(start, int) else pl.multiple_of(start, multiple)


def chunk_of(index, size):
    return pl.ds(aligned(index * size, size), size)


class Wire:
    def __init__(self, sends, receives, anyone):
        self.sends, self.receives, self.anyone = sends, receives, anyone
        self.firsts, self.used, self.groups, self.started = {}, 0, {}, {}

    def slot(self, name, count=1):
        if name not in self.firsts:
            self.firsts[name] = self.used, count
            self.used += count
            assert self.used <= self.receives.shape[0]
        first, had = self.firsts[name]
        assert had == count
        return first

    def copy(self, slot, source, target, where, group):
        place = self.groups.setdefault(group, len(self.groups))
        assert place < self.sends.shape[0]
        return pltpu.make_async_remote_copy(
            src_ref=source,
            dst_ref=target,
            send_sem=self.sends.at[place],
            recv_sem=self.receives.at[slot],
            device_id=where,
            device_id_type=MESH,
        )

    def send(self, name, source, target, where):
        copy = self.copy(self.slot(name), source, target, where, name)
        copy.start()
        self.started[name] = copy

    def send_in(self, group, name, source, target, where):
        self.copy(self.slot(name), source, target, where, group).start()

    def gone(self, group, ref):
        self.copy(0, ref, ref, self.anyone, group).wait_send()

    def arrived(self, name, target):
        self.copy(self.slot(name), target, target, self.anyone, "none").wait_recv()

    def left(self, *names):
        for name in names:
            self.started.pop(name).wait_send()

    def close(self):
        self.left(*tuple(self.started))


class Place:
    def __init__(self):
        self.w = w = lax.axis_index("wt")
        self.c = c = lax.axis_index("ctx")
        self.core = core = c % 2
        self.other = 1 - core
        self.z = z = c // 2
        self.near = z % 2
        self.far = 1 - self.near
        self.nx = w + 1 - 2 * (w % 2)
        self.ny = (w + 2) % 4
        self.nd = 3 - w
        self.sib = (w, c + 1 - 2 * core)
        self.to_x, self.to_y, self.to_d = (self.nx, c), (self.ny, c), (self.nd, c)
        self.cross = (w, c + 2 - 4 * self.near)
        self.partner = (w, (c + 4) % 8)
        self.lines = [(w, spot * 2 + core) for spot in (z + 1 - 2 * (z % 2), (z + 2) % 4, 3 - z)]
        self.others = [(w, (c + step) % 8) for step in range(1, 8)]
        self.mate, self.middle = self.lines[0], self.lines[2]
        self.outer, self.inner = (z == 0) | (z == 3), (z == 1) | (z == 2)


def greet(peers):
    barrier = pltpu.get_barrier_semaphore()
    for peer in peers:
        pl.semaphore_signal(barrier, inc=1, device_id=peer, device_id_type=MESH)
    pl.semaphore_wait(barrier, len(peers))


class Part:
    def __init__(self, name, local, full, first, columns, place, wire):
        self.name, self.local, self.full, self.place, self.wire = name, local, full, place, wire
        self.rows = local.shape[0]
        self.first, self.columns = first, columns // 2

    def piece(self, owner, core, half=None):
        rows, start = self.rows, owner * self.rows
        if half is not None:
            rows = self.rows // 2
            start = start + half * rows
        return self.full.at[
            pl.ds(aligned(start, 16), rows),
            pl.ds(aligned(self.first + core * self.columns, 128), self.columns),
        ]

    def send(self, kind, source, target, where):
        self.wire.send_in(self.name, self.name + kind, source, target, where)

    def begin(self):
        at = self.place
        mine = self.local.at[
            :, pl.ds(aligned(self.first + at.core * self.columns, 128), self.columns)
        ]
        target = self.piece(at.w, at.core)
        self.send("a", mine, target, at.to_x)
        self.send("b", mine, target, at.to_y)

    def relay(self):
        at, wire = self.place, self.wire
        for kind, owner, half, on, where in (
            ("a", at.nx, 0, "c", at.to_y),
            ("b", at.ny, 1, "e", at.to_x),
        ):
            block = self.piece(owner, at.core)
            wire.arrived(self.name + kind, block)
            part = self.piece(owner, at.core, half)
            self.send(on, part, part, where)
            self.send("s", block, block, at.sib)

    def share(self):
        at, wire = self.place, self.wire
        for half, came in ((0, "c"), (1, "e")):
            block = self.piece(at.nd, at.core, half)
            wire.arrived(self.name + came, block)
            self.send("s", block, block, at.sib)

    def finish(self):
        block = self.full.at[pl.ds(0, 3 * self.rows), pl.ds(self.first, self.columns)]
        self.wire.arrived(self.name + "s", block)

    def gone(self):
        block = self.full.at[pl.ds(0, 3 * self.rows), pl.ds(self.first, 2 * self.columns)]
        self.wire.gone(self.name, block)


def add_into(target, *sources):
    rows, columns = sources[0].shape
    band = 16
    while columns * band * 2 <= 1 << 15 and rows % (band * 2) == 0:
        band *= 2

    @pl.loop(0, rows // band)
    def _(index):
        where = chunk_of(index, band)
        total = sources[0][where, :].astype(F32)
        for source in sources[1:]:
            total = total + source[where, :].astype(F32)
        target[where, :] = total.astype(target.dtype)


class Grad:
    def __init__(self, name, chunks, blocks, buffers, finals, place, wire, local_sem):
        self.name, self.chunks, self.blocks, self.finals = name, chunks, blocks, finals
        self.place, self.wire, self.local_sem = place, wire, local_sem
        self.from_x, self.from_y, self.diag_x, self.diag_y, self.low, self.high = buffers
        self.rows, self.columns = self.from_x.shape

    def half(self, ref, index):
        return ref.at[pl.ds(index * (self.rows // 2), self.rows // 2), :]

    def begin(self):
        at, wire = self.place, self.wire
        block = self.blocks(at.nd)
        wire.send(self.name + "a", self.half(block, 0), self.diag_x, at.to_x)
        wire.send(self.name + "b", self.half(block, 1), self.diag_y, at.to_y)

    def fold(self):
        at, wire = self.place, self.wire
        for kind, came, owner, index in (("a", self.diag_x, at.ny, 0), ("b", self.diag_y, at.nx, 1)):
            wire.arrived(self.name + kind, came)
            part = self.half(self.blocks(owner), index)
            add_into(part, part, came)

    def lanes(self, chunk):
        at = self.place
        return (
            self.hop("c", chunk, self.blocks(at.nx), self.from_x, at.to_x),
            self.hop("d", chunk, self.blocks(at.ny), self.from_y, at.to_y),
        )

    def push(self, *chunks):
        for chunk in chunks:
            for copy in self.lanes(chunk):
                copy.start()

    def cut(self, ref, chunk):
        count = self.rows // self.chunks
        return ref.at[pl.ds(chunk * count, count), :]

    def hop(self, kind, chunk, source, target, where):
        slot = self.wire.slot(self.name + kind, self.chunks) + chunk
        return self.wire.copy(
            slot, self.cut(source, chunk), self.cut(target, chunk), where, self.name + kind
        )

    def outward(self, chunk):
        return self.hop("u", chunk, self.blocks(self.place.w), self.low, self.place.mate)

    def across(self, chunk):
        return self.hop("v", chunk, self.from_x, self.high, self.place.middle)

    def back(self, chunk):
        return self.hop("t", chunk, self.from_y, self.high, self.place.mate)

    def own(self, chunk):
        for copy in self.lanes(chunk):
            copy.wait_recv()
        part = self.cut(self.blocks(self.place.w), chunk)
        add_into(part, part, self.cut(self.from_x, chunk), self.cut(self.from_y, chunk))
        self.out(chunk)

    def out(self, chunk):
        @pl.when(self.place.outer)
        def _():
            self.outward(chunk).start()

    def chain(self, chunk):
        at = self.place

        @pl.when(at.inner)
        def _():
            self.outward(chunk).wait_recv()
            block = self.blocks(at.w)
            add_into(
                self.cut(self.from_x, chunk), self.cut(block, chunk), self.cut(self.low, chunk)
            )
            self.across(chunk).start()

    def total(self, chunk):
        at = self.place

        @pl.when(at.inner)
        def _():
            self.across(chunk).wait_recv()
            add_into(
                self.cut(self.from_y, chunk),
                self.cut(self.from_x, chunk),
                self.cut(self.high, chunk),
            )
            self.back(chunk).start()
            for copy in self.copies(chunk, self.from_y):
                copy.start()

    def copies(self, chunk, source):
        at, wire = self.place, self.wire
        piece, target = self.cut(source, chunk), self.finals(chunk, at.core)
        keep = pltpu.make_async_copy(piece, target, self.local_sem)
        slot = wire.slot(self.name + "s")
        return keep, wire.copy(slot, piece, target, at.sib, self.name + "s")

    def give(self, chunk):
        at = self.place

        @pl.when(at.outer)
        def _():
            self.back(chunk).wait_recv()
            for copy in self.copies(chunk, self.high):
                copy.start()

    def close(self):
        at, wire = self.place, self.wire
        whole = self.from_y
        pltpu.make_async_copy(whole, whole, self.local_sem).wait()
        wire.arrived(self.name + "s", whole)
        for kind in ("s", "c", "d"):
            wire.gone(self.name + kind, whole)

        @pl.when(at.outer)
        def _():
            wire.gone(self.name + "u", whole)

        @pl.when(at.inner)
        def _():
            wire.gone(self.name + "v", whole)
            wire.gone(self.name + "t", whole)


def layer_scratch(rows, width, inner, heads):
    pairs = heads // 2
    some = pairs // 2
    share = width // 4
    half = width // 2
    groups = 8

    def low(*shape):
        return pltpu.VMEM(shape, BF16)

    def wide(*shape):
        return pltpu.VMEM(shape, F32)

    scratch = dict(
        wqkv=low(width, 3 * width),
        wo=low(width, width),
        wu=low(width, inner),
        wd=low(inner, width),
        order=low(width, width),
        tok=low(2, rows, width),
        cot=low(rows, width),
        small_own=low(16, width),
        small_in=low(3, 16, width),
        small=wide(16, width),
        bias_qkv=wide(8, 3 * width),
        bias_up=wide(8, inner),
        kv=low(pairs, 4, rows, 256),
        proj=low(rows, 3 * width),
        q=low(pairs, rows, 128),
        q_out=low(some, rows, 128),
        exps=low(heads, 4 * rows, rows),
        inverse=wide(heads, 1, rows),
        out_t=wide(pairs, 128, rows),
        ctx=low(pairs, rows, 128),
        ctx_out=low(some, rows, 128),
        ctx_nat=low(2, rows, width),
        hat_one=wide(rows, width),
        r_one=wide(rows, 1),
        flow=wide(rows, width),
        stage=wide(rows, width),
        result=wide(rows, width),
        hid=low(2, rows, width),
        act=low(2, rows, inner),
        slope=low(rows, inner),
        slope_in=low(rows, inner // 2),
        gf=low(rows, width),
        gf_in=low(rows, half),
        gb=low(rows, width),
        gb_in=low(rows, half),
        do=low(pairs, rows, 128),
        do_out=low(some, rows, 128),
        dq=low(pairs, rows, 128),
        dq_out=low(some, rows, 128),
        dkv_in=low(pairs, rows, 256),
        tops=wide(heads, 1, rows),
        delta=wide(heads, 1, rows),
        dos=low(pairs, rows, 128),
        far_q=low(2, pairs, rows, 128),
        far_tops=wide(2, heads, 1, rows),
        far_delta=wide(2, heads, 1, rows),
        far_dos=low(2, pairs, rows, 128),
        gkv=low(2, rows, width),
        gj_in=low(rows, 3 * half),
        sums=wide(16, groups, width),
        sums_up=wide(groups, inner),
        vec=wide(16, width),
        vec_in=wide(7, 16, width),
        dwd=low(4, inner // 4, half),
    )
    shapes = dict(
        d=(inner // 4, half), u=(2 * share, width), o=(share, half), q=(3 * share, half)
    )
    for name, (r, c) in shapes.items():
        for kind in ("fx", "fy", "lo", "hi"):
            scratch["g" + name + kind] = low(r, c)
        for kind in ("dx", "dy"):
            scratch["g" + name + kind] = low(r // 2, c)
    scratch["sends"] = pltpu.SemaphoreType.DMA((80,))
    scratch["receives"] = pltpu.SemaphoreType.DMA((180,))
    scratch["own_sems"] = pltpu.SemaphoreType.DMA((12,))
    return scratch


def layer_kernel(names, *refs):
    (
        tokens,
        cot_l,
        pairing,
        small_raw,
        qkv_l,
        out_l,
        up_l,
        down_l,
        output,
        grad_tokens,
        g_qkv,
        g_out,
        g_up,
        g_down,
        g_small,
    ) = refs[:15]
    s = dict(zip(names, refs[15:]))
    at = Place()
    wire = Wire(s["sends"], s["receives"], at.sib)
    rows, width = tokens.shape
    inner = up_l.shape[1]
    heads = pairing.shape[0]
    pairs, some = heads // 2, heads // 4
    size = width // heads
    half = width // 2
    keys = 4 * rows
    chunks = width // 256
    share = width // 4
    core, other = at.core, at.other

    greet([at.to_x, at.to_y, at.to_d] + at.others)

    part_kv = Part("kv", qkv_l, s["wqkv"], width, 2 * width, at, wire)
    part_q = Part("q", qkv_l, s["wqkv"], 0, width, at, wire)
    part_o = Part("o", out_l, s["wo"], 0, width, at, wire)
    part_u = Part("u", up_l, s["wu"], 0, inner, at, wire)
    part_d = Part("d", down_l, s["wd"], 0, width, at, wire)
    part_kv.begin()
    part_q.begin()
    raw = small_raw[...]
    row = lax.broadcasted_iota(jnp.int32, (share, width), 0)
    column = lax.broadcasted_iota(jnp.int32, (share, width), 1)

    def spread(values, spot):
        place = jnp.where(column - row == spot * share, 1.0, 0.0).astype(BF16)
        return nn(values, place)

    own_row = lax.broadcasted_iota(jnp.int32, (8, width), 0) == at.w
    line = spread(raw[8:16], 0)[0:1]
    for index in range(1, 4):
        line = line + spread(raw[8:16], index)[index : index + 1]
    small_own = s["small_own"]
    small_own[...] = jnp.concatenate(
        [spread(raw[:8], at.w), jnp.where(own_row, line, 0.0)], axis=0
    ).astype(BF16)
    for index, where in enumerate((at.to_x, at.to_y, at.to_d)):
        wire.send("sm" + str(index), small_own, s["small_in"].at[index], where)
    keeps = []
    for slot, (local, full) in enumerate(
        (
            (qkv_l, s["wqkv"].at[pl.ds(aligned(at.w * share, 16), share)]),
            (tokens, s["tok"].at[core]),
            (cot_l, s["cot"]),
            (out_l, s["wo"].at[pl.ds(aligned(at.w * share, 16), share)]),
            (up_l, s["wu"].at[pl.ds(aligned(at.w * share, 16), share)]),
            (down_l, s["wd"].at[pl.ds(aligned(at.w * (inner // 4), 16), inner // 4)]),
        )
    ):
        keeps.append(pltpu.make_async_copy(local, full, s["own_sems"].at[slot]))
        keeps[-1].start()
    wire.send("tok", tokens, s["tok"].at[core], at.sib)

    before = 0
    for head in range(heads):
        flag = pairing[head]
        spot = flag * (heads // 2 + before) + (1 - flag) * (head - before)
        before = before + flag
        row = lax.broadcasted_iota(jnp.int32, (size, width), 0)
        column = lax.broadcasted_iota(jnp.int32, (size, width), 1)
        s["order"][head * size : (head + 1) * size, :] = jnp.where(
            column - row == spot * size, 1.0, 0.0
        ).astype(BF16)

    part_kv.relay()
    part_q.relay()
    part_o.begin()
    part_kv.share()
    for index in range(3):
        wire.arrived("sm" + str(index), s["small_in"].at[index])
    small = s["small"]
    small[...] = (
        small_own[...].astype(F32)
        + s["small_in"][0].astype(F32)
        + s["small_in"][1].astype(F32)
        + s["small_in"][2].astype(F32)
    )
    s["bias_qkv"][0:1, 0:width] = small[0:1, :]
    s["bias_qkv"][0:1, width : 2 * width] = jnp.zeros((1, width), F32)
    s["bias_qkv"][0:1, 2 * width :] = small[1:2, :]
    for index in range(inner // width):
        s["bias_up"][0:1, index * width : (index + 1) * width] = small[8 + index : 9 + index, :]
    keeps[0].wait()
    keeps[1].wait()
    part_kv.finish()

    tok, proj, order, kv = s["tok"], s["proj"], s["order"], s["kv"]
    own_slot = core * 2 + at.near

    def project(first, count):
        @pl.loop(first, first + count)
        def _(index):
            where = chunk_of(index, 256)
            made = nn(tok[core], s["wqkv"][:, where]) + s["bias_qkv"][0:1, where]
            proj[:, where] = made.astype(BF16)

    project(chunks, 2 * chunks)
    for index in range(chunks):
        columns = order[:, index * 256 : (index + 1) * 256]
        for kind in range(2):
            moved = nn(proj[:, (1 + kind) * width : (2 + kind) * width], columns).astype(BF16)
            for e in range(2):
                kv[2 * index + e, own_slot, :, kind * 128 : (kind + 1) * 128] = moved[
                    :, e * 128 : (e + 1) * 128
                ]
    near_base = wire.slot("near kv", pairs)
    far_base = wire.slot("far kv", pairs)
    pass_base = wire.slot("passed kv", pairs)

    def kv_copy(base, pair, slot, where):
        block = kv.at[pair, slot]
        return wire.copy(base + pair, block, block, where, "kv" + str(base))

    for pair in range(pairs):
        if pair < some:
            kv_copy(far_base, pair, own_slot, at.cross).start()
        kv_copy(near_base, pair, own_slot, at.sib).start()
    part_q.share()
    part_u.begin()
    part_q.finish()
    project(0, chunks)
    q, q_out = s["q"], s["q_out"]
    for index in range(chunks):
        moved = nn(proj[:, 0:width], order[:, index * 256 : (index + 1) * 256]).astype(BF16)
        for e in range(2):
            pair = 2 * index + e
            block = moved[:, e * 128 : (e + 1) * 128]
            if pair < some:
                q[pair] = block
            else:
                q_out[pair - some] = block
    wire.send("queries", q_out, q.at[pl.ds(some, some)], at.partner)
    part_o.relay()
    part_d.begin()

    exps, inverse, out_t = s["exps"], s["inverse"], s["out_t"]

    def both(pair, first):
        return kv[pair, :, :, first : first + 128].reshape(keys, 128)

    def masked(block, e, axis=1):
        spot = lax.broadcasted_iota(jnp.int32, block.shape, axis)
        mine = spot < size if e == 0 else spot >= size
        return jnp.where(mine, block, jnp.zeros_like(block))

    def attend(pair):
        key_rows, value_rows = both(pair, 0), both(pair, 128)
        values_t = value_rows.T
        queries = q[pair] * jnp.asarray(size**-0.5, BF16)
        parts = []
        for e in range(2):
            scores = nt(key_rows, masked(queries, e))
            top = jnp.max(scores, axis=0, keepdims=True)
            raised = jnp.exp(scores - top)
            total = jnp.sum(raised, axis=0, keepdims=True)
            low = raised.astype(BF16)
            exps[2 * pair + e] = low
            s["tops"][2 * pair + e] = top
            one_over = 1.0 / total
            inverse[2 * pair + e] = one_over
            parts.append(nn(values_t[e * size : (e + 1) * size], low) * one_over)
        merged = jnp.concatenate(parts, axis=0)
        out_t[pair] = merged
        return merged.T.astype(BF16)

    def receive_kv(pair):
        kv_copy(far_base, pair, core * 2 + at.far, at.cross).wait_recv()
        kv_copy(pass_base, pair, core * 2 + at.far, at.sib).start()
        kv_copy(near_base, pair, other * 2 + at.near, at.sib).wait_recv()
        kv_copy(pass_base, pair, other * 2 + at.far, at.sib).wait_recv()

    ctx, ctx_out = s["ctx"], s["ctx_out"]
    back_base = wire.slot("ctx", some)

    def ctx_copy(index):
        return wire.copy(back_base + index, ctx_out.at[index], ctx.at[some + index], at.partner, "ctx")

    def attend_far(index):
        receive_kv(index + some)
        ctx_out[index] = attend(index + some)
        ctx_copy(index).start()

    @pl.loop(0, some)
    def _(index):
        receive_kv(index)
        kv_copy(far_base, index + some, own_slot, at.cross).start()
        ctx[index] = attend(index)

    part_o.share()
    wire.arrived("queries", q.at[pl.ds(some, some)])
    attend_far(0)
    part_u.relay()

    @pl.loop(1, some)
    def _(index):
        attend_far(index)

    part_o.finish()
    far_q, far_tops, far_delta, far_dos = (
        s[name] for name in ("far_q", "far_tops", "far_delta", "far_dos")
    )
    tops, delta, dos = s["tops"], s["delta"], s["dos"]
    wire.send("far q", q, far_q.at[core], at.cross)
    wire.send("far tops", tops, far_tops.at[core], at.cross)
    part_d.relay()
    keeps[2].wait()
    keeps[3].wait()
    for index in range(some):
        ctx_copy(index).wait_recv()
    permuted = jnp.concatenate([ctx[pair] for pair in range(pairs)], axis=1)
    ctx_nat, stage = s["ctx_nat"], s["stage"]
    for index in range(chunks):
        where = slice(index * 256, (index + 1) * 256)
        ctx_nat[core, :, where] = nt(permuted, order[where, :]).astype(BF16)
    wire.send("ctxn", ctx_nat.at[core], ctx_nat.at[core], at.sib)

    @pl.loop(0, chunks)
    def _(index):
        where = chunk_of(index, 256)
        stage[:, where] = nn(ctx_nat[core], s["wo"][:, where])

    hat_one, r_one, flow, hid = s["hat_one"], s["r_one"], s["flow"], s["hid"]
    inv_width = 1.0 / width

    def mean(values):
        return jnp.sum(values, axis=-1, keepdims=True) * inv_width

    @pl.loop(0, rows // BAND, unroll=2)
    def _(index):
        where = chunk_of(index, BAND)
        total = tok[core, where, :].astype(F32) + stage[where, :] + small[2:3, :]
        centred = total - mean(total)
        scale = lax.rsqrt(mean(centred * centred) + 1e-12)
        hat = centred * scale
        hat_one[where, :] = hat
        r_one[where, :] = scale
        hidden = hat * small[3:4, :] + small[4:5, :]
        flow[where, :] = hidden
        hid[core, where, :] = hidden.astype(BF16)

    wire.send("hid", hid.at[core], hid.at[core], at.sib)
    part_u.share()
    part_u.finish()
    keeps[4].wait()
    act, slope = s["act"], s["slope"]

    @pl.loop(0, inner // 256, unroll=3)
    def _(index):
        where = chunk_of(index, 256)
        pre = nn(hid[core], s["wu"][:, where]) + s["bias_up"][0:1, where]
        below = 0.5 * (1.0 + lax.erf(pre * (0.5**0.5)))
        act[core, :, where] = (pre * below).astype(BF16)
        density = jnp.exp(pre * pre * -0.5) * 0.3989422804014327
        slope[:, where] = (below + pre * density).astype(BF16)

    wire.send("act", act.at[core], act.at[core], at.sib)
    wire.arrived("far q", far_q.at[core])
    wire.send("passed q", far_q.at[core], far_q.at[core], at.sib)
    wire.arrived("far tops", far_tops.at[core])
    wire.send("passed tops", far_tops.at[core], far_tops.at[core], at.sib)
    part_d.share()
    part_d.finish()
    keeps[5].wait()

    @pl.loop(0, chunks)
    def _(index):
        where = chunk_of(index, 256)
        stage[:, where] = nn(act[core], s["wd"][:, where])

    result, gf, cot = s["result"], s["gf"], s["cot"]
    sums, sums_up = s["sums"], s["sums_up"]
    sums[...] = jnp.zeros_like(sums)

    def gather_rows(values):
        return jnp.sum(values.reshape(BAND // 8, 8, values.shape[-1]), axis=0)

    @pl.loop(0, rows // BAND, unroll=2)
    def _(index):
        where = chunk_of(index, BAND)
        total = flow[where, :] + stage[where, :] + small[5:6, :]
        centred = total - mean(total)
        scale = lax.rsqrt(mean(centred * centred) + 1e-12)
        hat = centred * scale
        result[where, :] = hat * small[6:7, :] + small[7:8, :]
        back = cot[where, :].astype(F32)
        g = back * small[6:7, :]
        grad = scale * (g - mean(g) - hat * mean(g * hat))
        flow[where, :] = grad
        low = grad.astype(BF16)
        gf[where, :] = low
        sums[6] += gather_rows(back * hat)
        sums[7] += gather_rows(back)
        sums[5] += gather_rows(low.astype(F32))

    keep_out = pltpu.make_async_copy(result, output, s["own_sems"].at[7])
    keep_out.start()

    def columns_of(which, count):
        return pl.ds(aligned(which * count, 128), count)

    wire.send("gf", gf.at[:, columns_of(other, half)], s["gf_in"], at.sib)

    def buffers(name):
        return [s["g" + name + kind] for kind in ("fx", "fy", "dx", "dy", "lo", "hi")]

    dwd, wd, wu = s["dwd"], s["wd"], s["wu"]

    def side_by_side(first, count, owner):
        return wd.at[
            pl.ds(aligned(first + (owner // 2) * count, 16), count),
            pl.ds(aligned((owner % 2) * half, 128), half),
        ]

    def dwo(owner):
        return side_by_side(2 * width + 6 * share, share, owner)

    def dwq(owner):
        return side_by_side(2 * width, 3 * share, owner)

    grad_d = Grad(
        "gd",
        4,
        lambda r: dwd.at[r],
        buffers("d"),
        lambda i, k: g_down.at[pl.ds(i * (inner // 16), inner // 16), columns_of(k, half)],
        at,
        wire,
        s["own_sems"].at[8],
    )
    grad_u = Grad(
        "gu",
        4,
        lambda r: wd.at[pl.ds(aligned(r * (2 * share), 16), 2 * share), :],
        buffers("u"),
        lambda i, k: g_up.at[
            pl.ds((i % 2) * (share // 2), share // 2), columns_of(2 * k + i // 2, width)
        ],
        at,
        wire,
        s["own_sems"].at[9],
    )
    grad_o = Grad(
        "go",
        1,
        dwo,
        buffers("o"),
        lambda i, k: g_out.at[:, columns_of(k, half)],
        at,
        wire,
        s["own_sems"].at[10],
    )
    grad_q = Grad(
        "gq",
        6,
        dwq,
        buffers("q"),
        lambda i, k: g_qkv.at[
            pl.ds((i % 2) * (share // 2), share // 2), columns_of(3 * k + i // 2, half)
        ],
        at,
        wire,
        s["own_sems"].at[11],
    )

    wire.arrived("act", act.at[other])
    wire.arrived("gf", s["gf_in"])
    gf_mine = gf[:, columns_of(core, half)]
    gf_theirs = s["gf_in"][...]
    quarter = inner // 4
    for owner in (at.nd, at.nx, at.ny, at.w):
        where = pl.ds(aligned(owner * quarter, 128), quarter)
        made = nn(act[core, :, where].T, gf_mine) + nn(act[other, :, where].T, gf_theirs)
        dwd[owner] = made.astype(BF16)
        if owner is at.nd:
            grad_d.begin()

    @pl.loop(0, inner // 256, unroll=3)
    def _(index):
        where = chunk_of(index, 256)
        grad = nt(gf[...], wd[where, :]) * slope[:, where].astype(F32)
        low = grad.astype(BF16)
        slope[:, where] = low
        sums_up[:, where] = jnp.sum(low.astype(F32).reshape(rows // 8, 8, 256), axis=0)

    wire.send("slope", slope.at[:, columns_of(other, inner // 2)], s["slope_in"], at.sib)

    @pl.loop(0, chunks)
    def _(index):
        where = chunk_of(index, 256)
        stage[:, where] = nt(slope[...], wu[where, :])

    grad_d.fold()
    grad_d.push(0, 1, 2, 3)

    gb = s["gb"]

    @pl.loop(0, rows // BAND, unroll=2)
    def _(index):
        where = chunk_of(index, BAND)
        grad_hidden = flow[where, :] + stage[where, :]
        hat = hat_one[where, :]
        g = grad_hidden * small[3:4, :]
        grad = r_one[where, :] * (g - mean(g) - hat * mean(g * hat))
        flow[where, :] = grad
        low = grad.astype(BF16)
        gb[where, :] = low
        sums[3] += gather_rows(grad_hidden * hat)
        sums[4] += gather_rows(grad_hidden)
        sums[2] += gather_rows(low.astype(F32))

    wire.send("gb", gb.at[:, columns_of(other, half)], s["gb_in"], at.sib)

    @pl.loop(0, chunks)
    def _(index):
        where = chunk_of(index, 256)
        proj[:, where] = nt(gb[...], s["wo"][where, :]).astype(BF16)

    do, do_out = s["do"], s["do_out"]
    for index in range(chunks):
        moved = nn(proj[:, 0:width], order[:, index * 256 : (index + 1) * 256]).astype(BF16)
        for e in range(2):
            pair = 2 * index + e
            block = moved[:, e * 128 : (e + 1) * 128]
            if pair < some:
                do[pair] = block
            else:
                do_out[pair - some] = block
    wire.send("do", do_out, do.at[pl.ds(some, some)], at.partner)

    def prepare(pair):
        do_t = do[pair].astype(F32).T
        scaled = jnp.concatenate(
            [do_t[e * size : (e + 1) * size] * inverse[2 * pair + e] for e in range(2)], axis=0
        )
        product = scaled * out_t[pair]
        for e in range(2):
            delta[2 * pair + e] = jnp.sum(product[e * size : (e + 1) * size], axis=0, keepdims=True)
        dos[pair] = scaled.T.astype(BF16)

    group_d = [pl.ds(0, some), pl.ds(some, some)]
    group_h = [pl.ds(0, 2 * some), pl.ds(2 * some, 2 * some)]

    def send_group(g):
        wire.send(
            "far do" + str(g), dos.at[group_d[g]], far_dos.at[core, group_d[g]], at.cross
        )
        wire.send(
            "far de" + str(g), delta.at[group_h[g]], far_delta.at[core, group_h[g]], at.cross
        )

    def pass_group(g):
        for kind, ref, group in (("do", far_dos, group_d), ("de", far_delta, group_h)):
            block = ref.at[core, group[g]]
            wire.arrived("far " + kind + str(g), block)
            wire.send("passed " + kind + str(g), block, block, at.sib)

    def have_group(g):
        wire.arrived("passed do" + str(g), far_dos.at[other, group_d[g]])
        wire.arrived("passed de" + str(g), far_delta.at[other, group_h[g]])

    @pl.loop(0, some)
    def _(index):
        prepare(index)

    send_group(0)

    part_d.gone()
    wire.arrived("hid", hid.at[other])
    wire.arrived("slope", s["slope_in"])
    mine_t, theirs_t = hid[core].T, hid[other].T
    for index in range(inner // 2 // half):
        where = pl.ds(aligned(core * (inner // 2) + index * half, 128), half)
        made = nn(mine_t, slope[:, where]) + nn(
            theirs_t, s["slope_in"][:, index * half : (index + 1) * half]
        )
        made = made.astype(BF16)
        for owner in range(4):
            first = owner * 2 * share + (index // 2) * share
            wd[first : first + share, (index % 2) * half : (index % 2 + 1) * half] = made[
                owner * share : (owner + 1) * share
            ]
    grad_u.begin()
    wire.arrived("ctxn", ctx_nat.at[other])
    wire.arrived("gb", s["gb_in"])
    made = nn(ctx_nat[core].T, gb[:, columns_of(core, half)]) + nn(
        ctx_nat[other].T, s["gb_in"][...]
    )
    made = made.astype(BF16)
    for owner in range(4):
        dwo(owner)[...] = made[owner * share : (owner + 1) * share]
    grad_o.begin()

    part_u.gone()
    dq, dq_out, dkv_in = s["dq"], s["dq_out"], s["dkv_in"]
    near_d = wire.slot("near dkv", pairs)
    dq_base = wire.slot("dq", some)
    lots = inner // 512

    def tile(pair, which):
        return wu.at[
            pl.ds(aligned((pair // lots) * rows, 16), rows),
            pl.ds(aligned((pair % lots) * 512 + which * 256, 256), 256),
        ]

    def dkv_near(pair):
        return wire.copy(near_d + pair, tile(pair, other), dkv_in.at[pair], at.sib, "near dkv")

    def two_blocks(pair, chip, first):
        return jnp.concatenate(
            [kv[pair, k * 2 + chip, :, first : first + 128] for k in range(2)], axis=0
        )

    def attend_back(pair):
        queries = q[pair] * jnp.asarray(size**-0.5, BF16)
        dq_parts = [None, None]
        dv = dk = None
        for chip in (at.near, at.far):
            key_rows, value_rows = two_blocks(pair, chip, 0), two_blocks(pair, chip, 128)
            keys_t = key_rows.T
            for e in range(2):
                low = jnp.concatenate(
                    [
                        exps[2 * pair + e, pl.ds(aligned((k * 2 + chip) * rows, 16), rows), :]
                        for k in range(2)
                    ],
                    axis=0,
                )
                mine = masked(dos[pair], e)
                grad_w = nt(value_rows, mine)
                grad_s = (low.astype(F32) * (grad_w - delta[2 * pair + e])).astype(BF16)
                more_q = nn(keys_t[e * size : (e + 1) * size], grad_s)
                dq_parts[e] = more_q if dq_parts[e] is None else dq_parts[e] + more_q
                if chip is at.near:
                    more_v = nn(low, mine)
                    more_k = nn(grad_s, masked(queries, e))
                    dv = more_v if dv is None else dv + more_v
                    dk = more_k if dk is None else dk + more_k
            if chip is at.near:
                made = jnp.concatenate([dk, dv], axis=1).astype(BF16)
                for k in range(2):
                    tile(pair, k)[...] = made[k * rows : (k + 1) * rows]
                dkv_near(pair).start()
        return (jnp.concatenate(dq_parts, axis=0).T * size**-0.5).astype(BF16)

    gkv = s["gkv"]

    def far_back(pair):
        queries = far_q[:, pair].reshape(2 * rows, 128) * jnp.asarray(size**-0.5, BF16)
        grads = far_dos[:, pair].reshape(2 * rows, 128)
        key_rows, value_rows = kv[pair, own_slot, :, 0:128], kv[pair, own_slot, :, 128:256]
        dv = dk = None
        for e in range(2):
            head = 2 * pair + e
            top = jnp.concatenate([far_tops[k, head] for k in range(2)], axis=1)
            less = jnp.concatenate([far_delta[k, head] for k in range(2)], axis=1)
            mine, asking = masked(grads, e), masked(queries, e)
            low = jnp.exp(nt(key_rows, asking) - top).astype(BF16)
            grad_s = (low.astype(F32) * (nt(value_rows, mine) - less)).astype(BF16)
            more_v, more_k = nn(low, mine), nn(grad_s, asking)
            dv = more_v if dv is None else dv + more_v
            dk = more_k if dk is None else dk + more_k
        dkv_near(pair).wait_recv()
        own = tile(pair, core)
        where = pl.ds(aligned(pair * 128, 128), 128)
        for kind, made in ((0, dk), (1, dv)):
            cut = slice(kind * 128, (kind + 1) * 128)
            gkv[kind, :, where] = (
                made + own[:, cut].astype(F32) + dkv_in[pair, :, cut].astype(F32)
            ).astype(BF16)

    def dq_copy(index):
        return wire.copy(dq_base + index, dq_out.at[index], dq.at[some + index], at.partner, "dq")

    grad_d.own(0)

    @pl.loop(0, some)
    def _(index):
        dq[index] = attend_back(index)

    wire.arrived("do", do.at[pl.ds(some, some)])

    @pl.loop(some, pairs)
    def _(index):
        prepare(index)

    send_group(1)
    pass_group(0)

    @pl.loop(0, some)
    def _(index):
        dq_out[index] = attend_back(index + some)
        dq_copy(index).start()

    for chunk in range(1, 4):
        grad_d.own(chunk)
    pass_group(1)
    wire.arrived("passed q", far_q.at[other])
    wire.arrived("passed tops", far_tops.at[other])
    have_group(0)

    @pl.loop(0, some)
    def _(index):
        far_back(index)

    grad_d.chain(0)
    grad_u.fold()
    grad_u.push(0, 1, 2)
    wire.left(*[name for name in wire.started if name[:2] not in ("gd", "gu", "go")])
    part_kv.gone()
    part_q.gone()
    part_o.gone()
    for base in (far_base, near_base, pass_base):
        wire.gone("kv" + str(base), kv.at[:, 0])
    wire.gone("ctx", ctx_out)
    have_group(1)

    @pl.loop(some, pairs)
    def _(index):
        far_back(index)

    for index in range(some):
        dq_copy(index).wait_recv()
    merged = jnp.concatenate([dq[pair] for pair in range(pairs)], axis=1)
    for index in range(chunks):
        where = slice(index * 256, (index + 1) * 256)
        rows_of = order[where, :]
        for kind in range(3):
            source = merged if kind == 0 else gkv[kind - 1]
            low = nt(source, rows_of).astype(BF16)
            proj[:, kind * width + index * 256 : kind * width + (index + 1) * 256] = low
            if kind != 1:
                sums[kind // 2, :, where] = jnp.sum(
                    low.astype(F32).reshape(rows // 8, 8, 256), axis=0
                )
    wire.send("gj", proj.at[:, columns_of(other, 3 * half)], s["gj_in"], at.sib)
    grad_u.own(0)

    vec, vec_in = s["vec"], s["vec_in"]
    for row in range(8):
        vec[row : row + 1, :] = jnp.sum(sums[row], axis=0, keepdims=True)
    for index in range(inner // width):
        vec[8 + index : 9 + index, :] = jnp.sum(
            sums_up[:, index * width : (index + 1) * width], axis=0, keepdims=True
        )
    for row in range(8 + inner // width, 16):
        vec[row : row + 1, :] = jnp.zeros((1, width), F32)
    wire.send("va", vec, vec_in.at[0], at.sib)

    wire.arrived("tok", tok.at[other])
    wire.arrived("gj", s["gj_in"])
    mine_t, theirs_t = tok[core].T, tok[other].T
    for index in range(3):
        where = pl.ds(aligned(core * (3 * half) + index * half, 128), half)
        made = nn(mine_t, proj[:, where]) + nn(
            theirs_t, s["gj_in"][:, index * half : (index + 1) * half]
        )
        made = made.astype(BF16)
        for owner in range(4):
            dwq(owner)[index * share : (index + 1) * share, :] = made[
                owner * share : (owner + 1) * share
            ]
    grad_q.begin()
    grad_u.push(3)
    grad_o.fold()
    grad_o.push(0)
    grad_d.chain(1)

    wire.arrived("va", vec_in.at[0])
    vec_in[0] = vec_in[0] + vec[...]
    for index, where in enumerate((at.to_x, at.to_y, at.to_d)):
        wire.send("vb" + str(index), vec_in.at[0], vec_in.at[1 + index], where)
    keep_out.wait()

    @pl.loop(0, chunks)
    def _(index):
        where = chunk_of(index, 256)
        result[:, where] = nt(proj[...], s["wqkv"][where, :]) + flow[:, where]

    keep_grad = pltpu.make_async_copy(result, grad_tokens, s["own_sems"].at[7])
    keep_grad.start()
    grad_u.own(1)
    grad_d.chain(2)
    grad_d.total(0)
    grad_d.chain(3)
    grad_u.own(2)
    grad_q.fold()
    grad_q.push(0, 1, 2, 3, 4, 5)
    grad_d.total(1)
    grad_u.chain(0)
    grad_d.total(2)
    grad_u.chain(1)
    grad_d.total(3)
    grad_u.own(3)
    grad_o.own(0)
    grad_u.chain(2)
    grad_u.total(0)
    grad_u.total(1)
    grad_q.own(0)
    grad_u.chain(3)
    grad_q.own(1)
    grad_o.chain(0)
    grad_u.total(2)
    grad_q.chain(0)
    grad_q.own(2)
    grad_u.total(3)
    grad_q.chain(1)
    grad_q.own(3)
    grad_o.total(0)
    grad_q.total(0)
    grad_q.chain(2)
    grad_q.own(4)
    grad_q.total(1)
    grad_q.chain(3)
    grad_q.own(5)
    for index in range(3):
        wire.arrived("vb" + str(index), vec_in.at[1 + index])
    wire.left("va")
    vec[...] = (vec_in[0] + vec_in[1]) + (vec_in[2] + vec_in[3])
    wire.left("vb0", "vb1", "vb2")
    for index, where in enumerate(at.lines):
        wire.send("vc" + str(index), vec, vec_in.at[4 + index], where)
    grad_q.total(2)
    grad_q.chain(4)
    grad_q.total(3)
    grad_q.chain(5)
    for index in range(3):
        wire.arrived("vc" + str(index), vec_in.at[4 + index])
    vec_in[0] = (vec[...] + vec_in[4]) + (vec_in[5] + vec_in[6])
    keep_small = pltpu.make_async_copy(vec_in.at[0], g_small, s["own_sems"].at[6])
    keep_small.start()
    grad_q.total(4)
    grad_q.total(5)
    for chunk in range(4):
        grad_d.give(chunk)
    for chunk in range(4):
        grad_u.give(chunk)
    grad_o.give(0)
    for chunk in range(6):
        grad_q.give(chunk)
    grad_d.close()
    grad_u.close()
    grad_o.close()
    grad_q.close()
    keep_grad.wait()
    keep_small.wait()
    wire.gone("near dkv", dkv_in)
    wire.gone("dq", dq_out)
    wire.close()


def whole_layer(tokens, cotangent, pairing, small_raw, w_qkv, w_out, w_up, w_down):
    rows, width = tokens.shape
    inner = w_up.shape[1]
    scratch = layer_scratch(rows, width, inner, pairing.shape[0])
    hbm = pl.BlockSpec(memory_space=pl.ANY)
    vmem = pl.BlockSpec(memory_space=pltpu.VMEM)
    smem = pl.BlockSpec(memory_space=pltpu.SMEM)
    return pl.pallas_call(
        functools.partial(layer_kernel, tuple(scratch)),
        out_shape=[
            jax.ShapeDtypeStruct((rows, width), F32),
            jax.ShapeDtypeStruct((rows, width), F32),
            jax.ShapeDtypeStruct(w_qkv.shape, BF16),
            jax.ShapeDtypeStruct(w_out.shape, BF16),
            jax.ShapeDtypeStruct(w_up.shape, BF16),
            jax.ShapeDtypeStruct(w_down.shape, BF16),
            jax.ShapeDtypeStruct((16, width), F32),
        ],
        in_specs=[hbm, hbm, smem, vmem, hbm, hbm, hbm, hbm],
        out_specs=[hbm] * 7,
        scratch_shapes=list(scratch.values()),
        compiler_params=pltpu.CompilerParams(
            collective_id=0, has_side_effects=True, vmem_limit_bytes=60 << 20
        ),
        name="whole_layer",
    )(tokens, cotangent, pairing, small_raw, w_qkv, w_out, w_up, w_down)


def finish_kernel(share, *refs):
    wide, small, outs = refs[:6], refs[6], refs[7:]
    for source, target in zip(wide, outs[:6]):
        target[...] = source[...].astype(F32)

    @pl.when(pl.program_id(0) == 0)
    def _():
        w = lax.axis_index("wt")
        values = small[...]
        mine = jnp.zeros((8, share), F32)
        line = jnp.zeros((1, 4 * share), F32)
        for owner in range(4):
            mine = mine + jnp.where(
                w == owner, values[:8, owner * share : (owner + 1) * share], 0.0
            )
            line = line + jnp.where(w == owner, values[8 + owner : 9 + owner], 0.0)
        for row in range(8):
            outs[6 + row][...] = mine[row : row + 1]
        outs[14][...] = line.reshape(4 * share)


def finish(*arrays):
    steps = 2
    wide, small = arrays[:6], arrays[6]
    share = small.shape[1] // 4

    def blocks(array):
        return pl.BlockSpec((array.shape[0] // steps, array.shape[1]), lambda i: (i, 0))

    def fixed(shape):
        return pl.BlockSpec(shape, lambda i: (0,) * len(shape))

    shapes = [(1, share)] * 8 + [(4 * share,)]
    return pl.pallas_call(
        functools.partial(finish_kernel, share),
        grid=(steps,),
        out_shape=[jax.ShapeDtypeStruct(v.shape, F32) for v in wide]
        + [jax.ShapeDtypeStruct(v, F32) for v in shapes],
        in_specs=[blocks(v) for v in wide] + [fixed(small.shape)],
        out_specs=[blocks(v) for v in wide] + [fixed(v) for v in shapes],
        compiler_params=pltpu.CompilerParams(vmem_limit_bytes=60 << 20),
        name="finish",
    )(*arrays)


far_below = -1e30


def passed_along(value, axis, steps):
    count = lax.axis_size(axis)
    pairs = [(source, (source + steps) % count) for source in range(count)]
    return lax.ppermute(value, axis, pairs)


def norm_rows(values, gains, shifts):
    average = jnp.mean(values, axis=-1, keepdims=True)
    centred = values - average
    spread = jnp.mean(centred * centred, axis=-1, keepdims=True)
    return centred * lax.rsqrt(spread + 1e-12) * gains + shifts


def gelu_exact(pre_active):
    return jax.nn.gelu(pre_active, approximate=False)


def scores_of(queries, key_heads):
    return (
        jnp.einsum("thd,khd->htk", queries, key_heads, preferred_element_type=jnp.float32) * 0.125
    )


def unchanged(running):
    return running


def general_layer(
    tokens,
    pairing,
    w_qkv,
    bias_q,
    bias_v,
    w_out,
    bias_out,
    gain_one,
    shift_one,
    w_up,
    bias_up,
    w_down,
    bias_down,
    gain_two,
    shift_two,
    cotangent,
):
    local_params = (
        w_qkv,
        bias_q,
        bias_v,
        w_out,
        bias_out,
        gain_one,
        shift_one,
        w_up,
        bias_up,
        w_down,
        bias_down,
        gain_two,
        shift_two,
    )
    gathered = tuple(lax.all_gather(v, "wt", axis=0, tiled=True) for v in local_params)
    (
        wqkv_full,
        biasq_full,
        biasv_full,
        wout_full,
        biasout_full,
        gainone_full,
        shiftone_full,
        wup_full,
        biasup_full,
        wdown_full,
        biasdown_full,
        gaintwo_full,
        shifttwo_full,
    ) = gathered
    tok_rows = tokens.shape[1]
    model_width = tokens.shape[2]
    head_count = pairing.shape[0]
    head_size = model_width // head_count
    group_size = lax.axis_size("ctx")
    position_ctx = lax.axis_index("ctx")
    half_len = tok_rows * group_size // 2
    own_half = position_ctx * tok_rows // half_len
    flipped = pairing == 1
    inputs = tokens[0]
    bias_cat = jnp.concatenate(
        [
            biasq_full.astype(jnp.float32),
            jnp.zeros((model_width,), jnp.float32),
            biasv_full.astype(jnp.float32),
        ]
    )
    projected = jnp.dot(inputs, wqkv_full, preferred_element_type=jnp.float32) + bias_cat
    projected_low = projected.astype(jnp.bfloat16)
    queries = projected_low[:, :model_width].reshape(tok_rows, head_count, head_size)
    key_rows = projected_low[:, model_width : 2 * model_width]
    value_rows = projected_low[:, 2 * model_width :]

    def online_update(state, portion_keys, portion_values, needed):
        row_top, row_total, accumulated = state
        key_count = portion_keys.shape[0]
        key_heads = portion_keys.reshape(key_count, head_count, head_size)
        value_heads = portion_values.reshape(key_count, head_count, head_size)
        scores = scores_of(queries, key_heads)
        scores = jnp.where(needed[:, None, :], scores, far_below)
        new_top = jnp.maximum(row_top, jnp.max(scores, axis=-1))
        factor = jnp.exp(row_top - new_top)
        weights = jnp.exp(scores - new_top[..., None])
        row_total = jnp.sum(weights, axis=-1)
        added = jnp.einsum(
            "htk,khd->thd",
            weights.astype(jnp.bfloat16),
            value_heads,
            preferred_element_type=jnp.float32,
        )
        accumulated = accumulated * factor.T[..., None] + added
        return (new_top, row_total, accumulated)

    start_state = (
        jnp.full((head_count, tok_rows), far_below, jnp.float32),
        jnp.zeros((head_count, tok_rows), jnp.float32),
        jnp.zeros((tok_rows, head_count, head_size), jnp.float32),
    )

    def wanted(offset, key_count):
        key_half = (offset + jnp.arange(key_count)) // half_len
        target = jnp.where(flipped, 1 - own_half, own_half)
        return key_half[None, :] == target[:, None]

    portion_keys = lax.all_gather(key_rows, "ctx", axis=0, tiled=True)
    portion_values = lax.all_gather(value_rows, "ctx", axis=0, tiled=True)
    needed = wanted(jnp.int32(0), portion_keys.shape[0])

    def update(state):
        return online_update(state, portion_keys, portion_values, needed)

    row_top, row_total, accumulated = lax.cond(jnp.any(needed), update, unchanged, start_state)
    context = accumulated / row_total.T[..., None]
    log_sum = row_top + jnp.log(row_total)
    context_low = context.reshape(tok_rows, model_width).astype(jnp.bfloat16)
    branch = jnp.dot(
        context_low, wout_full, preferred_element_type=jnp.float32
    ) + biasout_full.astype(jnp.float32)
    summed_one = inputs.astype(jnp.float32) + branch
    hidden, norm_one_back = jax.vjp(
        norm_rows, summed_one, gainone_full.astype(jnp.float32), shiftone_full.astype(jnp.float32)
    )
    hidden_low = hidden.astype(jnp.bfloat16)
    pre_active = jnp.dot(
        hidden_low, wup_full, preferred_element_type=jnp.float32
    ) + biasup_full.astype(jnp.float32)
    active, gelu_back = jax.vjp(gelu_exact, pre_active)
    active_low = active.astype(jnp.bfloat16)
    ffn_out = jnp.dot(
        active_low, wdown_full, preferred_element_type=jnp.float32
    ) + biasdown_full.astype(jnp.float32)
    output, norm_two_back = jax.vjp(
        norm_rows,
        hidden + ffn_out,
        gaintwo_full.astype(jnp.float32),
        shifttwo_full.astype(jnp.float32),
    )
    again = gathered
    wqkv_back = again[0]
    wout_back = again[3]
    wup_back = again[7]
    wdown_back = again[9]
    grad_two, grad_gain_two, grad_shift_two = norm_two_back(cotangent[0].astype(jnp.float32))
    grad_ffn = grad_two.astype(jnp.bfloat16)
    grad_bias_down = jnp.sum(grad_ffn.astype(jnp.float32), axis=0)
    grad_w_down = jnp.einsum("tf,td->fd", active_low, grad_ffn, preferred_element_type=jnp.float32)
    grad_active = jnp.einsum("td,fd->tf", grad_ffn, wdown_back, preferred_element_type=jnp.float32)
    (grad_pre_f,) = gelu_back(grad_active)
    grad_pre = grad_pre_f.astype(jnp.bfloat16)
    grad_bias_up = jnp.sum(grad_pre.astype(jnp.float32), axis=0)
    grad_w_up = jnp.einsum("tc,tf->cf", hidden_low, grad_pre, preferred_element_type=jnp.float32)
    grad_hidden = grad_two + jnp.einsum(
        "tf,cf->tc", grad_pre, wup_back, preferred_element_type=jnp.float32
    )
    grad_one, grad_gain_one, grad_shift_one = norm_one_back(grad_hidden)
    grad_branch = grad_one.astype(jnp.bfloat16)
    grad_bias_out = jnp.sum(grad_branch.astype(jnp.float32), axis=0)
    grad_w_out = jnp.einsum(
        "tc,td->cd", context_low, grad_branch, preferred_element_type=jnp.float32
    )
    grad_context = jnp.einsum(
        "td,cd->tc", grad_branch, wout_back, preferred_element_type=jnp.float32
    )
    grad_context = grad_context.astype(jnp.bfloat16).reshape(tok_rows, head_count, head_size)
    row_delta = jnp.sum(grad_context.astype(jnp.float32) * context, axis=-1).T

    def piece_grads(portion_keys, portion_values, needed):
        key_count = portion_keys.shape[0]
        key_heads = portion_keys.reshape(key_count, head_count, head_size)
        value_heads = portion_values.reshape(key_count, head_count, head_size)
        scores = scores_of(queries, key_heads)
        scores = jnp.where(needed[:, None, :], scores, far_below)
        probs = jnp.exp(scores - log_sum[..., None])
        probs_low = probs.astype(jnp.bfloat16)
        piece_v = jnp.einsum(
            "htk,thd->khd", probs_low, grad_context, preferred_element_type=jnp.float32
        ).reshape(key_count, model_width)
        grad_weights = jnp.einsum(
            "thd,khd->htk", grad_context, value_heads, preferred_element_type=jnp.float32
        )
        grad_scores = (probs * (grad_weights - row_delta[..., None])).astype(jnp.bfloat16)
        piece_q = 0.125 * jnp.einsum(
            "htk,khd->thd", grad_scores, key_heads, preferred_element_type=jnp.float32
        )
        piece_k = 0.125 * jnp.einsum(
            "htk,thd->khd", grad_scores, queries, preferred_element_type=jnp.float32
        ).reshape(key_count, model_width)
        return (piece_k, piece_v, piece_q)

    zero_queries = jnp.zeros((tok_rows, head_count, head_size), jnp.float32)

    def circle_step(step_index, running):
        turn_keys, turn_values, grad_keys, grad_values, grad_queries = running
        owner = (position_ctx - step_index) % group_size
        needed = wanted(owner * tok_rows, tok_rows)

        def update_grads(state):
            grad_k, grad_v, grad_q = state
            piece_k, piece_v, piece_q = piece_grads(turn_keys, turn_values, needed)
            return (grad_k + piece_k, grad_v + piece_v, grad_q + piece_q)

        grad_keys, grad_values, grad_queries = lax.cond(
            jnp.any(needed), update_grads, unchanged, (grad_keys, grad_values, grad_queries)
        )
        turn_keys, turn_values = passed_along((turn_keys, turn_values), "ctx", 1)
        grad_keys, grad_values = (
            passed_along(grad_keys.astype(jnp.bfloat16), "ctx", 1).astype(grad_keys.dtype),
            passed_along(grad_values.astype(jnp.bfloat16), "ctx", 1).astype(grad_values.dtype),
        )
        return (turn_keys, turn_values, grad_keys, grad_values, grad_queries)

    zero_rows = jnp.zeros((tok_rows, model_width), jnp.float32)
    circle_start = (key_rows, value_rows, zero_rows, zero_rows, zero_queries)
    circle_end = lax.fori_loop(0, group_size, circle_step, circle_start)
    grad_keys = circle_end[2]
    grad_values = circle_end[3]
    grad_queries = circle_end[4]
    grad_projected = jnp.concatenate(
        [grad_queries.reshape(tok_rows, model_width), grad_keys, grad_values], axis=1
    ).astype(jnp.bfloat16)
    grad_bias_q = jnp.sum(grad_projected[:, :model_width].astype(jnp.float32), axis=0)
    grad_bias_v = jnp.sum(grad_projected[:, 2 * model_width :].astype(jnp.float32), axis=0)
    grad_w_qkv = jnp.einsum("tc,tj->cj", inputs, grad_projected, preferred_element_type=jnp.float32)
    grad_inputs = grad_one + jnp.einsum(
        "tj,cj->tc", grad_projected, wqkv_back, preferred_element_type=jnp.float32
    )
    terms = (
        grad_w_qkv,
        grad_bias_q,
        grad_bias_v,
        grad_w_out,
        grad_bias_out,
        grad_gain_one,
        grad_shift_one,
        grad_w_up,
        grad_bias_up,
        grad_w_down,
        grad_bias_down,
        grad_gain_two,
        grad_shift_two,
    )
    owned = tuple(
        lax.psum_scatter(term.astype(jnp.bfloat16), "wt", scatter_dimension=0, tiled=True)
        for term in terms
    )
    totals = tuple(lax.psum(term, "ctx").astype(jnp.float32) for term in owned)
    return (
        output[None],
        grad_inputs[None],
        totals[0],
        totals[1],
        totals[2],
        totals[3],
        totals[4],
        totals[5],
        totals[6],
        totals[7],
        totals[8],
        totals[9],
        totals[10],
        totals[11],
        totals[12],
    )


def fast_layer(
    tokens,
    pairing,
    w_qkv,
    bias_q,
    bias_v,
    w_out,
    bias_out,
    gain_one,
    shift_one,
    w_up,
    bias_up,
    w_down,
    bias_down,
    gain_two,
    shift_two,
    cotangent,
):
    share = tokens.shape[2] // 4
    vectors = (bias_q, bias_v, bias_out, gain_one, shift_one, bias_down, gain_two, shift_two)
    vectors = vectors + tuple(bias_up[k * share : (k + 1) * share] for k in range(4))
    row = lax.broadcasted_iota(jnp.int32, (16, share), 0)
    small_raw = jnp.zeros((16, share), jnp.bfloat16)
    for index, vector in enumerate(vectors):
        small_raw = jnp.where(row == index, vector[None, :], small_raw)
    made = whole_layer(
        tokens[0], cotangent[0], pairing, small_raw, w_qkv, w_out, w_up, w_down
    )
    output, grad_tokens, g_qkv, g_out, g_up, g_down, *small = finish(*made)
    small = [v.reshape(-1) for v in small]
    return (
        output[None],
        grad_tokens[None],
        g_qkv,
        small[0],
        small[1],
        g_out,
        small[2],
        small[3],
        small[4],
        g_up,
        small[8],
        g_down,
        small[5],
        small[6],
        small[7],
    )


def local(tokens, pairing, *rest):
    rows, width = tokens.shape[1:]
    heads = pairing.shape[0]
    inner = rest[7].shape[1]
    fits = (
        lax.axis_size("wt") == 4
        and lax.axis_size("ctx") == 8
        and tokens.shape[0] == 1
        and rows % BAND == 0
        and 3 * rows <= width
        and width % 256 == 0
        and heads % 4 == 0
        and width == 64 * heads
        and inner == 4 * width
    )
    layer = fast_layer if fits else general_layer
    return layer(tokens, pairing, *rest)


def solution(mesh):
    in_specs = (
        P("wt", "ctx", None),
        P(),
        P("wt", None),
        P("wt"),
        P("wt"),
        P("wt", None),
        P("wt"),
        P("wt"),
        P("wt"),
        P("wt", None),
        P("wt"),
        P("wt", None),
        P("wt"),
        P("wt"),
        P("wt"),
        P("wt", "ctx", None),
    )
    out_specs = (
        P("wt", "ctx", None),
        P("wt", "ctx", None),
        P("wt", None),
        P("wt"),
        P("wt"),
        P("wt", None),
        P("wt"),
        P("wt"),
        P("wt"),
        P("wt", None),
        P("wt"),
        P("wt", None),
        P("wt"),
        P("wt"),
        P("wt"),
    )
    return jax.shard_map(local, mesh=mesh, in_specs=in_specs, out_specs=out_specs, check_vma=False)
```

```python
import functools

import jax
import jax.numpy as jnp
from jax import lax
from jax.experimental import pallas as pl
from jax.experimental.pallas import tpu as pltpu
from jax.sharding import PartitionSpec as P

F32, BF16 = jnp.float32, jnp.bfloat16
MESH = pl.DeviceIdType.MESH
BAND = 32


def nn(a, b):
    return jnp.dot(a, b, preferred_element_type=F32)


def nt(a, b):
    return lax.dot_general(a, b, (((1,), (1,)), ((), ())), preferred_element_type=F32)


def aligned(start, multiple):
    return start if isinstance(start, int) else pl.multiple_of(start, multiple)


def chunk_of(index, size):
    return pl.ds(aligned(index * size, size), size)


class Wire:
    def __init__(self, sends, receives, anyone):
        self.sends, self.receives, self.anyone = sends, receives, anyone
        self.firsts, self.used, self.groups, self.started = {}, 0, {}, {}

    def slot(self, name, count=1):
        if name not in self.firsts:
            self.firsts[name] = self.used, count
            self.used += count
            assert self.used <= self.receives.shape[0]
        first, had = self.firsts[name]
        assert had == count
        return first

    def copy(self, slot, source, target, where, group):
        place = self.groups.setdefault(group, len(self.groups))
        assert place < self.sends.shape[0]
        return pltpu.make_async_remote_copy(
            src_ref=source,
            dst_ref=target,
            send_sem=self.sends.at[place],
            recv_sem=self.receives.at[slot],
            device_id=where,
            device_id_type=MESH,
        )

    def send(self, name, source, target, where):
        copy = self.copy(self.slot(name), source, target, where, name)
        copy.start()
        self.started[name] = copy

    def send_in(self, group, name, source, target, where):
        self.copy(self.slot(name), source, target, where, group).start()

    def gone(self, group, ref):
        self.copy(0, ref, ref, self.anyone, group).wait_send()

    def arrived(self, name, target):
        self.copy(self.slot(name), target, target, self.anyone, "none").wait_recv()

    def left(self, *names):
        for name in names:
            self.started.pop(name).wait_send()

    def close(self):
        self.left(*tuple(self.started))


class Place:
    def __init__(self):
        self.w = w = lax.axis_index("wt")
        self.c = c = lax.axis_index("ctx")
        self.core = core = c % 2
        self.other = 1 - core
        self.z = z = c // 2
        self.near = z % 2
        self.far = 1 - self.near
        self.nx = w + 1 - 2 * (w % 2)
        self.ny = (w + 2) % 4
        self.nd = 3 - w
        self.sib = (w, c + 1 - 2 * core)
        self.to_x, self.to_y, self.to_d = (self.nx, c), (self.ny, c), (self.nd, c)
        self.cross = (w, c + 2 - 4 * self.near)
        self.partner = (w, (c + 4) % 8)
        self.lines = [(w, spot * 2 + core) for spot in (z + 1 - 2 * (z % 2), (z + 2) % 4, 3 - z)]
        self.others = [(w, (c + step) % 8) for step in range(1, 8)]
        self.mate, self.middle = self.lines[0], self.lines[2]
        self.outer, self.inner = (z == 0) | (z == 3), (z == 1) | (z == 2)


def greet(peers):
    barrier = pltpu.get_barrier_semaphore()
    for peer in peers:
        pl.semaphore_signal(barrier, inc=1, device_id=peer, device_id_type=MESH)
    pl.semaphore_wait(barrier, len(peers))


class Part:
    def __init__(self, name, local, full, first, columns, place, wire):
        self.name, self.local, self.full, self.place, self.wire = name, local, full, place, wire
        self.rows = local.shape[0]
        self.first, self.columns = first, columns // 2

    def piece(self, owner, core, half=None):
        rows, start = self.rows, owner * self.rows
        if half is not None:
            rows = self.rows // 2
            start = start + half * rows
        return self.full.at[
            pl.ds(aligned(start, 16), rows),
            pl.ds(aligned(self.first + core * self.columns, 128), self.columns),
        ]

    def send(self, kind, source, target, where):
        self.wire.send_in(self.name, self.name + kind, source, target, where)

    def begin(self):
        at = self.place
        mine = self.local.at[
            :, pl.ds(aligned(self.first + at.core * self.columns, 128), self.columns)
        ]
        target = self.piece(at.w, at.core)
        self.send("a", mine, target, at.to_x)
        self.send("b", mine, target, at.to_y)

    def relay(self):
        at, wire = self.place, self.wire
        for kind, owner, half, on, where in (
            ("a", at.nx, 0, "c", at.to_y),
            ("b", at.ny, 1, "e", at.to_x),
        ):
            block = self.piece(owner, at.core)
            wire.arrived(self.name + kind, block)
            part = self.piece(owner, at.core, half)
            self.send(on, part, part, where)
            self.send("s", block, block, at.sib)

    def share(self):
        at, wire = self.place, self.wire
        for half, came in ((0, "c"), (1, "e")):
            block = self.piece(at.nd, at.core, half)
            wire.arrived(self.name + came, block)
            self.send("r", block, block, at.sib)

    def arrived(self, kind, pieces):
        block = self.full.at[pl.ds(0, pieces * self.rows), pl.ds(self.first, self.columns)]
        self.wire.arrived(self.name + kind, block)

    def near(self):
        self.arrived("s", 2)

    def last(self):
        self.arrived("r", 1)

    def finish(self):
        self.near()
        self.last()

    def gone(self):
        block = self.full.at[pl.ds(0, 3 * self.rows), pl.ds(self.first, 2 * self.columns)]
        self.wire.gone(self.name, block)


def add_into(target, *sources):
    rows, columns = sources[0].shape
    band = 16
    while columns * band * 2 <= 1 << 15 and rows % (band * 2) == 0:
        band *= 2

    @pl.loop(0, rows // band)
    def _(index):
        where = chunk_of(index, band)
        total = sources[0][where, :].astype(F32)
        for source in sources[1:]:
            total = total + source[where, :].astype(F32)
        target[where, :] = total.astype(target.dtype)


class Grad:
    def __init__(self, name, chunks, blocks, buffers, finals, place, wire, local_sem):
        self.name, self.chunks, self.blocks, self.finals = name, chunks, blocks, finals
        self.place, self.wire, self.local_sem = place, wire, local_sem
        self.from_x, self.from_y, self.diag_x, self.diag_y, self.low, self.high = buffers
        self.rows, self.columns = self.from_x.shape

    def half(self, ref, index):
        return ref.at[pl.ds(index * (self.rows // 2), self.rows // 2), :]

    def begin(self):
        at, wire = self.place, self.wire
        block = self.blocks(at.nd)
        wire.send(self.name + "a", self.half(block, 0), self.diag_x, at.to_x)
        wire.send(self.name + "b", self.half(block, 1), self.diag_y, at.to_y)

    def fold(self):
        at, wire = self.place, self.wire
        for kind, came, owner, index in (("a", self.diag_x, at.ny, 0), ("b", self.diag_y, at.nx, 1)):
            wire.arrived(self.name + kind, came)
            part = self.half(self.blocks(owner), index)
            add_into(part, part, came)

    def lanes(self, chunk):
        at = self.place
        return (
            self.hop("c", chunk, self.blocks(at.nx), self.from_x, at.to_x),
            self.hop("d", chunk, self.blocks(at.ny), self.from_y, at.to_y),
        )

    def push(self, *chunks):
        for chunk in chunks:
            for copy in self.lanes(chunk):
                copy.start()

    def cut(self, ref, chunk):
        count = self.rows // self.chunks
        return ref.at[pl.ds(chunk * count, count), :]

    def hop(self, kind, chunk, source, target, where):
        slot = self.wire.slot(self.name + kind, self.chunks) + chunk
        return self.wire.copy(
            slot, self.cut(source, chunk), self.cut(target, chunk), where, self.name + kind
        )

    def outward(self, chunk):
        return self.hop("u", chunk, self.blocks(self.place.w), self.low, self.place.mate)

    def across(self, chunk):
        return self.hop("v", chunk, self.from_x, self.high, self.place.middle)

    def back(self, chunk):
        return self.hop("t", chunk, self.from_y, self.high, self.place.mate)

    def own(self, chunk):
        for copy in self.lanes(chunk):
            copy.wait_recv()
        part = self.cut(self.blocks(self.place.w), chunk)
        add_into(part, part, self.cut(self.from_x, chunk), self.cut(self.from_y, chunk))
        self.out(chunk)

    def out(self, chunk):
        @pl.when(self.place.outer)
        def _():
            self.outward(chunk).start()

    def chain(self, chunk):
        at = self.place

        @pl.when(at.inner)
        def _():
            self.outward(chunk).wait_recv()
            block = self.blocks(at.w)
            add_into(
                self.cut(self.from_x, chunk), self.cut(block, chunk), self.cut(self.low, chunk)
            )
            self.across(chunk).start()

    def total(self, chunk):
        at = self.place

        @pl.when(at.inner)
        def _():
            self.across(chunk).wait_recv()
            add_into(
                self.cut(self.from_y, chunk),
                self.cut(self.from_x, chunk),
                self.cut(self.high, chunk),
            )
            self.back(chunk).start()
            for copy in self.copies(chunk, self.from_y):
                copy.start()

    def copies(self, chunk, source):
        at, wire = self.place, self.wire
        piece, target = self.cut(source, chunk), self.finals(chunk, at.core)
        keep = pltpu.make_async_copy(piece, target, self.local_sem)
        slot = wire.slot(self.name + "s")
        return keep, wire.copy(slot, piece, target, at.sib, self.name + "s")

    def give(self, chunk):
        at = self.place

        @pl.when(at.outer)
        def _():
            self.back(chunk).wait_recv()
            for copy in self.copies(chunk, self.high):
                copy.start()

    def close(self):
        at, wire = self.place, self.wire
        whole = self.from_y
        pltpu.make_async_copy(whole, whole, self.local_sem).wait()
        wire.arrived(self.name + "s", whole)
        for kind in ("s", "c", "d"):
            wire.gone(self.name + kind, whole)

        @pl.when(at.outer)
        def _():
            wire.gone(self.name + "u", whole)

        @pl.when(at.inner)
        def _():
            wire.gone(self.name + "v", whole)
            wire.gone(self.name + "t", whole)


def layer_scratch(rows, width, inner, heads):
    pairs = heads // 2
    some = pairs // 2
    share = width // 4
    half = width // 2
    groups = 8

    def low(*shape):
        return pltpu.VMEM(shape, BF16)

    def wide(*shape):
        return pltpu.VMEM(shape, F32)

    scratch = dict(
        wqkv=low(width, 3 * width),
        wo=low(width, width),
        wu=low(width, inner),
        wd=low(inner, width),
        order=low(width, width),
        tok=low(2, rows, width),
        cot=low(rows, width),
        small_own=low(16, width),
        small_in=low(3, 16, width),
        small=wide(16, width),
        bias_qkv=wide(8, 3 * width),
        bias_up=wide(8, inner),
        kv=low(pairs, 4, rows, 256),
        proj=low(rows, 3 * width),
        q=low(pairs, rows, 128),
        q_out=low(some, rows, 128),
        exps=low(heads, 4 * rows, rows),
        inverse=wide(heads, 1, rows),
        out_t=wide(pairs, 128, rows),
        ctx=low(pairs, rows, 128),
        ctx_out=low(some, rows, 128),
        ctx_nat=low(2, rows, width),
        hat_one=wide(rows, width),
        r_one=wide(rows, 1),
        flow=wide(rows, width),
        stage=wide(rows, width),
        result=wide(rows, width),
        hid=low(2, rows, width),
        act=low(2, rows, inner),
        slope=low(rows, inner),
        slope_in=low(rows, inner // 2),
        gf=low(rows, width),
        gf_in=low(rows, half),
        gb=low(rows, width),
        gb_in=low(rows, half),
        do=low(pairs, rows, 128),
        do_out=low(some, rows, 128),
        dq=low(pairs, rows, 128),
        dq_out=low(some, rows, 128),
        dkv_in=low(pairs, rows, 256),
        tops=wide(heads, 1, rows),
        delta=wide(heads, 1, rows),
        dos=low(pairs, rows, 128),
        far_q=low(2, pairs, rows, 128),
        far_tops=wide(2, heads, 1, rows),
        far_delta=wide(2, heads, 1, rows),
        far_dos=low(2, pairs, rows, 128),
        gkv=low(2, rows, width),
        gj_in=low(rows, 3 * half),
        sums=wide(16, groups, width),
        sums_up=wide(groups, inner),
        vec=wide(16, width),
        vec_in=wide(16, width),
        vec_low=low(4, 16, width),
        vec_far=low(6, 16, width),
        dwd=low(4, inner // 4, half),
    )
    shapes = dict(
        d=(inner // 4, half), u=(2 * share, width), o=(share, half), q=(3 * share, half)
    )
    for name, (r, c) in shapes.items():
        for kind in ("fx", "fy", "lo", "hi"):
            scratch["g" + name + kind] = low(r, c)
        for kind in ("dx", "dy"):
            scratch["g" + name + kind] = low(r // 2, c)
    scratch["sends"] = pltpu.SemaphoreType.DMA((80,))
    scratch["receives"] = pltpu.SemaphoreType.DMA((180,))
    scratch["own_sems"] = pltpu.SemaphoreType.DMA((12,))
    return scratch


def layer_kernel(names, *refs):
    (
        tokens,
        cot_l,
        pairing,
        small_raw,
        qkv_l,
        out_l,
        up_l,
        down_l,
        output,
        grad_tokens,
        g_qkv,
        g_out,
        g_up,
        g_down,
        g_small,
    ) = refs[:15]
    s = dict(zip(names, refs[15:]))
    at = Place()
    wire = Wire(s["sends"], s["receives"], at.sib)
    rows, width = tokens.shape
    inner = up_l.shape[1]
    heads = pairing.shape[0]
    pairs, some = heads // 2, heads // 4
    size = width // heads
    half = width // 2
    keys = 4 * rows
    chunks = width // 256
    share = width // 4
    core, other = at.core, at.other

    greet([at.to_x, at.to_y, at.to_d] + at.others)

    part_kv = Part("kv", qkv_l, s["wqkv"], width, 2 * width, at, wire)
    part_q = Part("q", qkv_l, s["wqkv"], 0, width, at, wire)
    part_o = Part("o", out_l, s["wo"], 0, width, at, wire)
    part_u = Part("u", up_l, s["wu"], 0, inner, at, wire)
    part_d = Part("d", down_l, s["wd"], 0, width, at, wire)
    part_kv.begin()
    part_q.begin()
    raw = small_raw[...]
    row = lax.broadcasted_iota(jnp.int32, (share, width), 0)
    column = lax.broadcasted_iota(jnp.int32, (share, width), 1)

    def spread(values, spot):
        place = jnp.where(column - row == spot * share, 1.0, 0.0).astype(BF16)
        return nn(values, place)

    own_row = lax.broadcasted_iota(jnp.int32, (8, width), 0) == at.w
    line = spread(raw[8:16], 0)[0:1]
    for index in range(1, 4):
        line = line + spread(raw[8:16], index)[index : index + 1]
    small_own = s["small_own"]
    small_own[...] = jnp.concatenate(
        [spread(raw[:8], at.w), jnp.where(own_row, line, 0.0)], axis=0
    ).astype(BF16)
    for index, where in enumerate((at.to_x, at.to_y, at.to_d)):
        wire.send("sm" + str(index), small_own, s["small_in"].at[index], where)
    keeps = []
    for slot, (local, full) in enumerate(
        (
            (qkv_l, s["wqkv"].at[pl.ds(aligned(at.w * share, 16), share)]),
            (tokens, s["tok"].at[core]),
            (cot_l, s["cot"]),
            (out_l, s["wo"].at[pl.ds(aligned(at.w * share, 16), share)]),
            (up_l, s["wu"].at[pl.ds(aligned(at.w * share, 16), share)]),
            (down_l, s["wd"].at[pl.ds(aligned(at.w * (inner // 4), 16), inner // 4)]),
        )
    ):
        keeps.append(pltpu.make_async_copy(local, full, s["own_sems"].at[slot]))
        keeps[-1].start()
    wire.send("tok", tokens, s["tok"].at[core], at.sib)

    before = 0
    for head in range(heads):
        flag = pairing[head]
        spot = flag * (heads // 2 + before) + (1 - flag) * (head - before)
        before = before + flag
        row = lax.broadcasted_iota(jnp.int32, (size, width), 0)
        column = lax.broadcasted_iota(jnp.int32, (size, width), 1)
        s["order"][head * size : (head + 1) * size, :] = jnp.where(
            column - row == spot * size, 1.0, 0.0
        ).astype(BF16)

    part_kv.relay()
    part_q.relay()
    part_o.begin()
    part_u.begin()
    part_kv.share()
    for index in range(3):
        wire.arrived("sm" + str(index), s["small_in"].at[index])
    small = s["small"]
    small[...] = (
        small_own[...].astype(F32)
        + s["small_in"][0].astype(F32)
        + s["small_in"][1].astype(F32)
        + s["small_in"][2].astype(F32)
    )
    s["bias_qkv"][0:1, 0:width] = small[0:1, :]
    s["bias_qkv"][0:1, width : 2 * width] = jnp.zeros((1, width), F32)
    s["bias_qkv"][0:1, 2 * width :] = small[1:2, :]
    for index in range(inner // width):
        s["bias_up"][0:1, index * width : (index + 1) * width] = small[8 + index : 9 + index, :]
    keeps[0].wait()
    keeps[1].wait()
    part_kv.finish()

    tok, proj, order, kv = s["tok"], s["proj"], s["order"], s["kv"]
    own_slot = core * 2 + at.near

    def project(first, count):
        @pl.loop(first, first + count)
        def _(index):
            where = chunk_of(index, 256)
            made = nn(tok[core], s["wqkv"][:, where]) + s["bias_qkv"][0:1, where]
            proj[:, where] = made.astype(BF16)

    project(chunks, 2 * chunks)
    for index in range(chunks):
        columns = order[:, index * 256 : (index + 1) * 256]
        for kind in range(2):
            moved = nn(proj[:, (1 + kind) * width : (2 + kind) * width], columns).astype(BF16)
            for e in range(2):
                kv[2 * index + e, own_slot, :, kind * 128 : (kind + 1) * 128] = moved[
                    :, e * 128 : (e + 1) * 128
                ]
    near_base = wire.slot("near kv", pairs)
    far_base = wire.slot("far kv", pairs)
    pass_base = wire.slot("passed kv", pairs)

    def kv_copy(base, pair, slot, where):
        block = kv.at[pair, slot]
        return wire.copy(base + pair, block, block, where, "kv" + str(base))

    for pair in range(pairs):
        if pair < some:
            kv_copy(far_base, pair, own_slot, at.cross).start()
        kv_copy(near_base, pair, own_slot, at.sib).start()
    part_q.share()
    part_q.finish()
    project(0, chunks)
    q, q_out = s["q"], s["q_out"]
    for index in range(chunks):
        moved = nn(proj[:, 0:width], order[:, index * 256 : (index + 1) * 256]).astype(BF16)
        for e in range(2):
            pair = 2 * index + e
            block = moved[:, e * 128 : (e + 1) * 128]
            if pair < some:
                q[pair] = block
            else:
                q_out[pair - some] = block
    wire.send("queries", q_out, q.at[pl.ds(some, some)], at.partner)
    part_o.relay()
    part_d.begin()

    exps, inverse, out_t = s["exps"], s["inverse"], s["out_t"]

    def both(pair, first):
        return kv[pair, :, :, first : first + 128].reshape(keys, 128)

    def masked(block, e, axis=1):
        spot = lax.broadcasted_iota(jnp.int32, block.shape, axis)
        mine = spot < size if e == 0 else spot >= size
        return jnp.where(mine, block, jnp.zeros_like(block))

    def attend(pair):
        key_rows, value_rows = both(pair, 0), both(pair, 128)
        values_t = value_rows.T
        queries = q[pair] * jnp.asarray(size**-0.5, BF16)
        parts = []
        for e in range(2):
            scores = nt(key_rows, masked(queries, e))
            top = jnp.max(scores, axis=0, keepdims=True)
            raised = jnp.exp(scores - top)
            total = jnp.sum(raised, axis=0, keepdims=True)
            low = raised.astype(BF16)
            exps[2 * pair + e] = low
            s["tops"][2 * pair + e] = top
            one_over = 1.0 / total
            inverse[2 * pair + e] = one_over
            parts.append(nn(values_t[e * size : (e + 1) * size], low) * one_over)
        merged = jnp.concatenate(parts, axis=0)
        out_t[pair] = merged
        return merged.T.astype(BF16)

    def receive_kv(pair):
        kv_copy(far_base, pair, core * 2 + at.far, at.cross).wait_recv()
        kv_copy(pass_base, pair, core * 2 + at.far, at.sib).start()
        kv_copy(near_base, pair, other * 2 + at.near, at.sib).wait_recv()
        kv_copy(pass_base, pair, other * 2 + at.far, at.sib).wait_recv()

    ctx, ctx_out = s["ctx"], s["ctx_out"]
    back_base = wire.slot("ctx", some)

    def ctx_copy(index):
        return wire.copy(back_base + index, ctx_out.at[index], ctx.at[some + index], at.partner, "ctx")

    def attend_far(index):
        receive_kv(index + some)
        ctx_out[index] = attend(index + some)
        ctx_copy(index).start()

    @pl.loop(0, some)
    def _(index):
        receive_kv(index)
        kv_copy(far_base, index + some, own_slot, at.cross).start()
        ctx[index] = attend(index)

    part_o.share()
    wire.arrived("queries", q.at[pl.ds(some, some)])
    attend_far(0)
    part_u.relay()

    @pl.loop(1, some)
    def _(index):
        attend_far(index)

    part_o.finish()
    far_q, far_tops, far_delta, far_dos = (
        s[name] for name in ("far_q", "far_tops", "far_delta", "far_dos")
    )
    tops, delta, dos = s["tops"], s["delta"], s["dos"]
    wire.send("far q", q, far_q.at[core], at.cross)
    wire.send("far tops", tops, far_tops.at[core], at.cross)
    part_d.relay()
    keeps[2].wait()
    keeps[3].wait()
    for index in range(some):
        ctx_copy(index).wait_recv()
    permuted = jnp.concatenate([ctx[pair] for pair in range(pairs)], axis=1)
    ctx_nat, stage = s["ctx_nat"], s["stage"]
    for index in range(chunks):
        where = slice(index * 256, (index + 1) * 256)
        ctx_nat[core, :, where] = nt(permuted, order[where, :]).astype(BF16)
    wire.send("ctxn", ctx_nat.at[core], ctx_nat.at[core], at.sib)

    @pl.loop(0, chunks)
    def _(index):
        where = chunk_of(index, 256)
        stage[:, where] = nn(ctx_nat[core], s["wo"][:, where])

    hat_one, r_one, flow, hid = s["hat_one"], s["r_one"], s["flow"], s["hid"]
    inv_width = 1.0 / width

    def mean(values):
        return jnp.sum(values, axis=-1, keepdims=True) * inv_width

    @pl.loop(0, rows // BAND, unroll=2)
    def _(index):
        where = chunk_of(index, BAND)
        total = tok[core, where, :].astype(F32) + stage[where, :] + small[2:3, :]
        centred = total - mean(total)
        scale = lax.rsqrt(mean(centred * centred) + 1e-12)
        hat = centred * scale
        hat_one[where, :] = hat
        r_one[where, :] = scale
        hidden = hat * small[3:4, :] + small[4:5, :]
        flow[where, :] = hidden
        hid[core, where, :] = hidden.astype(BF16)

    wire.send("hid", hid.at[core], hid.at[core], at.sib)
    part_u.share()
    part_u.finish()
    keeps[4].wait()
    act, slope = s["act"], s["slope"]

    @pl.loop(0, inner // 256, unroll=3)
    def _(index):
        where = chunk_of(index, 256)
        pre = nn(hid[core], s["wu"][:, where]) + s["bias_up"][0:1, where]
        below = 0.5 * (1.0 + lax.erf(pre * (0.5**0.5)))
        act[core, :, where] = (pre * below).astype(BF16)
        density = jnp.exp(pre * pre * -0.5) * 0.3989422804014327
        slope[:, where] = (below + pre * density).astype(BF16)

    wire.send("act", act.at[core], act.at[core], at.sib)
    wire.arrived("far q", far_q.at[core])
    wire.send("passed q", far_q.at[core], far_q.at[core], at.sib)
    wire.arrived("far tops", far_tops.at[core])
    wire.send("passed tops", far_tops.at[core], far_tops.at[core], at.sib)
    part_d.near()
    keeps[5].wait()
    quarter = inner // 4

    def down(owner, where):
        block = pl.ds(aligned(owner * quarter, 128), quarter)
        return nn(act[core, :, block], s["wd"][block, where])

    @pl.loop(0, chunks)
    def _(index):
        where = chunk_of(index, 256)
        stage[:, where] = down(at.w, where) + down(at.nx, where) + down(at.ny, where)

    part_d.share()
    part_d.last()

    @pl.loop(0, chunks)
    def _(index):
        where = chunk_of(index, 256)
        stage[:, where] += down(at.nd, where)

    result, gf, cot = s["result"], s["gf"], s["cot"]
    sums, sums_up = s["sums"], s["sums_up"]
    sums[...] = jnp.zeros_like(sums)

    def gather_rows(values):
        return jnp.sum(values.reshape(BAND // 8, 8, values.shape[-1]), axis=0)

    @pl.loop(0, rows // BAND, unroll=2)
    def _(index):
        where = chunk_of(index, BAND)
        total = flow[where, :] + stage[where, :] + small[5:6, :]
        centred = total - mean(total)
        scale = lax.rsqrt(mean(centred * centred) + 1e-12)
        hat = centred * scale
        result[where, :] = hat * small[6:7, :] + small[7:8, :]
        back = cot[where, :].astype(F32)
        g = back * small[6:7, :]
        grad = scale * (g - mean(g) - hat * mean(g * hat))
        flow[where, :] = grad
        low = grad.astype(BF16)
        gf[where, :] = low
        sums[6] += gather_rows(back * hat)
        sums[7] += gather_rows(back)
        sums[5] += gather_rows(low.astype(F32))

    keep_out = pltpu.make_async_copy(result, output, s["own_sems"].at[7])
    keep_out.start()

    def columns_of(which, count):
        return pl.ds(aligned(which * count, 128), count)

    wire.send("gf", gf.at[:, columns_of(other, half)], s["gf_in"], at.sib)

    def buffers(name):
        return [s["g" + name + kind] for kind in ("fx", "fy", "dx", "dy", "lo", "hi")]

    dwd, wd, wu = s["dwd"], s["wd"], s["wu"]

    def side_by_side(first, count, owner):
        return wd.at[
            pl.ds(aligned(first + (owner // 2) * count, 16), count),
            pl.ds(aligned((owner % 2) * half, 128), half),
        ]

    def dwo(owner):
        return side_by_side(2 * width + 6 * share, share, owner)

    def dwq(owner):
        return side_by_side(2 * width, 3 * share, owner)

    grad_d = Grad(
        "gd",
        4,
        lambda r: dwd.at[r],
        buffers("d"),
        lambda i, k: g_down.at[pl.ds(i * (inner // 16), inner // 16), columns_of(k, half)],
        at,
        wire,
        s["own_sems"].at[8],
    )
    grad_u = Grad(
        "gu",
        4,
        lambda r: wd.at[pl.ds(aligned(r * (2 * share), 16), 2 * share), :],
        buffers("u"),
        lambda i, k: g_up.at[
            pl.ds((i % 2) * (share // 2), share // 2), columns_of(2 * k + i // 2, width)
        ],
        at,
        wire,
        s["own_sems"].at[9],
    )
    grad_o = Grad(
        "go",
        1,
        dwo,
        buffers("o"),
        lambda i, k: g_out.at[:, columns_of(k, half)],
        at,
        wire,
        s["own_sems"].at[10],
    )
    grad_q = Grad(
        "gq",
        6,
        dwq,
        buffers("q"),
        lambda i, k: g_qkv.at[
            pl.ds((i % 2) * (share // 2), share // 2), columns_of(3 * k + i // 2, half)
        ],
        at,
        wire,
        s["own_sems"].at[11],
    )

    def back_through(first, last):
        @pl.loop(first, last, unroll=3)
        def _(index):
            where = chunk_of(index, 256)
            grad = nt(gf[...], wd[where, :]) * slope[:, where].astype(F32)
            low = grad.astype(BF16)
            slope[:, where] = low
            sums_up[:, where] = jnp.sum(low.astype(F32).reshape(rows // 8, 8, 256), axis=0)

    back_through(0, inner // 512)
    wire.arrived("act", act.at[other])
    wire.arrived("gf", s["gf_in"])

    def down_grad(owner):
        where = pl.ds(aligned(owner * quarter, 128), quarter)
        made = nn(act[core, :, where].T, gf[:, columns_of(core, half)])
        made = made + nn(act[other, :, where].T, s["gf_in"][...])
        dwd[owner] = made.astype(BF16)

    down_grad(at.nd)
    grad_d.begin()
    back_through(inner // 512, inner // 256)
    wire.send("slope", slope.at[:, columns_of(other, inner // 2)], s["slope_in"], at.sib)

    @pl.loop(0, chunks)
    def _(index):
        where = chunk_of(index, 256)
        stage[:, where] = nt(slope[...], wu[where, :])


    gb = s["gb"]

    @pl.loop(0, rows // BAND, unroll=2)
    def _(index):
        where = chunk_of(index, BAND)
        grad_hidden = flow[where, :] + stage[where, :]
        hat = hat_one[where, :]
        g = grad_hidden * small[3:4, :]
        grad = r_one[where, :] * (g - mean(g) - hat * mean(g * hat))
        flow[where, :] = grad
        low = grad.astype(BF16)
        gb[where, :] = low
        sums[3] += gather_rows(grad_hidden * hat)
        sums[4] += gather_rows(grad_hidden)
        sums[2] += gather_rows(low.astype(F32))

    wire.send("gb", gb.at[:, columns_of(other, half)], s["gb_in"], at.sib)

    @pl.loop(0, chunks)
    def _(index):
        where = chunk_of(index, 256)
        proj[:, where] = nt(gb[...], s["wo"][where, :]).astype(BF16)

    do, do_out = s["do"], s["do_out"]
    for index in range(chunks):
        moved = nn(proj[:, 0:width], order[:, index * 256 : (index + 1) * 256]).astype(BF16)
        for e in range(2):
            pair = 2 * index + e
            block = moved[:, e * 128 : (e + 1) * 128]
            if pair < some:
                do[pair] = block
            else:
                do_out[pair - some] = block
    wire.send("do", do_out, do.at[pl.ds(some, some)], at.partner)

    def prepare(pair):
        do_t = do[pair].astype(F32).T
        scaled = jnp.concatenate(
            [do_t[e * size : (e + 1) * size] * inverse[2 * pair + e] for e in range(2)], axis=0
        )
        product = scaled * out_t[pair]
        for e in range(2):
            delta[2 * pair + e] = jnp.sum(product[e * size : (e + 1) * size], axis=0, keepdims=True)
        dos[pair] = scaled.T.astype(BF16)

    group_d = [pl.ds(0, some), pl.ds(some, some)]
    group_h = [pl.ds(0, 2 * some), pl.ds(2 * some, 2 * some)]

    def send_group(g):
        wire.send(
            "far do" + str(g), dos.at[group_d[g]], far_dos.at[core, group_d[g]], at.cross
        )
        wire.send(
            "far de" + str(g), delta.at[group_h[g]], far_delta.at[core, group_h[g]], at.cross
        )

    def pass_group(g):
        for kind, ref, group in (("do", far_dos, group_d), ("de", far_delta, group_h)):
            block = ref.at[core, group[g]]
            wire.arrived("far " + kind + str(g), block)
            wire.send("passed " + kind + str(g), block, block, at.sib)

    def have_group(g):
        wire.arrived("passed do" + str(g), far_dos.at[other, group_d[g]])
        wire.arrived("passed de" + str(g), far_delta.at[other, group_h[g]])

    @pl.loop(0, some)
    def _(index):
        prepare(index)

    send_group(0)
    for owner in (at.nx, at.ny, at.w):
        down_grad(owner)
    grad_d.fold()
    grad_d.push(0, 1, 2, 3)

    part_d.gone()
    wire.arrived("hid", hid.at[other])
    wire.arrived("slope", s["slope_in"])
    mine_t, theirs_t = hid[core].T, hid[other].T
    for index in range(inner // 2 // half):
        where = pl.ds(aligned(core * (inner // 2) + index * half, 128), half)
        made = nn(mine_t, slope[:, where]) + nn(
            theirs_t, s["slope_in"][:, index * half : (index + 1) * half]
        )
        made = made.astype(BF16)
        for owner in range(4):
            first = owner * 2 * share + (index // 2) * share
            wd[first : first + share, (index % 2) * half : (index % 2 + 1) * half] = made[
                owner * share : (owner + 1) * share
            ]
    grad_u.begin()
    wire.arrived("ctxn", ctx_nat.at[other])
    wire.arrived("gb", s["gb_in"])
    made = nn(ctx_nat[core].T, gb[:, columns_of(core, half)]) + nn(
        ctx_nat[other].T, s["gb_in"][...]
    )
    made = made.astype(BF16)
    for owner in range(4):
        dwo(owner)[...] = made[owner * share : (owner + 1) * share]
    grad_o.begin()

    part_u.gone()
    dq, dq_out, dkv_in = s["dq"], s["dq_out"], s["dkv_in"]
    near_d = wire.slot("near dkv", pairs)
    dq_base = wire.slot("dq", some)
    lots = inner // 512

    def tile(pair, which):
        return wu.at[
            pl.ds(aligned((pair // lots) * rows, 16), rows),
            pl.ds(aligned((pair % lots) * 512 + which * 256, 256), 256),
        ]

    def dkv_near(pair):
        return wire.copy(near_d + pair, tile(pair, other), dkv_in.at[pair], at.sib, "near dkv")

    def two_blocks(pair, chip, first):
        return jnp.concatenate(
            [kv[pair, k * 2 + chip, :, first : first + 128] for k in range(2)], axis=0
        )

    def attend_back(pair):
        queries = q[pair] * jnp.asarray(size**-0.5, BF16)
        dq_parts = [None, None]
        dv = dk = None
        for chip in (at.near, at.far):
            key_rows, value_rows = two_blocks(pair, chip, 0), two_blocks(pair, chip, 128)
            keys_t = key_rows.T
            for e in range(2):
                low = jnp.concatenate(
                    [
                        exps[2 * pair + e, pl.ds(aligned((k * 2 + chip) * rows, 16), rows), :]
                        for k in range(2)
                    ],
                    axis=0,
                )
                mine = masked(dos[pair], e)
                grad_w = nt(value_rows, mine)
                grad_s = (low.astype(F32) * (grad_w - delta[2 * pair + e])).astype(BF16)
                more_q = nn(keys_t[e * size : (e + 1) * size], grad_s)
                dq_parts[e] = more_q if dq_parts[e] is None else dq_parts[e] + more_q
                if chip is at.near:
                    more_v = nn(low, mine)
                    more_k = nn(grad_s, masked(queries, e))
                    dv = more_v if dv is None else dv + more_v
                    dk = more_k if dk is None else dk + more_k
            if chip is at.near:
                made = jnp.concatenate([dk, dv], axis=1).astype(BF16)
                for k in range(2):
                    tile(pair, k)[...] = made[k * rows : (k + 1) * rows]
                dkv_near(pair).start()
        return (jnp.concatenate(dq_parts, axis=0).T * size**-0.5).astype(BF16)

    gkv = s["gkv"]

    def far_back(pair):
        queries = far_q[:, pair].reshape(2 * rows, 128) * jnp.asarray(size**-0.5, BF16)
        grads = far_dos[:, pair].reshape(2 * rows, 128)
        key_rows, value_rows = kv[pair, own_slot, :, 0:128], kv[pair, own_slot, :, 128:256]
        dv = dk = None
        for e in range(2):
            head = 2 * pair + e
            top = jnp.concatenate([far_tops[k, head] for k in range(2)], axis=1)
            less = jnp.concatenate([far_delta[k, head] for k in range(2)], axis=1)
            mine, asking = masked(grads, e), masked(queries, e)
            low = jnp.exp(nt(key_rows, asking) - top).astype(BF16)
            grad_s = (low.astype(F32) * (nt(value_rows, mine) - less)).astype(BF16)
            more_v, more_k = nn(low, mine), nn(grad_s, asking)
            dv = more_v if dv is None else dv + more_v
            dk = more_k if dk is None else dk + more_k
        dkv_near(pair).wait_recv()
        own = tile(pair, core)
        where = pl.ds(aligned(pair * 128, 128), 128)
        for kind, made in ((0, dk), (1, dv)):
            cut = slice(kind * 128, (kind + 1) * 128)
            gkv[kind, :, where] = (
                made + own[:, cut].astype(F32) + dkv_in[pair, :, cut].astype(F32)
            ).astype(BF16)

    def dq_copy(index):
        return wire.copy(dq_base + index, dq_out.at[index], dq.at[some + index], at.partner, "dq")

    grad_d.own(0)

    @pl.loop(0, some)
    def _(index):
        dq[index] = attend_back(index)

    wire.arrived("do", do.at[pl.ds(some, some)])

    @pl.loop(some, pairs)
    def _(index):
        prepare(index)

    send_group(1)
    pass_group(0)

    @pl.loop(0, some)
    def _(index):
        dq_out[index] = attend_back(index + some)
        dq_copy(index).start()

    for chunk in range(1, 4):
        grad_d.own(chunk)
    pass_group(1)
    wire.arrived("passed q", far_q.at[other])
    wire.arrived("passed tops", far_tops.at[other])
    have_group(0)

    @pl.loop(0, some)
    def _(index):
        far_back(index)

    grad_d.chain(0)
    grad_u.fold()
    grad_u.push(0, 1, 2)
    wire.left(*[name for name in wire.started if name[:2] not in ("gd", "gu", "go")])
    part_kv.gone()
    part_q.gone()
    part_o.gone()
    for base in (far_base, near_base, pass_base):
        wire.gone("kv" + str(base), kv.at[:, 0])
    wire.gone("ctx", ctx_out)
    have_group(1)

    @pl.loop(some, pairs)
    def _(index):
        far_back(index)

    grad_d.chain(1)
    for index in range(some):
        dq_copy(index).wait_recv()
    merged = jnp.concatenate([dq[pair] for pair in range(pairs)], axis=1)
    for index in range(chunks):
        where = slice(index * 256, (index + 1) * 256)
        rows_of = order[where, :]
        for kind in range(3):
            source = merged if kind == 0 else gkv[kind - 1]
            low = nt(source, rows_of).astype(BF16)
            proj[:, kind * width + index * 256 : kind * width + (index + 1) * 256] = low
            if kind != 1:
                sums[kind // 2, :, where] = jnp.sum(
                    low.astype(F32).reshape(rows // 8, 8, 256), axis=0
                )
    wire.send("gj", proj.at[:, columns_of(other, 3 * half)], s["gj_in"], at.sib)
    grad_u.own(0)
    grad_d.chain(2)

    vec, vec_in, vec_low, vec_far = s["vec"], s["vec_in"], s["vec_low"], s["vec_far"]
    for row in range(8):
        vec[row : row + 1, :] = jnp.sum(sums[row], axis=0, keepdims=True)
    for index in range(inner // width):
        vec[8 + index : 9 + index, :] = jnp.sum(
            sums_up[:, index * width : (index + 1) * width], axis=0, keepdims=True
        )
    for row in range(8 + inner // width, 16):
        vec[row : row + 1, :] = jnp.zeros((1, width), F32)
    wire.send("va", vec, vec_in, at.sib)

    wire.arrived("tok", tok.at[other])
    wire.arrived("gj", s["gj_in"])
    mine_t, theirs_t = tok[core].T, tok[other].T
    for index in range(3):
        where = pl.ds(aligned(core * (3 * half) + index * half, 128), half)
        made = nn(mine_t, proj[:, where]) + nn(
            theirs_t, s["gj_in"][:, index * half : (index + 1) * half]
        )
        made = made.astype(BF16)
        for owner in range(4):
            dwq(owner)[index * share : (index + 1) * share, :] = made[
                owner * share : (owner + 1) * share
            ]
    grad_q.begin()
    grad_u.push(3)
    grad_o.fold()
    grad_o.push(0)
    grad_d.total(0)
    wire.arrived("va", vec_in)
    vec_low[0] = (vec_in[...] + vec[...]).astype(BF16)
    for index, where in enumerate((at.to_x, at.to_y, at.to_d)):
        wire.send("vb" + str(index), vec_low.at[0], vec_far.at[index], where)

    keep_out.wait()

    @pl.loop(0, chunks)
    def _(index):
        where = chunk_of(index, 256)
        result[:, where] = nt(proj[...], s["wqkv"][where, :]) + flow[:, where]

    keep_grad = pltpu.make_async_copy(result, grad_tokens, s["own_sems"].at[7])
    keep_grad.start()
    def vec_hop(name, place, far, where):
        return wire.copy(wire.slot(name), vec_low.at[place], vec_far.at[far], where, name)

    def vec_out():
        return vec_hop("vu", 1, 3, at.mate)

    def vec_across():
        return vec_hop("vv", 2, 4, at.middle)

    def vec_back():
        return vec_hop("vt", 3, 5, at.mate)

    def vec_sum(*parts):
        total = parts[0].astype(F32)
        for part in parts[1:]:
            total = total + part.astype(F32)
        return total

    grad_u.own(1)
    grad_d.chain(3)
    grad_d.total(1)
    grad_u.own(2)
    grad_u.chain(0)
    grad_q.fold()
    grad_q.push(0, 1, 2, 3, 4, 5)
    grad_d.total(2)
    grad_u.chain(1)
    grad_d.total(3)
    grad_u.own(3)
    grad_o.own(0)
    grad_u.chain(2)
    grad_u.total(0)
    grad_q.own(0)
    grad_u.chain(3)
    grad_u.total(1)
    grad_q.own(1)
    for index in range(3):
        wire.arrived("vb" + str(index), vec_far.at[index])
    vec_low[1] = (
        vec_sum(vec_low[0], vec_far[0]) + vec_sum(vec_far[1], vec_far[2])
    ).astype(BF16)

    @pl.when(at.outer)
    def _():
        vec_out().start()

    grad_o.chain(0)
    grad_q.chain(0)
    grad_u.total(2)
    grad_q.own(2)
    grad_q.chain(1)
    grad_u.total(3)
    grad_q.own(3)

    @pl.when(at.inner)
    def _():
        vec_out().wait_recv()
        vec_low[2] = vec_sum(vec_low[1], vec_far[3]).astype(BF16)
        vec_across().start()

    grad_q.chain(2)
    grad_o.total(0)
    grad_q.total(0)
    grad_q.own(4)
    grad_q.chain(3)
    grad_q.total(1)
    grad_q.own(5)
    grad_q.chain(4)
    grad_q.total(2)
    grad_q.chain(5)
    grad_q.total(3)

    @pl.when(at.inner)
    def _():
        vec_across().wait_recv()
        total = vec_sum(vec_low[2], vec_far[4]).astype(BF16)
        vec_low[3] = total
        vec_back().start()
        vec_in[...] = total.astype(F32)

    grad_q.total(4)
    grad_q.total(5)
    for chunk in range(4):
        grad_d.give(chunk)
    for chunk in range(4):
        grad_u.give(chunk)
    grad_o.give(0)
    for chunk in range(4):
        grad_q.give(chunk)

    @pl.when(at.outer)
    def _():
        vec_back().wait_recv()
        vec_in[...] = vec_far[5].astype(F32)

    keep_small = pltpu.make_async_copy(vec_in, g_small, s["own_sems"].at[6])
    keep_small.start()
    grad_q.give(4)
    grad_q.give(5)

    @pl.when(at.outer)
    def _():
        vec_out().wait_send()

    @pl.when(at.inner)
    def _():
        vec_across().wait_send()
        vec_back().wait_send()

    grad_d.close()
    grad_u.close()
    grad_o.close()
    grad_q.close()
    keep_grad.wait()
    keep_small.wait()
    wire.gone("near dkv", dkv_in)
    wire.gone("dq", dq_out)
    wire.close()


def whole_layer(tokens, cotangent, pairing, small_raw, w_qkv, w_out, w_up, w_down):
    rows, width = tokens.shape
    inner = w_up.shape[1]
    scratch = layer_scratch(rows, width, inner, pairing.shape[0])
    hbm = pl.BlockSpec(memory_space=pl.ANY)
    vmem = pl.BlockSpec(memory_space=pltpu.VMEM)
    smem = pl.BlockSpec(memory_space=pltpu.SMEM)
    return pl.pallas_call(
        functools.partial(layer_kernel, tuple(scratch)),
        out_shape=[
            jax.ShapeDtypeStruct((rows, width), F32),
            jax.ShapeDtypeStruct((rows, width), F32),
            jax.ShapeDtypeStruct(w_qkv.shape, BF16),
            jax.ShapeDtypeStruct(w_out.shape, BF16),
            jax.ShapeDtypeStruct(w_up.shape, BF16),
            jax.ShapeDtypeStruct(w_down.shape, BF16),
            jax.ShapeDtypeStruct((16, width), F32),
        ],
        in_specs=[hbm, hbm, smem, vmem, hbm, hbm, hbm, hbm],
        out_specs=[hbm] * 7,
        scratch_shapes=list(scratch.values()),
        compiler_params=pltpu.CompilerParams(
            collective_id=0, has_side_effects=True, vmem_limit_bytes=60 << 20
        ),
        name="whole_layer",
    )(tokens, cotangent, pairing, small_raw, w_qkv, w_out, w_up, w_down)


def finish_kernel(share, *refs):
    wide, small, outs = refs[:6], refs[6], refs[7:]
    for source, target in zip(wide, outs[:6]):
        target[...] = source[...].astype(F32)

    @pl.when(pl.program_id(0) == 0)
    def _():
        w = lax.axis_index("wt")
        values = small[...]
        mine = jnp.zeros((8, share), F32)
        line = jnp.zeros((1, 4 * share), F32)
        for owner in range(4):
            mine = mine + jnp.where(
                w == owner, values[:8, owner * share : (owner + 1) * share], 0.0
            )
            line = line + jnp.where(w == owner, values[8 + owner : 9 + owner], 0.0)
        for row in range(8):
            outs[6 + row][...] = mine[row : row + 1]
        outs[14][...] = line.reshape(4 * share)


def finish(*arrays):
    steps = 2
    wide, small = arrays[:6], arrays[6]
    share = small.shape[1] // 4

    def blocks(array):
        return pl.BlockSpec((array.shape[0] // steps, array.shape[1]), lambda i: (i, 0))

    def fixed(shape):
        return pl.BlockSpec(shape, lambda i: (0,) * len(shape))

    shapes = [(1, share)] * 8 + [(4 * share,)]
    return pl.pallas_call(
        functools.partial(finish_kernel, share),
        grid=(steps,),
        out_shape=[jax.ShapeDtypeStruct(v.shape, F32) for v in wide]
        + [jax.ShapeDtypeStruct(v, F32) for v in shapes],
        in_specs=[blocks(v) for v in wide] + [fixed(small.shape)],
        out_specs=[blocks(v) for v in wide] + [fixed(v) for v in shapes],
        compiler_params=pltpu.CompilerParams(vmem_limit_bytes=60 << 20),
        name="finish",
    )(*arrays)


far_below = -1e30


def passed_along(value, axis, steps):
    count = lax.axis_size(axis)
    pairs = [(source, (source + steps) % count) for source in range(count)]
    return lax.ppermute(value, axis, pairs)


def norm_rows(values, gains, shifts):
    average = jnp.mean(values, axis=-1, keepdims=True)
    centred = values - average
    spread = jnp.mean(centred * centred, axis=-1, keepdims=True)
    return centred * lax.rsqrt(spread + 1e-12) * gains + shifts


def gelu_exact(pre_active):
    return jax.nn.gelu(pre_active, approximate=False)


def scores_of(queries, key_heads):
    return (
        jnp.einsum("thd,khd->htk", queries, key_heads, preferred_element_type=jnp.float32) * 0.125
    )


def unchanged(running):
    return running


def general_layer(
    tokens,
    pairing,
    w_qkv,
    bias_q,
    bias_v,
    w_out,
    bias_out,
    gain_one,
    shift_one,
    w_up,
    bias_up,
    w_down,
    bias_down,
    gain_two,
    shift_two,
    cotangent,
):
    local_params = (
        w_qkv,
        bias_q,
        bias_v,
        w_out,
        bias_out,
        gain_one,
        shift_one,
        w_up,
        bias_up,
        w_down,
        bias_down,
        gain_two,
        shift_two,
    )
    gathered = tuple(lax.all_gather(v, "wt", axis=0, tiled=True) for v in local_params)
    (
        wqkv_full,
        biasq_full,
        biasv_full,
        wout_full,
        biasout_full,
        gainone_full,
        shiftone_full,
        wup_full,
        biasup_full,
        wdown_full,
        biasdown_full,
        gaintwo_full,
        shifttwo_full,
    ) = gathered
    tok_rows = tokens.shape[1]
    model_width = tokens.shape[2]
    head_count = pairing.shape[0]
    head_size = model_width // head_count
    group_size = lax.axis_size("ctx")
    position_ctx = lax.axis_index("ctx")
    half_len = tok_rows * group_size // 2
    own_half = position_ctx * tok_rows // half_len
    flipped = pairing == 1
    inputs = tokens[0]
    bias_cat = jnp.concatenate(
        [
            biasq_full.astype(jnp.float32),
            jnp.zeros((model_width,), jnp.float32),
            biasv_full.astype(jnp.float32),
        ]
    )
    projected = jnp.dot(inputs, wqkv_full, preferred_element_type=jnp.float32) + bias_cat
    projected_low = projected.astype(jnp.bfloat16)
    queries = projected_low[:, :model_width].reshape(tok_rows, head_count, head_size)
    key_rows = projected_low[:, model_width : 2 * model_width]
    value_rows = projected_low[:, 2 * model_width :]

    def online_update(state, portion_keys, portion_values, needed):
        row_top, row_total, accumulated = state
        key_count = portion_keys.shape[0]
        key_heads = portion_keys.reshape(key_count, head_count, head_size)
        value_heads = portion_values.reshape(key_count, head_count, head_size)
        scores = scores_of(queries, key_heads)
        scores = jnp.where(needed[:, None, :], scores, far_below)
        new_top = jnp.maximum(row_top, jnp.max(scores, axis=-1))
        factor = jnp.exp(row_top - new_top)
        weights = jnp.exp(scores - new_top[..., None])
        row_total = jnp.sum(weights, axis=-1)
        added = jnp.einsum(
            "htk,khd->thd",
            weights.astype(jnp.bfloat16),
            value_heads,
            preferred_element_type=jnp.float32,
        )
        accumulated = accumulated * factor.T[..., None] + added
        return (new_top, row_total, accumulated)

    start_state = (
        jnp.full((head_count, tok_rows), far_below, jnp.float32),
        jnp.zeros((head_count, tok_rows), jnp.float32),
        jnp.zeros((tok_rows, head_count, head_size), jnp.float32),
    )

    def wanted(offset, key_count):
        key_half = (offset + jnp.arange(key_count)) // half_len
        target = jnp.where(flipped, 1 - own_half, own_half)
        return key_half[None, :] == target[:, None]

    portion_keys = lax.all_gather(key_rows, "ctx", axis=0, tiled=True)
    portion_values = lax.all_gather(value_rows, "ctx", axis=0, tiled=True)
    needed = wanted(jnp.int32(0), portion_keys.shape[0])

    def update(state):
        return online_update(state, portion_keys, portion_values, needed)

    row_top, row_total, accumulated = lax.cond(jnp.any(needed), update, unchanged, start_state)
    context = accumulated / row_total.T[..., None]
    log_sum = row_top + jnp.log(row_total)
    context_low = context.reshape(tok_rows, model_width).astype(jnp.bfloat16)
    branch = jnp.dot(
        context_low, wout_full, preferred_element_type=jnp.float32
    ) + biasout_full.astype(jnp.float32)
    summed_one = inputs.astype(jnp.float32) + branch
    hidden, norm_one_back = jax.vjp(
        norm_rows, summed_one, gainone_full.astype(jnp.float32), shiftone_full.astype(jnp.float32)
    )
    hidden_low = hidden.astype(jnp.bfloat16)
    pre_active = jnp.dot(
        hidden_low, wup_full, preferred_element_type=jnp.float32
    ) + biasup_full.astype(jnp.float32)
    active, gelu_back = jax.vjp(gelu_exact, pre_active)
    active_low = active.astype(jnp.bfloat16)
    ffn_out = jnp.dot(
        active_low, wdown_full, preferred_element_type=jnp.float32
    ) + biasdown_full.astype(jnp.float32)
    output, norm_two_back = jax.vjp(
        norm_rows,
        hidden + ffn_out,
        gaintwo_full.astype(jnp.float32),
        shifttwo_full.astype(jnp.float32),
    )
    again = gathered
    wqkv_back = again[0]
    wout_back = again[3]
    wup_back = again[7]
    wdown_back = again[9]
    grad_two, grad_gain_two, grad_shift_two = norm_two_back(cotangent[0].astype(jnp.float32))
    grad_ffn = grad_two.astype(jnp.bfloat16)
    grad_bias_down = jnp.sum(grad_ffn.astype(jnp.float32), axis=0)
    grad_w_down = jnp.einsum("tf,td->fd", active_low, grad_ffn, preferred_element_type=jnp.float32)
    grad_active = jnp.einsum("td,fd->tf", grad_ffn, wdown_back, preferred_element_type=jnp.float32)
    (grad_pre_f,) = gelu_back(grad_active)
    grad_pre = grad_pre_f.astype(jnp.bfloat16)
    grad_bias_up = jnp.sum(grad_pre.astype(jnp.float32), axis=0)
    grad_w_up = jnp.einsum("tc,tf->cf", hidden_low, grad_pre, preferred_element_type=jnp.float32)
    grad_hidden = grad_two + jnp.einsum(
        "tf,cf->tc", grad_pre, wup_back, preferred_element_type=jnp.float32
    )
    grad_one, grad_gain_one, grad_shift_one = norm_one_back(grad_hidden)
    grad_branch = grad_one.astype(jnp.bfloat16)
    grad_bias_out = jnp.sum(grad_branch.astype(jnp.float32), axis=0)
    grad_w_out = jnp.einsum(
        "tc,td->cd", context_low, grad_branch, preferred_element_type=jnp.float32
    )
    grad_context = jnp.einsum(
        "td,cd->tc", grad_branch, wout_back, preferred_element_type=jnp.float32
    )
    grad_context = grad_context.astype(jnp.bfloat16).reshape(tok_rows, head_count, head_size)
    row_delta = jnp.sum(grad_context.astype(jnp.float32) * context, axis=-1).T

    def piece_grads(portion_keys, portion_values, needed):
        key_count = portion_keys.shape[0]
        key_heads = portion_keys.reshape(key_count, head_count, head_size)
        value_heads = portion_values.reshape(key_count, head_count, head_size)
        scores = scores_of(queries, key_heads)
        scores = jnp.where(needed[:, None, :], scores, far_below)
        probs = jnp.exp(scores - log_sum[..., None])
        probs_low = probs.astype(jnp.bfloat16)
        piece_v = jnp.einsum(
            "htk,thd->khd", probs_low, grad_context, preferred_element_type=jnp.float32
        ).reshape(key_count, model_width)
        grad_weights = jnp.einsum(
            "thd,khd->htk", grad_context, value_heads, preferred_element_type=jnp.float32
        )
        grad_scores = (probs * (grad_weights - row_delta[..., None])).astype(jnp.bfloat16)
        piece_q = 0.125 * jnp.einsum(
            "htk,khd->thd", grad_scores, key_heads, preferred_element_type=jnp.float32
        )
        piece_k = 0.125 * jnp.einsum(
            "htk,thd->khd", grad_scores, queries, preferred_element_type=jnp.float32
        ).reshape(key_count, model_width)
        return (piece_k, piece_v, piece_q)

    zero_queries = jnp.zeros((tok_rows, head_count, head_size), jnp.float32)

    def circle_step(step_index, running):
        turn_keys, turn_values, grad_keys, grad_values, grad_queries = running
        owner = (position_ctx - step_index) % group_size
        needed = wanted(owner * tok_rows, tok_rows)

        def update_grads(state):
            grad_k, grad_v, grad_q = state
            piece_k, piece_v, piece_q = piece_grads(turn_keys, turn_values, needed)
            return (grad_k + piece_k, grad_v + piece_v, grad_q + piece_q)

        grad_keys, grad_values, grad_queries = lax.cond(
            jnp.any(needed), update_grads, unchanged, (grad_keys, grad_values, grad_queries)
        )
        turn_keys, turn_values = passed_along((turn_keys, turn_values), "ctx", 1)
        grad_keys, grad_values = (
            passed_along(grad_keys.astype(jnp.bfloat16), "ctx", 1).astype(grad_keys.dtype),
            passed_along(grad_values.astype(jnp.bfloat16), "ctx", 1).astype(grad_values.dtype),
        )
        return (turn_keys, turn_values, grad_keys, grad_values, grad_queries)

    zero_rows = jnp.zeros((tok_rows, model_width), jnp.float32)
    circle_start = (key_rows, value_rows, zero_rows, zero_rows, zero_queries)
    circle_end = lax.fori_loop(0, group_size, circle_step, circle_start)
    grad_keys = circle_end[2]
    grad_values = circle_end[3]
    grad_queries = circle_end[4]
    grad_projected = jnp.concatenate(
        [grad_queries.reshape(tok_rows, model_width), grad_keys, grad_values], axis=1
    ).astype(jnp.bfloat16)
    grad_bias_q = jnp.sum(grad_projected[:, :model_width].astype(jnp.float32), axis=0)
    grad_bias_v = jnp.sum(grad_projected[:, 2 * model_width :].astype(jnp.float32), axis=0)
    grad_w_qkv = jnp.einsum("tc,tj->cj", inputs, grad_projected, preferred_element_type=jnp.float32)
    grad_inputs = grad_one + jnp.einsum(
        "tj,cj->tc", grad_projected, wqkv_back, preferred_element_type=jnp.float32
    )
    terms = (
        grad_w_qkv,
        grad_bias_q,
        grad_bias_v,
        grad_w_out,
        grad_bias_out,
        grad_gain_one,
        grad_shift_one,
        grad_w_up,
        grad_bias_up,
        grad_w_down,
        grad_bias_down,
        grad_gain_two,
        grad_shift_two,
    )
    owned = tuple(
        lax.psum_scatter(term.astype(jnp.bfloat16), "wt", scatter_dimension=0, tiled=True)
        for term in terms
    )
    totals = tuple(lax.psum(term, "ctx").astype(jnp.float32) for term in owned)
    return (
        output[None],
        grad_inputs[None],
        totals[0],
        totals[1],
        totals[2],
        totals[3],
        totals[4],
        totals[5],
        totals[6],
        totals[7],
        totals[8],
        totals[9],
        totals[10],
        totals[11],
        totals[12],
    )


def fast_layer(
    tokens,
    pairing,
    w_qkv,
    bias_q,
    bias_v,
    w_out,
    bias_out,
    gain_one,
    shift_one,
    w_up,
    bias_up,
    w_down,
    bias_down,
    gain_two,
    shift_two,
    cotangent,
):
    share = tokens.shape[2] // 4
    vectors = (bias_q, bias_v, bias_out, gain_one, shift_one, bias_down, gain_two, shift_two)
    vectors = vectors + tuple(bias_up[k * share : (k + 1) * share] for k in range(4))
    row = lax.broadcasted_iota(jnp.int32, (16, share), 0)
    small_raw = jnp.zeros((16, share), jnp.bfloat16)
    for index, vector in enumerate(vectors):
        small_raw = jnp.where(row == index, vector[None, :], small_raw)
    made = whole_layer(
        tokens[0], cotangent[0], pairing, small_raw, w_qkv, w_out, w_up, w_down
    )
    output, grad_tokens, g_qkv, g_out, g_up, g_down, *small = finish(*made)
    small = [v.reshape(-1) for v in small]
    return (
        output[None],
        grad_tokens[None],
        g_qkv,
        small[0],
        small[1],
        g_out,
        small[2],
        small[3],
        small[4],
        g_up,
        small[8],
        g_down,
        small[5],
        small[6],
        small[7],
    )


def local(tokens, pairing, *rest):
    rows, width = tokens.shape[1:]
    heads = pairing.shape[0]
    inner = rest[7].shape[1]
    fits = (
        lax.axis_size("wt") == 4
        and lax.axis_size("ctx") == 8
        and tokens.shape[0] == 1
        and rows % BAND == 0
        and 3 * rows <= width
        and width % 256 == 0
        and heads % 4 == 0
        and width == 64 * heads
        and inner == 4 * width
    )
    layer = fast_layer if fits else general_layer
    return layer(tokens, pairing, *rest)


def solution(mesh):
    in_specs = (
        P("wt", "ctx", None),
        P(),
        P("wt", None),
        P("wt"),
        P("wt"),
        P("wt", None),
        P("wt"),
        P("wt"),
        P("wt"),
        P("wt", None),
        P("wt"),
        P("wt", None),
        P("wt"),
        P("wt"),
        P("wt"),
        P("wt", "ctx", None),
    )
    out_specs = (
        P("wt", "ctx", None),
        P("wt", "ctx", None),
        P("wt", None),
        P("wt"),
        P("wt"),
        P("wt", None),
        P("wt"),
        P("wt"),
        P("wt"),
        P("wt", None),
        P("wt"),
        P("wt", None),
        P("wt"),
        P("wt"),
        P("wt"),
    )
    return jax.shard_map(local, mesh=mesh, in_specs=in_specs, out_specs=out_specs, check_vma=False)
```

```python
import functools

import jax
import jax.numpy as jnp
from jax import lax
from jax.experimental import pallas as pl
from jax.experimental.pallas import tpu as pltpu
from jax.sharding import PartitionSpec as P

F32, BF16 = jnp.float32, jnp.bfloat16
MESH = pl.DeviceIdType.MESH
BAND = 32


def nn(a, b):
    return jnp.dot(a, b, preferred_element_type=F32)


def nt(a, b):
    return lax.dot_general(a, b, (((1,), (1,)), ((), ())), preferred_element_type=F32)


def aligned(start, multiple):
    return start if isinstance(start, int) else pl.multiple_of(start, multiple)


def chunk_of(index, size):
    return pl.ds(aligned(index * size, size), size)


class Wire:
    def __init__(self, sends, receives, anyone):
        self.sends, self.receives, self.anyone = sends, receives, anyone
        self.firsts, self.used, self.groups, self.started = {}, 0, {}, {}

    def slot(self, name, count=1):
        if name not in self.firsts:
            self.firsts[name] = self.used, count
            self.used += count
            assert self.used <= self.receives.shape[0]
        first, had = self.firsts[name]
        assert had == count
        return first

    def copy(self, slot, source, target, where, group):
        place = self.groups.setdefault(group, len(self.groups))
        assert place < self.sends.shape[0]
        return pltpu.make_async_remote_copy(
            src_ref=source,
            dst_ref=target,
            send_sem=self.sends.at[place],
            recv_sem=self.receives.at[slot],
            device_id=where,
            device_id_type=MESH,
        )

    def send(self, name, source, target, where):
        copy = self.copy(self.slot(name), source, target, where, name)
        copy.start()
        self.started[name] = copy

    def send_in(self, group, name, source, target, where):
        self.copy(self.slot(name), source, target, where, group).start()

    def gone(self, group, ref):
        self.copy(0, ref, ref, self.anyone, group).wait_send()

    def arrived(self, name, target):
        self.copy(self.slot(name), target, target, self.anyone, "none").wait_recv()

    def left(self, *names):
        for name in names:
            self.started.pop(name).wait_send()

    def close(self):
        self.left(*tuple(self.started))


class Place:
    def __init__(self):
        self.w = w = lax.axis_index("wt")
        self.c = c = lax.axis_index("ctx")
        self.core = core = c % 2
        self.other = 1 - core
        self.z = z = c // 2
        self.near = z % 2
        self.far = 1 - self.near
        self.nx = w + 1 - 2 * (w % 2)
        self.ny = (w + 2) % 4
        self.nd = 3 - w
        self.sib = (w, c + 1 - 2 * core)
        self.to_x, self.to_y, self.to_d = (self.nx, c), (self.ny, c), (self.nd, c)
        self.cross = (w, c + 2 - 4 * self.near)
        self.partner = (w, (c + 4) % 8)
        self.lines = [(w, spot * 2 + core) for spot in (z + 1 - 2 * (z % 2), (z + 2) % 4, 3 - z)]
        self.others = [(w, (c + step) % 8) for step in range(1, 8)]
        self.mate, self.middle = self.lines[0], self.lines[2]
        self.outer, self.inner = (z == 0) | (z == 3), (z == 1) | (z == 2)


def greet(peers):
    barrier = pltpu.get_barrier_semaphore()
    for peer in peers:
        pl.semaphore_signal(barrier, inc=1, device_id=peer, device_id_type=MESH)
    pl.semaphore_wait(barrier, len(peers))


class Part:
    def __init__(self, name, local, full, first, columns, place, wire):
        self.name, self.local, self.full, self.place, self.wire = name, local, full, place, wire
        self.rows = local.shape[0]
        self.first, self.columns = first, columns // 2

    def piece(self, owner, core, half=None):
        rows, start = self.rows, owner * self.rows
        if half is not None:
            rows = self.rows // 2
            start = start + half * rows
        return self.full.at[
            pl.ds(aligned(start, 16), rows),
            pl.ds(aligned(self.first + core * self.columns, 128), self.columns),
        ]

    def send(self, kind, source, target, where):
        self.wire.send_in(self.name, self.name + kind, source, target, where)

    def begin(self):
        at = self.place
        mine = self.local.at[
            :, pl.ds(aligned(self.first + at.core * self.columns, 128), self.columns)
        ]
        target = self.piece(at.w, at.core)
        self.send("a", mine, target, at.to_x)
        self.send("b", mine, target, at.to_y)

    def relay(self):
        at, wire = self.place, self.wire
        for kind, owner, half, on, where in (
            ("a", at.nx, 0, "c", at.to_y),
            ("b", at.ny, 1, "e", at.to_x),
        ):
            block = self.piece(owner, at.core)
            wire.arrived(self.name + kind, block)
            part = self.piece(owner, at.core, half)
            self.send(on, part, part, where)
            self.send("s", block, block, at.sib)

    def share(self):
        at, wire = self.place, self.wire
        for half, came in ((0, "c"), (1, "e")):
            block = self.piece(at.nd, at.core, half)
            wire.arrived(self.name + came, block)
            self.send("r", block, block, at.sib)

    def arrived(self, kind, pieces):
        block = self.full.at[pl.ds(0, pieces * self.rows), pl.ds(self.first, self.columns)]
        self.wire.arrived(self.name + kind, block)

    def near(self):
        self.arrived("s", 2)

    def last(self):
        self.arrived("r", 1)

    def finish(self):
        self.near()
        self.last()

    def gone(self):
        block = self.full.at[pl.ds(0, 3 * self.rows), pl.ds(self.first, 2 * self.columns)]
        self.wire.gone(self.name, block)


def add_into(target, *sources):
    rows, columns = sources[0].shape
    band = 16
    while columns * band * 2 <= 1 << 15 and rows % (band * 2) == 0:
        band *= 2

    @pl.loop(0, rows // band)
    def _(index):
        where = chunk_of(index, band)
        total = sources[0][where, :].astype(F32)
        for source in sources[1:]:
            total = total + source[where, :].astype(F32)
        target[where, :] = total.astype(target.dtype)


class Grad:
    def __init__(self, name, chunks, blocks, buffers, finals, place, wire, local_sem):
        self.name, self.chunks, self.blocks, self.finals = name, chunks, blocks, finals
        self.place, self.wire, self.local_sem = place, wire, local_sem
        self.from_x, self.from_y, self.diag_x, self.diag_y, self.low, self.high = buffers
        self.rows, self.columns = self.from_x.shape

    def half(self, ref, index):
        return ref.at[pl.ds(index * (self.rows // 2), self.rows // 2), :]

    def begin(self):
        at, wire = self.place, self.wire
        block = self.blocks(at.nd)
        wire.send(self.name + "a", self.half(block, 0), self.diag_x, at.to_x)
        wire.send(self.name + "b", self.half(block, 1), self.diag_y, at.to_y)

    def fold(self):
        at, wire = self.place, self.wire
        for kind, came, owner, index in (("a", self.diag_x, at.ny, 0), ("b", self.diag_y, at.nx, 1)):
            wire.arrived(self.name + kind, came)
            part = self.half(self.blocks(owner), index)
            add_into(part, part, came)

    def lanes(self, chunk):
        at = self.place
        return (
            self.hop("c", chunk, self.blocks(at.nx), self.from_x, at.to_x),
            self.hop("d", chunk, self.blocks(at.ny), self.from_y, at.to_y),
        )

    def push(self, to_x=(), to_y=()):
        for chunk in to_x:
            self.lanes(chunk)[0].start()
        for chunk in to_y:
            self.lanes(chunk)[1].start()

    def cut(self, ref, chunk):
        count = self.rows // self.chunks
        return ref.at[pl.ds(chunk * count, count), :]

    def hop(self, kind, chunk, source, target, where):
        slot = self.wire.slot(self.name + kind, self.chunks) + chunk
        return self.wire.copy(
            slot, self.cut(source, chunk), self.cut(target, chunk), where, self.name + kind
        )

    def outward(self, chunk):
        return self.hop("u", chunk, self.blocks(self.place.w), self.low, self.place.mate)

    def across(self, chunk):
        return self.hop("v", chunk, self.from_x, self.high, self.place.middle)

    def back(self, chunk):
        return self.hop("t", chunk, self.from_y, self.high, self.place.mate)

    def own(self, chunk):
        for copy in self.lanes(chunk):
            copy.wait_recv()
        part = self.cut(self.blocks(self.place.w), chunk)
        add_into(part, part, self.cut(self.from_x, chunk), self.cut(self.from_y, chunk))
        self.out(chunk)

    def out(self, chunk):
        @pl.when(self.place.outer)
        def _():
            self.outward(chunk).start()

    def chain(self, chunk):
        at = self.place

        @pl.when(at.inner)
        def _():
            self.outward(chunk).wait_recv()
            block = self.blocks(at.w)
            add_into(
                self.cut(self.from_x, chunk), self.cut(block, chunk), self.cut(self.low, chunk)
            )
            self.across(chunk).start()

    def total(self, chunk):
        at = self.place

        @pl.when(at.inner)
        def _():
            self.across(chunk).wait_recv()
            add_into(
                self.cut(self.from_y, chunk),
                self.cut(self.from_x, chunk),
                self.cut(self.high, chunk),
            )
            self.back(chunk).start()
            for copy in self.copies(chunk, self.from_y):
                copy.start()

    def copies(self, chunk, source):
        at, wire = self.place, self.wire
        piece, target = self.cut(source, chunk), self.finals(chunk, at.core)
        keep = pltpu.make_async_copy(piece, target, self.local_sem)
        slot = wire.slot(self.name + "s")
        return keep, wire.copy(slot, piece, target, at.sib, self.name + "s")

    def give(self, chunk):
        at = self.place

        @pl.when(at.outer)
        def _():
            self.back(chunk).wait_recv()
            for copy in self.copies(chunk, self.high):
                copy.start()

    def close(self):
        at, wire = self.place, self.wire
        whole = self.from_y
        pltpu.make_async_copy(whole, whole, self.local_sem).wait()
        wire.arrived(self.name + "s", whole)
        for kind in ("s", "c", "d"):
            wire.gone(self.name + kind, whole)

        @pl.when(at.outer)
        def _():
            wire.gone(self.name + "u", whole)

        @pl.when(at.inner)
        def _():
            wire.gone(self.name + "v", whole)
            wire.gone(self.name + "t", whole)


def layer_scratch(rows, width, inner, heads):
    pairs = heads // 2
    some = pairs // 2
    share = width // 4
    half = width // 2
    groups = 8

    def low(*shape):
        return pltpu.VMEM(shape, BF16)

    def wide(*shape):
        return pltpu.VMEM(shape, F32)

    scratch = dict(
        wqkv=low(width, 3 * width),
        wo=low(width, width),
        wu=low(width, inner),
        wd=low(inner, width),
        order=low(width, width),
        tok=low(2, rows, width),
        cot=low(rows, width),
        small_own=low(16, width),
        small_in=low(3, 16, width),
        small=wide(16, width),
        bias_qkv=wide(8, 3 * width),
        bias_up=wide(8, inner),
        kv=low(pairs, 4, rows, 256),
        proj=low(rows, 3 * width),
        q=low(pairs, rows, 128),
        q_out=low(some, rows, 128),
        exps=low(heads, 4 * rows, rows),
        inverse=wide(heads, 1, rows),
        out_t=wide(pairs, 128, rows),
        ctx=low(pairs, rows, 128),
        ctx_out=low(some, rows, 128),
        ctx_nat=low(2, rows, width),
        hat_one=wide(rows, width),
        r_one=wide(rows, 1),
        flow=wide(rows, width),
        stage=wide(rows, width),
        result=wide(rows, width),
        hid=low(2, rows, width),
        act=low(2, rows, inner),
        slope=low(rows, inner),
        slope_in=low(rows, inner // 2),
        gf=low(rows, width),
        gf_in=low(rows, half),
        gb=low(rows, width),
        gb_in=low(rows, half),
        do=low(pairs, rows, 128),
        do_out=low(some, rows, 128),
        dq=low(pairs, rows, 128),
        dq_out=low(some, rows, 128),
        dkv_in=low(pairs, rows, 256),
        tops=wide(heads, 1, rows),
        delta=wide(heads, 1, rows),
        dos=low(pairs, rows, 128),
        far_q=low(2, pairs, rows, 128),
        far_tops=wide(2, heads, 1, rows),
        far_delta=wide(2, heads, 1, rows),
        far_dos=low(2, pairs, rows, 128),
        gkv=low(2, rows, width),
        gj_in=low(rows, 3 * half),
        sums=wide(16, groups, width),
        sums_up=wide(groups, inner),
        vec=wide(16, width),
        vec_in=wide(16, width),
        vec_low=low(4, 16, width),
        vec_far=low(6, 16, width),
        dwd=low(4, inner // 4, half),
    )
    shapes = dict(
        d=(inner // 4, half), u=(2 * share, width), o=(share, half), q=(3 * share, half)
    )
    for name, (r, c) in shapes.items():
        for kind in ("fx", "fy", "lo", "hi"):
            scratch["g" + name + kind] = low(r, c)
        for kind in ("dx", "dy"):
            scratch["g" + name + kind] = low(r // 2, c)
    scratch["sends"] = pltpu.SemaphoreType.DMA((80,))
    scratch["receives"] = pltpu.SemaphoreType.DMA((180,))
    scratch["own_sems"] = pltpu.SemaphoreType.DMA((12,))
    return scratch


def layer_kernel(names, *refs):
    (
        tokens,
        cot_l,
        pairing,
        small_raw,
        qkv_l,
        out_l,
        up_l,
        down_l,
        output,
        grad_tokens,
        g_qkv,
        g_out,
        g_up,
        g_down,
        g_small,
    ) = refs[:15]
    s = dict(zip(names, refs[15:]))
    at = Place()
    wire = Wire(s["sends"], s["receives"], at.sib)
    rows, width = tokens.shape
    inner = up_l.shape[1]
    heads = pairing.shape[0]
    pairs, some = heads // 2, heads // 4
    size = width // heads
    half = width // 2
    keys = 4 * rows
    chunks = width // 256
    share = width // 4
    core, other = at.core, at.other

    greet([at.to_x, at.to_y, at.to_d] + at.others)

    part_kv = Part("kv", qkv_l, s["wqkv"], width, 2 * width, at, wire)
    part_q = Part("q", qkv_l, s["wqkv"], 0, width, at, wire)
    part_o = Part("o", out_l, s["wo"], 0, width, at, wire)
    part_u = Part("u", up_l, s["wu"], 0, inner, at, wire)
    part_d = Part("d", down_l, s["wd"], 0, width, at, wire)
    part_kv.begin()
    part_q.begin()
    raw = small_raw[...]
    row = lax.broadcasted_iota(jnp.int32, (share, width), 0)
    column = lax.broadcasted_iota(jnp.int32, (share, width), 1)

    def spread(values, spot):
        place = jnp.where(column - row == spot * share, 1.0, 0.0).astype(BF16)
        return nn(values, place)

    own_row = lax.broadcasted_iota(jnp.int32, (8, width), 0) == at.w
    line = spread(raw[8:16], 0)[0:1]
    for index in range(1, 4):
        line = line + spread(raw[8:16], index)[index : index + 1]
    small_own = s["small_own"]
    small_own[...] = jnp.concatenate(
        [spread(raw[:8], at.w), jnp.where(own_row, line, 0.0)], axis=0
    ).astype(BF16)
    for index, where in enumerate((at.to_x, at.to_y, at.to_d)):
        wire.send("sm" + str(index), small_own, s["small_in"].at[index], where)
    keeps = []
    for slot, (local, full) in enumerate(
        (
            (qkv_l, s["wqkv"].at[pl.ds(aligned(at.w * share, 16), share)]),
            (tokens, s["tok"].at[core]),
            (cot_l, s["cot"]),
            (out_l, s["wo"].at[pl.ds(aligned(at.w * share, 16), share)]),
            (up_l, s["wu"].at[pl.ds(aligned(at.w * share, 16), share)]),
            (down_l, s["wd"].at[pl.ds(aligned(at.w * (inner // 4), 16), inner // 4)]),
        )
    ):
        keeps.append(pltpu.make_async_copy(local, full, s["own_sems"].at[slot]))
        keeps[-1].start()
    wire.send("tok", tokens, s["tok"].at[core], at.sib)

    before = 0
    for head in range(heads):
        flag = pairing[head]
        spot = flag * (heads // 2 + before) + (1 - flag) * (head - before)
        before = before + flag
        row = lax.broadcasted_iota(jnp.int32, (size, width), 0)
        column = lax.broadcasted_iota(jnp.int32, (size, width), 1)
        s["order"][head * size : (head + 1) * size, :] = jnp.where(
            column - row == spot * size, 1.0, 0.0
        ).astype(BF16)

    part_kv.relay()
    part_q.relay()
    part_o.begin()
    part_u.begin()
    part_kv.share()
    for index in range(3):
        wire.arrived("sm" + str(index), s["small_in"].at[index])
    small = s["small"]
    small[...] = (
        small_own[...].astype(F32)
        + s["small_in"][0].astype(F32)
        + s["small_in"][1].astype(F32)
        + s["small_in"][2].astype(F32)
    )
    s["bias_qkv"][0:1, 0:width] = small[0:1, :]
    s["bias_qkv"][0:1, width : 2 * width] = jnp.zeros((1, width), F32)
    s["bias_qkv"][0:1, 2 * width :] = small[1:2, :]
    for index in range(inner // width):
        s["bias_up"][0:1, index * width : (index + 1) * width] = small[8 + index : 9 + index, :]
    keeps[0].wait()
    keeps[1].wait()
    part_kv.finish()

    tok, proj, order, kv = s["tok"], s["proj"], s["order"], s["kv"]
    own_slot = core * 2 + at.near

    def project(first, count):
        @pl.loop(first, first + count)
        def _(index):
            where = chunk_of(index, 256)
            made = nn(tok[core], s["wqkv"][:, where]) + s["bias_qkv"][0:1, where]
            proj[:, where] = made.astype(BF16)

    project(chunks, 2 * chunks)
    for index in range(chunks):
        columns = order[:, index * 256 : (index + 1) * 256]
        for kind in range(2):
            moved = nn(proj[:, (1 + kind) * width : (2 + kind) * width], columns).astype(BF16)
            for e in range(2):
                kv[2 * index + e, own_slot, :, kind * 128 : (kind + 1) * 128] = moved[
                    :, e * 128 : (e + 1) * 128
                ]
    near_base = wire.slot("near kv", pairs)
    far_base = wire.slot("far kv", pairs)
    pass_base = wire.slot("passed kv", pairs)

    def kv_copy(base, pair, slot, where):
        block = kv.at[pair, slot]
        return wire.copy(base + pair, block, block, where, "kv" + str(base))

    for pair in range(pairs):
        if pair < some:
            kv_copy(far_base, pair, own_slot, at.cross).start()
        kv_copy(near_base, pair, own_slot, at.sib).start()
    part_q.share()
    part_q.finish()
    project(0, chunks)
    q, q_out = s["q"], s["q_out"]
    for index in range(chunks):
        moved = nn(proj[:, 0:width], order[:, index * 256 : (index + 1) * 256]).astype(BF16)
        for e in range(2):
            pair = 2 * index + e
            block = moved[:, e * 128 : (e + 1) * 128]
            if pair < some:
                q[pair] = block
            else:
                q_out[pair - some] = block
    wire.send("queries", q_out, q.at[pl.ds(some, some)], at.partner)
    part_o.relay()
    part_d.begin()

    exps, inverse, out_t = s["exps"], s["inverse"], s["out_t"]

    def both(pair, first):
        return kv[pair, :, :, first : first + 128].reshape(keys, 128)

    def masked(block, e, axis=1):
        spot = lax.broadcasted_iota(jnp.int32, block.shape, axis)
        mine = spot < size if e == 0 else spot >= size
        return jnp.where(mine, block, jnp.zeros_like(block))

    def attend(pair):
        key_rows, value_rows = both(pair, 0), both(pair, 128)
        values_t = value_rows.T
        queries = q[pair] * jnp.asarray(size**-0.5, BF16)
        parts = []
        for e in range(2):
            scores = nt(key_rows, masked(queries, e))
            top = jnp.max(scores, axis=0, keepdims=True)
            raised = jnp.exp(scores - top)
            total = jnp.sum(raised, axis=0, keepdims=True)
            low = raised.astype(BF16)
            exps[2 * pair + e] = low
            s["tops"][2 * pair + e] = top
            one_over = 1.0 / total
            inverse[2 * pair + e] = one_over
            parts.append(nn(values_t[e * size : (e + 1) * size], low) * one_over)
        merged = jnp.concatenate(parts, axis=0)
        out_t[pair] = merged
        return merged.T.astype(BF16)

    def receive_kv(pair):
        kv_copy(far_base, pair, core * 2 + at.far, at.cross).wait_recv()
        kv_copy(pass_base, pair, core * 2 + at.far, at.sib).start()
        kv_copy(near_base, pair, other * 2 + at.near, at.sib).wait_recv()
        kv_copy(pass_base, pair, other * 2 + at.far, at.sib).wait_recv()

    ctx, ctx_out = s["ctx"], s["ctx_out"]
    back_base = wire.slot("ctx", some)

    def ctx_copy(index):
        return wire.copy(back_base + index, ctx_out.at[index], ctx.at[some + index], at.partner, "ctx")

    def attend_far(index):
        receive_kv(index + some)
        ctx_out[index] = attend(index + some)
        ctx_copy(index).start()

    @pl.loop(0, some)
    def _(index):
        receive_kv(index)
        kv_copy(far_base, index + some, own_slot, at.cross).start()
        ctx[index] = attend(index)

    part_o.share()
    wire.arrived("queries", q.at[pl.ds(some, some)])
    attend_far(0)
    part_u.relay()

    @pl.loop(1, some)
    def _(index):
        attend_far(index)

    part_o.finish()
    far_q, far_tops, far_delta, far_dos = (
        s[name] for name in ("far_q", "far_tops", "far_delta", "far_dos")
    )
    tops, delta, dos = s["tops"], s["delta"], s["dos"]
    wire.send("far q", q, far_q.at[core], at.cross)
    wire.send("far tops", tops, far_tops.at[core], at.cross)
    part_d.relay()
    keeps[2].wait()
    keeps[3].wait()
    for index in range(some):
        ctx_copy(index).wait_recv()
    permuted = jnp.concatenate([ctx[pair] for pair in range(pairs)], axis=1)
    ctx_nat, stage = s["ctx_nat"], s["stage"]
    for index in range(chunks):
        where = slice(index * 256, (index + 1) * 256)
        ctx_nat[core, :, where] = nt(permuted, order[where, :]).astype(BF16)
    wire.send("ctxn", ctx_nat.at[core], ctx_nat.at[core], at.sib)

    @pl.loop(0, chunks)
    def _(index):
        where = chunk_of(index, 256)
        stage[:, where] = nn(ctx_nat[core], s["wo"][:, where])

    hat_one, r_one, flow, hid = s["hat_one"], s["r_one"], s["flow"], s["hid"]
    inv_width = 1.0 / width

    def mean(values):
        return jnp.sum(values, axis=-1, keepdims=True) * inv_width

    @pl.loop(0, rows // BAND, unroll=4)
    def _(index):
        where = chunk_of(index, BAND)
        total = tok[core, where, :].astype(F32) + stage[where, :] + small[2:3, :]
        centred = total - mean(total)
        scale = lax.rsqrt(mean(centred * centred) + 1e-12)
        hat = centred * scale
        hat_one[where, :] = hat
        r_one[where, :] = scale
        hidden = hat * small[3:4, :] + small[4:5, :]
        flow[where, :] = hidden
        hid[core, where, :] = hidden.astype(BF16)

    wire.send("hid", hid.at[core], hid.at[core], at.sib)
    part_u.share()
    part_u.finish()
    keeps[4].wait()
    act, slope = s["act"], s["slope"]

    @pl.loop(0, inner // 256, unroll=3)
    def _(index):
        where = chunk_of(index, 256)
        pre = nn(hid[core], s["wu"][:, where]) + s["bias_up"][0:1, where]
        below = 0.5 * (1.0 + lax.erf(pre * (0.5**0.5)))
        act[core, :, where] = (pre * below).astype(BF16)
        density = jnp.exp(pre * pre * -0.5) * 0.3989422804014327
        slope[:, where] = (below + pre * density).astype(BF16)

    wire.send("act", act.at[core], act.at[core], at.sib)
    wire.arrived("far q", far_q.at[core])
    wire.send("passed q", far_q.at[core], far_q.at[core], at.sib)
    wire.arrived("far tops", far_tops.at[core])
    wire.send("passed tops", far_tops.at[core], far_tops.at[core], at.sib)
    part_d.near()
    keeps[5].wait()
    quarter = inner // 4

    def down(owner, where):
        block = pl.ds(aligned(owner * quarter, 128), quarter)
        return nn(act[core, :, block], s["wd"][block, where])

    @pl.loop(0, chunks)
    def _(index):
        where = chunk_of(index, 256)
        stage[:, where] = down(at.w, where) + down(at.nx, where) + down(at.ny, where)

    part_d.share()
    part_d.last()

    @pl.loop(0, chunks)
    def _(index):
        where = chunk_of(index, 256)
        stage[:, where] += down(at.nd, where)

    result, gf, cot = s["result"], s["gf"], s["cot"]
    sums, sums_up = s["sums"], s["sums_up"]
    sums[...] = jnp.zeros_like(sums)

    def gather_rows(values):
        return jnp.sum(values.reshape(BAND // 8, 8, values.shape[-1]), axis=0)

    @pl.loop(0, rows // BAND, unroll=4)
    def _(index):
        where = chunk_of(index, BAND)
        total = flow[where, :] + stage[where, :] + small[5:6, :]
        centred = total - mean(total)
        scale = lax.rsqrt(mean(centred * centred) + 1e-12)
        hat = centred * scale
        result[where, :] = hat * small[6:7, :] + small[7:8, :]
        back = cot[where, :].astype(F32)
        g = back * small[6:7, :]
        grad = scale * (g - mean(g) - hat * mean(g * hat))
        flow[where, :] = grad
        low = grad.astype(BF16)
        gf[where, :] = low
        sums[6] += gather_rows(back * hat)
        sums[7] += gather_rows(back)
        sums[5] += gather_rows(low.astype(F32))

    keep_out = pltpu.make_async_copy(result, output, s["own_sems"].at[7])
    keep_out.start()

    def columns_of(which, count):
        return pl.ds(aligned(which * count, 128), count)

    wire.send("gf", gf.at[:, columns_of(other, half)], s["gf_in"], at.sib)

    def buffers(name):
        return [s["g" + name + kind] for kind in ("fx", "fy", "dx", "dy", "lo", "hi")]

    dwd, wd, wu = s["dwd"], s["wd"], s["wu"]

    def side_by_side(first, count, owner):
        return wd.at[
            pl.ds(aligned(first + (owner // 2) * count, 16), count),
            pl.ds(aligned((owner % 2) * half, 128), half),
        ]

    def dwo(owner):
        return side_by_side(2 * width + 6 * share, share, owner)

    def dwq(owner):
        return side_by_side(2 * width, 3 * share, owner)

    grad_d = Grad(
        "gd",
        4,
        lambda r: dwd.at[r],
        buffers("d"),
        lambda i, k: g_down.at[pl.ds(i * (inner // 16), inner // 16), columns_of(k, half)],
        at,
        wire,
        s["own_sems"].at[8],
    )
    grad_u = Grad(
        "gu",
        4,
        lambda r: wd.at[pl.ds(aligned(r * (2 * share), 16), 2 * share), :],
        buffers("u"),
        lambda i, k: g_up.at[
            pl.ds((i % 2) * (share // 2), share // 2), columns_of(2 * k + i // 2, width)
        ],
        at,
        wire,
        s["own_sems"].at[9],
    )
    grad_o = Grad(
        "go",
        1,
        dwo,
        buffers("o"),
        lambda i, k: g_out.at[:, columns_of(k, half)],
        at,
        wire,
        s["own_sems"].at[10],
    )
    grad_q = Grad(
        "gq",
        6,
        dwq,
        buffers("q"),
        lambda i, k: g_qkv.at[
            pl.ds((i % 2) * (share // 2), share // 2), columns_of(3 * k + i // 2, half)
        ],
        at,
        wire,
        s["own_sems"].at[11],
    )

    def back_through(first, last):
        @pl.loop(first, last, unroll=3)
        def _(index):
            where = chunk_of(index, 256)
            grad = nt(gf[...], wd[where, :]) * slope[:, where].astype(F32)
            low = grad.astype(BF16)
            slope[:, where] = low
            sums_up[:, where] = jnp.sum(low.astype(F32).reshape(rows // 8, 8, 256), axis=0)

    back_through(0, inner // 512)
    wire.arrived("act", act.at[other])
    wire.arrived("gf", s["gf_in"])

    def down_grad(owner):
        where = pl.ds(aligned(owner * quarter, 128), quarter)
        made = nn(act[core, :, where].T, gf[:, columns_of(core, half)])
        made = made + nn(act[other, :, where].T, s["gf_in"][...])
        dwd[owner] = made.astype(BF16)

    down_grad(at.nd)
    grad_d.begin()
    back_through(inner // 512, inner // 256)
    wire.send("slope", slope.at[:, columns_of(other, inner // 2)], s["slope_in"], at.sib)

    @pl.loop(0, chunks)
    def _(index):
        where = chunk_of(index, 256)
        stage[:, where] = nt(slope[...], wu[where, :])


    gb = s["gb"]

    @pl.loop(0, rows // BAND, unroll=4)
    def _(index):
        where = chunk_of(index, BAND)
        grad_hidden = flow[where, :] + stage[where, :]
        hat = hat_one[where, :]
        g = grad_hidden * small[3:4, :]
        grad = r_one[where, :] * (g - mean(g) - hat * mean(g * hat))
        flow[where, :] = grad
        low = grad.astype(BF16)
        gb[where, :] = low
        sums[3] += gather_rows(grad_hidden * hat)
        sums[4] += gather_rows(grad_hidden)
        sums[2] += gather_rows(low.astype(F32))

    wire.send("gb", gb.at[:, columns_of(other, half)], s["gb_in"], at.sib)

    @pl.loop(0, chunks)
    def _(index):
        where = chunk_of(index, 256)
        proj[:, where] = nt(gb[...], s["wo"][where, :]).astype(BF16)

    do, do_out = s["do"], s["do_out"]
    for index in range(chunks):
        moved = nn(proj[:, 0:width], order[:, index * 256 : (index + 1) * 256]).astype(BF16)
        for e in range(2):
            pair = 2 * index + e
            block = moved[:, e * 128 : (e + 1) * 128]
            if pair < some:
                do[pair] = block
            else:
                do_out[pair - some] = block
    wire.send("do", do_out, do.at[pl.ds(some, some)], at.partner)

    def prepare(pair):
        do_t = do[pair].astype(F32).T
        scaled = jnp.concatenate(
            [do_t[e * size : (e + 1) * size] * inverse[2 * pair + e] for e in range(2)], axis=0
        )
        product = scaled * out_t[pair]
        for e in range(2):
            delta[2 * pair + e] = jnp.sum(product[e * size : (e + 1) * size], axis=0, keepdims=True)
        dos[pair] = scaled.T.astype(BF16)

    group_d = [pl.ds(0, some), pl.ds(some, some)]
    group_h = [pl.ds(0, 2 * some), pl.ds(2 * some, 2 * some)]

    def send_group(g):
        wire.send(
            "far do" + str(g), dos.at[group_d[g]], far_dos.at[core, group_d[g]], at.cross
        )
        wire.send(
            "far de" + str(g), delta.at[group_h[g]], far_delta.at[core, group_h[g]], at.cross
        )

    def pass_group(g):
        for kind, ref, group in (("do", far_dos, group_d), ("de", far_delta, group_h)):
            block = ref.at[core, group[g]]
            wire.arrived("far " + kind + str(g), block)
            wire.send("passed " + kind + str(g), block, block, at.sib)

    def have_group(g):
        wire.arrived("passed do" + str(g), far_dos.at[other, group_d[g]])
        wire.arrived("passed de" + str(g), far_delta.at[other, group_h[g]])

    @pl.loop(0, some)
    def _(index):
        prepare(index)

    send_group(0)
    for owner in (at.nx, at.ny):
        down_grad(owner)
    grad_d.push((0, 1), (2, 3))
    down_grad(at.w)
    grad_d.fold()
    grad_d.push((2, 3), (0, 1))

    part_d.gone()
    wire.arrived("hid", hid.at[other])
    wire.arrived("slope", s["slope_in"])
    mine_t, theirs_t = hid[core].T, hid[other].T
    for index in range(inner // 2 // half):
        where = pl.ds(aligned(core * (inner // 2) + index * half, 128), half)
        made = nn(mine_t, slope[:, where]) + nn(
            theirs_t, s["slope_in"][:, index * half : (index + 1) * half]
        )
        made = made.astype(BF16)
        for owner in range(4):
            first = owner * 2 * share + (index // 2) * share
            wd[first : first + share, (index % 2) * half : (index % 2 + 1) * half] = made[
                owner * share : (owner + 1) * share
            ]
    grad_u.begin()
    grad_u.push((0,), (2,))
    wire.arrived("ctxn", ctx_nat.at[other])
    wire.arrived("gb", s["gb_in"])
    made = nn(ctx_nat[core].T, gb[:, columns_of(core, half)]) + nn(
        ctx_nat[other].T, s["gb_in"][...]
    )
    made = made.astype(BF16)
    for owner in range(4):
        dwo(owner)[...] = made[owner * share : (owner + 1) * share]
    grad_o.begin()

    part_u.gone()
    dq, dq_out, dkv_in = s["dq"], s["dq_out"], s["dkv_in"]
    near_d = wire.slot("near dkv", pairs)
    dq_base = wire.slot("dq", some)
    lots = inner // 512

    def tile(pair, which):
        return wu.at[
            pl.ds(aligned((pair // lots) * rows, 16), rows),
            pl.ds(aligned((pair % lots) * 512 + which * 256, 256), 256),
        ]

    def dkv_near(pair):
        return wire.copy(near_d + pair, tile(pair, other), dkv_in.at[pair], at.sib, "near dkv")

    def two_blocks(pair, chip, first):
        return jnp.concatenate(
            [kv[pair, k * 2 + chip, :, first : first + 128] for k in range(2)], axis=0
        )

    def attend_back(pair):
        queries = q[pair] * jnp.asarray(size**-0.5, BF16)
        dq_parts = [None, None]
        dv = dk = None
        for chip in (at.near, at.far):
            key_rows, value_rows = two_blocks(pair, chip, 0), two_blocks(pair, chip, 128)
            keys_t = key_rows.T
            for e in range(2):
                low = jnp.concatenate(
                    [
                        exps[2 * pair + e, pl.ds(aligned((k * 2 + chip) * rows, 16), rows), :]
                        for k in range(2)
                    ],
                    axis=0,
                )
                mine = masked(dos[pair], e)
                grad_w = nt(value_rows, mine)
                grad_s = (low.astype(F32) * (grad_w - delta[2 * pair + e])).astype(BF16)
                more_q = nn(keys_t[e * size : (e + 1) * size], grad_s)
                dq_parts[e] = more_q if dq_parts[e] is None else dq_parts[e] + more_q
                if chip is at.near:
                    more_v = nn(low, mine)
                    more_k = nn(grad_s, masked(queries, e))
                    dv = more_v if dv is None else dv + more_v
                    dk = more_k if dk is None else dk + more_k
            if chip is at.near:
                made = jnp.concatenate([dk, dv], axis=1).astype(BF16)
                for k in range(2):
                    tile(pair, k)[...] = made[k * rows : (k + 1) * rows]
                dkv_near(pair).start()
        return (jnp.concatenate(dq_parts, axis=0).T * size**-0.5).astype(BF16)

    gkv = s["gkv"]

    def far_back(pair):
        queries = far_q[:, pair].reshape(2 * rows, 128) * jnp.asarray(size**-0.5, BF16)
        grads = far_dos[:, pair].reshape(2 * rows, 128)
        key_rows, value_rows = kv[pair, own_slot, :, 0:128], kv[pair, own_slot, :, 128:256]
        dv = dk = None
        for e in range(2):
            head = 2 * pair + e
            top = jnp.concatenate([far_tops[k, head] for k in range(2)], axis=1)
            less = jnp.concatenate([far_delta[k, head] for k in range(2)], axis=1)
            mine, asking = masked(grads, e), masked(queries, e)
            low = jnp.exp(nt(key_rows, asking) - top).astype(BF16)
            grad_s = (low.astype(F32) * (nt(value_rows, mine) - less)).astype(BF16)
            more_v, more_k = nn(low, mine), nn(grad_s, asking)
            dv = more_v if dv is None else dv + more_v
            dk = more_k if dk is None else dk + more_k
        dkv_near(pair).wait_recv()
        own = tile(pair, core)
        where = pl.ds(aligned(pair * 128, 128), 128)
        for kind, made in ((0, dk), (1, dv)):
            cut = slice(kind * 128, (kind + 1) * 128)
            gkv[kind, :, where] = (
                made + own[:, cut].astype(F32) + dkv_in[pair, :, cut].astype(F32)
            ).astype(BF16)

    def dq_copy(index):
        return wire.copy(dq_base + index, dq_out.at[index], dq.at[some + index], at.partner, "dq")

    @pl.loop(0, some)
    def _(index):
        dq[index] = attend_back(index)

    wire.arrived("do", do.at[pl.ds(some, some)])

    @pl.loop(some, pairs)
    def _(index):
        prepare(index)

    send_group(1)
    pass_group(0)
    grad_d.own(0)

    @pl.loop(0, some)
    def _(index):
        dq_out[index] = attend_back(index + some)
        dq_copy(index).start()

    for chunk in (2, 1, 3):
        grad_d.own(chunk)
    pass_group(1)
    wire.arrived("passed q", far_q.at[other])
    wire.arrived("passed tops", far_tops.at[other])
    have_group(0)

    @pl.loop(0, some)
    def _(index):
        far_back(index)

    grad_d.chain(0)
    grad_u.fold()
    grad_u.push((1, 2), (0, 1))
    wire.left(*[name for name in wire.started if name[:2] not in ("gd", "gu", "go")])
    part_kv.gone()
    part_q.gone()
    part_o.gone()
    for base in (far_base, near_base, pass_base):
        wire.gone("kv" + str(base), kv.at[:, 0])
    wire.gone("ctx", ctx_out)
    have_group(1)

    @pl.loop(some, pairs)
    def _(index):
        far_back(index)

    for index in range(some):
        dq_copy(index).wait_recv()
    merged = jnp.concatenate([dq[pair] for pair in range(pairs)], axis=1)
    for index in range(chunks):
        where = slice(index * 256, (index + 1) * 256)
        rows_of = order[where, :]
        for kind in range(3):
            source = merged if kind == 0 else gkv[kind - 1]
            low = nt(source, rows_of).astype(BF16)
            proj[:, kind * width + index * 256 : kind * width + (index + 1) * 256] = low
            if kind != 1:
                sums[kind // 2, :, where] = jnp.sum(
                    low.astype(F32).reshape(rows // 8, 8, 256), axis=0
                )
    wire.send("gj", proj.at[:, columns_of(other, 3 * half)], s["gj_in"], at.sib)

    vec, vec_in, vec_low, vec_far = s["vec"], s["vec_in"], s["vec_low"], s["vec_far"]
    for row in range(8):
        vec[row : row + 1, :] = jnp.sum(sums[row], axis=0, keepdims=True)
    for index in range(inner // width):
        vec[8 + index : 9 + index, :] = jnp.sum(
            sums_up[:, index * width : (index + 1) * width], axis=0, keepdims=True
        )
    for row in range(8 + inner // width, 16):
        vec[row : row + 1, :] = jnp.zeros((1, width), F32)
    wire.send("va", vec, vec_in, at.sib)

    grad_d.chain(2)
    grad_d.total(0)
    wire.arrived("tok", tok.at[other])
    wire.arrived("gj", s["gj_in"])
    mine_t, theirs_t = tok[core].T, tok[other].T
    for index in range(3):
        where = pl.ds(aligned(core * (3 * half) + index * half, 128), half)
        made = nn(mine_t, proj[:, where]) + nn(
            theirs_t, s["gj_in"][:, index * half : (index + 1) * half]
        )
        made = made.astype(BF16)
        for owner in range(4):
            dwq(owner)[index * share : (index + 1) * share, :] = made[
                owner * share : (owner + 1) * share
            ]
    grad_q.begin()
    grad_u.push((3,), (3,))
    grad_o.fold()
    grad_o.push((0,), (0,))
    grad_u.own(0)
    grad_d.chain(1)
    grad_d.total(2)
    wire.arrived("va", vec_in)
    vec_low[0] = (vec_in[...] + vec[...]).astype(BF16)
    for index, where in enumerate((at.to_x, at.to_y, at.to_d)):
        wire.send("vb" + str(index), vec_low.at[0], vec_far.at[index], where)

    keep_out.wait()

    @pl.loop(0, chunks)
    def _(index):
        where = chunk_of(index, 256)
        result[:, where] = nt(proj[...], s["wqkv"][where, :]) + flow[:, where]

    keep_grad = pltpu.make_async_copy(result, grad_tokens, s["own_sems"].at[7])
    keep_grad.start()
    def vec_hop(name, place, far, where):
        return wire.copy(wire.slot(name), vec_low.at[place], vec_far.at[far], where, name)

    def vec_out():
        return vec_hop("vu", 1, 3, at.mate)

    def vec_across():
        return vec_hop("vv", 2, 4, at.middle)

    def vec_back():
        return vec_hop("vt", 3, 5, at.mate)

    def vec_sum(*parts):
        total = parts[0].astype(F32)
        for part in parts[1:]:
            total = total + part.astype(F32)
        return total

    grad_u.own(1)
    grad_d.chain(3)
    grad_d.total(1)
    grad_u.own(2)
    grad_u.chain(0)
    grad_q.fold()
    grad_q.push((0, 1, 2, 3, 4, 5), (0, 1, 2, 3, 4, 5))
    grad_d.total(3)
    grad_u.total(0)
    grad_u.chain(1)
    grad_u.own(3)
    grad_u.chain(2)
    grad_u.total(1)
    grad_o.own(0)
    grad_u.total(2)
    grad_q.own(0)
    grad_u.chain(3)
    grad_q.own(1)
    for index in range(3):
        wire.arrived("vb" + str(index), vec_far.at[index])
    vec_low[1] = (
        vec_sum(vec_low[0], vec_far[0]) + vec_sum(vec_far[1], vec_far[2])
    ).astype(BF16)

    @pl.when(at.outer)
    def _():
        vec_out().start()

    grad_o.chain(0)
    grad_u.total(3)
    grad_q.own(2)
    grad_q.chain(0)
    grad_q.chain(1)
    grad_q.own(3)

    @pl.when(at.inner)
    def _():
        vec_out().wait_recv()
        vec_low[2] = vec_sum(vec_low[1], vec_far[3]).astype(BF16)
        vec_across().start()

    grad_q.chain(2)
    grad_o.total(0)
    grad_q.total(0)
    grad_q.own(4)
    grad_q.chain(3)
    grad_q.total(1)
    grad_q.own(5)
    grad_q.chain(4)
    grad_q.total(2)
    grad_q.chain(5)
    grad_q.total(3)

    @pl.when(at.inner)
    def _():
        vec_across().wait_recv()
        total = vec_sum(vec_low[2], vec_far[4]).astype(BF16)
        vec_low[3] = total
        vec_back().start()
        vec_in[...] = total.astype(F32)

    grad_q.total(4)
    grad_q.total(5)
    for chunk in range(4):
        grad_d.give(chunk)
    for chunk in range(4):
        grad_u.give(chunk)
    grad_o.give(0)
    for chunk in range(4):
        grad_q.give(chunk)

    @pl.when(at.outer)
    def _():
        vec_back().wait_recv()
        vec_in[...] = vec_far[5].astype(F32)

    keep_small = pltpu.make_async_copy(vec_in, g_small, s["own_sems"].at[6])
    keep_small.start()
    grad_q.give(4)
    grad_q.give(5)

    @pl.when(at.outer)
    def _():
        vec_out().wait_send()

    @pl.when(at.inner)
    def _():
        vec_across().wait_send()
        vec_back().wait_send()

    grad_d.close()
    grad_u.close()
    grad_o.close()
    grad_q.close()
    keep_grad.wait()
    keep_small.wait()
    wire.gone("near dkv", dkv_in)
    wire.gone("dq", dq_out)
    wire.close()


def whole_layer(tokens, cotangent, pairing, small_raw, w_qkv, w_out, w_up, w_down):
    rows, width = tokens.shape
    inner = w_up.shape[1]
    scratch = layer_scratch(rows, width, inner, pairing.shape[0])
    hbm = pl.BlockSpec(memory_space=pl.ANY)
    vmem = pl.BlockSpec(memory_space=pltpu.VMEM)
    smem = pl.BlockSpec(memory_space=pltpu.SMEM)
    return pl.pallas_call(
        functools.partial(layer_kernel, tuple(scratch)),
        out_shape=[
            jax.ShapeDtypeStruct((rows, width), F32),
            jax.ShapeDtypeStruct((rows, width), F32),
            jax.ShapeDtypeStruct(w_qkv.shape, BF16),
            jax.ShapeDtypeStruct(w_out.shape, BF16),
            jax.ShapeDtypeStruct(w_up.shape, BF16),
            jax.ShapeDtypeStruct(w_down.shape, BF16),
            jax.ShapeDtypeStruct((16, width), F32),
        ],
        in_specs=[hbm, hbm, smem, vmem, hbm, hbm, hbm, hbm],
        out_specs=[hbm] * 7,
        scratch_shapes=list(scratch.values()),
        compiler_params=pltpu.CompilerParams(
            collective_id=0, has_side_effects=True, vmem_limit_bytes=60 << 20
        ),
        name="whole_layer",
    )(tokens, cotangent, pairing, small_raw, w_qkv, w_out, w_up, w_down)


def finish_kernel(share, *refs):
    wide, small, outs = refs[:6], refs[6], refs[7:]
    for source, target in zip(wide, outs[:6]):
        target[...] = source[...].astype(F32)

    @pl.when(pl.program_id(0) == 0)
    def _():
        w = lax.axis_index("wt")
        values = small[...]
        mine = jnp.zeros((8, share), F32)
        line = jnp.zeros((1, 4 * share), F32)
        for owner in range(4):
            mine = mine + jnp.where(
                w == owner, values[:8, owner * share : (owner + 1) * share], 0.0
            )
            line = line + jnp.where(w == owner, values[8 + owner : 9 + owner], 0.0)
        for row in range(8):
            outs[6 + row][...] = mine[row : row + 1]
        outs[14][...] = line.reshape(4 * share)


def finish(*arrays):
    steps = 2
    wide, small = arrays[:6], arrays[6]
    share = small.shape[1] // 4

    def blocks(array):
        return pl.BlockSpec((array.shape[0] // steps, array.shape[1]), lambda i: (i, 0))

    def fixed(shape):
        return pl.BlockSpec(shape, lambda i: (0,) * len(shape))

    shapes = [(1, share)] * 8 + [(4 * share,)]
    return pl.pallas_call(
        functools.partial(finish_kernel, share),
        grid=(steps,),
        out_shape=[jax.ShapeDtypeStruct(v.shape, F32) for v in wide]
        + [jax.ShapeDtypeStruct(v, F32) for v in shapes],
        in_specs=[blocks(v) for v in wide] + [fixed(small.shape)],
        out_specs=[blocks(v) for v in wide] + [fixed(v) for v in shapes],
        compiler_params=pltpu.CompilerParams(vmem_limit_bytes=60 << 20),
        name="finish",
    )(*arrays)


far_below = -1e30


def passed_along(value, axis, steps):
    count = lax.axis_size(axis)
    pairs = [(source, (source + steps) % count) for source in range(count)]
    return lax.ppermute(value, axis, pairs)


def norm_rows(values, gains, shifts):
    average = jnp.mean(values, axis=-1, keepdims=True)
    centred = values - average
    spread = jnp.mean(centred * centred, axis=-1, keepdims=True)
    return centred * lax.rsqrt(spread + 1e-12) * gains + shifts


def gelu_exact(pre_active):
    return jax.nn.gelu(pre_active, approximate=False)


def scores_of(queries, key_heads):
    return (
        jnp.einsum("thd,khd->htk", queries, key_heads, preferred_element_type=jnp.float32) * 0.125
    )


def unchanged(running):
    return running


def general_layer(
    tokens,
    pairing,
    w_qkv,
    bias_q,
    bias_v,
    w_out,
    bias_out,
    gain_one,
    shift_one,
    w_up,
    bias_up,
    w_down,
    bias_down,
    gain_two,
    shift_two,
    cotangent,
):
    local_params = (
        w_qkv,
        bias_q,
        bias_v,
        w_out,
        bias_out,
        gain_one,
        shift_one,
        w_up,
        bias_up,
        w_down,
        bias_down,
        gain_two,
        shift_two,
    )
    gathered = tuple(lax.all_gather(v, "wt", axis=0, tiled=True) for v in local_params)
    (
        wqkv_full,
        biasq_full,
        biasv_full,
        wout_full,
        biasout_full,
        gainone_full,
        shiftone_full,
        wup_full,
        biasup_full,
        wdown_full,
        biasdown_full,
        gaintwo_full,
        shifttwo_full,
    ) = gathered
    tok_rows = tokens.shape[1]
    model_width = tokens.shape[2]
    head_count = pairing.shape[0]
    head_size = model_width // head_count
    group_size = lax.axis_size("ctx")
    position_ctx = lax.axis_index("ctx")
    half_len = tok_rows * group_size // 2
    own_half = position_ctx * tok_rows // half_len
    flipped = pairing == 1
    inputs = tokens[0]
    bias_cat = jnp.concatenate(
        [
            biasq_full.astype(jnp.float32),
            jnp.zeros((model_width,), jnp.float32),
            biasv_full.astype(jnp.float32),
        ]
    )
    projected = jnp.dot(inputs, wqkv_full, preferred_element_type=jnp.float32) + bias_cat
    projected_low = projected.astype(jnp.bfloat16)
    queries = projected_low[:, :model_width].reshape(tok_rows, head_count, head_size)
    key_rows = projected_low[:, model_width : 2 * model_width]
    value_rows = projected_low[:, 2 * model_width :]

    def online_update(state, portion_keys, portion_values, needed):
        row_top, row_total, accumulated = state
        key_count = portion_keys.shape[0]
        key_heads = portion_keys.reshape(key_count, head_count, head_size)
        value_heads = portion_values.reshape(key_count, head_count, head_size)
        scores = scores_of(queries, key_heads)
        scores = jnp.where(needed[:, None, :], scores, far_below)
        new_top = jnp.maximum(row_top, jnp.max(scores, axis=-1))
        factor = jnp.exp(row_top - new_top)
        weights = jnp.exp(scores - new_top[..., None])
        row_total = jnp.sum(weights, axis=-1)
        added = jnp.einsum(
            "htk,khd->thd",
            weights.astype(jnp.bfloat16),
            value_heads,
            preferred_element_type=jnp.float32,
        )
        accumulated = accumulated * factor.T[..., None] + added
        return (new_top, row_total, accumulated)

    start_state = (
        jnp.full((head_count, tok_rows), far_below, jnp.float32),
        jnp.zeros((head_count, tok_rows), jnp.float32),
        jnp.zeros((tok_rows, head_count, head_size), jnp.float32),
    )

    def wanted(offset, key_count):
        key_half = (offset + jnp.arange(key_count)) // half_len
        target = jnp.where(flipped, 1 - own_half, own_half)
        return key_half[None, :] == target[:, None]

    portion_keys = lax.all_gather(key_rows, "ctx", axis=0, tiled=True)
    portion_values = lax.all_gather(value_rows, "ctx", axis=0, tiled=True)
    needed = wanted(jnp.int32(0), portion_keys.shape[0])

    def update(state):
        return online_update(state, portion_keys, portion_values, needed)

    row_top, row_total, accumulated = lax.cond(jnp.any(needed), update, unchanged, start_state)
    context = accumulated / row_total.T[..., None]
    log_sum = row_top + jnp.log(row_total)
    context_low = context.reshape(tok_rows, model_width).astype(jnp.bfloat16)
    branch = jnp.dot(
        context_low, wout_full, preferred_element_type=jnp.float32
    ) + biasout_full.astype(jnp.float32)
    summed_one = inputs.astype(jnp.float32) + branch
    hidden, norm_one_back = jax.vjp(
        norm_rows, summed_one, gainone_full.astype(jnp.float32), shiftone_full.astype(jnp.float32)
    )
    hidden_low = hidden.astype(jnp.bfloat16)
    pre_active = jnp.dot(
        hidden_low, wup_full, preferred_element_type=jnp.float32
    ) + biasup_full.astype(jnp.float32)
    active, gelu_back = jax.vjp(gelu_exact, pre_active)
    active_low = active.astype(jnp.bfloat16)
    ffn_out = jnp.dot(
        active_low, wdown_full, preferred_element_type=jnp.float32
    ) + biasdown_full.astype(jnp.float32)
    output, norm_two_back = jax.vjp(
        norm_rows,
        hidden + ffn_out,
        gaintwo_full.astype(jnp.float32),
        shifttwo_full.astype(jnp.float32),
    )
    again = gathered
    wqkv_back = again[0]
    wout_back = again[3]
    wup_back = again[7]
    wdown_back = again[9]
    grad_two, grad_gain_two, grad_shift_two = norm_two_back(cotangent[0].astype(jnp.float32))
    grad_ffn = grad_two.astype(jnp.bfloat16)
    grad_bias_down = jnp.sum(grad_ffn.astype(jnp.float32), axis=0)
    grad_w_down = jnp.einsum("tf,td->fd", active_low, grad_ffn, preferred_element_type=jnp.float32)
    grad_active = jnp.einsum("td,fd->tf", grad_ffn, wdown_back, preferred_element_type=jnp.float32)
    (grad_pre_f,) = gelu_back(grad_active)
    grad_pre = grad_pre_f.astype(jnp.bfloat16)
    grad_bias_up = jnp.sum(grad_pre.astype(jnp.float32), axis=0)
    grad_w_up = jnp.einsum("tc,tf->cf", hidden_low, grad_pre, preferred_element_type=jnp.float32)
    grad_hidden = grad_two + jnp.einsum(
        "tf,cf->tc", grad_pre, wup_back, preferred_element_type=jnp.float32
    )
    grad_one, grad_gain_one, grad_shift_one = norm_one_back(grad_hidden)
    grad_branch = grad_one.astype(jnp.bfloat16)
    grad_bias_out = jnp.sum(grad_branch.astype(jnp.float32), axis=0)
    grad_w_out = jnp.einsum(
        "tc,td->cd", context_low, grad_branch, preferred_element_type=jnp.float32
    )
    grad_context = jnp.einsum(
        "td,cd->tc", grad_branch, wout_back, preferred_element_type=jnp.float32
    )
    grad_context = grad_context.astype(jnp.bfloat16).reshape(tok_rows, head_count, head_size)
    row_delta = jnp.sum(grad_context.astype(jnp.float32) * context, axis=-1).T

    def piece_grads(portion_keys, portion_values, needed):
        key_count = portion_keys.shape[0]
        key_heads = portion_keys.reshape(key_count, head_count, head_size)
        value_heads = portion_values.reshape(key_count, head_count, head_size)
        scores = scores_of(queries, key_heads)
        scores = jnp.where(needed[:, None, :], scores, far_below)
        probs = jnp.exp(scores - log_sum[..., None])
        probs_low = probs.astype(jnp.bfloat16)
        piece_v = jnp.einsum(
            "htk,thd->khd", probs_low, grad_context, preferred_element_type=jnp.float32
        ).reshape(key_count, model_width)
        grad_weights = jnp.einsum(
            "thd,khd->htk", grad_context, value_heads, preferred_element_type=jnp.float32
        )
        grad_scores = (probs * (grad_weights - row_delta[..., None])).astype(jnp.bfloat16)
        piece_q = 0.125 * jnp.einsum(
            "htk,khd->thd", grad_scores, key_heads, preferred_element_type=jnp.float32
        )
        piece_k = 0.125 * jnp.einsum(
            "htk,thd->khd", grad_scores, queries, preferred_element_type=jnp.float32
        ).reshape(key_count, model_width)
        return (piece_k, piece_v, piece_q)

    zero_queries = jnp.zeros((tok_rows, head_count, head_size), jnp.float32)

    def circle_step(step_index, running):
        turn_keys, turn_values, grad_keys, grad_values, grad_queries = running
        owner = (position_ctx - step_index) % group_size
        needed = wanted(owner * tok_rows, tok_rows)

        def update_grads(state):
            grad_k, grad_v, grad_q = state
            piece_k, piece_v, piece_q = piece_grads(turn_keys, turn_values, needed)
            return (grad_k + piece_k, grad_v + piece_v, grad_q + piece_q)

        grad_keys, grad_values, grad_queries = lax.cond(
            jnp.any(needed), update_grads, unchanged, (grad_keys, grad_values, grad_queries)
        )
        turn_keys, turn_values = passed_along((turn_keys, turn_values), "ctx", 1)
        grad_keys, grad_values = (
            passed_along(grad_keys.astype(jnp.bfloat16), "ctx", 1).astype(grad_keys.dtype),
            passed_along(grad_values.astype(jnp.bfloat16), "ctx", 1).astype(grad_values.dtype),
        )
        return (turn_keys, turn_values, grad_keys, grad_values, grad_queries)

    zero_rows = jnp.zeros((tok_rows, model_width), jnp.float32)
    circle_start = (key_rows, value_rows, zero_rows, zero_rows, zero_queries)
    circle_end = lax.fori_loop(0, group_size, circle_step, circle_start)
    grad_keys = circle_end[2]
    grad_values = circle_end[3]
    grad_queries = circle_end[4]
    grad_projected = jnp.concatenate(
        [grad_queries.reshape(tok_rows, model_width), grad_keys, grad_values], axis=1
    ).astype(jnp.bfloat16)
    grad_bias_q = jnp.sum(grad_projected[:, :model_width].astype(jnp.float32), axis=0)
    grad_bias_v = jnp.sum(grad_projected[:, 2 * model_width :].astype(jnp.float32), axis=0)
    grad_w_qkv = jnp.einsum("tc,tj->cj", inputs, grad_projected, preferred_element_type=jnp.float32)
    grad_inputs = grad_one + jnp.einsum(
        "tj,cj->tc", grad_projected, wqkv_back, preferred_element_type=jnp.float32
    )
    terms = (
        grad_w_qkv,
        grad_bias_q,
        grad_bias_v,
        grad_w_out,
        grad_bias_out,
        grad_gain_one,
        grad_shift_one,
        grad_w_up,
        grad_bias_up,
        grad_w_down,
        grad_bias_down,
        grad_gain_two,
        grad_shift_two,
    )
    owned = tuple(
        lax.psum_scatter(term.astype(jnp.bfloat16), "wt", scatter_dimension=0, tiled=True)
        for term in terms
    )
    totals = tuple(lax.psum(term, "ctx").astype(jnp.float32) for term in owned)
    return (
        output[None],
        grad_inputs[None],
        totals[0],
        totals[1],
        totals[2],
        totals[3],
        totals[4],
        totals[5],
        totals[6],
        totals[7],
        totals[8],
        totals[9],
        totals[10],
        totals[11],
        totals[12],
    )


def fast_layer(
    tokens,
    pairing,
    w_qkv,
    bias_q,
    bias_v,
    w_out,
    bias_out,
    gain_one,
    shift_one,
    w_up,
    bias_up,
    w_down,
    bias_down,
    gain_two,
    shift_two,
    cotangent,
):
    share = tokens.shape[2] // 4
    vectors = (bias_q, bias_v, bias_out, gain_one, shift_one, bias_down, gain_two, shift_two)
    vectors = vectors + tuple(bias_up[k * share : (k + 1) * share] for k in range(4))
    row = lax.broadcasted_iota(jnp.int32, (16, share), 0)
    small_raw = jnp.zeros((16, share), jnp.bfloat16)
    for index, vector in enumerate(vectors):
        small_raw = jnp.where(row == index, vector[None, :], small_raw)
    made = whole_layer(
        tokens[0], cotangent[0], pairing, small_raw, w_qkv, w_out, w_up, w_down
    )
    output, grad_tokens, g_qkv, g_out, g_up, g_down, *small = finish(*made)
    small = [v.reshape(-1) for v in small]
    return (
        output[None],
        grad_tokens[None],
        g_qkv,
        small[0],
        small[1],
        g_out,
        small[2],
        small[3],
        small[4],
        g_up,
        small[8],
        g_down,
        small[5],
        small[6],
        small[7],
    )


def local(tokens, pairing, *rest):
    rows, width = tokens.shape[1:]
    heads = pairing.shape[0]
    inner = rest[7].shape[1]
    fits = (
        lax.axis_size("wt") == 4
        and lax.axis_size("ctx") == 8
        and tokens.shape[0] == 1
        and rows % BAND == 0
        and 3 * rows <= width
        and width % 256 == 0
        and heads % 4 == 0
        and width == 64 * heads
        and inner == 4 * width
    )
    layer = fast_layer if fits else general_layer
    return layer(tokens, pairing, *rest)


def solution(mesh):
    in_specs = (
        P("wt", "ctx", None),
        P(),
        P("wt", None),
        P("wt"),
        P("wt"),
        P("wt", None),
        P("wt"),
        P("wt"),
        P("wt"),
        P("wt", None),
        P("wt"),
        P("wt", None),
        P("wt"),
        P("wt"),
        P("wt"),
        P("wt", "ctx", None),
    )
    out_specs = (
        P("wt", "ctx", None),
        P("wt", "ctx", None),
        P("wt", None),
        P("wt"),
        P("wt"),
        P("wt", None),
        P("wt"),
        P("wt"),
        P("wt"),
        P("wt", None),
        P("wt"),
        P("wt", None),
        P("wt"),
        P("wt"),
        P("wt"),
    )
    return jax.shard_map(local, mesh=mesh, in_specs=in_specs, out_specs=out_specs, check_vma=False)
```

```python
import functools

import jax
import jax.numpy as jnp
from jax import lax
from jax.experimental import pallas as pl
from jax.experimental.pallas import tpu as pltpu
from jax.sharding import PartitionSpec as P

F32, BF16 = jnp.float32, jnp.bfloat16
MESH = pl.DeviceIdType.MESH
BAND = 32


def nn(a, b):
    return jnp.dot(a, b, preferred_element_type=F32)


def nt(a, b):
    return lax.dot_general(a, b, (((1,), (1,)), ((), ())), preferred_element_type=F32)


def aligned(start, multiple):
    return start if isinstance(start, int) else pl.multiple_of(start, multiple)


def chunk_of(index, size):
    return pl.ds(aligned(index * size, size), size)


class Wire:
    def __init__(self, sends, receives, anyone):
        self.sends, self.receives, self.anyone = sends, receives, anyone
        self.firsts, self.used, self.groups, self.started = {}, 0, {}, {}

    def slot(self, name, count=1):
        if name not in self.firsts:
            self.firsts[name] = self.used, count
            self.used += count
            assert self.used <= self.receives.shape[0]
        first, had = self.firsts[name]
        assert had == count
        return first

    def copy(self, slot, source, target, where, group):
        place = self.groups.setdefault(group, len(self.groups))
        assert place < self.sends.shape[0]
        return pltpu.make_async_remote_copy(
            src_ref=source,
            dst_ref=target,
            send_sem=self.sends.at[place],
            recv_sem=self.receives.at[slot],
            device_id=where,
            device_id_type=MESH,
        )

    def send(self, name, source, target, where):
        copy = self.copy(self.slot(name), source, target, where, name)
        copy.start()
        self.started[name] = copy

    def send_in(self, group, name, source, target, where):
        self.copy(self.slot(name), source, target, where, group).start()

    def gone(self, group, ref):
        self.copy(0, ref, ref, self.anyone, group).wait_send()

    def arrived(self, name, target):
        self.copy(self.slot(name), target, target, self.anyone, "none").wait_recv()

    def left(self, *names):
        for name in names:
            self.started.pop(name).wait_send()

    def close(self):
        self.left(*tuple(self.started))


class Place:
    def __init__(self):
        self.w = w = lax.axis_index("wt")
        self.c = c = lax.axis_index("ctx")
        self.core = core = c % 2
        self.other = 1 - core
        self.z = z = c // 2
        self.near = z % 2
        self.far = 1 - self.near
        self.nx = w + 1 - 2 * (w % 2)
        self.ny = (w + 2) % 4
        self.nd = 3 - w
        self.sib = (w, c + 1 - 2 * core)
        self.to_x, self.to_y, self.to_d = (self.nx, c), (self.ny, c), (self.nd, c)
        self.cross = (w, c + 2 - 4 * self.near)
        self.partner = (w, (c + 4) % 8)
        self.lines = [(w, spot * 2 + core) for spot in (z + 1 - 2 * (z % 2), (z + 2) % 4, 3 - z)]
        self.others = [(w, (c + step) % 8) for step in range(1, 8)]
        self.mate, self.middle = self.lines[0], self.lines[2]
        self.outer, self.inner = (z == 0) | (z == 3), (z == 1) | (z == 2)


def greet(peers):
    barrier = pltpu.get_barrier_semaphore()
    for peer in peers:
        pl.semaphore_signal(barrier, inc=1, device_id=peer, device_id_type=MESH)
    pl.semaphore_wait(barrier, len(peers))


class Part:
    def __init__(self, name, local, full, first, columns, place, wire):
        self.name, self.local, self.full, self.place, self.wire = name, local, full, place, wire
        self.rows = local.shape[0]
        self.first, self.columns = first, columns // 2

    def piece(self, owner, core, half=None):
        rows, start = self.rows, owner * self.rows
        if half is not None:
            rows = self.rows // 2
            start = start + half * rows
        return self.full.at[
            pl.ds(aligned(start, 16), rows),
            pl.ds(aligned(self.first + core * self.columns, 128), self.columns),
        ]

    def send(self, kind, source, target, where):
        self.wire.send_in(self.name, self.name + kind, source, target, where)

    def begin(self):
        at = self.place
        mine = self.local.at[
            :, pl.ds(aligned(self.first + at.core * self.columns, 128), self.columns)
        ]
        target = self.piece(at.w, at.core)
        self.send("a", mine, target, at.to_x)
        self.send("b", mine, target, at.to_y)

    def relay(self):
        at, wire = self.place, self.wire
        for kind, owner, half, on, where in (
            ("a", at.nx, 0, "c", at.to_y),
            ("b", at.ny, 1, "e", at.to_x),
        ):
            block = self.piece(owner, at.core)
            wire.arrived(self.name + kind, block)
            part = self.piece(owner, at.core, half)
            self.send(on, part, part, where)
            self.send("s", block, block, at.sib)

    def share(self):
        at, wire = self.place, self.wire
        for half, came in ((0, "c"), (1, "e")):
            block = self.piece(at.nd, at.core, half)
            wire.arrived(self.name + came, block)
            self.send("r", block, block, at.sib)

    def arrived(self, kind, pieces):
        block = self.full.at[pl.ds(0, pieces * self.rows), pl.ds(self.first, self.columns)]
        self.wire.arrived(self.name + kind, block)

    def near(self):
        self.arrived("s", 2)

    def last(self):
        self.arrived("r", 1)

    def finish(self):
        self.near()
        self.last()

    def gone(self):
        block = self.full.at[pl.ds(0, 3 * self.rows), pl.ds(self.first, 2 * self.columns)]
        self.wire.gone(self.name, block)


def in_bands(rows):
    def run(body):
        for first in range(0, rows, BAND):
            body(slice(first, first + BAND))

    return run


def in_columns(first, last):
    def run(body):
        for start in range(first, last, 256):
            body(slice(start, start + 256))

    return run


def add_into(target, *sources):
    rows, columns = sources[0].shape
    band = 16
    while columns * band * 2 <= 1 << 15 and rows % (band * 2) == 0:
        band *= 2

    @pl.loop(0, rows // band)
    def _(index):
        where = chunk_of(index, band)
        total = sources[0][where, :].astype(F32)
        for source in sources[1:]:
            total = total + source[where, :].astype(F32)
        target[where, :] = total.astype(target.dtype)


class Grad:
    def __init__(self, name, chunks, blocks, buffers, finals, place, wire, local_sem):
        self.name, self.chunks, self.blocks, self.finals = name, chunks, blocks, finals
        self.place, self.wire, self.local_sem = place, wire, local_sem
        self.from_x, self.from_y, self.diag_x, self.diag_y, self.low, self.high = buffers
        self.rows, self.columns = self.from_x.shape

    def half(self, ref, index):
        return ref.at[pl.ds(index * (self.rows // 2), self.rows // 2), :]

    def begin(self):
        at, wire = self.place, self.wire
        block = self.blocks(at.nd)
        wire.send(self.name + "a", self.half(block, 0), self.diag_x, at.to_x)
        wire.send(self.name + "b", self.half(block, 1), self.diag_y, at.to_y)

    def fold(self):
        at, wire = self.place, self.wire
        for kind, came, owner, index in (("a", self.diag_x, at.ny, 0), ("b", self.diag_y, at.nx, 1)):
            wire.arrived(self.name + kind, came)
            part = self.half(self.blocks(owner), index)
            add_into(part, part, came)

    def lanes(self, chunk):
        at = self.place
        return (
            self.hop("c", chunk, self.blocks(at.nx), self.from_x, at.to_x),
            self.hop("d", chunk, self.blocks(at.ny), self.from_y, at.to_y),
        )

    def push(self, to_x=(), to_y=()):
        for chunk in to_x:
            self.lanes(chunk)[0].start()
        for chunk in to_y:
            self.lanes(chunk)[1].start()

    def cut(self, ref, chunk):
        count = self.rows // self.chunks
        return ref.at[pl.ds(chunk * count, count), :]

    def hop(self, kind, chunk, source, target, where):
        slot = self.wire.slot(self.name + kind, self.chunks) + chunk
        return self.wire.copy(
            slot, self.cut(source, chunk), self.cut(target, chunk), where, self.name + kind
        )

    def outward(self, chunk):
        return self.hop("u", chunk, self.blocks(self.place.w), self.low, self.place.mate)

    def across(self, chunk):
        return self.hop("v", chunk, self.from_x, self.high, self.place.middle)

    def back(self, chunk):
        return self.hop("t", chunk, self.from_y, self.high, self.place.mate)

    def own(self, chunk):
        for copy in self.lanes(chunk):
            copy.wait_recv()
        part = self.cut(self.blocks(self.place.w), chunk)
        add_into(part, part, self.cut(self.from_x, chunk), self.cut(self.from_y, chunk))
        self.out(chunk)

    def out(self, chunk):
        @pl.when(self.place.outer)
        def _():
            self.outward(chunk).start()

    def chain(self, chunk):
        at = self.place

        @pl.when(at.inner)
        def _():
            self.outward(chunk).wait_recv()
            block = self.blocks(at.w)
            add_into(
                self.cut(self.from_x, chunk), self.cut(block, chunk), self.cut(self.low, chunk)
            )
            self.across(chunk).start()

    def total(self, chunk):
        at = self.place

        @pl.when(at.inner)
        def _():
            self.across(chunk).wait_recv()
            add_into(
                self.cut(self.from_y, chunk),
                self.cut(self.from_x, chunk),
                self.cut(self.high, chunk),
            )
            self.back(chunk).start()
            for copy in self.copies(chunk, self.from_y):
                copy.start()

    def copies(self, chunk, source):
        at, wire = self.place, self.wire
        piece, target = self.cut(source, chunk), self.finals(chunk, at.core)
        keep = pltpu.make_async_copy(piece, target, self.local_sem)
        slot = wire.slot(self.name + "s")
        return keep, wire.copy(slot, piece, target, at.sib, self.name + "s")

    def give(self, chunk):
        at = self.place

        @pl.when(at.outer)
        def _():
            self.back(chunk).wait_recv()
            for copy in self.copies(chunk, self.high):
                copy.start()

    def close(self):
        at, wire = self.place, self.wire
        whole = self.from_y
        pltpu.make_async_copy(whole, whole, self.local_sem).wait()
        wire.arrived(self.name + "s", whole)
        for kind in ("s", "c", "d"):
            wire.gone(self.name + kind, whole)

        @pl.when(at.outer)
        def _():
            wire.gone(self.name + "u", whole)

        @pl.when(at.inner)
        def _():
            wire.gone(self.name + "v", whole)
            wire.gone(self.name + "t", whole)


def layer_scratch(rows, width, inner, heads):
    pairs = heads // 2
    some = pairs // 2
    share = width // 4
    half = width // 2
    groups = 8

    def low(*shape):
        return pltpu.VMEM(shape, BF16)

    def wide(*shape):
        return pltpu.VMEM(shape, F32)

    scratch = dict(
        wqkv=low(width, 3 * width),
        wo=low(width, width),
        wu=low(width, inner),
        wd=low(inner, width),
        order=low(width, width),
        wo_order=low(width, width),
        tok=low(2, rows, width),
        cot=low(rows, width),
        small_own=low(16, width),
        small_in=low(3, 16, width),
        small=wide(16, width),
        bias_qkv=wide(8, 3 * width),
        bias_up=wide(8, inner),
        kv=low(pairs, 4, rows, 256),
        proj=low(rows, 3 * width),
        q=low(pairs, rows, 128),
        q_out=low(some, rows, 128),
        exps=low(heads, 4 * rows, rows),
        inverse=wide(heads, 1, rows),
        out_t=wide(pairs, 128, rows),
        ctx=low(pairs, rows, 128),
        ctx_out=low(some, rows, 128),
        ctx_nat=low(2, rows, width),
        hat_one=wide(rows, width),
        r_one=wide(rows, 1),
        flow=wide(rows, width),
        stage=wide(rows, width),
        result=wide(rows, width),
        hid=low(2, rows, width),
        act=low(2, rows, inner),
        slope=low(rows, inner),
        slope_in=low(rows, inner // 2),
        gf=low(rows, width),
        gf_in=low(rows, half),
        gb=low(rows, width),
        gb_in=low(rows, half),
        do=low(pairs, rows, 128),
        do_out=low(some, rows, 128),
        dq=low(pairs, rows, 128),
        dkv_in=low(pairs, rows, 256),
        tops=wide(heads, 1, rows),
        delta=wide(heads, 1, rows),
        dos=low(pairs, rows, 128),
        far_q=low(2, pairs, rows, 128),
        far_tops=wide(2, heads, 1, rows),
        far_delta=wide(2, heads, 1, rows),
        far_dos=low(2, pairs, rows, 128),
        gkv=low(2, rows, width),
        gj_in=low(rows, 3 * half),
        sums=wide(16, groups, width),
        sums_up=wide(groups, inner),
        vec=wide(16, width),
        vec_in=wide(16, width),
        vec_low=low(4, 16, width),
        vec_far=low(6, 16, width),
        dwd=low(4, inner // 4, half),
    )
    shapes = dict(
        d=(inner // 4, half), u=(2 * share, width), o=(share, half), q=(3 * share, half)
    )
    for name, (r, c) in shapes.items():
        for kind in ("fx", "fy", "lo", "hi"):
            scratch["g" + name + kind] = low(r, c)
        for kind in ("dx", "dy"):
            scratch["g" + name + kind] = low(r // 2, c)
    scratch["sends"] = pltpu.SemaphoreType.DMA((80,))
    scratch["receives"] = pltpu.SemaphoreType.DMA((180,))
    scratch["own_sems"] = pltpu.SemaphoreType.DMA((12,))
    return scratch


def layer_kernel(names, *refs):
    (
        tokens,
        cot_l,
        pairing,
        small_raw,
        bias_raw,
        qkv_l,
        out_l,
        up_l,
        down_l,
        output,
        grad_tokens,
        g_qkv,
        g_out,
        g_up,
        g_down,
        g_small,
    ) = refs[:16]
    s = dict(zip(names, refs[16:]))
    at = Place()
    wire = Wire(s["sends"], s["receives"], at.sib)
    rows, width = tokens.shape
    inner = up_l.shape[1]
    heads = pairing.shape[0]
    pairs, some = heads // 2, heads // 4
    size = width // heads
    half = width // 2
    keys = 4 * rows
    chunks = width // 256
    share = width // 4
    core, other = at.core, at.other

    greet([at.to_x, at.to_y, at.to_d] + at.others)

    part_kv = Part("kv", qkv_l, s["wqkv"], width, 2 * width, at, wire)
    part_q = Part("q", qkv_l, s["wqkv"], 0, width, at, wire)
    part_o = Part("o", out_l, s["wo"], 0, width, at, wire)
    part_u = Part("u", up_l, s["wu"], 0, inner, at, wire)
    part_d = Part("d", down_l, s["wd"], 0, width, at, wire)
    part_kv.begin()
    part_q.begin()
    raw = small_raw[...]
    row = lax.broadcasted_iota(jnp.int32, (share, width), 0)
    column = lax.broadcasted_iota(jnp.int32, (share, width), 1)

    def spread(values, spot):
        place = jnp.where(column - row == spot * share, 1.0, 0.0).astype(BF16)
        return nn(values, place)

    own_row = lax.broadcasted_iota(jnp.int32, (8, width), 0) == at.w
    line = jnp.concatenate(
        [bias_raw[k : k + 1, :] for k in range(width // 128)], axis=1
    ).astype(F32)
    small_own = s["small_own"]
    small_own[...] = jnp.concatenate(
        [spread(raw, at.w), jnp.where(own_row, line, 0.0)], axis=0
    ).astype(BF16)
    for index, where in enumerate((at.to_x, at.to_y, at.to_d)):
        wire.send("sm" + str(index), small_own, s["small_in"].at[index], where)
    keeps = []
    for slot, (local, full) in enumerate(
        (
            (qkv_l, s["wqkv"].at[pl.ds(aligned(at.w * share, 16), share)]),
            (tokens, s["tok"].at[core]),
            (cot_l, s["cot"]),
            (out_l, s["wo"].at[pl.ds(aligned(at.w * share, 16), share)]),
            (up_l, s["wu"].at[pl.ds(aligned(at.w * share, 16), share)]),
            (down_l, s["wd"].at[pl.ds(aligned(at.w * (inner // 4), 16), inner // 4)]),
        )
    ):
        keeps.append(pltpu.make_async_copy(local, full, s["own_sems"].at[slot]))
        keeps[-1].start()
    wire.send("tok", tokens, s["tok"].at[core], at.sib)

    before = 0
    for head in range(heads):
        flag = pairing[head]
        spot = flag * (heads // 2 + before) + (1 - flag) * (head - before)
        before = before + flag
        row = lax.broadcasted_iota(jnp.int32, (size, width), 0)
        column = lax.broadcasted_iota(jnp.int32, (size, width), 1)
        s["order"][head * size : (head + 1) * size, :] = jnp.where(
            column - row == spot * size, 1.0, 0.0
        ).astype(BF16)

    part_kv.relay()
    part_q.relay()
    part_o.begin()
    part_u.begin()
    part_kv.share()
    for index in range(3):
        wire.arrived("sm" + str(index), s["small_in"].at[index])
    small = s["small"]
    small[...] = (
        small_own[...].astype(F32)
        + s["small_in"][0].astype(F32)
        + s["small_in"][1].astype(F32)
        + s["small_in"][2].astype(F32)
    )
    s["bias_qkv"][0:1, 0:width] = small[0:1, :]
    s["bias_qkv"][0:1, width : 2 * width] = jnp.zeros((1, width), F32)
    s["bias_qkv"][0:1, 2 * width :] = small[1:2, :]
    for index in range(inner // width):
        s["bias_up"][0:1, index * width : (index + 1) * width] = small[8 + index : 9 + index, :]
    keeps[0].wait()
    keeps[1].wait()
    part_kv.finish()

    tok, proj, order, kv = s["tok"], s["proj"], s["order"], s["kv"]
    own_slot = core * 2 + at.near

    def project(first, count):
        @in_columns(first * 256, (first + count) * 256)
        def _(where):
            made = nn(tok[core], s["wqkv"][:, where]) + s["bias_qkv"][0:1, where]
            proj[:, where] = made.astype(BF16)

    project(chunks, 2 * chunks)
    for index in range(chunks):
        columns = order[:, index * 256 : (index + 1) * 256]
        for kind in range(2):
            moved = nn(proj[:, (1 + kind) * width : (2 + kind) * width], columns).astype(BF16)
            for e in range(2):
                kv[2 * index + e, own_slot, :, kind * 128 : (kind + 1) * 128] = moved[
                    :, e * 128 : (e + 1) * 128
                ]
    near_base = wire.slot("near kv", pairs)
    far_base = wire.slot("far kv", pairs)
    pass_base = wire.slot("passed kv", pairs)

    def kv_copy(base, pair, slot, where):
        block = kv.at[pair, slot]
        return wire.copy(base + pair, block, block, where, "kv" + str(base))

    for pair in range(pairs):
        if pair < some:
            kv_copy(far_base, pair, own_slot, at.cross).start()
        kv_copy(near_base, pair, own_slot, at.sib).start()
    part_q.share()
    part_q.finish()
    project(0, chunks)
    q, q_out = s["q"], s["q_out"]
    for index in range(chunks):
        moved = nn(proj[:, 0:width], order[:, index * 256 : (index + 1) * 256]).astype(BF16)
        for e in range(2):
            pair = 2 * index + e
            block = moved[:, e * 128 : (e + 1) * 128]
            if pair < some:
                q[pair] = block
            else:
                q_out[pair - some] = block
    wire.send("queries", q_out, q.at[pl.ds(some, some)], at.partner)
    part_o.relay()
    part_d.begin()

    exps, inverse, out_t = s["exps"], s["inverse"], s["out_t"]

    def both(pair, first):
        return kv[pair, :, :, first : first + 128].reshape(keys, 128)

    def masked(block, e, axis=1):
        spot = lax.broadcasted_iota(jnp.int32, block.shape, axis)
        mine = spot < size if e == 0 else spot >= size
        return jnp.where(mine, block, jnp.zeros_like(block))

    def attend(pair):
        key_rows, value_rows = both(pair, 0), both(pair, 128)
        values_t = value_rows.T
        queries = q[pair] * jnp.asarray(size**-0.5, BF16)
        parts = []
        for e in range(2):
            scores = nt(key_rows, masked(queries, e))
            top = jnp.max(scores, axis=0, keepdims=True)
            raised = jnp.exp(scores - top)
            total = jnp.sum(raised, axis=0, keepdims=True)
            low = raised.astype(BF16)
            exps[2 * pair + e] = low
            s["tops"][2 * pair + e] = top
            one_over = 1.0 / total
            inverse[2 * pair + e] = one_over
            parts.append(nn(values_t[e * size : (e + 1) * size], low) * one_over)
        merged = jnp.concatenate(parts, axis=0)
        out_t[pair] = merged
        return merged.T.astype(BF16)

    def receive_kv(pair):
        kv_copy(far_base, pair, core * 2 + at.far, at.cross).wait_recv()
        kv_copy(pass_base, pair, core * 2 + at.far, at.sib).start()
        kv_copy(near_base, pair, other * 2 + at.near, at.sib).wait_recv()
        kv_copy(pass_base, pair, other * 2 + at.far, at.sib).wait_recv()

    ctx, ctx_out = s["ctx"], s["ctx_out"]
    back_base = wire.slot("ctx", some)

    def ctx_copy(index):
        return wire.copy(back_base + index, ctx_out.at[index], ctx.at[some + index], at.partner, "ctx")

    def attend_far(index):
        receive_kv(index + some)
        ctx_out[index] = attend(index + some)
        ctx_copy(index).start()

    @pl.loop(0, some)
    def _(index):
        receive_kv(index)
        kv_copy(far_base, index + some, own_slot, at.cross).start()
        ctx[index] = attend(index)

    part_o.share()
    wire.arrived("queries", q.at[pl.ds(some, some)])
    attend_far(0)
    part_u.relay()

    @pl.loop(1, some)
    def _(index):
        attend_far(index)

    part_o.finish()
    far_q, far_tops, far_delta, far_dos = (
        s[name] for name in ("far_q", "far_tops", "far_delta", "far_dos")
    )
    tops, delta, dos = s["tops"], s["delta"], s["dos"]
    wire.send("far q", q, far_q.at[core], at.cross)
    wire.send("far tops", tops, far_tops.at[core], at.cross)
    part_d.relay()
    keeps[2].wait()
    keeps[3].wait()
    ctx_nat, stage, wo_order = s["ctx_nat"], s["stage"], s["wo_order"]
    for index in range(chunks):
        where = slice(index * 256, (index + 1) * 256)
        wo_order[where, :] = nn(order[:, where].T, s["wo"][...]).astype(BF16)
    for index in range(some):
        ctx_copy(index).wait_recv()

    def permuted():
        return jnp.concatenate([ctx[pair] for pair in range(pairs)], axis=1)

    for index in range(chunks):
        where = slice(index * 256, (index + 1) * 256)
        stage[:, where] = nn(permuted(), wo_order[:, where])

    hat_one, r_one, flow, hid = s["hat_one"], s["r_one"], s["flow"], s["hid"]
    inv_width = 1.0 / width

    def mean(values):
        return jnp.sum(values, axis=-1, keepdims=True) * inv_width

    @in_bands(rows)
    def _(where):
        total = tok[core, where, :].astype(F32) + stage[where, :] + small[2:3, :]
        centred = total - mean(total)
        scale = lax.rsqrt(mean(centred * centred) + 1e-12)
        hat = centred * scale
        hat_one[where, :] = hat
        r_one[where, :] = scale
        hidden = hat * small[3:4, :] + small[4:5, :]
        flow[where, :] = hidden
        hid[core, where, :] = hidden.astype(BF16)

    wire.send("hid", hid.at[core], hid.at[core], at.sib)
    part_u.share()
    part_u.finish()
    keeps[4].wait()
    act, slope = s["act"], s["slope"]

    @in_columns(0, inner)
    def _(where):
        pre = nn(hid[core], s["wu"][:, where]) + s["bias_up"][0:1, where]
        below = 0.5 * (1.0 + lax.erf(pre * (0.5**0.5)))
        act[core, :, where] = (pre * below).astype(BF16)
        density = jnp.exp(pre * pre * -0.5) * 0.3989422804014327
        slope[:, where] = (below + pre * density).astype(BF16)

    wire.send("act", act.at[core], act.at[core], at.sib)
    wire.arrived("far q", far_q.at[core])
    wire.send("passed q", far_q.at[core], far_q.at[core], at.sib)
    wire.arrived("far tops", far_tops.at[core])
    wire.send("passed tops", far_tops.at[core], far_tops.at[core], at.sib)
    for index in range(chunks):
        where = slice(index * 256, (index + 1) * 256)
        ctx_nat[core, :, where] = nt(permuted(), order[where, :]).astype(BF16)
    wire.send("ctxn", ctx_nat.at[core], ctx_nat.at[core], at.sib)
    part_d.near()
    keeps[5].wait()
    quarter = inner // 4

    def down(owner, where):
        block = pl.ds(aligned(owner * quarter, 128), quarter)
        return nn(act[core, :, block], s["wd"][block, where])

    @in_columns(0, width)
    def _(where):
        stage[:, where] = down(at.w, where) + down(at.nx, where) + down(at.ny, where)

    part_d.share()
    part_d.last()

    @in_columns(0, width)
    def _(where):
        stage[:, where] += down(at.nd, where)

    result, gf, cot = s["result"], s["gf"], s["cot"]
    sums, sums_up = s["sums"], s["sums_up"]
    sums[...] = jnp.zeros_like(sums)

    def gather_rows(values):
        return jnp.sum(values.reshape(BAND // 8, 8, values.shape[-1]), axis=0)

    @in_bands(rows)
    def _(where):
        total = flow[where, :] + stage[where, :] + small[5:6, :]
        centred = total - mean(total)
        scale = lax.rsqrt(mean(centred * centred) + 1e-12)
        hat = centred * scale
        result[where, :] = hat
        g = cot[where, :].astype(F32) * small[6:7, :]
        grad = scale * (g - mean(g) - hat * mean(g * hat))
        flow[where, :] = grad
        gf[where, :] = grad.astype(BF16)

    def columns_of(which, count):
        return pl.ds(aligned(which * count, 128), count)

    wire.send("gf", gf.at[:, columns_of(other, half)], s["gf_in"], at.sib)

    def buffers(name):
        return [s["g" + name + kind] for kind in ("fx", "fy", "dx", "dy", "lo", "hi")]

    dwd, wd, wu = s["dwd"], s["wd"], s["wu"]

    def side_by_side(first, count, owner):
        return wd.at[
            pl.ds(aligned(first + (owner // 2) * count, 16), count),
            pl.ds(aligned((owner % 2) * half, 128), half),
        ]

    def dwo(owner):
        return side_by_side(2 * width + 6 * share, share, owner)

    def dwq(owner):
        return side_by_side(2 * width, 3 * share, owner)

    grad_d = Grad(
        "gd",
        4,
        lambda r: dwd.at[r],
        buffers("d"),
        lambda i, k: g_down.at[pl.ds(i * (inner // 16), inner // 16), columns_of(k, half)],
        at,
        wire,
        s["own_sems"].at[8],
    )
    grad_u = Grad(
        "gu",
        4,
        lambda r: wd.at[pl.ds(aligned(r * (2 * share), 16), 2 * share), :],
        buffers("u"),
        lambda i, k: g_up.at[
            pl.ds((i % 2) * (share // 2), share // 2), columns_of(2 * k + i // 2, width)
        ],
        at,
        wire,
        s["own_sems"].at[9],
    )
    grad_o = Grad(
        "go",
        1,
        dwo,
        buffers("o"),
        lambda i, k: g_out.at[:, columns_of(k, half)],
        at,
        wire,
        s["own_sems"].at[10],
    )
    grad_q = Grad(
        "gq",
        6,
        dwq,
        buffers("q"),
        lambda i, k: g_qkv.at[
            pl.ds((i % 2) * (share // 2), share // 2), columns_of(3 * k + i // 2, half)
        ],
        at,
        wire,
        s["own_sems"].at[11],
    )

    def back_through(first, last):
        @in_columns(first, last)
        def _(where):
            grad = nt(gf[...], wd[where, :]) * slope[:, where].astype(F32)
            low = grad.astype(BF16)
            slope[:, where] = low
            sums_up[:, where] = jnp.sum(low.astype(F32).reshape(rows // 8, 8, 256), axis=0)

    back_through(0, inner // 2)
    wire.arrived("act", act.at[other])
    wire.arrived("gf", s["gf_in"])

    def down_grad(owner):
        where = pl.ds(aligned(owner * quarter, 128), quarter)
        made = nn(act[core, :, where].T, gf[:, columns_of(core, half)])
        made = made + nn(act[other, :, where].T, s["gf_in"][...])
        dwd[owner] = made.astype(BF16)

    down_grad(at.nd)
    grad_d.begin()
    back_through(inner // 2, inner)
    wire.send("slope", slope.at[:, columns_of(other, inner // 2)], s["slope_in"], at.sib)

    @in_columns(0, width)
    def _(where):
        stage[:, where] = nt(slope[...], wu[where, :])


    gb = s["gb"]

    @in_bands(rows)
    def _(where):
        grad_hidden = flow[where, :] + stage[where, :]
        hat = hat_one[where, :]
        g = grad_hidden * small[3:4, :]
        grad = r_one[where, :] * (g - mean(g) - hat * mean(g * hat))
        flow[where, :] = grad
        gb[where, :] = grad.astype(BF16)
        stage[where, :] = grad_hidden

    wire.send("gb", gb.at[:, columns_of(other, half)], s["gb_in"], at.sib)

    do, do_out = s["do"], s["do_out"]
    for index in range(chunks):
        moved = nt(gb[...], wo_order[index * 256 : (index + 1) * 256, :]).astype(BF16)
        for e in range(2):
            pair = 2 * index + e
            block = moved[:, e * 128 : (e + 1) * 128]
            if pair < some:
                do[pair] = block
            else:
                do_out[pair - some] = block
    wire.send("do", do_out, do.at[pl.ds(some, some)], at.partner)

    def prepare(pair):
        do_t = do[pair].astype(F32).T
        scaled = jnp.concatenate(
            [do_t[e * size : (e + 1) * size] * inverse[2 * pair + e] for e in range(2)], axis=0
        )
        product = scaled * out_t[pair]
        for e in range(2):
            delta[2 * pair + e] = jnp.sum(product[e * size : (e + 1) * size], axis=0, keepdims=True)
        dos[pair] = scaled.T.astype(BF16)

    group_d = [pl.ds(0, some), pl.ds(some, some)]
    group_h = [pl.ds(0, 2 * some), pl.ds(2 * some, 2 * some)]

    def send_group(g):
        wire.send(
            "far do" + str(g), dos.at[group_d[g]], far_dos.at[core, group_d[g]], at.cross
        )
        wire.send(
            "far de" + str(g), delta.at[group_h[g]], far_delta.at[core, group_h[g]], at.cross
        )

    def pass_group(g):
        for kind, ref, group in (("do", far_dos, group_d), ("de", far_delta, group_h)):
            block = ref.at[core, group[g]]
            wire.arrived("far " + kind + str(g), block)
            wire.send("passed " + kind + str(g), block, block, at.sib)

    def have_group(g):
        wire.arrived("passed do" + str(g), far_dos.at[other, group_d[g]])
        wire.arrived("passed de" + str(g), far_delta.at[other, group_h[g]])

    @pl.loop(0, some)
    def _(index):
        prepare(index)

    send_group(0)
    for owner in (at.nx, at.ny):
        down_grad(owner)
    grad_d.push((0, 1), (2, 3))
    down_grad(at.w)
    grad_d.fold()
    grad_d.push((2, 3), (0, 1))

    part_d.gone()
    wire.arrived("hid", hid.at[other])
    wire.arrived("slope", s["slope_in"])
    mine_t, theirs_t = hid[core].T, hid[other].T
    for index in range(inner // 2 // half):
        where = pl.ds(aligned(core * (inner // 2) + index * half, 128), half)
        made = nn(mine_t, slope[:, where]) + nn(
            theirs_t, s["slope_in"][:, index * half : (index + 1) * half]
        )
        made = made.astype(BF16)
        for owner in range(4):
            first = owner * 2 * share + (index // 2) * share
            wd[first : first + share, (index % 2) * half : (index % 2 + 1) * half] = made[
                owner * share : (owner + 1) * share
            ]
    grad_u.begin()
    grad_u.push((0,), (2,))
    wire.arrived("ctxn", ctx_nat.at[other])
    wire.arrived("gb", s["gb_in"])
    made = nn(ctx_nat[core].T, gb[:, columns_of(core, half)]) + nn(
        ctx_nat[other].T, s["gb_in"][...]
    )
    made = made.astype(BF16)
    for owner in range(4):
        dwo(owner)[...] = made[owner * share : (owner + 1) * share]
    grad_o.begin()

    part_u.gone()
    dq, dq_out, dkv_in = s["dq"], s["do_out"], s["dkv_in"]
    near_d = wire.slot("near dkv", pairs)
    dq_base = wire.slot("dq", some)
    lots = inner // 512

    def tile(pair, which):
        return wu.at[
            pl.ds(aligned((pair // lots) * rows, 16), rows),
            pl.ds(aligned((pair % lots) * 512 + which * 256, 256), 256),
        ]

    def dkv_near(pair):
        return wire.copy(near_d + pair, tile(pair, other), dkv_in.at[pair], at.sib, "near dkv")

    def two_blocks(pair, chip, first):
        return jnp.concatenate(
            [kv[pair, k * 2 + chip, :, first : first + 128] for k in range(2)], axis=0
        )

    def attend_back(pair):
        queries = q[pair] * jnp.asarray(size**-0.5, BF16)
        dq_parts = [None, None]
        dv = dk = None
        for chip in (at.near, at.far):
            key_rows, value_rows = two_blocks(pair, chip, 0), two_blocks(pair, chip, 128)
            keys_t = key_rows.T
            for e in range(2):
                low = jnp.concatenate(
                    [
                        exps[2 * pair + e, pl.ds(aligned((k * 2 + chip) * rows, 16), rows), :]
                        for k in range(2)
                    ],
                    axis=0,
                )
                mine = masked(dos[pair], e)
                grad_w = nt(value_rows, mine)
                grad_s = (low.astype(F32) * (grad_w - delta[2 * pair + e])).astype(BF16)
                more_q = nn(keys_t[e * size : (e + 1) * size], grad_s)
                dq_parts[e] = more_q if dq_parts[e] is None else dq_parts[e] + more_q
                if chip is at.near:
                    more_v = nn(low, mine)
                    more_k = nn(grad_s, masked(queries, e))
                    dv = more_v if dv is None else dv + more_v
                    dk = more_k if dk is None else dk + more_k
            if chip is at.near:
                made = jnp.concatenate([dk, dv], axis=1).astype(BF16)
                for k in range(2):
                    tile(pair, k)[...] = made[k * rows : (k + 1) * rows]
                dkv_near(pair).start()
        return (jnp.concatenate(dq_parts, axis=0).T * size**-0.5).astype(BF16)

    gkv = s["gkv"]

    def far_back(pair):
        queries = far_q[:, pair].reshape(2 * rows, 128) * jnp.asarray(size**-0.5, BF16)
        grads = far_dos[:, pair].reshape(2 * rows, 128)
        key_rows, value_rows = kv[pair, own_slot, :, 0:128], kv[pair, own_slot, :, 128:256]
        dv = dk = None
        for e in range(2):
            head = 2 * pair + e
            top = jnp.concatenate([far_tops[k, head] for k in range(2)], axis=1)
            less = jnp.concatenate([far_delta[k, head] for k in range(2)], axis=1)
            mine, asking = masked(grads, e), masked(queries, e)
            low = jnp.exp(nt(key_rows, asking) - top).astype(BF16)
            grad_s = (low.astype(F32) * (nt(value_rows, mine) - less)).astype(BF16)
            more_v, more_k = nn(low, mine), nn(grad_s, asking)
            dv = more_v if dv is None else dv + more_v
            dk = more_k if dk is None else dk + more_k
        dkv_near(pair).wait_recv()
        own = tile(pair, core)
        where = pl.ds(aligned(pair * 128, 128), 128)
        for kind, made in ((0, dk), (1, dv)):
            cut = slice(kind * 128, (kind + 1) * 128)
            gkv[kind, :, where] = (
                made + own[:, cut].astype(F32) + dkv_in[pair, :, cut].astype(F32)
            ).astype(BF16)

    def dq_copy(index):
        return wire.copy(dq_base + index, dq_out.at[index], dq.at[some + index], at.partner, "dq")

    @pl.loop(0, some)
    def _(index):
        dq[index] = attend_back(index)

    wire.arrived("do", do.at[pl.ds(some, some)])

    @pl.loop(some, pairs)
    def _(index):
        prepare(index)

    send_group(1)
    pass_group(0)
    wire.left("do")
    grad_d.own(0)

    @pl.loop(0, some)
    def _(index):
        dq_out[index] = attend_back(index + some)
        dq_copy(index).start()

    for chunk in (2, 1, 3):
        grad_d.own(chunk)
    pass_group(1)
    wire.arrived("passed q", far_q.at[other])
    wire.arrived("passed tops", far_tops.at[other])
    have_group(0)

    @pl.loop(0, some)
    def _(index):
        far_back(index)

    grad_d.chain(0)
    @pl.loop(0, rows // BAND, unroll=2)
    def _(index):
        where = chunk_of(index, BAND)
        hat = result[where, :]
        result[where, :] = hat * small[6:7, :] + small[7:8, :]
        back = cot[where, :].astype(F32)
        sums[6] += gather_rows(back * hat)
        sums[7] += gather_rows(back)
        sums[5] += gather_rows(gf[where, :].astype(F32))
        grad_hidden = stage[where, :]
        sums[3] += gather_rows(grad_hidden * hat_one[where, :])
        sums[4] += gather_rows(grad_hidden)
        sums[2] += gather_rows(gb[where, :].astype(F32))

    keep_out = pltpu.make_async_copy(result, output, s["own_sems"].at[7])
    keep_out.start()
    grad_u.fold()
    grad_u.push((1, 2), (0, 1))
    wire.left(*[name for name in wire.started if name[:2] not in ("gd", "gu", "go")])
    part_kv.gone()
    part_q.gone()
    part_o.gone()
    for base in (far_base, near_base, pass_base):
        wire.gone("kv" + str(base), kv.at[:, 0])
    wire.gone("ctx", ctx_out)
    have_group(1)

    @pl.loop(some, pairs)
    def _(index):
        far_back(index)

    for index in range(some):
        dq_copy(index).wait_recv()
    merged = jnp.concatenate([dq[pair] for pair in range(pairs)], axis=1)
    for index in range(chunks):
        where = slice(index * 256, (index + 1) * 256)
        rows_of = order[where, :]
        for kind in range(3):
            source = merged if kind == 0 else gkv[kind - 1]
            low = nt(source, rows_of).astype(BF16)
            proj[:, kind * width + index * 256 : kind * width + (index + 1) * 256] = low
            if kind != 1:
                sums[kind // 2, :, where] = jnp.sum(
                    low.astype(F32).reshape(rows // 8, 8, 256), axis=0
                )
    wire.send("gj", proj.at[:, columns_of(other, 3 * half)], s["gj_in"], at.sib)

    vec, vec_in, vec_low, vec_far = s["vec"], s["vec_in"], s["vec_low"], s["vec_far"]
    for row in range(8):
        vec[row : row + 1, :] = jnp.sum(sums[row], axis=0, keepdims=True)
    for index in range(inner // width):
        vec[8 + index : 9 + index, :] = jnp.sum(
            sums_up[:, index * width : (index + 1) * width], axis=0, keepdims=True
        )
    for row in range(8 + inner // width, 16):
        vec[row : row + 1, :] = jnp.zeros((1, width), F32)
    wire.send("va", vec, vec_in, at.sib)

    grad_d.chain(2)
    grad_d.total(0)
    wire.arrived("tok", tok.at[other])
    wire.arrived("gj", s["gj_in"])
    mine_t, theirs_t = tok[core].T, tok[other].T
    for index in range(3):
        where = pl.ds(aligned(core * (3 * half) + index * half, 128), half)
        made = nn(mine_t, proj[:, where]) + nn(
            theirs_t, s["gj_in"][:, index * half : (index + 1) * half]
        )
        made = made.astype(BF16)
        for owner in range(4):
            dwq(owner)[index * share : (index + 1) * share, :] = made[
                owner * share : (owner + 1) * share
            ]
    grad_q.begin()
    grad_u.push((3,), (3,))
    grad_o.fold()
    grad_o.push((0,), (0,))
    grad_u.own(0)
    grad_d.chain(1)
    grad_d.total(2)
    wire.arrived("va", vec_in)
    vec_low[0] = (vec_in[...] + vec[...]).astype(BF16)
    for index, where in enumerate((at.to_x, at.to_y, at.to_d)):
        wire.send("vb" + str(index), vec_low.at[0], vec_far.at[index], where)

    keep_out.wait()

    @in_columns(0, width)
    def _(where):
        result[:, where] = nt(proj[...], s["wqkv"][where, :]) + flow[:, where]

    keep_grad = pltpu.make_async_copy(result, grad_tokens, s["own_sems"].at[7])
    keep_grad.start()
    def vec_hop(name, place, far, where):
        return wire.copy(wire.slot(name), vec_low.at[place], vec_far.at[far], where, name)

    def vec_out():
        return vec_hop("vu", 1, 3, at.mate)

    def vec_across():
        return vec_hop("vv", 2, 4, at.middle)

    def vec_back():
        return vec_hop("vt", 3, 5, at.mate)

    def vec_sum(*parts):
        total = parts[0].astype(F32)
        for part in parts[1:]:
            total = total + part.astype(F32)
        return total

    grad_u.own(1)
    grad_d.chain(3)
    grad_d.total(1)
    grad_u.own(2)
    grad_u.chain(0)
    grad_q.fold()
    grad_q.push((0, 1, 2, 3, 4, 5), (0, 1, 2, 3, 4, 5))
    grad_d.total(3)
    grad_u.total(0)
    grad_u.chain(1)
    grad_u.own(3)
    grad_u.chain(2)
    grad_u.total(1)
    grad_o.own(0)
    grad_u.total(2)
    grad_q.own(0)
    grad_u.chain(3)
    grad_q.own(1)
    for index in range(3):
        wire.arrived("vb" + str(index), vec_far.at[index])
    vec_low[1] = (
        vec_sum(vec_low[0], vec_far[0]) + vec_sum(vec_far[1], vec_far[2])
    ).astype(BF16)

    @pl.when(at.outer)
    def _():
        vec_out().start()

    grad_o.chain(0)
    grad_u.total(3)
    grad_q.own(2)
    grad_q.chain(0)
    grad_q.chain(1)
    grad_q.own(3)

    @pl.when(at.inner)
    def _():
        vec_out().wait_recv()
        vec_low[2] = vec_sum(vec_low[1], vec_far[3]).astype(BF16)
        vec_across().start()

    grad_q.chain(2)
    grad_o.total(0)
    grad_q.total(0)
    grad_q.own(4)
    grad_q.chain(3)
    grad_q.total(1)
    grad_q.own(5)
    grad_q.chain(4)
    grad_q.total(2)
    grad_q.chain(5)
    grad_q.total(3)

    @pl.when(at.inner)
    def _():
        vec_across().wait_recv()
        total = vec_sum(vec_low[2], vec_far[4]).astype(BF16)
        vec_low[3] = total
        vec_back().start()
        vec_in[...] = total.astype(F32)

    grad_q.total(4)
    grad_q.total(5)
    for chunk in range(4):
        grad_d.give(chunk)
    for chunk in range(4):
        grad_u.give(chunk)
    grad_o.give(0)
    for chunk in range(4):
        grad_q.give(chunk)

    @pl.when(at.outer)
    def _():
        vec_back().wait_recv()
        vec_in[...] = vec_far[5].astype(F32)

    keep_small = pltpu.make_async_copy(vec_in, g_small, s["own_sems"].at[6])
    keep_small.start()
    grad_q.give(4)
    grad_q.give(5)

    @pl.when(at.outer)
    def _():
        vec_out().wait_send()

    @pl.when(at.inner)
    def _():
        vec_across().wait_send()
        vec_back().wait_send()

    grad_d.close()
    grad_u.close()
    grad_o.close()
    grad_q.close()
    keep_grad.wait()
    keep_small.wait()
    wire.gone("near dkv", dkv_in)
    wire.gone("dq", dq_out)
    wire.close()


def whole_layer(
    tokens, cotangent, pairing, small_raw, bias_raw, w_qkv, w_out, w_up, w_down
):
    rows, width = tokens.shape
    inner = w_up.shape[1]
    scratch = layer_scratch(rows, width, inner, pairing.shape[0])
    hbm = pl.BlockSpec(memory_space=pl.ANY)
    vmem = pl.BlockSpec(memory_space=pltpu.VMEM)
    smem = pl.BlockSpec(memory_space=pltpu.SMEM)
    return pl.pallas_call(
        functools.partial(layer_kernel, tuple(scratch)),
        out_shape=[
            jax.ShapeDtypeStruct((rows, width), F32),
            jax.ShapeDtypeStruct((rows, width), F32),
            jax.ShapeDtypeStruct(w_qkv.shape, BF16),
            jax.ShapeDtypeStruct(w_out.shape, BF16),
            jax.ShapeDtypeStruct(w_up.shape, BF16),
            jax.ShapeDtypeStruct(w_down.shape, BF16),
            jax.ShapeDtypeStruct((16, width), F32),
        ],
        in_specs=[hbm, hbm, smem, vmem, vmem, hbm, hbm, hbm, hbm],
        out_specs=[hbm] * 7,
        scratch_shapes=list(scratch.values()),
        compiler_params=pltpu.CompilerParams(
            collective_id=0, has_side_effects=True, vmem_limit_bytes=60 << 20
        ),
        name="whole_layer",
    )(tokens, cotangent, pairing, small_raw, bias_raw, w_qkv, w_out, w_up, w_down)


def finish_kernel(share, *refs):
    wide, small, outs = refs[:6], refs[6], refs[7:]
    for source, target in zip(wide, outs[:6]):
        target[...] = source[...].astype(F32)

    @pl.when(pl.program_id(0) == 0)
    def _():
        w = lax.axis_index("wt")
        values = small[...]
        mine = jnp.zeros((8, share), F32)
        line = jnp.zeros((1, 4 * share), F32)
        for owner in range(4):
            mine = mine + jnp.where(
                w == owner, values[:8, owner * share : (owner + 1) * share], 0.0
            )
            line = line + jnp.where(w == owner, values[8 + owner : 9 + owner], 0.0)
        for row in range(8):
            outs[6 + row][...] = mine[row : row + 1]
        outs[14][...] = line.reshape(4 * share)


def finish(*arrays):
    steps = 2
    wide, small = arrays[:6], arrays[6]
    share = small.shape[1] // 4

    def blocks(array):
        return pl.BlockSpec((array.shape[0] // steps, array.shape[1]), lambda i: (i, 0))

    def fixed(shape):
        return pl.BlockSpec(shape, lambda i: (0,) * len(shape))

    shapes = [(1, share)] * 8 + [(4 * share,)]
    return pl.pallas_call(
        functools.partial(finish_kernel, share),
        grid=(steps,),
        out_shape=[jax.ShapeDtypeStruct(v.shape, F32) for v in wide]
        + [jax.ShapeDtypeStruct(v, F32) for v in shapes],
        in_specs=[blocks(v) for v in wide] + [fixed(small.shape)],
        out_specs=[blocks(v) for v in wide] + [fixed(v) for v in shapes],
        compiler_params=pltpu.CompilerParams(vmem_limit_bytes=60 << 20),
        name="finish",
    )(*arrays)


far_below = -1e30


def passed_along(value, axis, steps):
    count = lax.axis_size(axis)
    pairs = [(source, (source + steps) % count) for source in range(count)]
    return lax.ppermute(value, axis, pairs)


def norm_rows(values, gains, shifts):
    average = jnp.mean(values, axis=-1, keepdims=True)
    centred = values - average
    spread = jnp.mean(centred * centred, axis=-1, keepdims=True)
    return centred * lax.rsqrt(spread + 1e-12) * gains + shifts


def gelu_exact(pre_active):
    return jax.nn.gelu(pre_active, approximate=False)


def scores_of(queries, key_heads):
    return (
        jnp.einsum("thd,khd->htk", queries, key_heads, preferred_element_type=jnp.float32) * 0.125
    )


def unchanged(running):
    return running


def general_layer(
    tokens,
    pairing,
    w_qkv,
    bias_q,
    bias_v,
    w_out,
    bias_out,
    gain_one,
    shift_one,
    w_up,
    bias_up,
    w_down,
    bias_down,
    gain_two,
    shift_two,
    cotangent,
):
    local_params = (
        w_qkv,
        bias_q,
        bias_v,
        w_out,
        bias_out,
        gain_one,
        shift_one,
        w_up,
        bias_up,
        w_down,
        bias_down,
        gain_two,
        shift_two,
    )
    gathered = tuple(lax.all_gather(v, "wt", axis=0, tiled=True) for v in local_params)
    (
        wqkv_full,
        biasq_full,
        biasv_full,
        wout_full,
        biasout_full,
        gainone_full,
        shiftone_full,
        wup_full,
        biasup_full,
        wdown_full,
        biasdown_full,
        gaintwo_full,
        shifttwo_full,
    ) = gathered
    tok_rows = tokens.shape[1]
    model_width = tokens.shape[2]
    head_count = pairing.shape[0]
    head_size = model_width // head_count
    group_size = lax.axis_size("ctx")
    position_ctx = lax.axis_index("ctx")
    half_len = tok_rows * group_size // 2
    own_half = position_ctx * tok_rows // half_len
    flipped = pairing == 1
    inputs = tokens[0]
    bias_cat = jnp.concatenate(
        [
            biasq_full.astype(jnp.float32),
            jnp.zeros((model_width,), jnp.float32),
            biasv_full.astype(jnp.float32),
        ]
    )
    projected = jnp.dot(inputs, wqkv_full, preferred_element_type=jnp.float32) + bias_cat
    projected_low = projected.astype(jnp.bfloat16)
    queries = projected_low[:, :model_width].reshape(tok_rows, head_count, head_size)
    key_rows = projected_low[:, model_width : 2 * model_width]
    value_rows = projected_low[:, 2 * model_width :]

    def online_update(state, portion_keys, portion_values, needed):
        row_top, row_total, accumulated = state
        key_count = portion_keys.shape[0]
        key_heads = portion_keys.reshape(key_count, head_count, head_size)
        value_heads = portion_values.reshape(key_count, head_count, head_size)
        scores = scores_of(queries, key_heads)
        scores = jnp.where(needed[:, None, :], scores, far_below)
        new_top = jnp.maximum(row_top, jnp.max(scores, axis=-1))
        factor = jnp.exp(row_top - new_top)
        weights = jnp.exp(scores - new_top[..., None])
        row_total = jnp.sum(weights, axis=-1)
        added = jnp.einsum(
            "htk,khd->thd",
            weights.astype(jnp.bfloat16),
            value_heads,
            preferred_element_type=jnp.float32,
        )
        accumulated = accumulated * factor.T[..., None] + added
        return (new_top, row_total, accumulated)

    start_state = (
        jnp.full((head_count, tok_rows), far_below, jnp.float32),
        jnp.zeros((head_count, tok_rows), jnp.float32),
        jnp.zeros((tok_rows, head_count, head_size), jnp.float32),
    )

    def wanted(offset, key_count):
        key_half = (offset + jnp.arange(key_count)) // half_len
        target = jnp.where(flipped, 1 - own_half, own_half)
        return key_half[None, :] == target[:, None]

    portion_keys = lax.all_gather(key_rows, "ctx", axis=0, tiled=True)
    portion_values = lax.all_gather(value_rows, "ctx", axis=0, tiled=True)
    needed = wanted(jnp.int32(0), portion_keys.shape[0])

    def update(state):
        return online_update(state, portion_keys, portion_values, needed)

    row_top, row_total, accumulated = lax.cond(jnp.any(needed), update, unchanged, start_state)
    context = accumulated / row_total.T[..., None]
    log_sum = row_top + jnp.log(row_total)
    context_low = context.reshape(tok_rows, model_width).astype(jnp.bfloat16)
    branch = jnp.dot(
        context_low, wout_full, preferred_element_type=jnp.float32
    ) + biasout_full.astype(jnp.float32)
    summed_one = inputs.astype(jnp.float32) + branch
    hidden, norm_one_back = jax.vjp(
        norm_rows, summed_one, gainone_full.astype(jnp.float32), shiftone_full.astype(jnp.float32)
    )
    hidden_low = hidden.astype(jnp.bfloat16)
    pre_active = jnp.dot(
        hidden_low, wup_full, preferred_element_type=jnp.float32
    ) + biasup_full.astype(jnp.float32)
    active, gelu_back = jax.vjp(gelu_exact, pre_active)
    active_low = active.astype(jnp.bfloat16)
    ffn_out = jnp.dot(
        active_low, wdown_full, preferred_element_type=jnp.float32
    ) + biasdown_full.astype(jnp.float32)
    output, norm_two_back = jax.vjp(
        norm_rows,
        hidden + ffn_out,
        gaintwo_full.astype(jnp.float32),
        shifttwo_full.astype(jnp.float32),
    )
    again = gathered
    wqkv_back = again[0]
    wout_back = again[3]
    wup_back = again[7]
    wdown_back = again[9]
    grad_two, grad_gain_two, grad_shift_two = norm_two_back(cotangent[0].astype(jnp.float32))
    grad_ffn = grad_two.astype(jnp.bfloat16)
    grad_bias_down = jnp.sum(grad_ffn.astype(jnp.float32), axis=0)
    grad_w_down = jnp.einsum("tf,td->fd", active_low, grad_ffn, preferred_element_type=jnp.float32)
    grad_active = jnp.einsum("td,fd->tf", grad_ffn, wdown_back, preferred_element_type=jnp.float32)
    (grad_pre_f,) = gelu_back(grad_active)
    grad_pre = grad_pre_f.astype(jnp.bfloat16)
    grad_bias_up = jnp.sum(grad_pre.astype(jnp.float32), axis=0)
    grad_w_up = jnp.einsum("tc,tf->cf", hidden_low, grad_pre, preferred_element_type=jnp.float32)
    grad_hidden = grad_two + jnp.einsum(
        "tf,cf->tc", grad_pre, wup_back, preferred_element_type=jnp.float32
    )
    grad_one, grad_gain_one, grad_shift_one = norm_one_back(grad_hidden)
    grad_branch = grad_one.astype(jnp.bfloat16)
    grad_bias_out = jnp.sum(grad_branch.astype(jnp.float32), axis=0)
    grad_w_out = jnp.einsum(
        "tc,td->cd", context_low, grad_branch, preferred_element_type=jnp.float32
    )
    grad_context = jnp.einsum(
        "td,cd->tc", grad_branch, wout_back, preferred_element_type=jnp.float32
    )
    grad_context = grad_context.astype(jnp.bfloat16).reshape(tok_rows, head_count, head_size)
    row_delta = jnp.sum(grad_context.astype(jnp.float32) * context, axis=-1).T

    def piece_grads(portion_keys, portion_values, needed):
        key_count = portion_keys.shape[0]
        key_heads = portion_keys.reshape(key_count, head_count, head_size)
        value_heads = portion_values.reshape(key_count, head_count, head_size)
        scores = scores_of(queries, key_heads)
        scores = jnp.where(needed[:, None, :], scores, far_below)
        probs = jnp.exp(scores - log_sum[..., None])
        probs_low = probs.astype(jnp.bfloat16)
        piece_v = jnp.einsum(
            "htk,thd->khd", probs_low, grad_context, preferred_element_type=jnp.float32
        ).reshape(key_count, model_width)
        grad_weights = jnp.einsum(
            "thd,khd->htk", grad_context, value_heads, preferred_element_type=jnp.float32
        )
        grad_scores = (probs * (grad_weights - row_delta[..., None])).astype(jnp.bfloat16)
        piece_q = 0.125 * jnp.einsum(
            "htk,khd->thd", grad_scores, key_heads, preferred_element_type=jnp.float32
        )
        piece_k = 0.125 * jnp.einsum(
            "htk,thd->khd", grad_scores, queries, preferred_element_type=jnp.float32
        ).reshape(key_count, model_width)
        return (piece_k, piece_v, piece_q)

    zero_queries = jnp.zeros((tok_rows, head_count, head_size), jnp.float32)

    def circle_step(step_index, running):
        turn_keys, turn_values, grad_keys, grad_values, grad_queries = running
        owner = (position_ctx - step_index) % group_size
        needed = wanted(owner * tok_rows, tok_rows)

        def update_grads(state):
            grad_k, grad_v, grad_q = state
            piece_k, piece_v, piece_q = piece_grads(turn_keys, turn_values, needed)
            return (grad_k + piece_k, grad_v + piece_v, grad_q + piece_q)

        grad_keys, grad_values, grad_queries = lax.cond(
            jnp.any(needed), update_grads, unchanged, (grad_keys, grad_values, grad_queries)
        )
        turn_keys, turn_values = passed_along((turn_keys, turn_values), "ctx", 1)
        grad_keys, grad_values = (
            passed_along(grad_keys.astype(jnp.bfloat16), "ctx", 1).astype(grad_keys.dtype),
            passed_along(grad_values.astype(jnp.bfloat16), "ctx", 1).astype(grad_values.dtype),
        )
        return (turn_keys, turn_values, grad_keys, grad_values, grad_queries)

    zero_rows = jnp.zeros((tok_rows, model_width), jnp.float32)
    circle_start = (key_rows, value_rows, zero_rows, zero_rows, zero_queries)
    circle_end = lax.fori_loop(0, group_size, circle_step, circle_start)
    grad_keys = circle_end[2]
    grad_values = circle_end[3]
    grad_queries = circle_end[4]
    grad_projected = jnp.concatenate(
        [grad_queries.reshape(tok_rows, model_width), grad_keys, grad_values], axis=1
    ).astype(jnp.bfloat16)
    grad_bias_q = jnp.sum(grad_projected[:, :model_width].astype(jnp.float32), axis=0)
    grad_bias_v = jnp.sum(grad_projected[:, 2 * model_width :].astype(jnp.float32), axis=0)
    grad_w_qkv = jnp.einsum("tc,tj->cj", inputs, grad_projected, preferred_element_type=jnp.float32)
    grad_inputs = grad_one + jnp.einsum(
        "tj,cj->tc", grad_projected, wqkv_back, preferred_element_type=jnp.float32
    )
    terms = (
        grad_w_qkv,
        grad_bias_q,
        grad_bias_v,
        grad_w_out,
        grad_bias_out,
        grad_gain_one,
        grad_shift_one,
        grad_w_up,
        grad_bias_up,
        grad_w_down,
        grad_bias_down,
        grad_gain_two,
        grad_shift_two,
    )
    owned = tuple(
        lax.psum_scatter(term.astype(jnp.bfloat16), "wt", scatter_dimension=0, tiled=True)
        for term in terms
    )
    totals = tuple(lax.psum(term, "ctx").astype(jnp.float32) for term in owned)
    return (
        output[None],
        grad_inputs[None],
        totals[0],
        totals[1],
        totals[2],
        totals[3],
        totals[4],
        totals[5],
        totals[6],
        totals[7],
        totals[8],
        totals[9],
        totals[10],
        totals[11],
        totals[12],
    )


def fast_layer(
    tokens,
    pairing,
    w_qkv,
    bias_q,
    bias_v,
    w_out,
    bias_out,
    gain_one,
    shift_one,
    w_up,
    bias_up,
    w_down,
    bias_down,
    gain_two,
    shift_two,
    cotangent,
):
    share = tokens.shape[2] // 4
    vectors = (bias_q, bias_v, bias_out, gain_one, shift_one, bias_down, gain_two, shift_two)
    row = lax.broadcasted_iota(jnp.int32, (8, share), 0)
    small_raw = jnp.zeros((8, share), jnp.bfloat16)
    for index, vector in enumerate(vectors):
        small_raw = jnp.where(row == index, vector[None, :], small_raw)
    made = whole_layer(
        tokens[0],
        cotangent[0],
        pairing,
        small_raw,
        bias_up.reshape(-1, 128),
        w_qkv,
        w_out,
        w_up,
        w_down,
    )
    output, grad_tokens, g_qkv, g_out, g_up, g_down, *small = finish(*made)
    small = [v.reshape(-1) for v in small]
    return (
        output[None],
        grad_tokens[None],
        g_qkv,
        small[0],
        small[1],
        g_out,
        small[2],
        small[3],
        small[4],
        g_up,
        small[8],
        g_down,
        small[5],
        small[6],
        small[7],
    )


def local(tokens, pairing, *rest):
    rows, width = tokens.shape[1:]
    heads = pairing.shape[0]
    inner = rest[7].shape[1]
    fits = (
        lax.axis_size("wt") == 4
        and lax.axis_size("ctx") == 8
        and tokens.shape[0] == 1
        and rows % BAND == 0
        and 3 * rows <= width
        and width % 256 == 0
        and heads % 4 == 0
        and width == 64 * heads
        and inner == 4 * width
    )
    layer = fast_layer if fits else general_layer
    return layer(tokens, pairing, *rest)


def solution(mesh):
    in_specs = (
        P("wt", "ctx", None),
        P(),
        P("wt", None),
        P("wt"),
        P("wt"),
        P("wt", None),
        P("wt"),
        P("wt"),
        P("wt"),
        P("wt", None),
        P("wt"),
        P("wt", None),
        P("wt"),
        P("wt"),
        P("wt"),
        P("wt", "ctx", None),
    )
    out_specs = (
        P("wt", "ctx", None),
        P("wt", "ctx", None),
        P("wt", None),
        P("wt"),
        P("wt"),
        P("wt", None),
        P("wt"),
        P("wt"),
        P("wt"),
        P("wt", None),
        P("wt"),
        P("wt", None),
        P("wt"),
        P("wt"),
        P("wt"),
    )
    return jax.shard_map(local, mesh=mesh, in_specs=in_specs, out_specs=out_specs, check_vma=False)
```

```python
import functools

import jax
import jax.numpy as jnp
from jax import lax
from jax.experimental import pallas as pl
from jax.experimental.pallas import tpu as pltpu
from jax.sharding import PartitionSpec as P

F32, BF16 = jnp.float32, jnp.bfloat16
MESH = pl.DeviceIdType.MESH
BAND = 32


def nn(a, b):
    return jnp.dot(a, b, preferred_element_type=F32)


def nt(a, b):
    return lax.dot_general(a, b, (((1,), (1,)), ((), ())), preferred_element_type=F32)


def aligned(start, multiple):
    return start if isinstance(start, int) else pl.multiple_of(start, multiple)


def chunk_of(index, size):
    return pl.ds(aligned(index * size, size), size)


class Wire:
    def __init__(self, sends, receives, anyone):
        self.sends, self.receives, self.anyone = sends, receives, anyone
        self.firsts, self.used, self.groups, self.started = {}, 0, {}, {}

    def slot(self, name, count=1):
        if name not in self.firsts:
            self.firsts[name] = self.used, count
            self.used += count
            assert self.used <= self.receives.shape[0]
        first, had = self.firsts[name]
        assert had == count
        return first

    def copy(self, slot, source, target, where, group):
        place = self.groups.setdefault(group, len(self.groups))
        assert place < self.sends.shape[0]
        return pltpu.make_async_remote_copy(
            src_ref=source,
            dst_ref=target,
            send_sem=self.sends.at[place],
            recv_sem=self.receives.at[slot],
            device_id=where,
            device_id_type=MESH,
        )

    def send(self, name, source, target, where):
        copy = self.copy(self.slot(name), source, target, where, name)
        copy.start()
        self.started[name] = copy

    def send_in(self, group, name, source, target, where):
        self.copy(self.slot(name), source, target, where, group).start()

    def gone(self, group, ref):
        self.copy(0, ref, ref, self.anyone, group).wait_send()

    def arrived(self, name, target):
        self.copy(self.slot(name), target, target, self.anyone, "none").wait_recv()

    def left(self, *names):
        for name in names:
            self.started.pop(name).wait_send()

    def close(self):
        self.left(*tuple(self.started))


class Place:
    def __init__(self):
        self.w = w = lax.axis_index("wt")
        self.c = c = lax.axis_index("ctx")
        self.core = core = c % 2
        self.other = 1 - core
        self.z = z = c // 2
        self.near = z % 2
        self.far = 1 - self.near
        self.nx = w + 1 - 2 * (w % 2)
        self.ny = (w + 2) % 4
        self.nd = 3 - w
        self.sib = (w, c + 1 - 2 * core)
        self.to_x, self.to_y, self.to_d = (self.nx, c), (self.ny, c), (self.nd, c)
        self.cross = (w, c + 2 - 4 * self.near)
        self.partner = (w, (c + 4) % 8)
        self.lines = [(w, spot * 2 + core) for spot in (z + 1 - 2 * (z % 2), (z + 2) % 4, 3 - z)]
        self.mate, self.middle = self.lines[0], self.lines[2]
        self.outer, self.inner = (z == 0) | (z == 3), (z == 1) | (z == 2)


def greet(peers):
    barrier = pltpu.get_barrier_semaphore()
    for peer in peers:
        pl.semaphore_signal(barrier, inc=1, device_id=peer, device_id_type=MESH)
    pl.semaphore_wait(barrier, len(peers))


class Part:
    def __init__(self, name, local, full, first, columns, place, wire):
        self.name, self.local, self.full, self.place, self.wire = name, local, full, place, wire
        self.rows = local.shape[0]
        self.first, self.columns = first, columns // 2

    def piece(self, owner, core, half=None):
        rows, start = self.rows, owner * self.rows
        if half is not None:
            rows = self.rows // 2
            start = start + half * rows
        return self.full.at[
            pl.ds(aligned(start, 16), rows),
            pl.ds(aligned(self.first + core * self.columns, 128), self.columns),
        ]

    def send(self, kind, source, target, where):
        self.wire.send_in(self.name, self.name + kind, source, target, where)

    def begin(self):
        at = self.place
        mine = self.local.at[
            :, pl.ds(aligned(self.first + at.core * self.columns, 128), self.columns)
        ]
        target = self.piece(at.w, at.core)
        self.send("a", mine, target, at.to_x)
        self.send("b", mine, target, at.to_y)

    def relay(self):
        at, wire = self.place, self.wire
        for kind, owner, half, on, where in (
            ("a", at.nx, 0, "c", at.to_y),
            ("b", at.ny, 1, "e", at.to_x),
        ):
            block = self.piece(owner, at.core)
            wire.arrived(self.name + kind, block)
            part = self.piece(owner, at.core, half)
            self.send(on, part, part, where)
            self.send("s", block, block, at.sib)

    def share(self):
        at, wire = self.place, self.wire
        for half, came in ((0, "c"), (1, "e")):
            block = self.piece(at.nd, at.core, half)
            wire.arrived(self.name + came, block)
            self.send("r", block, block, at.sib)

    def arrived(self, kind, pieces):
        block = self.full.at[pl.ds(0, pieces * self.rows), pl.ds(self.first, self.columns)]
        self.wire.arrived(self.name + kind, block)

    def near(self):
        self.arrived("s", 2)

    def last(self):
        self.arrived("r", 1)

    def finish(self):
        self.near()
        self.last()

    def gone(self):
        block = self.full.at[pl.ds(0, 3 * self.rows), pl.ds(self.first, 2 * self.columns)]
        self.wire.gone(self.name, block)


def in_bands(rows):
    def run(body):
        for first in range(0, rows, BAND):
            body(slice(first, first + BAND))

    return run


def in_columns(first, last):
    def run(body):
        for start in range(first, last, 256):
            body(slice(start, start + 256))

    return run


def add_into(target, *sources):
    rows, columns = sources[0].shape
    band = 16
    while columns * band * 2 <= 1 << 15 and rows % (band * 2) == 0:
        band *= 2

    @pl.loop(0, rows // band)
    def _(index):
        where = chunk_of(index, band)
        total = sources[0][where, :].astype(F32)
        for source in sources[1:]:
            total = total + source[where, :].astype(F32)
        target[where, :] = total.astype(target.dtype)


class Grad:
    def __init__(self, name, chunks, blocks, buffers, finals, place, wire, local_sem):
        self.name, self.chunks, self.blocks, self.finals = name, chunks, blocks, finals
        self.place, self.wire, self.local_sem = place, wire, local_sem
        self.from_x, self.from_y, self.diag_x, self.diag_y, self.low, self.high = buffers
        self.rows, self.columns = self.from_x.shape

    def half(self, ref, index):
        return ref.at[pl.ds(index * (self.rows // 2), self.rows // 2), :]

    def begin(self):
        at, wire = self.place, self.wire
        block = self.blocks(at.nd)
        wire.send(self.name + "a", self.half(block, 0), self.diag_x, at.to_x)
        wire.send(self.name + "b", self.half(block, 1), self.diag_y, at.to_y)

    def fold(self):
        at, wire = self.place, self.wire
        for kind, came, owner, index in (("a", self.diag_x, at.ny, 0), ("b", self.diag_y, at.nx, 1)):
            wire.arrived(self.name + kind, came)
            part = self.half(self.blocks(owner), index)
            add_into(part, part, came)

    def lanes(self, chunk):
        at = self.place
        return (
            self.hop("c", chunk, self.blocks(at.nx), self.from_x, at.to_x),
            self.hop("d", chunk, self.blocks(at.ny), self.from_y, at.to_y),
        )

    def push(self, to_x=(), to_y=()):
        for chunk in to_x:
            self.lanes(chunk)[0].start()
        for chunk in to_y:
            self.lanes(chunk)[1].start()

    def cut(self, ref, chunk):
        count = self.rows // self.chunks
        return ref.at[pl.ds(chunk * count, count), :]

    def hop(self, kind, chunk, source, target, where):
        slot = self.wire.slot(self.name + kind, self.chunks) + chunk
        return self.wire.copy(
            slot, self.cut(source, chunk), self.cut(target, chunk), where, self.name + kind
        )

    def outward(self, chunk):
        return self.hop("u", chunk, self.blocks(self.place.w), self.low, self.place.mate)

    def across(self, chunk):
        return self.hop("v", chunk, self.from_x, self.high, self.place.middle)

    def back(self, chunk):
        return self.hop("t", chunk, self.from_y, self.high, self.place.mate)

    def own(self, chunk):
        for copy in self.lanes(chunk):
            copy.wait_recv()
        part = self.cut(self.blocks(self.place.w), chunk)
        add_into(part, part, self.cut(self.from_x, chunk), self.cut(self.from_y, chunk))
        self.out(chunk)

    def out(self, chunk):
        @pl.when(self.place.outer)
        def _():
            self.outward(chunk).start()

    def chain(self, chunk):
        at = self.place

        @pl.when(at.inner)
        def _():
            self.outward(chunk).wait_recv()
            block = self.blocks(at.w)
            add_into(
                self.cut(self.from_x, chunk), self.cut(block, chunk), self.cut(self.low, chunk)
            )
            self.across(chunk).start()

    def total(self, chunk):
        at = self.place

        @pl.when(at.inner)
        def _():
            self.across(chunk).wait_recv()
            add_into(
                self.cut(self.from_y, chunk),
                self.cut(self.from_x, chunk),
                self.cut(self.high, chunk),
            )
            self.back(chunk).start()
            for copy in self.copies(chunk, self.from_y):
                copy.start()

    def copies(self, chunk, source):
        at, wire = self.place, self.wire
        piece, target = self.cut(source, chunk), self.finals(chunk, at.core)
        keep = pltpu.make_async_copy(piece, target, self.local_sem)
        slot = wire.slot(self.name + "s")
        return keep, wire.copy(slot, piece, target, at.sib, self.name + "s")

    def give(self, chunk):
        at = self.place

        @pl.when(at.outer)
        def _():
            self.back(chunk).wait_recv()
            for copy in self.copies(chunk, self.high):
                copy.start()

    def close(self):
        at, wire = self.place, self.wire
        whole = self.from_y
        pltpu.make_async_copy(whole, whole, self.local_sem).wait()
        wire.arrived(self.name + "s", whole)
        for kind in ("s", "c", "d"):
            wire.gone(self.name + kind, whole)

        @pl.when(at.outer)
        def _():
            wire.gone(self.name + "u", whole)

        @pl.when(at.inner)
        def _():
            wire.gone(self.name + "v", whole)
            wire.gone(self.name + "t", whole)


def layer_scratch(rows, width, inner, heads):
    pairs = heads // 2
    some = pairs // 2
    share = width // 4
    half = width // 2
    groups = 8

    def low(*shape):
        return pltpu.VMEM(shape, BF16)

    def wide(*shape):
        return pltpu.VMEM(shape, F32)

    scratch = dict(
        wqkv=low(width, 3 * width),
        wo=low(width, width),
        wu=low(width, inner),
        wd=low(inner, width),
        order=low(width, width),
        wo_order=low(width, width),
        tok=low(2, rows, width),
        cot=low(rows, width),
        small_own=low(16, width),
        small_in=low(3, 16, width),
        small=wide(16, width),
        bias_qkv=wide(8, 3 * width),
        bias_up=wide(8, inner),
        kv=low(pairs, 4, rows, 256),
        proj=low(rows, 3 * width),
        q=low(pairs, rows, 128),
        q_out=low(some, rows, 128),
        exps=low(heads, 4 * rows, rows),
        inverse=wide(heads, 1, rows),
        out_t=wide(pairs, 128, rows),
        ctx=low(pairs, rows, 128),
        ctx_out=low(some, rows, 128),
        ctx_nat=low(2, rows, width),
        hat_one=wide(rows, width),
        r_one=wide(rows, 1),
        flow=wide(rows, width),
        stage=wide(rows, width),
        result=wide(rows, width),
        hid=low(2, rows, width),
        act=low(2, rows, inner),
        slope=low(rows, inner),
        slope_in=low(rows, inner // 2),
        gf=low(rows, width),
        gf_in=low(rows, half),
        gb=low(rows, width),
        gb_in=low(rows, half),
        do=low(pairs, rows, 128),
        do_out=low(some, rows, 128),
        dq=low(pairs, rows, 128),
        dkv_in=low(pairs, rows, 256),
        tops=wide(heads, 1, rows),
        delta=wide(heads, 1, rows),
        dos=low(pairs, rows, 128),
        far_q=low(2, pairs, rows, 128),
        far_tops=wide(2, heads, 1, rows),
        far_delta=wide(2, heads, 1, rows),
        far_dos=low(2, pairs, rows, 128),
        gkv=low(2, rows, width),
        gj_in=low(rows, 3 * half),
        sums=wide(16, groups, width),
        sums_up=wide(groups, inner),
        vec=wide(16, width),
        vec_in=wide(16, width),
        vec_low=low(4, 16, width),
        vec_far=low(6, 16, width),
        dwd=low(4, inner // 4, half),
    )
    shapes = dict(
        d=(inner // 4, half), u=(2 * share, width), o=(share, half), q=(3 * share, half)
    )
    for name, (r, c) in shapes.items():
        for kind in ("fx", "fy", "lo", "hi"):
            scratch["g" + name + kind] = low(r, c)
        for kind in ("dx", "dy"):
            scratch["g" + name + kind] = low(r // 2, c)
    scratch["sends"] = pltpu.SemaphoreType.DMA((80,))
    scratch["receives"] = pltpu.SemaphoreType.DMA((180,))
    scratch["own_sems"] = pltpu.SemaphoreType.DMA((12,))
    return scratch


def layer_kernel(names, *refs):
    (
        tokens,
        cot_l,
        pairing,
        small_raw,
        bias_raw,
        qkv_l,
        out_l,
        up_l,
        down_l,
        output,
        grad_tokens,
        g_qkv,
        g_out,
        g_up,
        g_down,
        g_small,
    ) = refs[:16]
    s = dict(zip(names, refs[16:]))
    at = Place()
    wire = Wire(s["sends"], s["receives"], at.sib)
    rows, width = tokens.shape
    inner = up_l.shape[1]
    heads = pairing.shape[0]
    pairs, some = heads // 2, heads // 4
    size = width // heads
    half = width // 2
    keys = 4 * rows
    chunks = width // 256
    share = width // 4
    core, other = at.core, at.other

    greet([at.to_x, at.to_y, at.to_d, at.sib, at.cross, at.partner, at.middle])

    part_kv = Part("kv", qkv_l, s["wqkv"], width, 2 * width, at, wire)
    part_q = Part("q", qkv_l, s["wqkv"], 0, width, at, wire)
    part_o = Part("o", out_l, s["wo"], 0, width, at, wire)
    part_u = Part("u", up_l, s["wu"], 0, inner, at, wire)
    part_d = Part("d", down_l, s["wd"], 0, width, at, wire)
    part_kv.begin()
    part_q.begin()
    raw = small_raw[...]
    row = lax.broadcasted_iota(jnp.int32, (share, width), 0)
    column = lax.broadcasted_iota(jnp.int32, (share, width), 1)

    def spread(values, spot):
        place = jnp.where(column - row == spot * share, 1.0, 0.0).astype(BF16)
        return nn(values, place)

    own_row = lax.broadcasted_iota(jnp.int32, (8, width), 0) == at.w
    line = jnp.concatenate(
        [bias_raw[k : k + 1, :] for k in range(width // 128)], axis=1
    ).astype(F32)
    small_own = s["small_own"]
    small_own[...] = jnp.concatenate(
        [spread(raw, at.w), jnp.where(own_row, line, 0.0)], axis=0
    ).astype(BF16)
    for index, where in enumerate((at.to_x, at.to_y, at.to_d)):
        wire.send("sm" + str(index), small_own, s["small_in"].at[index], where)
    keeps = []
    for slot, (local, full) in enumerate(
        (
            (qkv_l, s["wqkv"].at[pl.ds(aligned(at.w * share, 16), share)]),
            (tokens, s["tok"].at[core]),
            (cot_l, s["cot"]),
            (out_l, s["wo"].at[pl.ds(aligned(at.w * share, 16), share)]),
            (up_l, s["wu"].at[pl.ds(aligned(at.w * share, 16), share)]),
            (down_l, s["wd"].at[pl.ds(aligned(at.w * (inner // 4), 16), inner // 4)]),
        )
    ):
        keeps.append(pltpu.make_async_copy(local, full, s["own_sems"].at[slot]))
        keeps[-1].start()
    wire.send("tok", tokens, s["tok"].at[core], at.sib)

    before = 0
    for head in range(heads):
        flag = pairing[head]
        spot = flag * (heads // 2 + before) + (1 - flag) * (head - before)
        before = before + flag
        row = lax.broadcasted_iota(jnp.int32, (size, width), 0)
        column = lax.broadcasted_iota(jnp.int32, (size, width), 1)
        s["order"][head * size : (head + 1) * size, :] = jnp.where(
            column - row == spot * size, 1.0, 0.0
        ).astype(BF16)

    part_kv.relay()
    part_q.relay()
    part_o.begin()
    part_u.begin()
    part_kv.share()
    for index in range(3):
        wire.arrived("sm" + str(index), s["small_in"].at[index])
    small = s["small"]
    small[...] = (
        small_own[...].astype(F32)
        + s["small_in"][0].astype(F32)
        + s["small_in"][1].astype(F32)
        + s["small_in"][2].astype(F32)
    )
    s["bias_qkv"][0:1, 0:width] = small[0:1, :]
    s["bias_qkv"][0:1, width : 2 * width] = jnp.zeros((1, width), F32)
    s["bias_qkv"][0:1, 2 * width :] = small[1:2, :]
    for index in range(inner // width):
        s["bias_up"][0:1, index * width : (index + 1) * width] = small[8 + index : 9 + index, :]
    keeps[0].wait()
    keeps[1].wait()
    part_kv.finish()

    tok, proj, order, kv = s["tok"], s["proj"], s["order"], s["kv"]
    own_slot = core * 2 + at.near

    def project(first, count):
        @in_columns(first * 256, (first + count) * 256)
        def _(where):
            made = nn(tok[core], s["wqkv"][:, where]) + s["bias_qkv"][0:1, where]
            proj[:, where] = made.astype(BF16)

    project(chunks, 2 * chunks)
    for index in range(chunks):
        columns = order[:, index * 256 : (index + 1) * 256]
        for kind in range(2):
            moved = nn(proj[:, (1 + kind) * width : (2 + kind) * width], columns).astype(BF16)
            for e in range(2):
                kv[2 * index + e, own_slot, :, kind * 128 : (kind + 1) * 128] = moved[
                    :, e * 128 : (e + 1) * 128
                ]
    near_base = wire.slot("near kv", pairs)
    far_base = wire.slot("far kv", pairs)
    pass_base = wire.slot("passed kv", pairs)

    def kv_copy(base, pair, slot, where):
        block = kv.at[pair, slot]
        return wire.copy(base + pair, block, block, where, "kv" + str(base))

    for pair in range(pairs):
        if pair < some:
            kv_copy(far_base, pair, own_slot, at.cross).start()
        kv_copy(near_base, pair, own_slot, at.sib).start()
    part_q.share()
    part_q.finish()
    project(0, chunks)
    q, q_out = s["q"], s["q_out"]
    for index in range(chunks):
        moved = nn(proj[:, 0:width], order[:, index * 256 : (index + 1) * 256]).astype(BF16)
        for e in range(2):
            pair = 2 * index + e
            block = moved[:, e * 128 : (e + 1) * 128]
            if pair < some:
                q[pair] = block
            else:
                q_out[pair - some] = block
    wire.send("queries", q_out, q.at[pl.ds(some, some)], at.partner)
    part_o.relay()
    part_d.begin()

    exps, inverse, out_t = s["exps"], s["inverse"], s["out_t"]

    def both(pair, first):
        return kv[pair, :, :, first : first + 128].reshape(keys, 128)

    def masked(block, e, axis=1):
        spot = lax.broadcasted_iota(jnp.int32, block.shape, axis)
        mine = spot < size if e == 0 else spot >= size
        return jnp.where(mine, block, jnp.zeros_like(block))

    def attend(pair):
        key_rows, value_rows = both(pair, 0), both(pair, 128)
        values_t = value_rows.T
        queries = q[pair] * jnp.asarray(size**-0.5, BF16)
        parts = []
        for e in range(2):
            scores = nt(key_rows, masked(queries, e))
            top = jnp.max(scores, axis=0, keepdims=True)
            raised = jnp.exp(scores - top)
            total = jnp.sum(raised, axis=0, keepdims=True)
            low = raised.astype(BF16)
            exps[2 * pair + e] = low
            s["tops"][2 * pair + e] = top
            one_over = 1.0 / total
            inverse[2 * pair + e] = one_over
            parts.append(nn(values_t[e * size : (e + 1) * size], low) * one_over)
        merged = jnp.concatenate(parts, axis=0)
        out_t[pair] = merged
        return merged.T.astype(BF16)

    def receive_kv(pair):
        kv_copy(far_base, pair, core * 2 + at.far, at.cross).wait_recv()
        kv_copy(pass_base, pair, core * 2 + at.far, at.sib).start()
        kv_copy(near_base, pair, other * 2 + at.near, at.sib).wait_recv()
        kv_copy(pass_base, pair, other * 2 + at.far, at.sib).wait_recv()

    ctx, ctx_out = s["ctx"], s["ctx_out"]
    back_base = wire.slot("ctx", some)

    def ctx_copy(index):
        return wire.copy(back_base + index, ctx_out.at[index], ctx.at[some + index], at.partner, "ctx")

    def attend_far(index):
        receive_kv(index + some)
        ctx_out[index] = attend(index + some)
        ctx_copy(index).start()

    @pl.loop(0, some)
    def _(index):
        receive_kv(index)
        kv_copy(far_base, index + some, own_slot, at.cross).start()
        ctx[index] = attend(index)

    part_o.share()
    wire.arrived("queries", q.at[pl.ds(some, some)])
    attend_far(0)
    part_u.relay()

    @pl.loop(1, some)
    def _(index):
        attend_far(index)

    part_o.finish()
    far_q, far_tops, far_delta, far_dos = (
        s[name] for name in ("far_q", "far_tops", "far_delta", "far_dos")
    )
    tops, delta, dos = s["tops"], s["delta"], s["dos"]
    wire.send("far q", q, far_q.at[core], at.cross)
    wire.send("far tops", tops, far_tops.at[core], at.cross)
    part_d.relay()
    keeps[2].wait()
    keeps[3].wait()
    ctx_nat, stage, wo_order = s["ctx_nat"], s["stage"], s["wo_order"]
    for index in range(chunks):
        where = slice(index * 256, (index + 1) * 256)
        wo_order[where, :] = nn(order[:, where].T, s["wo"][...]).astype(BF16)
    for index in range(some):
        ctx_copy(index).wait_recv()

    def permuted():
        return jnp.concatenate([ctx[pair] for pair in range(pairs)], axis=1)

    for index in range(chunks):
        where = slice(index * 256, (index + 1) * 256)
        stage[:, where] = nn(permuted(), wo_order[:, where])

    hat_one, r_one, flow, hid = s["hat_one"], s["r_one"], s["flow"], s["hid"]
    inv_width = 1.0 / width

    def mean(values):
        return jnp.sum(values, axis=-1, keepdims=True) * inv_width

    @in_bands(rows)
    def _(where):
        total = tok[core, where, :].astype(F32) + stage[where, :] + small[2:3, :]
        centred = total - mean(total)
        scale = lax.rsqrt(mean(centred * centred) + 1e-12)
        hat = centred * scale
        hat_one[where, :] = hat
        r_one[where, :] = scale
        hidden = hat * small[3:4, :] + small[4:5, :]
        flow[where, :] = hidden
        hid[core, where, :] = hidden.astype(BF16)

    wire.send("hid", hid.at[core], hid.at[core], at.sib)
    part_u.share()
    part_u.finish()
    keeps[4].wait()
    act, slope = s["act"], s["slope"]

    @in_columns(0, inner)
    def _(where):
        pre = nn(hid[core], s["wu"][:, where]) + s["bias_up"][0:1, where]
        below = 0.5 * (1.0 + lax.erf(pre * (0.5**0.5)))
        act[core, :, where] = (pre * below).astype(BF16)
        density = jnp.exp(pre * pre * -0.5) * 0.3989422804014327
        slope[:, where] = (below + pre * density).astype(BF16)

    wire.send("act", act.at[core], act.at[core], at.sib)
    wire.arrived("far q", far_q.at[core])
    wire.send("passed q", far_q.at[core], far_q.at[core], at.sib)
    wire.arrived("far tops", far_tops.at[core])
    wire.send("passed tops", far_tops.at[core], far_tops.at[core], at.sib)
    for index in range(chunks):
        where = slice(index * 256, (index + 1) * 256)
        ctx_nat[core, :, where] = nt(permuted(), order[where, :]).astype(BF16)
    wire.send("ctxn", ctx_nat.at[core], ctx_nat.at[core], at.sib)
    part_d.near()
    keeps[5].wait()
    quarter = inner // 4

    def down(owner, where):
        block = pl.ds(aligned(owner * quarter, 128), quarter)
        return nn(act[core, :, block], s["wd"][block, where])

    @in_columns(0, width)
    def _(where):
        stage[:, where] = down(at.w, where) + down(at.nx, where) + down(at.ny, where)

    part_d.share()
    part_d.last()

    @in_columns(0, width)
    def _(where):
        stage[:, where] += down(at.nd, where)

    result, gf, cot = s["result"], s["gf"], s["cot"]
    sums, sums_up = s["sums"], s["sums_up"]
    sums[...] = jnp.zeros_like(sums)

    def gather_rows(values):
        return jnp.sum(values.reshape(BAND // 8, 8, values.shape[-1]), axis=0)

    @in_bands(rows)
    def _(where):
        total = flow[where, :] + stage[where, :] + small[5:6, :]
        centred = total - mean(total)
        scale = lax.rsqrt(mean(centred * centred) + 1e-12)
        hat = centred * scale
        result[where, :] = hat
        g = cot[where, :].astype(F32) * small[6:7, :]
        grad = scale * (g - mean(g) - hat * mean(g * hat))
        flow[where, :] = grad
        gf[where, :] = grad.astype(BF16)

    def columns_of(which, count):
        return pl.ds(aligned(which * count, 128), count)

    wire.send("gf", gf.at[:, columns_of(other, half)], s["gf_in"], at.sib)

    def buffers(name):
        return [s["g" + name + kind] for kind in ("fx", "fy", "dx", "dy", "lo", "hi")]

    dwd, wd, wu = s["dwd"], s["wd"], s["wu"]

    def side_by_side(first, count, owner):
        return wd.at[
            pl.ds(aligned(first + (owner // 2) * count, 16), count),
            pl.ds(aligned((owner % 2) * half, 128), half),
        ]

    def dwo(owner):
        return side_by_side(2 * width + 6 * share, share, owner)

    def dwq(owner):
        return side_by_side(2 * width, 3 * share, owner)

    grad_d = Grad(
        "gd",
        4,
        lambda r: dwd.at[r],
        buffers("d"),
        lambda i, k: g_down.at[pl.ds(i * (inner // 16), inner // 16), columns_of(k, half)],
        at,
        wire,
        s["own_sems"].at[8],
    )
    grad_u = Grad(
        "gu",
        4,
        lambda r: wd.at[pl.ds(aligned(r * (2 * share), 16), 2 * share), :],
        buffers("u"),
        lambda i, k: g_up.at[
            pl.ds((i % 2) * (share // 2), share // 2), columns_of(2 * k + i // 2, width)
        ],
        at,
        wire,
        s["own_sems"].at[9],
    )
    grad_o = Grad(
        "go",
        1,
        dwo,
        buffers("o"),
        lambda i, k: g_out.at[:, columns_of(k, half)],
        at,
        wire,
        s["own_sems"].at[10],
    )
    grad_q = Grad(
        "gq",
        6,
        dwq,
        buffers("q"),
        lambda i, k: g_qkv.at[
            pl.ds((i % 2) * (share // 2), share // 2), columns_of(3 * k + i // 2, half)
        ],
        at,
        wire,
        s["own_sems"].at[11],
    )

    def back_through(first, last):
        @in_columns(first, last)
        def _(where):
            grad = nt(gf[...], wd[where, :]) * slope[:, where].astype(F32)
            low = grad.astype(BF16)
            slope[:, where] = low
            sums_up[:, where] = jnp.sum(low.astype(F32).reshape(rows // 8, 8, 256), axis=0)

    back_through(0, 3 * inner // 4)
    wire.arrived("act", act.at[other])
    wire.arrived("gf", s["gf_in"])

    def down_grad(owner):
        where = pl.ds(aligned(owner * quarter, 128), quarter)
        made = nn(act[core, :, where].T, gf[:, columns_of(core, half)])
        made = made + nn(act[other, :, where].T, s["gf_in"][...])
        dwd[owner] = made.astype(BF16)

    down_grad(at.nd)
    grad_d.begin()
    back_through(3 * inner // 4, inner)
    wire.send("slope", slope.at[:, columns_of(other, inner // 2)], s["slope_in"], at.sib)

    @in_columns(0, width)
    def _(where):
        stage[:, where] = nt(slope[...], wu[where, :])


    gb = s["gb"]

    @in_bands(rows)
    def _(where):
        grad_hidden = flow[where, :] + stage[where, :]
        hat = hat_one[where, :]
        g = grad_hidden * small[3:4, :]
        grad = r_one[where, :] * (g - mean(g) - hat * mean(g * hat))
        flow[where, :] = grad
        gb[where, :] = grad.astype(BF16)
        stage[where, :] = grad_hidden

    wire.send("gb", gb.at[:, columns_of(other, half)], s["gb_in"], at.sib)

    do, do_out = s["do"], s["do_out"]
    for index in range(chunks):
        moved = nt(gb[...], wo_order[index * 256 : (index + 1) * 256, :]).astype(BF16)
        for e in range(2):
            pair = 2 * index + e
            block = moved[:, e * 128 : (e + 1) * 128]
            if pair < some:
                do[pair] = block
            else:
                do_out[pair - some] = block
    wire.send("do", do_out, do.at[pl.ds(some, some)], at.partner)

    def prepare(pair):
        do_t = do[pair].astype(F32).T
        scaled = jnp.concatenate(
            [do_t[e * size : (e + 1) * size] * inverse[2 * pair + e] for e in range(2)], axis=0
        )
        product = scaled * out_t[pair]
        for e in range(2):
            delta[2 * pair + e] = jnp.sum(product[e * size : (e + 1) * size], axis=0, keepdims=True)
        dos[pair] = scaled.T.astype(BF16)

    group_d = [pl.ds(0, some), pl.ds(some, some)]
    group_h = [pl.ds(0, 2 * some), pl.ds(2 * some, 2 * some)]

    def send_group(g):
        wire.send(
            "far do" + str(g), dos.at[group_d[g]], far_dos.at[core, group_d[g]], at.cross
        )
        wire.send(
            "far de" + str(g), delta.at[group_h[g]], far_delta.at[core, group_h[g]], at.cross
        )

    def pass_group(g):
        for kind, ref, group in (("do", far_dos, group_d), ("de", far_delta, group_h)):
            block = ref.at[core, group[g]]
            wire.arrived("far " + kind + str(g), block)
            wire.send("passed " + kind + str(g), block, block, at.sib)

    def have_group(g):
        wire.arrived("passed do" + str(g), far_dos.at[other, group_d[g]])
        wire.arrived("passed de" + str(g), far_delta.at[other, group_h[g]])

    @pl.loop(0, some)
    def _(index):
        prepare(index)

    send_group(0)
    for owner in (at.nx, at.ny):
        down_grad(owner)
    grad_d.push((0, 1), (2, 3))
    down_grad(at.w)
    part_d.gone()
    wire.arrived("hid", hid.at[other])
    wire.arrived("slope", s["slope_in"])
    mine_t, theirs_t = hid[core].T, hid[other].T
    for index in range(inner // 2 // half):
        where = pl.ds(aligned(core * (inner // 2) + index * half, 128), half)
        made = nn(mine_t, slope[:, where]) + nn(
            theirs_t, s["slope_in"][:, index * half : (index + 1) * half]
        )
        made = made.astype(BF16)
        for owner in range(4):
            first = owner * 2 * share + (index // 2) * share
            wd[first : first + share, (index % 2) * half : (index % 2 + 1) * half] = made[
                owner * share : (owner + 1) * share
            ]
    wire.arrived("ctxn", ctx_nat.at[other])
    wire.arrived("gb", s["gb_in"])
    made = nn(ctx_nat[core].T, gb[:, columns_of(core, half)]) + nn(
        ctx_nat[other].T, s["gb_in"][...]
    )
    made = made.astype(BF16)
    for owner in range(4):
        dwo(owner)[...] = made[owner * share : (owner + 1) * share]
    grad_d.fold()
    grad_d.push((2, 3), (0, 1))
    grad_u.begin()
    grad_u.push((0,), (2,))
    grad_o.begin()

    part_u.gone()
    dq, dq_out, dkv_in = s["dq"], s["do_out"], s["dkv_in"]
    near_d = wire.slot("near dkv", pairs)
    dq_base = wire.slot("dq", some)
    lots = inner // 512

    def tile(pair, which):
        return wu.at[
            pl.ds(aligned((pair // lots) * rows, 16), rows),
            pl.ds(aligned((pair % lots) * 512 + which * 256, 256), 256),
        ]

    def dkv_near(pair):
        return wire.copy(near_d + pair, tile(pair, other), dkv_in.at[pair], at.sib, "near dkv")

    def two_blocks(pair, chip, first):
        return jnp.concatenate(
            [kv[pair, k * 2 + chip, :, first : first + 128] for k in range(2)], axis=0
        )

    def attend_back(pair):
        queries = q[pair] * jnp.asarray(size**-0.5, BF16)
        dq_parts = [None, None]
        dv = dk = None
        for chip in (at.near, at.far):
            key_rows, value_rows = two_blocks(pair, chip, 0), two_blocks(pair, chip, 128)
            keys_t = key_rows.T
            for e in range(2):
                low = jnp.concatenate(
                    [
                        exps[2 * pair + e, pl.ds(aligned((k * 2 + chip) * rows, 16), rows), :]
                        for k in range(2)
                    ],
                    axis=0,
                )
                mine = masked(dos[pair], e)
                grad_w = nt(value_rows, mine)
                grad_s = (low.astype(F32) * (grad_w - delta[2 * pair + e])).astype(BF16)
                more_q = nn(keys_t[e * size : (e + 1) * size], grad_s)
                dq_parts[e] = more_q if dq_parts[e] is None else dq_parts[e] + more_q
                if chip is at.near:
                    more_v = nn(low, mine)
                    more_k = nn(grad_s, masked(queries, e))
                    dv = more_v if dv is None else dv + more_v
                    dk = more_k if dk is None else dk + more_k
            if chip is at.near:
                made = jnp.concatenate([dk, dv], axis=1).astype(BF16)
                for k in range(2):
                    tile(pair, k)[...] = made[k * rows : (k + 1) * rows]
                dkv_near(pair).start()
        return (jnp.concatenate(dq_parts, axis=0).T * size**-0.5).astype(BF16)

    gkv = s["gkv"]

    def far_back(pair):
        queries = far_q[:, pair].reshape(2 * rows, 128) * jnp.asarray(size**-0.5, BF16)
        grads = far_dos[:, pair].reshape(2 * rows, 128)
        key_rows, value_rows = kv[pair, own_slot, :, 0:128], kv[pair, own_slot, :, 128:256]
        dv = dk = None
        for e in range(2):
            head = 2 * pair + e
            top = jnp.concatenate([far_tops[k, head] for k in range(2)], axis=1)
            less = jnp.concatenate([far_delta[k, head] for k in range(2)], axis=1)
            mine, asking = masked(grads, e), masked(queries, e)
            low = jnp.exp(nt(key_rows, asking) - top).astype(BF16)
            grad_s = (low.astype(F32) * (nt(value_rows, mine) - less)).astype(BF16)
            more_v, more_k = nn(low, mine), nn(grad_s, asking)
            dv = more_v if dv is None else dv + more_v
            dk = more_k if dk is None else dk + more_k
        dkv_near(pair).wait_recv()
        own = tile(pair, core)
        where = pl.ds(aligned(pair * 128, 128), 128)
        for kind, made in ((0, dk), (1, dv)):
            cut = slice(kind * 128, (kind + 1) * 128)
            gkv[kind, :, where] = (
                made + own[:, cut].astype(F32) + dkv_in[pair, :, cut].astype(F32)
            ).astype(BF16)

    def dq_copy(index):
        return wire.copy(dq_base + index, dq_out.at[index], dq.at[some + index], at.partner, "dq")

    @pl.loop(0, some)
    def _(index):
        dq[index] = attend_back(index)

    wire.arrived("do", do.at[pl.ds(some, some)])

    @pl.loop(some, pairs)
    def _(index):
        prepare(index)

    send_group(1)
    pass_group(0)
    wire.left("do")
    grad_d.own(0)

    @pl.loop(0, some)
    def _(index):
        dq_out[index] = attend_back(index + some)
        dq_copy(index).start()

    for chunk in (2, 1, 3):
        grad_d.own(chunk)
    pass_group(1)
    wire.arrived("passed q", far_q.at[other])
    wire.arrived("passed tops", far_tops.at[other])
    have_group(0)

    @pl.loop(0, some)
    def _(index):
        far_back(index)

    grad_d.chain(0)
    @pl.loop(0, rows // BAND, unroll=2)
    def _(index):
        where = chunk_of(index, BAND)
        hat = result[where, :]
        result[where, :] = hat * small[6:7, :] + small[7:8, :]
        back = cot[where, :].astype(F32)
        sums[6] += gather_rows(back * hat)
        sums[7] += gather_rows(back)
        sums[5] += gather_rows(gf[where, :].astype(F32))
        grad_hidden = stage[where, :]
        sums[3] += gather_rows(grad_hidden * hat_one[where, :])
        sums[4] += gather_rows(grad_hidden)
        sums[2] += gather_rows(gb[where, :].astype(F32))

    keep_out = pltpu.make_async_copy(result, output, s["own_sems"].at[7])
    keep_out.start()
    wire.left(*[name for name in wire.started if name[:2] not in ("gd", "gu", "go")])
    part_kv.gone()
    part_q.gone()
    part_o.gone()
    for base in (far_base, near_base, pass_base):
        wire.gone("kv" + str(base), kv.at[:, 0])
    wire.gone("ctx", ctx_out)
    have_group(1)

    @pl.loop(some, pairs)
    def _(index):
        far_back(index)

    grad_u.fold()
    grad_u.push((1, 2), (0, 1))

    for index in range(some):
        dq_copy(index).wait_recv()
    merged = jnp.concatenate([dq[pair] for pair in range(pairs)], axis=1)
    for index in range(chunks):
        where = slice(index * 256, (index + 1) * 256)
        rows_of = order[where, :]
        for kind in range(3):
            source = merged if kind == 0 else gkv[kind - 1]
            low = nt(source, rows_of).astype(BF16)
            proj[:, kind * width + index * 256 : kind * width + (index + 1) * 256] = low
            if kind != 1:
                sums[kind // 2, :, where] = jnp.sum(
                    low.astype(F32).reshape(rows // 8, 8, 256), axis=0
                )
    wire.send("gj", proj.at[:, columns_of(other, 3 * half)], s["gj_in"], at.sib)

    vec, vec_in, vec_low, vec_far = s["vec"], s["vec_in"], s["vec_low"], s["vec_far"]
    for row in range(8):
        vec[row : row + 1, :] = jnp.sum(sums[row], axis=0, keepdims=True)
    for index in range(inner // width):
        vec[8 + index : 9 + index, :] = jnp.sum(
            sums_up[:, index * width : (index + 1) * width], axis=0, keepdims=True
        )
    for row in range(8 + inner // width, 16):
        vec[row : row + 1, :] = jnp.zeros((1, width), F32)
    wire.send("va", vec, vec_in, at.sib)

    grad_d.chain(2)
    grad_d.total(0)
    wire.arrived("tok", tok.at[other])
    wire.arrived("gj", s["gj_in"])
    mine_t, theirs_t = tok[core].T, tok[other].T
    for index in range(3):
        where = pl.ds(aligned(core * (3 * half) + index * half, 128), half)
        made = nn(mine_t, proj[:, where]) + nn(
            theirs_t, s["gj_in"][:, index * half : (index + 1) * half]
        )
        made = made.astype(BF16)
        for owner in range(4):
            dwq(owner)[index * share : (index + 1) * share, :] = made[
                owner * share : (owner + 1) * share
            ]
    grad_q.begin()
    grad_u.push((3,), (3,))
    grad_o.fold()
    grad_o.push((0,), (0,))
    grad_u.own(0)
    grad_d.chain(1)
    grad_d.total(2)
    wire.arrived("va", vec_in)
    vec_low[0] = (vec_in[...] + vec[...]).astype(BF16)
    for index, where in enumerate((at.to_x, at.to_y, at.to_d)):
        wire.send("vb" + str(index), vec_low.at[0], vec_far.at[index], where)

    keep_out.wait()

    @in_columns(0, width)
    def _(where):
        result[:, where] = nt(proj[...], s["wqkv"][where, :]) + flow[:, where]

    keep_grad = pltpu.make_async_copy(result, grad_tokens, s["own_sems"].at[7])
    keep_grad.start()
    def vec_hop(name, place, far, where):
        return wire.copy(wire.slot(name), vec_low.at[place], vec_far.at[far], where, name)

    def vec_out():
        return vec_hop("vu", 1, 3, at.mate)

    def vec_across():
        return vec_hop("vv", 2, 4, at.middle)

    def vec_back():
        return vec_hop("vt", 3, 5, at.mate)

    def vec_sum(*parts):
        total = parts[0].astype(F32)
        for part in parts[1:]:
            total = total + part.astype(F32)
        return total

    grad_u.own(1)
    grad_d.chain(3)
    grad_d.total(1)
    grad_u.own(2)
    grad_u.chain(0)
    grad_q.fold()
    grad_q.push((0, 1, 2, 3, 4, 5), (0, 1, 2, 3, 4, 5))
    grad_d.total(3)
    grad_u.total(0)
    grad_u.chain(1)
    grad_u.own(3)
    grad_u.chain(2)
    grad_u.total(1)
    grad_o.own(0)
    grad_u.total(2)
    grad_q.own(0)
    grad_u.chain(3)
    grad_q.own(1)
    for index in range(3):
        wire.arrived("vb" + str(index), vec_far.at[index])
    vec_low[1] = (
        vec_sum(vec_low[0], vec_far[0]) + vec_sum(vec_far[1], vec_far[2])
    ).astype(BF16)

    @pl.when(at.outer)
    def _():
        vec_out().start()

    grad_o.chain(0)
    grad_u.total(3)
    grad_q.own(2)
    grad_q.chain(0)
    grad_q.chain(1)
    grad_q.own(3)

    @pl.when(at.inner)
    def _():
        vec_out().wait_recv()
        vec_low[2] = vec_sum(vec_low[1], vec_far[3]).astype(BF16)
        vec_across().start()

    grad_q.chain(2)
    grad_o.total(0)
    grad_q.total(0)
    grad_q.own(4)
    grad_q.chain(3)
    grad_q.total(1)
    grad_q.own(5)
    grad_q.chain(4)
    grad_q.total(2)
    grad_q.chain(5)
    grad_q.total(3)

    @pl.when(at.inner)
    def _():
        vec_across().wait_recv()
        total = vec_sum(vec_low[2], vec_far[4]).astype(BF16)
        vec_low[3] = total
        vec_back().start()
        vec_in[...] = total.astype(F32)

    grad_q.total(4)
    grad_q.total(5)
    for chunk in range(4):
        grad_d.give(chunk)
    for chunk in range(4):
        grad_u.give(chunk)
    grad_o.give(0)
    for chunk in range(4):
        grad_q.give(chunk)

    @pl.when(at.outer)
    def _():
        vec_back().wait_recv()
        vec_in[...] = vec_far[5].astype(F32)

    keep_small = pltpu.make_async_copy(vec_in, g_small, s["own_sems"].at[6])
    keep_small.start()
    grad_q.give(4)
    grad_q.give(5)

    @pl.when(at.outer)
    def _():
        vec_out().wait_send()

    @pl.when(at.inner)
    def _():
        vec_across().wait_send()
        vec_back().wait_send()

    grad_d.close()
    grad_u.close()
    grad_o.close()
    grad_q.close()
    keep_grad.wait()
    keep_small.wait()
    wire.gone("near dkv", dkv_in)
    wire.gone("dq", dq_out)
    wire.close()


def whole_layer(
    tokens, cotangent, pairing, small_raw, bias_raw, w_qkv, w_out, w_up, w_down
):
    rows, width = tokens.shape
    inner = w_up.shape[1]
    scratch = layer_scratch(rows, width, inner, pairing.shape[0])
    hbm = pl.BlockSpec(memory_space=pl.ANY)
    vmem = pl.BlockSpec(memory_space=pltpu.VMEM)
    smem = pl.BlockSpec(memory_space=pltpu.SMEM)
    return pl.pallas_call(
        functools.partial(layer_kernel, tuple(scratch)),
        out_shape=[
            jax.ShapeDtypeStruct((rows, width), F32),
            jax.ShapeDtypeStruct((rows, width), F32),
            jax.ShapeDtypeStruct(w_qkv.shape, BF16),
            jax.ShapeDtypeStruct(w_out.shape, BF16),
            jax.ShapeDtypeStruct(w_up.shape, BF16),
            jax.ShapeDtypeStruct(w_down.shape, BF16),
            jax.ShapeDtypeStruct((16, width), F32),
        ],
        in_specs=[hbm, hbm, smem, vmem, vmem, hbm, hbm, hbm, hbm],
        out_specs=[hbm] * 7,
        scratch_shapes=list(scratch.values()),
        compiler_params=pltpu.CompilerParams(
            collective_id=0, has_side_effects=True, vmem_limit_bytes=60 << 20
        ),
        name="whole_layer",
    )(tokens, cotangent, pairing, small_raw, bias_raw, w_qkv, w_out, w_up, w_down)


def finish_kernel(share, *refs):
    wide, small, outs = refs[:6], refs[6], refs[7:]
    for source, target in zip(wide, outs[:6]):
        target[...] = source[...].astype(F32)

    @pl.when(pl.program_id(0) == 0)
    def _():
        w = lax.axis_index("wt")
        values = small[...]
        mine = jnp.zeros((8, share), F32)
        line = jnp.zeros((1, 4 * share), F32)
        for owner in range(4):
            mine = mine + jnp.where(
                w == owner, values[:8, owner * share : (owner + 1) * share], 0.0
            )
            line = line + jnp.where(w == owner, values[8 + owner : 9 + owner], 0.0)
        for row in range(8):
            outs[6 + row][...] = mine[row : row + 1]
        outs[14][...] = line.reshape(4 * share)


def finish(*arrays):
    steps = 2
    wide, small = arrays[:6], arrays[6]
    share = small.shape[1] // 4

    def blocks(array):
        return pl.BlockSpec((array.shape[0] // steps, array.shape[1]), lambda i: (i, 0))

    def fixed(shape):
        return pl.BlockSpec(shape, lambda i: (0,) * len(shape))

    shapes = [(1, share)] * 8 + [(4 * share,)]
    return pl.pallas_call(
        functools.partial(finish_kernel, share),
        grid=(steps,),
        out_shape=[jax.ShapeDtypeStruct(v.shape, F32) for v in wide]
        + [jax.ShapeDtypeStruct(v, F32) for v in shapes],
        in_specs=[blocks(v) for v in wide] + [fixed(small.shape)],
        out_specs=[blocks(v) for v in wide] + [fixed(v) for v in shapes],
        compiler_params=pltpu.CompilerParams(vmem_limit_bytes=60 << 20),
        name="finish",
    )(*arrays)


far_below = -1e30


def passed_along(value, axis, steps):
    count = lax.axis_size(axis)
    pairs = [(source, (source + steps) % count) for source in range(count)]
    return lax.ppermute(value, axis, pairs)


def norm_rows(values, gains, shifts):
    average = jnp.mean(values, axis=-1, keepdims=True)
    centred = values - average
    spread = jnp.mean(centred * centred, axis=-1, keepdims=True)
    return centred * lax.rsqrt(spread + 1e-12) * gains + shifts


def gelu_exact(pre_active):
    return jax.nn.gelu(pre_active, approximate=False)


def scores_of(queries, key_heads):
    return (
        jnp.einsum("thd,khd->htk", queries, key_heads, preferred_element_type=jnp.float32) * 0.125
    )


def unchanged(running):
    return running


def general_layer(
    tokens,
    pairing,
    w_qkv,
    bias_q,
    bias_v,
    w_out,
    bias_out,
    gain_one,
    shift_one,
    w_up,
    bias_up,
    w_down,
    bias_down,
    gain_two,
    shift_two,
    cotangent,
):
    local_params = (
        w_qkv,
        bias_q,
        bias_v,
        w_out,
        bias_out,
        gain_one,
        shift_one,
        w_up,
        bias_up,
        w_down,
        bias_down,
        gain_two,
        shift_two,
    )
    gathered = tuple(lax.all_gather(v, "wt", axis=0, tiled=True) for v in local_params)
    (
        wqkv_full,
        biasq_full,
        biasv_full,
        wout_full,
        biasout_full,
        gainone_full,
        shiftone_full,
        wup_full,
        biasup_full,
        wdown_full,
        biasdown_full,
        gaintwo_full,
        shifttwo_full,
    ) = gathered
    tok_rows = tokens.shape[1]
    model_width = tokens.shape[2]
    head_count = pairing.shape[0]
    head_size = model_width // head_count
    group_size = lax.axis_size("ctx")
    position_ctx = lax.axis_index("ctx")
    half_len = tok_rows * group_size // 2
    own_half = position_ctx * tok_rows // half_len
    flipped = pairing == 1
    inputs = tokens[0]
    bias_cat = jnp.concatenate(
        [
            biasq_full.astype(jnp.float32),
            jnp.zeros((model_width,), jnp.float32),
            biasv_full.astype(jnp.float32),
        ]
    )
    projected = jnp.dot(inputs, wqkv_full, preferred_element_type=jnp.float32) + bias_cat
    projected_low = projected.astype(jnp.bfloat16)
    queries = projected_low[:, :model_width].reshape(tok_rows, head_count, head_size)
    key_rows = projected_low[:, model_width : 2 * model_width]
    value_rows = projected_low[:, 2 * model_width :]

    def online_update(state, portion_keys, portion_values, needed):
        row_top, row_total, accumulated = state
        key_count = portion_keys.shape[0]
        key_heads = portion_keys.reshape(key_count, head_count, head_size)
        value_heads = portion_values.reshape(key_count, head_count, head_size)
        scores = scores_of(queries, key_heads)
        scores = jnp.where(needed[:, None, :], scores, far_below)
        new_top = jnp.maximum(row_top, jnp.max(scores, axis=-1))
        factor = jnp.exp(row_top - new_top)
        weights = jnp.exp(scores - new_top[..., None])
        row_total = jnp.sum(weights, axis=-1)
        added = jnp.einsum(
            "htk,khd->thd",
            weights.astype(jnp.bfloat16),
            value_heads,
            preferred_element_type=jnp.float32,
        )
        accumulated = accumulated * factor.T[..., None] + added
        return (new_top, row_total, accumulated)

    start_state = (
        jnp.full((head_count, tok_rows), far_below, jnp.float32),
        jnp.zeros((head_count, tok_rows), jnp.float32),
        jnp.zeros((tok_rows, head_count, head_size), jnp.float32),
    )

    def wanted(offset, key_count):
        key_half = (offset + jnp.arange(key_count)) // half_len
        target = jnp.where(flipped, 1 - own_half, own_half)
        return key_half[None, :] == target[:, None]

    portion_keys = lax.all_gather(key_rows, "ctx", axis=0, tiled=True)
    portion_values = lax.all_gather(value_rows, "ctx", axis=0, tiled=True)
    needed = wanted(jnp.int32(0), portion_keys.shape[0])

    def update(state):
        return online_update(state, portion_keys, portion_values, needed)

    row_top, row_total, accumulated = lax.cond(jnp.any(needed), update, unchanged, start_state)
    context = accumulated / row_total.T[..., None]
    log_sum = row_top + jnp.log(row_total)
    context_low = context.reshape(tok_rows, model_width).astype(jnp.bfloat16)
    branch = jnp.dot(
        context_low, wout_full, preferred_element_type=jnp.float32
    ) + biasout_full.astype(jnp.float32)
    summed_one = inputs.astype(jnp.float32) + branch
    hidden, norm_one_back = jax.vjp(
        norm_rows, summed_one, gainone_full.astype(jnp.float32), shiftone_full.astype(jnp.float32)
    )
    hidden_low = hidden.astype(jnp.bfloat16)
    pre_active = jnp.dot(
        hidden_low, wup_full, preferred_element_type=jnp.float32
    ) + biasup_full.astype(jnp.float32)
    active, gelu_back = jax.vjp(gelu_exact, pre_active)
    active_low = active.astype(jnp.bfloat16)
    ffn_out = jnp.dot(
        active_low, wdown_full, preferred_element_type=jnp.float32
    ) + biasdown_full.astype(jnp.float32)
    output, norm_two_back = jax.vjp(
        norm_rows,
        hidden + ffn_out,
        gaintwo_full.astype(jnp.float32),
        shifttwo_full.astype(jnp.float32),
    )
    again = gathered
    wqkv_back = again[0]
    wout_back = again[3]
    wup_back = again[7]
    wdown_back = again[9]
    grad_two, grad_gain_two, grad_shift_two = norm_two_back(cotangent[0].astype(jnp.float32))
    grad_ffn = grad_two.astype(jnp.bfloat16)
    grad_bias_down = jnp.sum(grad_ffn.astype(jnp.float32), axis=0)
    grad_w_down = jnp.einsum("tf,td->fd", active_low, grad_ffn, preferred_element_type=jnp.float32)
    grad_active = jnp.einsum("td,fd->tf", grad_ffn, wdown_back, preferred_element_type=jnp.float32)
    (grad_pre_f,) = gelu_back(grad_active)
    grad_pre = grad_pre_f.astype(jnp.bfloat16)
    grad_bias_up = jnp.sum(grad_pre.astype(jnp.float32), axis=0)
    grad_w_up = jnp.einsum("tc,tf->cf", hidden_low, grad_pre, preferred_element_type=jnp.float32)
    grad_hidden = grad_two + jnp.einsum(
        "tf,cf->tc", grad_pre, wup_back, preferred_element_type=jnp.float32
    )
    grad_one, grad_gain_one, grad_shift_one = norm_one_back(grad_hidden)
    grad_branch = grad_one.astype(jnp.bfloat16)
    grad_bias_out = jnp.sum(grad_branch.astype(jnp.float32), axis=0)
    grad_w_out = jnp.einsum(
        "tc,td->cd", context_low, grad_branch, preferred_element_type=jnp.float32
    )
    grad_context = jnp.einsum(
        "td,cd->tc", grad_branch, wout_back, preferred_element_type=jnp.float32
    )
    grad_context = grad_context.astype(jnp.bfloat16).reshape(tok_rows, head_count, head_size)
    row_delta = jnp.sum(grad_context.astype(jnp.float32) * context, axis=-1).T

    def piece_grads(portion_keys, portion_values, needed):
        key_count = portion_keys.shape[0]
        key_heads = portion_keys.reshape(key_count, head_count, head_size)
        value_heads = portion_values.reshape(key_count, head_count, head_size)
        scores = scores_of(queries, key_heads)
        scores = jnp.where(needed[:, None, :], scores, far_below)
        probs = jnp.exp(scores - log_sum[..., None])
        probs_low = probs.astype(jnp.bfloat16)
        piece_v = jnp.einsum(
            "htk,thd->khd", probs_low, grad_context, preferred_element_type=jnp.float32
        ).reshape(key_count, model_width)
        grad_weights = jnp.einsum(
            "thd,khd->htk", grad_context, value_heads, preferred_element_type=jnp.float32
        )
        grad_scores = (probs * (grad_weights - row_delta[..., None])).astype(jnp.bfloat16)
        piece_q = 0.125 * jnp.einsum(
            "htk,khd->thd", grad_scores, key_heads, preferred_element_type=jnp.float32
        )
        piece_k = 0.125 * jnp.einsum(
            "htk,thd->khd", grad_scores, queries, preferred_element_type=jnp.float32
        ).reshape(key_count, model_width)
        return (piece_k, piece_v, piece_q)

    zero_queries = jnp.zeros((tok_rows, head_count, head_size), jnp.float32)

    def circle_step(step_index, running):
        turn_keys, turn_values, grad_keys, grad_values, grad_queries = running
        owner = (position_ctx - step_index) % group_size
        needed = wanted(owner * tok_rows, tok_rows)

        def update_grads(state):
            grad_k, grad_v, grad_q = state
            piece_k, piece_v, piece_q = piece_grads(turn_keys, turn_values, needed)
            return (grad_k + piece_k, grad_v + piece_v, grad_q + piece_q)

        grad_keys, grad_values, grad_queries = lax.cond(
            jnp.any(needed), update_grads, unchanged, (grad_keys, grad_values, grad_queries)
        )
        turn_keys, turn_values = passed_along((turn_keys, turn_values), "ctx", 1)
        grad_keys, grad_values = (
            passed_along(grad_keys.astype(jnp.bfloat16), "ctx", 1).astype(grad_keys.dtype),
            passed_along(grad_values.astype(jnp.bfloat16), "ctx", 1).astype(grad_values.dtype),
        )
        return (turn_keys, turn_values, grad_keys, grad_values, grad_queries)

    zero_rows = jnp.zeros((tok_rows, model_width), jnp.float32)
    circle_start = (key_rows, value_rows, zero_rows, zero_rows, zero_queries)
    circle_end = lax.fori_loop(0, group_size, circle_step, circle_start)
    grad_keys = circle_end[2]
    grad_values = circle_end[3]
    grad_queries = circle_end[4]
    grad_projected = jnp.concatenate(
        [grad_queries.reshape(tok_rows, model_width), grad_keys, grad_values], axis=1
    ).astype(jnp.bfloat16)
    grad_bias_q = jnp.sum(grad_projected[:, :model_width].astype(jnp.float32), axis=0)
    grad_bias_v = jnp.sum(grad_projected[:, 2 * model_width :].astype(jnp.float32), axis=0)
    grad_w_qkv = jnp.einsum("tc,tj->cj", inputs, grad_projected, preferred_element_type=jnp.float32)
    grad_inputs = grad_one + jnp.einsum(
        "tj,cj->tc", grad_projected, wqkv_back, preferred_element_type=jnp.float32
    )
    terms = (
        grad_w_qkv,
        grad_bias_q,
        grad_bias_v,
        grad_w_out,
        grad_bias_out,
        grad_gain_one,
        grad_shift_one,
        grad_w_up,
        grad_bias_up,
        grad_w_down,
        grad_bias_down,
        grad_gain_two,
        grad_shift_two,
    )
    owned = tuple(
        lax.psum_scatter(term.astype(jnp.bfloat16), "wt", scatter_dimension=0, tiled=True)
        for term in terms
    )
    totals = tuple(lax.psum(term, "ctx").astype(jnp.float32) for term in owned)
    return (
        output[None],
        grad_inputs[None],
        totals[0],
        totals[1],
        totals[2],
        totals[3],
        totals[4],
        totals[5],
        totals[6],
        totals[7],
        totals[8],
        totals[9],
        totals[10],
        totals[11],
        totals[12],
    )


def fast_layer(
    tokens,
    pairing,
    w_qkv,
    bias_q,
    bias_v,
    w_out,
    bias_out,
    gain_one,
    shift_one,
    w_up,
    bias_up,
    w_down,
    bias_down,
    gain_two,
    shift_two,
    cotangent,
):
    share = tokens.shape[2] // 4
    vectors = (bias_q, bias_v, bias_out, gain_one, shift_one, bias_down, gain_two, shift_two)
    row = lax.broadcasted_iota(jnp.int32, (8, share), 0)
    small_raw = jnp.zeros((8, share), jnp.bfloat16)
    for index, vector in enumerate(vectors):
        small_raw = jnp.where(row == index, vector[None, :], small_raw)
    made = whole_layer(
        tokens[0],
        cotangent[0],
        pairing,
        small_raw,
        bias_up.reshape(-1, 128),
        w_qkv,
        w_out,
        w_up,
        w_down,
    )
    output, grad_tokens, g_qkv, g_out, g_up, g_down, *small = finish(*made)
    small = [v.reshape(-1) for v in small]
    return (
        output[None],
        grad_tokens[None],
        g_qkv,
        small[0],
        small[1],
        g_out,
        small[2],
        small[3],
        small[4],
        g_up,
        small[8],
        g_down,
        small[5],
        small[6],
        small[7],
    )


def local(tokens, pairing, *rest):
    rows, width = tokens.shape[1:]
    heads = pairing.shape[0]
    inner = rest[7].shape[1]
    fits = (
        lax.axis_size("wt") == 4
        and lax.axis_size("ctx") == 8
        and tokens.shape[0] == 1
        and rows % BAND == 0
        and 3 * rows <= width
        and width % 256 == 0
        and heads % 4 == 0
        and width == 64 * heads
        and inner == 4 * width
    )
    layer = fast_layer if fits else general_layer
    return layer(tokens, pairing, *rest)


def solution(mesh):
    in_specs = (
        P("wt", "ctx", None),
        P(),
        P("wt", None),
        P("wt"),
        P("wt"),
        P("wt", None),
        P("wt"),
        P("wt"),
        P("wt"),
        P("wt", None),
        P("wt"),
        P("wt", None),
        P("wt"),
        P("wt"),
        P("wt"),
        P("wt", "ctx", None),
    )
    out_specs = (
        P("wt", "ctx", None),
        P("wt", "ctx", None),
        P("wt", None),
        P("wt"),
        P("wt"),
        P("wt", None),
        P("wt"),
        P("wt"),
        P("wt"),
        P("wt", None),
        P("wt"),
        P("wt", None),
        P("wt"),
        P("wt"),
        P("wt"),
    )
    return jax.shard_map(local, mesh=mesh, in_specs=in_specs, out_specs=out_specs, check_vma=False)
```

```python
import functools

import jax
import jax.numpy as jnp
from jax import lax
from jax.experimental import pallas as pl
from jax.experimental.pallas import tpu as pltpu
from jax.sharding import PartitionSpec as P

F32, BF16 = jnp.float32, jnp.bfloat16
MESH = pl.DeviceIdType.MESH
BAND = 32


def nn(a, b):
    return jnp.dot(a, b, preferred_element_type=F32)


def nt(a, b):
    return lax.dot_general(a, b, (((1,), (1,)), ((), ())), preferred_element_type=F32)


def aligned(start, multiple):
    return start if isinstance(start, int) else pl.multiple_of(start, multiple)


def chunk_of(index, size):
    return pl.ds(aligned(index * size, size), size)


class Wire:
    def __init__(self, sends, receives, anyone):
        self.sends, self.receives, self.anyone = sends, receives, anyone
        self.firsts, self.used, self.groups, self.started = {}, 0, {}, {}

    def slot(self, name, count=1):
        if name not in self.firsts:
            self.firsts[name] = self.used, count
            self.used += count
            assert self.used <= self.receives.shape[0]
        first, had = self.firsts[name]
        assert had == count
        return first

    def copy(self, slot, source, target, where, group):
        place = self.groups.setdefault(group, len(self.groups))
        assert place < self.sends.shape[0]
        return pltpu.make_async_remote_copy(
            src_ref=source,
            dst_ref=target,
            send_sem=self.sends.at[place],
            recv_sem=self.receives.at[slot],
            device_id=where,
            device_id_type=MESH,
        )

    def send(self, name, source, target, where):
        copy = self.copy(self.slot(name), source, target, where, name)
        copy.start()
        self.started[name] = copy

    def send_in(self, group, name, source, target, where):
        self.copy(self.slot(name), source, target, where, group).start()

    def gone(self, group, ref):
        self.copy(0, ref, ref, self.anyone, group).wait_send()

    def arrived(self, name, target):
        self.copy(self.slot(name), target, target, self.anyone, "none").wait_recv()

    def left(self, *names):
        for name in names:
            self.started.pop(name).wait_send()

    def close(self):
        self.left(*tuple(self.started))


class Place:
    def __init__(self):
        self.w = w = lax.axis_index("wt")
        self.c = c = lax.axis_index("ctx")
        self.core = core = c % 2
        self.other = 1 - core
        self.z = z = c // 2
        self.near = z % 2
        self.far = 1 - self.near
        self.nx = w + 1 - 2 * (w % 2)
        self.ny = (w + 2) % 4
        self.nd = 3 - w
        self.sib = (w, c + 1 - 2 * core)
        self.to_x, self.to_y, self.to_d = (self.nx, c), (self.ny, c), (self.nd, c)
        self.cross = (w, c + 2 - 4 * self.near)
        self.partner = (w, (c + 4) % 8)
        self.lines = [(w, spot * 2 + core) for spot in (z + 1 - 2 * (z % 2), (z + 2) % 4, 3 - z)]
        self.mate, self.middle = self.lines[0], self.lines[2]
        self.outer, self.inner = (z == 0) | (z == 3), (z == 1) | (z == 2)


def greet(peers):
    barrier = pltpu.get_barrier_semaphore()
    for peer in peers:
        pl.semaphore_signal(barrier, inc=1, device_id=peer, device_id_type=MESH)
    pl.semaphore_wait(barrier, len(peers))


class Part:
    def __init__(self, name, local, full, first, columns, place, wire):
        self.name, self.local, self.full, self.place, self.wire = name, local, full, place, wire
        self.rows = local.shape[0]
        self.first, self.columns = first, columns // 2

    def piece(self, owner, core, half=None):
        rows, start = self.rows, owner * self.rows
        if half is not None:
            rows = self.rows // 2
            start = start + half * rows
        return self.full.at[
            pl.ds(aligned(start, 16), rows),
            pl.ds(aligned(self.first + core * self.columns, 128), self.columns),
        ]

    def send(self, kind, source, target, where):
        self.wire.send_in(self.name, self.name + kind, source, target, where)

    def begin(self):
        at = self.place
        mine = self.local.at[
            :, pl.ds(aligned(self.first + at.core * self.columns, 128), self.columns)
        ]
        target = self.piece(at.w, at.core)
        self.send("a", mine, target, at.to_x)
        self.send("b", mine, target, at.to_y)

    def relay(self):
        at, wire = self.place, self.wire
        for kind, owner, half, on, where in (
            ("a", at.nx, 0, "c", at.to_y),
            ("b", at.ny, 1, "e", at.to_x),
        ):
            block = self.piece(owner, at.core)
            wire.arrived(self.name + kind, block)
            part = self.piece(owner, at.core, half)
            self.send(on, part, part, where)
            self.send("s", block, block, at.sib)

    def share(self):
        at, wire = self.place, self.wire
        for half, came in ((0, "c"), (1, "e")):
            block = self.piece(at.nd, at.core, half)
            wire.arrived(self.name + came, block)
            self.send("r", block, block, at.sib)

    def arrived(self, kind, pieces):
        block = self.full.at[pl.ds(0, pieces * self.rows), pl.ds(self.first, self.columns)]
        self.wire.arrived(self.name + kind, block)

    def near(self):
        self.arrived("s", 2)

    def last(self):
        self.arrived("r", 1)

    def finish(self):
        self.near()
        self.last()

    def gone(self):
        block = self.full.at[pl.ds(0, 3 * self.rows), pl.ds(self.first, 2 * self.columns)]
        self.wire.gone(self.name, block)


def in_bands(rows):
    def run(body):
        for first in range(0, rows, BAND):
            body(slice(first, first + BAND))

    return run


def in_columns(first, last):
    def run(body):
        for start in range(first, last, 256):
            body(slice(start, start + 256))

    return run


def add_into(target, *sources):
    rows, columns = sources[0].shape
    band = 16
    while columns * band * 2 <= 1 << 15 and rows % (band * 2) == 0:
        band *= 2

    @pl.loop(0, rows // band)
    def _(index):
        where = chunk_of(index, band)
        total = sources[0][where, :].astype(F32)
        for source in sources[1:]:
            total = total + source[where, :].astype(F32)
        target[where, :] = total.astype(target.dtype)


class Grad:
    def __init__(self, name, chunks, blocks, buffers, finals, place, wire, local_sem):
        self.name, self.chunks, self.blocks, self.finals = name, chunks, blocks, finals
        self.place, self.wire, self.local_sem = place, wire, local_sem
        self.from_x, self.from_y, self.diag_x, self.diag_y, self.low, self.high = buffers
        self.rows, self.columns = self.from_x.shape

    def half(self, ref, index):
        return ref.at[pl.ds(index * (self.rows // 2), self.rows // 2), :]

    def begin(self):
        at, wire = self.place, self.wire
        block = self.blocks(at.nd)
        wire.send(self.name + "a", self.half(block, 0), self.diag_x, at.to_x)
        wire.send(self.name + "b", self.half(block, 1), self.diag_y, at.to_y)

    def fold(self):
        at, wire = self.place, self.wire
        for kind, came, owner, index in (("a", self.diag_x, at.ny, 0), ("b", self.diag_y, at.nx, 1)):
            wire.arrived(self.name + kind, came)
            part = self.half(self.blocks(owner), index)
            add_into(part, part, came)

    def lanes(self, chunk):
        at = self.place
        return (
            self.hop("c", chunk, self.blocks(at.nx), self.from_x, at.to_x),
            self.hop("d", chunk, self.blocks(at.ny), self.from_y, at.to_y),
        )

    def push(self, to_x=(), to_y=()):
        for chunk in to_x:
            self.lanes(chunk)[0].start()
        for chunk in to_y:
            self.lanes(chunk)[1].start()

    def cut(self, ref, chunk):
        count = self.rows // self.chunks
        return ref.at[pl.ds(chunk * count, count), :]

    def hop(self, kind, chunk, source, target, where):
        slot = self.wire.slot(self.name + kind, self.chunks) + chunk
        return self.wire.copy(
            slot, self.cut(source, chunk), self.cut(target, chunk), where, self.name + kind
        )

    def outward(self, chunk):
        return self.hop("u", chunk, self.blocks(self.place.w), self.low, self.place.mate)

    def across(self, chunk):
        return self.hop("v", chunk, self.from_x, self.high, self.place.middle)

    def back(self, chunk):
        return self.hop("t", chunk, self.from_y, self.high, self.place.mate)

    def own(self, chunk):
        for copy in self.lanes(chunk):
            copy.wait_recv()
        part = self.cut(self.blocks(self.place.w), chunk)
        add_into(part, part, self.cut(self.from_x, chunk), self.cut(self.from_y, chunk))
        self.out(chunk)

    def out(self, chunk):
        @pl.when(self.place.outer)
        def _():
            self.outward(chunk).start()

    def chain(self, chunk):
        at = self.place

        @pl.when(at.inner)
        def _():
            self.outward(chunk).wait_recv()
            block = self.blocks(at.w)
            add_into(
                self.cut(self.from_x, chunk), self.cut(block, chunk), self.cut(self.low, chunk)
            )
            self.across(chunk).start()

    def total(self, chunk):
        at = self.place

        @pl.when(at.inner)
        def _():
            self.across(chunk).wait_recv()
            add_into(
                self.cut(self.from_y, chunk),
                self.cut(self.from_x, chunk),
                self.cut(self.high, chunk),
            )
            self.back(chunk).start()
            for copy in self.copies(chunk, self.from_y):
                copy.start()

    def copies(self, chunk, source):
        at, wire = self.place, self.wire
        piece, target = self.cut(source, chunk), self.finals(chunk, at.core)
        keep = pltpu.make_async_copy(piece, target, self.local_sem)
        slot = wire.slot(self.name + "s")
        return keep, wire.copy(slot, piece, target, at.sib, self.name + "s")

    def give(self, chunk):
        at = self.place

        @pl.when(at.outer)
        def _():
            self.back(chunk).wait_recv()
            for copy in self.copies(chunk, self.high):
                copy.start()

    def close(self):
        at, wire = self.place, self.wire
        whole = self.from_y
        pltpu.make_async_copy(whole, whole, self.local_sem).wait()
        wire.arrived(self.name + "s", whole)
        for kind in ("s", "c", "d"):
            wire.gone(self.name + kind, whole)

        @pl.when(at.outer)
        def _():
            wire.gone(self.name + "u", whole)

        @pl.when(at.inner)
        def _():
            wire.gone(self.name + "v", whole)
            wire.gone(self.name + "t", whole)


def layer_scratch(rows, width, inner, heads):
    pairs = heads // 2
    some = pairs // 2
    share = width // 4
    half = width // 2
    groups = 8

    def low(*shape):
        return pltpu.VMEM(shape, BF16)

    def wide(*shape):
        return pltpu.VMEM(shape, F32)

    scratch = dict(
        wqkv=low(width, 3 * width),
        wo=low(width, width),
        wu=low(width, inner),
        wd=low(inner, width),
        order=low(width, width),
        wo_order=low(width, width),
        tok=low(2, rows, width),
        cot=low(rows, width),
        small_own=low(16, width),
        small_in=low(3, 16, width),
        small=wide(16, width),
        bias_qkv=wide(8, 3 * width),
        bias_up=wide(8, inner),
        kv=low(pairs, 4, rows, 256),
        proj=low(rows, 3 * width),
        q=low(pairs, rows, 128),
        q_out=low(some, rows, 128),
        exps=low(heads, 4 * rows, rows),
        inverse=wide(heads, 1, rows),
        out_t=wide(pairs, 128, rows),
        ctx=low(pairs, rows, 128),
        ctx_out=low(some, rows, 128),
        ctx_nat=low(2, rows, width),
        hat_one=wide(rows, width),
        r_one=wide(rows, 1),
        flow=wide(rows, width),
        stage=wide(rows, width),
        result=wide(rows, width),
        hid=low(2, rows, width),
        act=low(2, rows, inner),
        slope=low(rows, inner),
        slope_in=low(rows, inner // 2),
        gf=low(rows, width),
        gf_in=low(rows, half),
        gb=low(rows, width),
        gb_in=low(rows, half),
        do=low(pairs, rows, 128),
        do_out=low(some, rows, 128),
        dq=low(pairs, rows, 128),
        dkv_in=low(pairs, rows, 256),
        tops=wide(heads, 1, rows),
        delta=wide(heads, 1, rows),
        dos=low(pairs, rows, 128),
        far_q=low(2, pairs, rows, 128),
        far_tops=wide(2, heads, 1, rows),
        far_delta=wide(2, heads, 1, rows),
        far_dos=low(2, pairs, rows, 128),
        gkv=low(2, rows, width),
        gj_in=low(rows, 3 * half),
        sums=wide(16, groups, width),
        sums_up=wide(groups, inner),
        vec=wide(16, width),
        vec_in=wide(16, width),
        vec_low=low(4, 16, width),
        vec_far=low(6, 16, width),
        dwd=low(4, inner // 4, half),
    )
    shapes = dict(
        d=(inner // 4, half), u=(2 * share, width), o=(share, half), q=(3 * share, half)
    )
    for name, (r, c) in shapes.items():
        for kind in ("fx", "fy", "lo", "hi"):
            scratch["g" + name + kind] = low(r, c)
        for kind in ("dx", "dy"):
            scratch["g" + name + kind] = low(r // 2, c)
    scratch["sends"] = pltpu.SemaphoreType.DMA((80,))
    scratch["receives"] = pltpu.SemaphoreType.DMA((180,))
    scratch["own_sems"] = pltpu.SemaphoreType.DMA((12,))
    return scratch


def layer_kernel(names, *refs):
    (
        tokens,
        cot_l,
        pairing,
        small_raw,
        bias_raw,
        qkv_l,
        out_l,
        up_l,
        down_l,
        output,
        grad_tokens,
        g_qkv,
        g_out,
        g_up,
        g_down,
        g_small,
    ) = refs[:16]
    s = dict(zip(names, refs[16:]))
    at = Place()
    wire = Wire(s["sends"], s["receives"], at.sib)
    rows, width = tokens.shape
    inner = up_l.shape[1]
    heads = pairing.shape[0]
    pairs, some = heads // 2, heads // 4
    size = width // heads
    half = width // 2
    keys = 4 * rows
    chunks = width // 256
    share = width // 4
    core, other = at.core, at.other

    greet([at.to_x, at.to_y, at.to_d, at.sib, at.cross, at.partner, at.middle])

    part_kv = Part("kv", qkv_l, s["wqkv"], width, 2 * width, at, wire)
    part_q = Part("q", qkv_l, s["wqkv"], 0, width, at, wire)
    part_o = Part("o", out_l, s["wo"], 0, width, at, wire)
    part_u = Part("u", up_l, s["wu"], 0, inner, at, wire)
    part_d = Part("d", down_l, s["wd"], 0, width, at, wire)
    part_kv.begin()
    part_q.begin()
    raw = small_raw[...]
    row = lax.broadcasted_iota(jnp.int32, (share, width), 0)
    column = lax.broadcasted_iota(jnp.int32, (share, width), 1)

    def spread(values, spot):
        place = jnp.where(column - row == spot * share, 1.0, 0.0).astype(BF16)
        return nn(values, place)

    own_row = lax.broadcasted_iota(jnp.int32, (8, width), 0) == at.w
    line = jnp.concatenate(
        [bias_raw[k : k + 1, :] for k in range(width // 128)], axis=1
    ).astype(F32)
    small_own = s["small_own"]
    small_own[...] = jnp.concatenate(
        [spread(raw, at.w), jnp.where(own_row, line, 0.0)], axis=0
    ).astype(BF16)
    for index, where in enumerate((at.to_x, at.to_y, at.to_d)):
        wire.send("sm" + str(index), small_own, s["small_in"].at[index], where)
    keeps = []
    for slot, (local, full) in enumerate(
        (
            (qkv_l, s["wqkv"].at[pl.ds(aligned(at.w * share, 16), share)]),
            (tokens, s["tok"].at[core]),
            (cot_l, s["cot"]),
            (out_l, s["wo"].at[pl.ds(aligned(at.w * share, 16), share)]),
            (up_l, s["wu"].at[pl.ds(aligned(at.w * share, 16), share)]),
            (down_l, s["wd"].at[pl.ds(aligned(at.w * (inner // 4), 16), inner // 4)]),
        )
    ):
        keeps.append(pltpu.make_async_copy(local, full, s["own_sems"].at[slot]))
        keeps[-1].start()
    wire.send("tok", tokens, s["tok"].at[core], at.sib)

    before = 0
    for head in range(heads):
        flag = pairing[head]
        spot = flag * (heads // 2 + before) + (1 - flag) * (head - before)
        before = before + flag
        row = lax.broadcasted_iota(jnp.int32, (size, width), 0)
        column = lax.broadcasted_iota(jnp.int32, (size, width), 1)
        s["order"][head * size : (head + 1) * size, :] = jnp.where(
            column - row == spot * size, 1.0, 0.0
        ).astype(BF16)

    part_kv.relay()
    part_q.relay()
    part_o.begin()
    part_u.begin()
    part_kv.share()
    for index in range(3):
        wire.arrived("sm" + str(index), s["small_in"].at[index])
    small = s["small"]
    small[...] = (
        small_own[...].astype(F32)
        + s["small_in"][0].astype(F32)
        + s["small_in"][1].astype(F32)
        + s["small_in"][2].astype(F32)
    )
    s["bias_qkv"][0:1, 0:width] = small[0:1, :]
    s["bias_qkv"][0:1, width : 2 * width] = jnp.zeros((1, width), F32)
    s["bias_qkv"][0:1, 2 * width :] = small[1:2, :]
    for index in range(inner // width):
        s["bias_up"][0:1, index * width : (index + 1) * width] = small[8 + index : 9 + index, :]
    keeps[0].wait()
    keeps[1].wait()
    part_kv.finish()

    tok, proj, order, kv = s["tok"], s["proj"], s["order"], s["kv"]
    own_slot = core * 2 + at.near

    def project(first, count):
        @in_columns(first * 256, (first + count) * 256)
        def _(where):
            made = nn(tok[core], s["wqkv"][:, where]) + s["bias_qkv"][0:1, where]
            proj[:, where] = made.astype(BF16)

    project(chunks, 2 * chunks)
    for index in range(chunks):
        columns = order[:, index * 256 : (index + 1) * 256]
        for kind in range(2):
            moved = nn(proj[:, (1 + kind) * width : (2 + kind) * width], columns).astype(BF16)
            for e in range(2):
                kv[2 * index + e, own_slot, :, kind * 128 : (kind + 1) * 128] = moved[
                    :, e * 128 : (e + 1) * 128
                ]
    near_base = wire.slot("near kv", pairs)
    far_base = wire.slot("far kv", pairs)
    pass_base = wire.slot("passed kv", pairs)

    def kv_copy(base, pair, slot, where):
        block = kv.at[pair, slot]
        return wire.copy(base + pair, block, block, where, "kv" + str(base))

    for pair in range(pairs):
        if pair < some:
            kv_copy(far_base, pair, own_slot, at.cross).start()
        kv_copy(near_base, pair, own_slot, at.sib).start()
    part_q.share()
    part_q.finish()
    project(0, chunks)
    q, q_out = s["q"], s["q_out"]
    for index in range(chunks):
        moved = nn(proj[:, 0:width], order[:, index * 256 : (index + 1) * 256]).astype(BF16)
        for e in range(2):
            pair = 2 * index + e
            block = moved[:, e * 128 : (e + 1) * 128]
            if pair < some:
                q[pair] = block
            else:
                q_out[pair - some] = block
    wire.send("queries", q_out, q.at[pl.ds(some, some)], at.partner)
    part_o.relay()
    part_d.begin()

    exps, inverse, out_t = s["exps"], s["inverse"], s["out_t"]

    def both(pair, first):
        return kv[pair, :, :, first : first + 128].reshape(keys, 128)

    def masked(block, e, axis=1):
        spot = lax.broadcasted_iota(jnp.int32, block.shape, axis)
        mine = spot < size if e == 0 else spot >= size
        return jnp.where(mine, block, jnp.zeros_like(block))

    def attend(pair):
        key_rows, value_rows = both(pair, 0), both(pair, 128)
        values_t = value_rows.T
        queries = q[pair] * jnp.asarray(size**-0.5, BF16)
        parts = []
        for e in range(2):
            scores = nt(key_rows, masked(queries, e))
            top = jnp.max(scores, axis=0, keepdims=True)
            raised = jnp.exp(scores - top)
            total = jnp.sum(raised, axis=0, keepdims=True)
            low = raised.astype(BF16)
            exps[2 * pair + e] = low
            s["tops"][2 * pair + e] = top
            one_over = 1.0 / total
            inverse[2 * pair + e] = one_over
            parts.append(nn(values_t[e * size : (e + 1) * size], low) * one_over)
        merged = jnp.concatenate(parts, axis=0)
        out_t[pair] = merged
        return merged.T.astype(BF16)

    def receive_kv(pair):
        kv_copy(far_base, pair, core * 2 + at.far, at.cross).wait_recv()
        kv_copy(pass_base, pair, core * 2 + at.far, at.sib).start()
        kv_copy(near_base, pair, other * 2 + at.near, at.sib).wait_recv()
        kv_copy(pass_base, pair, other * 2 + at.far, at.sib).wait_recv()

    ctx, ctx_out = s["ctx"], s["ctx_out"]
    back_base = wire.slot("ctx", some)

    def ctx_copy(index):
        return wire.copy(back_base + index, ctx_out.at[index], ctx.at[some + index], at.partner, "ctx")

    def attend_far(index):
        receive_kv(index + some)
        ctx_out[index] = attend(index + some)
        ctx_copy(index).start()

    @pl.loop(0, some)
    def _(index):
        receive_kv(index)
        kv_copy(far_base, index + some, own_slot, at.cross).start()
        ctx[index] = attend(index)

    part_o.share()
    wire.arrived("queries", q.at[pl.ds(some, some)])
    attend_far(0)
    part_u.relay()

    @pl.loop(1, some)
    def _(index):
        attend_far(index)

    part_o.finish()
    far_q, far_tops, far_delta, far_dos = (
        s[name] for name in ("far_q", "far_tops", "far_delta", "far_dos")
    )
    tops, delta, dos = s["tops"], s["delta"], s["dos"]
    wire.send("far q", q, far_q.at[core], at.cross)
    wire.send("far tops", tops, far_tops.at[core], at.cross)
    part_d.relay()
    keeps[2].wait()
    keeps[3].wait()
    ctx_nat, stage, wo_order = s["ctx_nat"], s["stage"], s["wo_order"]
    for index in range(chunks):
        where = slice(index * 256, (index + 1) * 256)
        wo_order[where, :] = nn(order[:, where].T, s["wo"][...]).astype(BF16)
    for index in range(some):
        ctx_copy(index).wait_recv()

    def permuted():
        return jnp.concatenate([ctx[pair] for pair in range(pairs)], axis=1)

    for index in range(chunks):
        where = slice(index * 256, (index + 1) * 256)
        stage[:, where] = nn(permuted(), wo_order[:, where])

    hat_one, r_one, flow, hid = s["hat_one"], s["r_one"], s["flow"], s["hid"]
    inv_width = 1.0 / width

    def mean(values):
        return jnp.sum(values, axis=-1, keepdims=True) * inv_width

    @in_bands(rows)
    def _(where):
        total = tok[core, where, :].astype(F32) + stage[where, :] + small[2:3, :]
        centred = total - mean(total)
        scale = lax.rsqrt(mean(centred * centred) + 1e-12)
        hat = centred * scale
        hat_one[where, :] = hat
        r_one[where, :] = scale
        hidden = hat * small[3:4, :] + small[4:5, :]
        flow[where, :] = hidden
        hid[core, where, :] = hidden.astype(BF16)

    wire.send("hid", hid.at[core], hid.at[core], at.sib)
    part_u.share()
    part_u.finish()
    keeps[4].wait()
    act, slope = s["act"], s["slope"]

    @in_columns(0, inner)
    def _(where):
        pre = nn(hid[core], s["wu"][:, where]) + s["bias_up"][0:1, where]
        below = 0.5 * (1.0 + lax.erf(pre * (0.5**0.5)))
        act[core, :, where] = (pre * below).astype(BF16)
        density = jnp.exp(pre * pre * -0.5) * 0.3989422804014327
        slope[:, where] = (below + pre * density).astype(BF16)

    wire.send("act", act.at[core], act.at[core], at.sib)
    wire.arrived("far q", far_q.at[core])
    wire.send("passed q", far_q.at[core], far_q.at[core], at.sib)
    wire.arrived("far tops", far_tops.at[core])
    wire.send("passed tops", far_tops.at[core], far_tops.at[core], at.sib)
    for index in range(chunks):
        where = slice(index * 256, (index + 1) * 256)
        ctx_nat[core, :, where] = nt(permuted(), order[where, :]).astype(BF16)
    wire.send("ctxn", ctx_nat.at[core], ctx_nat.at[core], at.sib)
    part_d.near()
    keeps[5].wait()
    quarter = inner // 4

    def down(owner, where):
        block = pl.ds(aligned(owner * quarter, 128), quarter)
        return nn(act[core, :, block], s["wd"][block, where])

    @in_columns(0, width)
    def _(where):
        stage[:, where] = down(at.w, where) + down(at.nx, where) + down(at.ny, where)

    part_d.share()
    part_d.last()

    @in_columns(0, width)
    def _(where):
        stage[:, where] += down(at.nd, where)

    result, gf, cot = s["result"], s["gf"], s["cot"]
    sums, sums_up = s["sums"], s["sums_up"]
    sums[...] = jnp.zeros_like(sums)

    def gather_rows(values):
        return jnp.sum(values.reshape(BAND // 8, 8, values.shape[-1]), axis=0)

    @in_bands(rows)
    def _(where):
        total = flow[where, :] + stage[where, :] + small[5:6, :]
        centred = total - mean(total)
        scale = lax.rsqrt(mean(centred * centred) + 1e-12)
        hat = centred * scale
        result[where, :] = hat
        g = cot[where, :].astype(F32) * small[6:7, :]
        grad = scale * (g - mean(g) - hat * mean(g * hat))
        flow[where, :] = grad
        gf[where, :] = grad.astype(BF16)

    def columns_of(which, count):
        return pl.ds(aligned(which * count, 128), count)

    wire.send("gf", gf.at[:, columns_of(other, half)], s["gf_in"], at.sib)

    def buffers(name):
        return [s["g" + name + kind] for kind in ("fx", "fy", "dx", "dy", "lo", "hi")]

    dwd, wd, wu = s["dwd"], s["wd"], s["wu"]

    def side_by_side(first, count, owner):
        return wd.at[
            pl.ds(aligned(first + (owner // 2) * count, 16), count),
            pl.ds(aligned((owner % 2) * half, 128), half),
        ]

    def dwo(owner):
        return side_by_side(2 * width + 6 * share, share, owner)

    def dwq(owner):
        return side_by_side(2 * width, 3 * share, owner)

    grad_d = Grad(
        "gd",
        4,
        lambda r: dwd.at[r],
        buffers("d"),
        lambda i, k: g_down.at[pl.ds(i * (inner // 16), inner // 16), columns_of(k, half)],
        at,
        wire,
        s["own_sems"].at[8],
    )
    grad_u = Grad(
        "gu",
        4,
        lambda r: wd.at[pl.ds(aligned(r * (2 * share), 16), 2 * share), :],
        buffers("u"),
        lambda i, k: g_up.at[
            pl.ds((i % 2) * (share // 2), share // 2), columns_of(2 * k + i // 2, width)
        ],
        at,
        wire,
        s["own_sems"].at[9],
    )
    grad_o = Grad(
        "go",
        1,
        dwo,
        buffers("o"),
        lambda i, k: g_out.at[:, columns_of(k, half)],
        at,
        wire,
        s["own_sems"].at[10],
    )
    grad_q = Grad(
        "gq",
        6,
        dwq,
        buffers("q"),
        lambda i, k: g_qkv.at[
            pl.ds((i % 2) * (share // 2), share // 2), columns_of(3 * k + i // 2, half)
        ],
        at,
        wire,
        s["own_sems"].at[11],
    )

    def back_through(first, last):
        @in_columns(first, last)
        def _(where):
            grad = nt(gf[...], wd[where, :]) * slope[:, where].astype(F32)
            low = grad.astype(BF16)
            slope[:, where] = low
            sums_up[:, where] = jnp.sum(low.astype(F32).reshape(rows // 8, 8, 256), axis=0)

    back_through(0, 3 * inner // 4)
    wire.arrived("act", act.at[other])
    wire.arrived("gf", s["gf_in"])

    def down_grad(owner):
        where = pl.ds(aligned(owner * quarter, 128), quarter)
        made = nn(act[core, :, where].T, gf[:, columns_of(core, half)])
        made = made + nn(act[other, :, where].T, s["gf_in"][...])
        dwd[owner] = made.astype(BF16)

    down_grad(at.nd)
    grad_d.begin()
    back_through(3 * inner // 4, inner)
    wire.send("slope", slope.at[:, columns_of(other, inner // 2)], s["slope_in"], at.sib)

    @in_columns(0, width)
    def _(where):
        stage[:, where] = nt(slope[...], wu[where, :])


    gb = s["gb"]

    @in_bands(rows)
    def _(where):
        grad_hidden = flow[where, :] + stage[where, :]
        hat = hat_one[where, :]
        g = grad_hidden * small[3:4, :]
        grad = r_one[where, :] * (g - mean(g) - hat * mean(g * hat))
        flow[where, :] = grad
        gb[where, :] = grad.astype(BF16)
        stage[where, :] = grad_hidden

    wire.send("gb", gb.at[:, columns_of(other, half)], s["gb_in"], at.sib)

    do, do_out = s["do"], s["do_out"]
    for index in range(chunks):
        moved = nt(gb[...], wo_order[index * 256 : (index + 1) * 256, :]).astype(BF16)
        for e in range(2):
            pair = 2 * index + e
            block = moved[:, e * 128 : (e + 1) * 128]
            if pair < some:
                do[pair] = block
            else:
                do_out[pair - some] = block
    wire.send("do", do_out, do.at[pl.ds(some, some)], at.partner)

    def prepare(pair):
        do_t = do[pair].astype(F32).T
        scaled = jnp.concatenate(
            [do_t[e * size : (e + 1) * size] * inverse[2 * pair + e] for e in range(2)], axis=0
        )
        product = scaled * out_t[pair]
        for e in range(2):
            delta[2 * pair + e] = jnp.sum(product[e * size : (e + 1) * size], axis=0, keepdims=True)
        dos[pair] = scaled.T.astype(BF16)

    group_d = [pl.ds(0, some), pl.ds(some, some)]
    group_h = [pl.ds(0, 2 * some), pl.ds(2 * some, 2 * some)]

    def send_group(g):
        wire.send(
            "far do" + str(g), dos.at[group_d[g]], far_dos.at[core, group_d[g]], at.cross
        )
        wire.send(
            "far de" + str(g), delta.at[group_h[g]], far_delta.at[core, group_h[g]], at.cross
        )

    def pass_group(g):
        for kind, ref, group in (("do", far_dos, group_d), ("de", far_delta, group_h)):
            block = ref.at[core, group[g]]
            wire.arrived("far " + kind + str(g), block)
            wire.send("passed " + kind + str(g), block, block, at.sib)

    def have_group(g):
        wire.arrived("passed do" + str(g), far_dos.at[other, group_d[g]])
        wire.arrived("passed de" + str(g), far_delta.at[other, group_h[g]])

    for index in range(some):
        prepare(index)

    send_group(0)
    for owner in (at.nx, at.ny):
        down_grad(owner)
    grad_d.push((0, 1), (2, 3))
    down_grad(at.w)
    part_d.gone()
    wire.arrived("hid", hid.at[other])
    wire.arrived("slope", s["slope_in"])
    mine_t, theirs_t = hid[core].T, hid[other].T
    for index in range(inner // 2 // half):
        where = pl.ds(aligned(core * (inner // 2) + index * half, 128), half)
        made = nn(mine_t, slope[:, where]) + nn(
            theirs_t, s["slope_in"][:, index * half : (index + 1) * half]
        )
        made = made.astype(BF16)
        for owner in range(4):
            first = owner * 2 * share + (index // 2) * share
            wd[first : first + share, (index % 2) * half : (index % 2 + 1) * half] = made[
                owner * share : (owner + 1) * share
            ]
    wire.arrived("ctxn", ctx_nat.at[other])
    wire.arrived("gb", s["gb_in"])
    made = nn(ctx_nat[core].T, gb[:, columns_of(core, half)]) + nn(
        ctx_nat[other].T, s["gb_in"][...]
    )
    made = made.astype(BF16)
    for owner in range(4):
        dwo(owner)[...] = made[owner * share : (owner + 1) * share]
    grad_d.fold()
    grad_d.push((2, 3), (0, 1))
    grad_u.begin()
    grad_u.push((0,), (2,))
    grad_o.begin()

    part_u.gone()
    dq, dq_out, dkv_in = s["dq"], s["do_out"], s["dkv_in"]
    near_d = wire.slot("near dkv", pairs)
    dq_base = wire.slot("dq", some)
    lots = inner // 512

    def tile(pair, which):
        return wu.at[
            pl.ds(aligned((pair // lots) * rows, 16), rows),
            pl.ds(aligned((pair % lots) * 512 + which * 256, 256), 256),
        ]

    def dkv_near(pair):
        return wire.copy(near_d + pair, tile(pair, other), dkv_in.at[pair], at.sib, "near dkv")

    def two_blocks(pair, chip, first):
        return jnp.concatenate(
            [kv[pair, k * 2 + chip, :, first : first + 128] for k in range(2)], axis=0
        )

    def attend_back(pair):
        queries = q[pair] * jnp.asarray(size**-0.5, BF16)
        dq_parts = [None, None]
        dv = dk = None
        for chip in (at.near, at.far):
            key_rows, value_rows = two_blocks(pair, chip, 0), two_blocks(pair, chip, 128)
            keys_t = key_rows.T
            for e in range(2):
                low = jnp.concatenate(
                    [
                        exps[2 * pair + e, pl.ds(aligned((k * 2 + chip) * rows, 16), rows), :]
                        for k in range(2)
                    ],
                    axis=0,
                )
                mine = masked(dos[pair], e)
                grad_w = nt(value_rows, mine)
                grad_s = (low.astype(F32) * (grad_w - delta[2 * pair + e])).astype(BF16)
                more_q = nn(keys_t[e * size : (e + 1) * size], grad_s)
                dq_parts[e] = more_q if dq_parts[e] is None else dq_parts[e] + more_q
                if chip is at.near:
                    more_v = nn(low, mine)
                    more_k = nn(grad_s, masked(queries, e))
                    dv = more_v if dv is None else dv + more_v
                    dk = more_k if dk is None else dk + more_k
            if chip is at.near:
                made = jnp.concatenate([dk, dv], axis=1).astype(BF16)
                for k in range(2):
                    tile(pair, k)[...] = made[k * rows : (k + 1) * rows]
                dkv_near(pair).start()
        return (jnp.concatenate(dq_parts, axis=0).T * size**-0.5).astype(BF16)

    gkv = s["gkv"]

    def far_back(pair):
        queries = far_q[:, pair].reshape(2 * rows, 128) * jnp.asarray(size**-0.5, BF16)
        grads = far_dos[:, pair].reshape(2 * rows, 128)
        key_rows, value_rows = kv[pair, own_slot, :, 0:128], kv[pair, own_slot, :, 128:256]
        dv = dk = None
        for e in range(2):
            head = 2 * pair + e
            top = jnp.concatenate([far_tops[k, head] for k in range(2)], axis=1)
            less = jnp.concatenate([far_delta[k, head] for k in range(2)], axis=1)
            mine, asking = masked(grads, e), masked(queries, e)
            low = jnp.exp(nt(key_rows, asking) - top).astype(BF16)
            grad_s = (low.astype(F32) * (nt(value_rows, mine) - less)).astype(BF16)
            more_v, more_k = nn(low, mine), nn(grad_s, asking)
            dv = more_v if dv is None else dv + more_v
            dk = more_k if dk is None else dk + more_k
        dkv_near(pair).wait_recv()
        own = tile(pair, core)
        where = pl.ds(aligned(pair * 128, 128), 128)
        for kind, made in ((0, dk), (1, dv)):
            cut = slice(kind * 128, (kind + 1) * 128)
            gkv[kind, :, where] = (
                made + own[:, cut].astype(F32) + dkv_in[pair, :, cut].astype(F32)
            ).astype(BF16)

    def dq_copy(index):
        return wire.copy(dq_base + index, dq_out.at[index], dq.at[some + index], at.partner, "dq")

    @pl.loop(0, some)
    def _(index):
        dq[index] = attend_back(index)

    wire.arrived("do", do.at[pl.ds(some, some)])

    for index in range(some, pairs):
        prepare(index)

    send_group(1)
    pass_group(0)
    wire.left("do")
    grad_d.own(0)

    @pl.loop(0, some)
    def _(index):
        dq_out[index] = attend_back(index + some)
        dq_copy(index).start()

    for chunk in (2, 1, 3):
        grad_d.own(chunk)
    pass_group(1)
    wire.arrived("passed q", far_q.at[other])
    wire.arrived("passed tops", far_tops.at[other])
    have_group(0)

    @pl.loop(0, some)
    def _(index):
        far_back(index)

    grad_d.chain(0)
    @pl.loop(0, rows // BAND, unroll=2)
    def _(index):
        where = chunk_of(index, BAND)
        hat = result[where, :]
        result[where, :] = hat * small[6:7, :] + small[7:8, :]
        back = cot[where, :].astype(F32)
        sums[6] += gather_rows(back * hat)
        sums[7] += gather_rows(back)
        sums[5] += gather_rows(gf[where, :].astype(F32))
        grad_hidden = stage[where, :]
        sums[3] += gather_rows(grad_hidden * hat_one[where, :])
        sums[4] += gather_rows(grad_hidden)
        sums[2] += gather_rows(gb[where, :].astype(F32))

    keep_out = pltpu.make_async_copy(result, output, s["own_sems"].at[7])
    keep_out.start()
    wire.left(*[name for name in wire.started if name[:2] not in ("gd", "gu", "go")])
    part_kv.gone()
    part_q.gone()
    part_o.gone()
    for base in (far_base, near_base, pass_base):
        wire.gone("kv" + str(base), kv.at[:, 0])
    wire.gone("ctx", ctx_out)
    have_group(1)

    @pl.loop(some, pairs)
    def _(index):
        far_back(index)

    grad_u.fold()
    grad_u.push((1, 2), (0, 1))

    for index in range(some):
        dq_copy(index).wait_recv()
    merged = jnp.concatenate([dq[pair] for pair in range(pairs)], axis=1)
    for index in range(chunks):
        where = slice(index * 256, (index + 1) * 256)
        rows_of = order[where, :]
        for kind in range(3):
            source = merged if kind == 0 else gkv[kind - 1]
            low = nt(source, rows_of).astype(BF16)
            proj[:, kind * width + index * 256 : kind * width + (index + 1) * 256] = low
            if kind != 1:
                sums[kind // 2, :, where] = jnp.sum(
                    low.astype(F32).reshape(rows // 8, 8, 256), axis=0
                )
    wire.send("gj", proj.at[:, columns_of(other, 3 * half)], s["gj_in"], at.sib)

    vec, vec_in, vec_low, vec_far = s["vec"], s["vec_in"], s["vec_low"], s["vec_far"]
    for row in range(8):
        vec[row : row + 1, :] = jnp.sum(sums[row], axis=0, keepdims=True)
    for index in range(inner // width):
        vec[8 + index : 9 + index, :] = jnp.sum(
            sums_up[:, index * width : (index + 1) * width], axis=0, keepdims=True
        )
    for row in range(8 + inner // width, 16):
        vec[row : row + 1, :] = jnp.zeros((1, width), F32)
    wire.send("va", vec, vec_in, at.sib)

    grad_d.chain(2)
    grad_d.total(0)
    wire.arrived("tok", tok.at[other])
    wire.arrived("gj", s["gj_in"])
    mine_t, theirs_t = tok[core].T, tok[other].T
    for index in range(3):
        where = pl.ds(aligned(core * (3 * half) + index * half, 128), half)
        made = nn(mine_t, proj[:, where]) + nn(
            theirs_t, s["gj_in"][:, index * half : (index + 1) * half]
        )
        made = made.astype(BF16)
        for owner in range(4):
            dwq(owner)[index * share : (index + 1) * share, :] = made[
                owner * share : (owner + 1) * share
            ]
    grad_q.begin()
    grad_u.push((3,), (3,))
    grad_o.fold()
    grad_o.push((0,), (0,))
    grad_u.own(0)
    grad_d.chain(1)
    grad_d.total(2)
    wire.arrived("va", vec_in)
    vec_low[0] = (vec_in[...] + vec[...]).astype(BF16)
    for index, where in enumerate((at.to_x, at.to_y, at.to_d)):
        wire.send("vb" + str(index), vec_low.at[0], vec_far.at[index], where)

    keep_out.wait()

    @in_columns(0, width)
    def _(where):
        result[:, where] = nt(proj[...], s["wqkv"][where, :]) + flow[:, where]

    keep_grad = pltpu.make_async_copy(result, grad_tokens, s["own_sems"].at[7])
    keep_grad.start()
    def vec_hop(name, place, far, where):
        return wire.copy(wire.slot(name), vec_low.at[place], vec_far.at[far], where, name)

    def vec_out():
        return vec_hop("vu", 1, 3, at.mate)

    def vec_across():
        return vec_hop("vv", 2, 4, at.middle)

    def vec_back():
        return vec_hop("vt", 3, 5, at.mate)

    def vec_sum(*parts):
        total = parts[0].astype(F32)
        for part in parts[1:]:
            total = total + part.astype(F32)
        return total

    grad_u.own(1)
    grad_d.chain(3)
    grad_d.total(1)
    grad_u.own(2)
    grad_u.chain(0)
    grad_q.fold()
    grad_q.push((0, 1, 2, 3, 4, 5), (0, 1, 2, 3, 4, 5))
    grad_d.total(3)
    grad_u.total(0)
    grad_u.chain(1)
    grad_u.own(3)
    grad_u.chain(2)
    grad_u.total(1)
    grad_o.own(0)
    grad_u.total(2)
    grad_q.own(0)
    grad_u.chain(3)
    grad_q.own(1)
    for index in range(3):
        wire.arrived("vb" + str(index), vec_far.at[index])
    vec_low[1] = (
        vec_sum(vec_low[0], vec_far[0]) + vec_sum(vec_far[1], vec_far[2])
    ).astype(BF16)

    @pl.when(at.outer)
    def _():
        vec_out().start()

    grad_o.chain(0)
    grad_u.total(3)
    grad_q.own(2)
    grad_q.chain(0)
    grad_q.chain(1)
    grad_q.own(3)

    @pl.when(at.inner)
    def _():
        vec_out().wait_recv()
        vec_low[2] = vec_sum(vec_low[1], vec_far[3]).astype(BF16)
        vec_across().start()

    grad_q.chain(2)
    grad_o.total(0)
    grad_q.total(0)
    grad_q.own(4)
    grad_q.chain(3)
    grad_q.total(1)
    grad_q.own(5)
    grad_q.chain(4)
    grad_q.total(2)
    grad_q.chain(5)
    grad_q.total(3)

    @pl.when(at.inner)
    def _():
        vec_across().wait_recv()
        total = vec_sum(vec_low[2], vec_far[4]).astype(BF16)
        vec_low[3] = total
        vec_back().start()
        vec_in[...] = total.astype(F32)

    grad_q.total(4)
    grad_q.total(5)
    for chunk in range(4):
        grad_d.give(chunk)
    for chunk in range(4):
        grad_u.give(chunk)
    grad_o.give(0)
    for chunk in range(4):
        grad_q.give(chunk)

    @pl.when(at.outer)
    def _():
        vec_back().wait_recv()
        vec_in[...] = vec_far[5].astype(F32)

    keep_small = pltpu.make_async_copy(vec_in, g_small, s["own_sems"].at[6])
    keep_small.start()
    grad_q.give(4)
    grad_q.give(5)

    @pl.when(at.outer)
    def _():
        vec_out().wait_send()

    @pl.when(at.inner)
    def _():
        vec_across().wait_send()
        vec_back().wait_send()

    grad_d.close()
    grad_u.close()
    grad_o.close()
    grad_q.close()
    keep_grad.wait()
    keep_small.wait()
    wire.gone("near dkv", dkv_in)
    wire.gone("dq", dq_out)
    wire.close()


def whole_layer(
    tokens, cotangent, pairing, small_raw, bias_raw, w_qkv, w_out, w_up, w_down
):
    rows, width = tokens.shape
    inner = w_up.shape[1]
    scratch = layer_scratch(rows, width, inner, pairing.shape[0])
    hbm = pl.BlockSpec(memory_space=pl.ANY)
    vmem = pl.BlockSpec(memory_space=pltpu.VMEM)
    smem = pl.BlockSpec(memory_space=pltpu.SMEM)
    return pl.pallas_call(
        functools.partial(layer_kernel, tuple(scratch)),
        out_shape=[
            jax.ShapeDtypeStruct((rows, width), F32),
            jax.ShapeDtypeStruct((rows, width), F32),
            jax.ShapeDtypeStruct(w_qkv.shape, BF16),
            jax.ShapeDtypeStruct(w_out.shape, BF16),
            jax.ShapeDtypeStruct(w_up.shape, BF16),
            jax.ShapeDtypeStruct(w_down.shape, BF16),
            jax.ShapeDtypeStruct((16, width), F32),
        ],
        in_specs=[hbm, hbm, smem, vmem, vmem, hbm, hbm, hbm, hbm],
        out_specs=[hbm] * 7,
        scratch_shapes=list(scratch.values()),
        compiler_params=pltpu.CompilerParams(
            collective_id=0, has_side_effects=True, vmem_limit_bytes=60 << 20
        ),
        name="whole_layer",
    )(tokens, cotangent, pairing, small_raw, bias_raw, w_qkv, w_out, w_up, w_down)


def finish_kernel(share, *refs):
    wide, small, outs = refs[:6], refs[6], refs[7:]
    for source, target in zip(wide, outs[:6]):
        target[...] = source[...].astype(F32)

    @pl.when(pl.program_id(0) == 0)
    def _():
        w = lax.axis_index("wt")
        values = small[...]
        mine = jnp.zeros((8, share), F32)
        line = jnp.zeros((1, 4 * share), F32)
        for owner in range(4):
            mine = mine + jnp.where(
                w == owner, values[:8, owner * share : (owner + 1) * share], 0.0
            )
            line = line + jnp.where(w == owner, values[8 + owner : 9 + owner], 0.0)
        for row in range(8):
            outs[6 + row][...] = mine[row : row + 1]
        outs[14][...] = line.reshape(4 * share)


def finish(*arrays):
    steps = 2
    wide, small = arrays[:6], arrays[6]
    share = small.shape[1] // 4

    def blocks(array):
        return pl.BlockSpec((array.shape[0] // steps, array.shape[1]), lambda i: (i, 0))

    def fixed(shape):
        return pl.BlockSpec(shape, lambda i: (0,) * len(shape))

    shapes = [(1, share)] * 8 + [(4 * share,)]
    return pl.pallas_call(
        functools.partial(finish_kernel, share),
        grid=(steps,),
        out_shape=[jax.ShapeDtypeStruct(v.shape, F32) for v in wide]
        + [jax.ShapeDtypeStruct(v, F32) for v in shapes],
        in_specs=[blocks(v) for v in wide] + [fixed(small.shape)],
        out_specs=[blocks(v) for v in wide] + [fixed(v) for v in shapes],
        compiler_params=pltpu.CompilerParams(vmem_limit_bytes=60 << 20),
        name="finish",
    )(*arrays)


far_below = -1e30


def passed_along(value, axis, steps):
    count = lax.axis_size(axis)
    pairs = [(source, (source + steps) % count) for source in range(count)]
    return lax.ppermute(value, axis, pairs)


def norm_rows(values, gains, shifts):
    average = jnp.mean(values, axis=-1, keepdims=True)
    centred = values - average
    spread = jnp.mean(centred * centred, axis=-1, keepdims=True)
    return centred * lax.rsqrt(spread + 1e-12) * gains + shifts


def gelu_exact(pre_active):
    return jax.nn.gelu(pre_active, approximate=False)


def scores_of(queries, key_heads):
    return (
        jnp.einsum("thd,khd->htk", queries, key_heads, preferred_element_type=jnp.float32) * 0.125
    )


def unchanged(running):
    return running


def general_layer(
    tokens,
    pairing,
    w_qkv,
    bias_q,
    bias_v,
    w_out,
    bias_out,
    gain_one,
    shift_one,
    w_up,
    bias_up,
    w_down,
    bias_down,
    gain_two,
    shift_two,
    cotangent,
):
    local_params = (
        w_qkv,
        bias_q,
        bias_v,
        w_out,
        bias_out,
        gain_one,
        shift_one,
        w_up,
        bias_up,
        w_down,
        bias_down,
        gain_two,
        shift_two,
    )
    gathered = tuple(lax.all_gather(v, "wt", axis=0, tiled=True) for v in local_params)
    (
        wqkv_full,
        biasq_full,
        biasv_full,
        wout_full,
        biasout_full,
        gainone_full,
        shiftone_full,
        wup_full,
        biasup_full,
        wdown_full,
        biasdown_full,
        gaintwo_full,
        shifttwo_full,
    ) = gathered
    tok_rows = tokens.shape[1]
    model_width = tokens.shape[2]
    head_count = pairing.shape[0]
    head_size = model_width // head_count
    group_size = lax.axis_size("ctx")
    position_ctx = lax.axis_index("ctx")
    half_len = tok_rows * group_size // 2
    own_half = position_ctx * tok_rows // half_len
    flipped = pairing == 1
    inputs = tokens[0]
    bias_cat = jnp.concatenate(
        [
            biasq_full.astype(jnp.float32),
            jnp.zeros((model_width,), jnp.float32),
            biasv_full.astype(jnp.float32),
        ]
    )
    projected = jnp.dot(inputs, wqkv_full, preferred_element_type=jnp.float32) + bias_cat
    projected_low = projected.astype(jnp.bfloat16)
    queries = projected_low[:, :model_width].reshape(tok_rows, head_count, head_size)
    key_rows = projected_low[:, model_width : 2 * model_width]
    value_rows = projected_low[:, 2 * model_width :]

    def online_update(state, portion_keys, portion_values, needed):
        row_top, row_total, accumulated = state
        key_count = portion_keys.shape[0]
        key_heads = portion_keys.reshape(key_count, head_count, head_size)
        value_heads = portion_values.reshape(key_count, head_count, head_size)
        scores = scores_of(queries, key_heads)
        scores = jnp.where(needed[:, None, :], scores, far_below)
        new_top = jnp.maximum(row_top, jnp.max(scores, axis=-1))
        factor = jnp.exp(row_top - new_top)
        weights = jnp.exp(scores - new_top[..., None])
        row_total = jnp.sum(weights, axis=-1)
        added = jnp.einsum(
            "htk,khd->thd",
            weights.astype(jnp.bfloat16),
            value_heads,
            preferred_element_type=jnp.float32,
        )
        accumulated = accumulated * factor.T[..., None] + added
        return (new_top, row_total, accumulated)

    start_state = (
        jnp.full((head_count, tok_rows), far_below, jnp.float32),
        jnp.zeros((head_count, tok_rows), jnp.float32),
        jnp.zeros((tok_rows, head_count, head_size), jnp.float32),
    )

    def wanted(offset, key_count):
        key_half = (offset + jnp.arange(key_count)) // half_len
        target = jnp.where(flipped, 1 - own_half, own_half)
        return key_half[None, :] == target[:, None]

    portion_keys = lax.all_gather(key_rows, "ctx", axis=0, tiled=True)
    portion_values = lax.all_gather(value_rows, "ctx", axis=0, tiled=True)
    needed = wanted(jnp.int32(0), portion_keys.shape[0])

    def update(state):
        return online_update(state, portion_keys, portion_values, needed)

    row_top, row_total, accumulated = lax.cond(jnp.any(needed), update, unchanged, start_state)
    context = accumulated / row_total.T[..., None]
    log_sum = row_top + jnp.log(row_total)
    context_low = context.reshape(tok_rows, model_width).astype(jnp.bfloat16)
    branch = jnp.dot(
        context_low, wout_full, preferred_element_type=jnp.float32
    ) + biasout_full.astype(jnp.float32)
    summed_one = inputs.astype(jnp.float32) + branch
    hidden, norm_one_back = jax.vjp(
        norm_rows, summed_one, gainone_full.astype(jnp.float32), shiftone_full.astype(jnp.float32)
    )
    hidden_low = hidden.astype(jnp.bfloat16)
    pre_active = jnp.dot(
        hidden_low, wup_full, preferred_element_type=jnp.float32
    ) + biasup_full.astype(jnp.float32)
    active, gelu_back = jax.vjp(gelu_exact, pre_active)
    active_low = active.astype(jnp.bfloat16)
    ffn_out = jnp.dot(
        active_low, wdown_full, preferred_element_type=jnp.float32
    ) + biasdown_full.astype(jnp.float32)
    output, norm_two_back = jax.vjp(
        norm_rows,
        hidden + ffn_out,
        gaintwo_full.astype(jnp.float32),
        shifttwo_full.astype(jnp.float32),
    )
    again = gathered
    wqkv_back = again[0]
    wout_back = again[3]
    wup_back = again[7]
    wdown_back = again[9]
    grad_two, grad_gain_two, grad_shift_two = norm_two_back(cotangent[0].astype(jnp.float32))
    grad_ffn = grad_two.astype(jnp.bfloat16)
    grad_bias_down = jnp.sum(grad_ffn.astype(jnp.float32), axis=0)
    grad_w_down = jnp.einsum("tf,td->fd", active_low, grad_ffn, preferred_element_type=jnp.float32)
    grad_active = jnp.einsum("td,fd->tf", grad_ffn, wdown_back, preferred_element_type=jnp.float32)
    (grad_pre_f,) = gelu_back(grad_active)
    grad_pre = grad_pre_f.astype(jnp.bfloat16)
    grad_bias_up = jnp.sum(grad_pre.astype(jnp.float32), axis=0)
    grad_w_up = jnp.einsum("tc,tf->cf", hidden_low, grad_pre, preferred_element_type=jnp.float32)
    grad_hidden = grad_two + jnp.einsum(
        "tf,cf->tc", grad_pre, wup_back, preferred_element_type=jnp.float32
    )
    grad_one, grad_gain_one, grad_shift_one = norm_one_back(grad_hidden)
    grad_branch = grad_one.astype(jnp.bfloat16)
    grad_bias_out = jnp.sum(grad_branch.astype(jnp.float32), axis=0)
    grad_w_out = jnp.einsum(
        "tc,td->cd", context_low, grad_branch, preferred_element_type=jnp.float32
    )
    grad_context = jnp.einsum(
        "td,cd->tc", grad_branch, wout_back, preferred_element_type=jnp.float32
    )
    grad_context = grad_context.astype(jnp.bfloat16).reshape(tok_rows, head_count, head_size)
    row_delta = jnp.sum(grad_context.astype(jnp.float32) * context, axis=-1).T

    def piece_grads(portion_keys, portion_values, needed):
        key_count = portion_keys.shape[0]
        key_heads = portion_keys.reshape(key_count, head_count, head_size)
        value_heads = portion_values.reshape(key_count, head_count, head_size)
        scores = scores_of(queries, key_heads)
        scores = jnp.where(needed[:, None, :], scores, far_below)
        probs = jnp.exp(scores - log_sum[..., None])
        probs_low = probs.astype(jnp.bfloat16)
        piece_v = jnp.einsum(
            "htk,thd->khd", probs_low, grad_context, preferred_element_type=jnp.float32
        ).reshape(key_count, model_width)
        grad_weights = jnp.einsum(
            "thd,khd->htk", grad_context, value_heads, preferred_element_type=jnp.float32
        )
        grad_scores = (probs * (grad_weights - row_delta[..., None])).astype(jnp.bfloat16)
        piece_q = 0.125 * jnp.einsum(
            "htk,khd->thd", grad_scores, key_heads, preferred_element_type=jnp.float32
        )
        piece_k = 0.125 * jnp.einsum(
            "htk,thd->khd", grad_scores, queries, preferred_element_type=jnp.float32
        ).reshape(key_count, model_width)
        return (piece_k, piece_v, piece_q)

    zero_queries = jnp.zeros((tok_rows, head_count, head_size), jnp.float32)

    def circle_step(step_index, running):
        turn_keys, turn_values, grad_keys, grad_values, grad_queries = running
        owner = (position_ctx - step_index) % group_size
        needed = wanted(owner * tok_rows, tok_rows)

        def update_grads(state):
            grad_k, grad_v, grad_q = state
            piece_k, piece_v, piece_q = piece_grads(turn_keys, turn_values, needed)
            return (grad_k + piece_k, grad_v + piece_v, grad_q + piece_q)

        grad_keys, grad_values, grad_queries = lax.cond(
            jnp.any(needed), update_grads, unchanged, (grad_keys, grad_values, grad_queries)
        )
        turn_keys, turn_values = passed_along((turn_keys, turn_values), "ctx", 1)
        grad_keys, grad_values = (
            passed_along(grad_keys.astype(jnp.bfloat16), "ctx", 1).astype(grad_keys.dtype),
            passed_along(grad_values.astype(jnp.bfloat16), "ctx", 1).astype(grad_values.dtype),
        )
        return (turn_keys, turn_values, grad_keys, grad_values, grad_queries)

    zero_rows = jnp.zeros((tok_rows, model_width), jnp.float32)
    circle_start = (key_rows, value_rows, zero_rows, zero_rows, zero_queries)
    circle_end = lax.fori_loop(0, group_size, circle_step, circle_start)
    grad_keys = circle_end[2]
    grad_values = circle_end[3]
    grad_queries = circle_end[4]
    grad_projected = jnp.concatenate(
        [grad_queries.reshape(tok_rows, model_width), grad_keys, grad_values], axis=1
    ).astype(jnp.bfloat16)
    grad_bias_q = jnp.sum(grad_projected[:, :model_width].astype(jnp.float32), axis=0)
    grad_bias_v = jnp.sum(grad_projected[:, 2 * model_width :].astype(jnp.float32), axis=0)
    grad_w_qkv = jnp.einsum("tc,tj->cj", inputs, grad_projected, preferred_element_type=jnp.float32)
    grad_inputs = grad_one + jnp.einsum(
        "tj,cj->tc", grad_projected, wqkv_back, preferred_element_type=jnp.float32
    )
    terms = (
        grad_w_qkv,
        grad_bias_q,
        grad_bias_v,
        grad_w_out,
        grad_bias_out,
        grad_gain_one,
        grad_shift_one,
        grad_w_up,
        grad_bias_up,
        grad_w_down,
        grad_bias_down,
        grad_gain_two,
        grad_shift_two,
    )
    owned = tuple(
        lax.psum_scatter(term.astype(jnp.bfloat16), "wt", scatter_dimension=0, tiled=True)
        for term in terms
    )
    totals = tuple(lax.psum(term, "ctx").astype(jnp.float32) for term in owned)
    return (
        output[None],
        grad_inputs[None],
        totals[0],
        totals[1],
        totals[2],
        totals[3],
        totals[4],
        totals[5],
        totals[6],
        totals[7],
        totals[8],
        totals[9],
        totals[10],
        totals[11],
        totals[12],
    )


def fast_layer(
    tokens,
    pairing,
    w_qkv,
    bias_q,
    bias_v,
    w_out,
    bias_out,
    gain_one,
    shift_one,
    w_up,
    bias_up,
    w_down,
    bias_down,
    gain_two,
    shift_two,
    cotangent,
):
    share = tokens.shape[2] // 4
    vectors = (bias_q, bias_v, bias_out, gain_one, shift_one, bias_down, gain_two, shift_two)
    row = lax.broadcasted_iota(jnp.int32, (8, share), 0)
    small_raw = jnp.zeros((8, share), jnp.bfloat16)
    for index, vector in enumerate(vectors):
        small_raw = jnp.where(row == index, vector[None, :], small_raw)
    made = whole_layer(
        tokens[0],
        cotangent[0],
        pairing,
        small_raw,
        bias_up.reshape(-1, 128),
        w_qkv,
        w_out,
        w_up,
        w_down,
    )
    output, grad_tokens, g_qkv, g_out, g_up, g_down, *small = finish(*made)
    small = [v.reshape(-1) for v in small]
    return (
        output[None],
        grad_tokens[None],
        g_qkv,
        small[0],
        small[1],
        g_out,
        small[2],
        small[3],
        small[4],
        g_up,
        small[8],
        g_down,
        small[5],
        small[6],
        small[7],
    )


def local(tokens, pairing, *rest):
    rows, width = tokens.shape[1:]
    heads = pairing.shape[0]
    inner = rest[7].shape[1]
    fits = (
        lax.axis_size("wt") == 4
        and lax.axis_size("ctx") == 8
        and tokens.shape[0] == 1
        and rows % BAND == 0
        and 3 * rows <= width
        and width % 256 == 0
        and heads % 4 == 0
        and width == 64 * heads
        and inner == 4 * width
    )
    layer = fast_layer if fits else general_layer
    return layer(tokens, pairing, *rest)


def solution(mesh):
    in_specs = (
        P("wt", "ctx", None),
        P(),
        P("wt", None),
        P("wt"),
        P("wt"),
        P("wt", None),
        P("wt"),
        P("wt"),
        P("wt"),
        P("wt", None),
        P("wt"),
        P("wt", None),
        P("wt"),
        P("wt"),
        P("wt"),
        P("wt", "ctx", None),
    )
    out_specs = (
        P("wt", "ctx", None),
        P("wt", "ctx", None),
        P("wt", None),
        P("wt"),
        P("wt"),
        P("wt", None),
        P("wt"),
        P("wt"),
        P("wt"),
        P("wt", None),
        P("wt"),
        P("wt", None),
        P("wt"),
        P("wt"),
        P("wt"),
    )
    return jax.shard_map(local, mesh=mesh, in_specs=in_specs, out_specs=out_specs, check_vma=False)
```
